32 devices in a mesh: shard: 8 (over y, x, core), seq: 4 (over z).
Axes of the slice: x: 2, y: 2, z: 4, core: 2. Of those that a mesh axis runs over, the one named last changes fastest.
Arguments:
- tokens: bfloat16 [9216, 1536], P(('shard', 'seq')), may hold values from -6 to 6
- routes: int32 [9216, 8], P(('shard', 'seq')), may hold values from 0 to 15, all different within a row; in each aligned block of 288 rows (0 to 287, 288 to 575, ...) at most 216 rows name the same one
- w_query: bfloat16 [1536, 1536], P('shard', 'seq'), may hold values from -0.15625 to 0.15625
- key_projection: bfloat16 [1536, 512], P('shard', 'seq'), may hold values from -0.15625 to 0.15625
- value_projection: bfloat16 [1536, 512], P('shard', 'seq'), may hold values from -0.15625 to 0.15625
- w_out: bfloat16 [1536, 1536], P('seq', 'shard'), may hold values from -2.5 to 2.5
- gain_attn: bfloat16 [1536], P(('shard', 'seq')), may hold values from 0.5 to 1.5
- gain_ffn: bfloat16 [1536], P(('shard', 'seq')), may hold values from 0.5 to 1.5
- w_router: bfloat16 [1536, 16], P(('shard', 'seq')), may hold values from -0.078125 to 0.078125
- w_gate: bfloat16 [16, 1536, 512], P('shard'), may hold values from -0.15625 to 0.15625
- w_up: bfloat16 [16, 1536, 512], P('shard'), may hold values from -0.15625 to 0.15625
- w_down: bfloat16 [16, 512, 1536], P('shard'), may hold values from -0.5 to 0.5
- out_grad: bfloat16 [9216, 1536], P(('shard', 'seq')), may hold values from -6 to 6
Outputs:
- output: bfloat16 [9216, 1536], P(('shard', 'seq'))
- grad_tokens: float32 [9216, 1536], P(('shard', 'seq'))
- grad_query: float32 [1536, 1536], P('shard', 'seq')
- grad_key: float32 [1536, 512], P('shard', 'seq')
- grad_value: float32 [1536, 512], P('shard', 'seq')
- grad_out: float32 [1536, 1536], P('seq', 'shard')
- grad_gain_attn: float32 [1536], P(('shard', 'seq'))
- grad_gain_ffn: float32 [1536], P(('shard', 'seq'))
- grad_router: float32 [1536, 16], P(('shard', 'seq'))
- grad_gate: float32 [16, 1536, 512], P('shard', 'seq')
- grad_up: float32 [16, 1536, 512], P('shard', 'seq')
- grad_down: float32 [16, 512, 1536], P('shard', None, 'seq')
The draws below stay inside these ranges and needn't reach their ends.
Inputs may be any that keep to these rules, and one draw needn't show every extreme that they name: `routes`: each row names 8 different experts; among the rows of one device no expert is named by more than 216 rows, and in every draw some expert is named by exactly 216 rows of some device.
All inputs are finite; a program needn't handle non-finite values.
Results may differ from the reference program's by a relative error of at most 0.023.
Values may be sent and summed in bfloat16 or wider, within the bound.
No kernel may reach another device: no remote copies, remote signals or barrier semaphores. Data moves between devices by JAX's collectives and lax.ppermute only.
A program may use at most 320 MiB of HBM per device.

```python
import math
from functools import partial
import jax
import jax.numpy as jnp
import numpy as np
from jax import lax

MODEL_DIMENSION = 1536
QUERY_HEAD_COUNT = 24
KEY_VALUE_HEADS = 8
HEAD_DIMENSION = 64
F = 512
TOP = 8
CONT_LEN = 512
PROMPT_BLK = 128
CONTS = 2
EXPERTS = 16
BLOCK = 1152
PROMPT = 1024
T_DEV = 288
TOKENS = 9216
CAP = 216
N_SHARD = 8


def levels(key, dims, cuts, smallest, top_value):
    loudness, own = 1.0, jax.random.fold_in(key, 6)
    for axis_at, parts in cuts:
        steps = jnp.exp(jax.random.uniform(jax.random.fold_in(own, axis_at), (parts,), jnp.float32, smallest / len(cuts), top_value / len(cuts)))
        loudness = loudness * jnp.repeat(steps, dims[axis_at] // parts).reshape([-1 if axis == axis_at else 1 for axis in range(len(dims))])
    return loudness


def deal_out(rng, own, number, rows, count, top, most, slope):
    sequence = jax.random.permutation(rng, count)
    packed, common = portions_of(count, rows * top, most, slope, True), portions_of(count, rows * top, most, slope, False)
    places = jnp.arange(count)

    def named(tallies, turn):
        used = int((tallies > 0).sum())
        fixed = max(1, used // 4)
        moved = fixed + (places - fixed + turn * (used - fixed)) % max(1, count - fixed)
        return jnp.zeros((count,), jnp.int32).at[sequence[jnp.where(places < fixed, places, moved)]].set(jnp.asarray(tallies, jnp.int32))

    tallies = jnp.where(number % 4 == 0, named(packed, number // 4), named(common, number - number // 4 - 1))
    mixed = jax.random.permutation(jax.random.fold_in(own, 3), count)
    giver, receiver = mixed[0:count // 2 * 2:2], mixed[1:count // 2 * 2:2]
    slack = jnp.minimum(tallies[giver] - 1, most - tallies[receiver]) // 2
    slack = jnp.where((giver == sequence[0]) | (receiver == sequence[0]) | (tallies[receiver] == 0), 0, jnp.maximum(slack, 0))
    moved = jax.random.randint(jax.random.fold_in(own, 4), (count // 2,), 0, 1 << 20) % (slack + 1)
    tallies = tallies.at[giver].add(-moved).at[receiver].add(moved)
    items = jnp.searchsorted(jnp.cumsum(tallies), jnp.arange(rows * top), side="right").astype(jnp.int32)
    table = items.reshape(top, rows).T
    table = table[jax.random.permutation(jax.random.fold_in(own, 1), rows)]
    turn = jax.random.randint(jax.random.fold_in(own, 2), (rows, 1), 0, top)
    return jnp.take_along_axis(table, (jnp.arange(top)[None, :] + turn) % top, axis=1)


def portions_of(number_of, total, limit, lean, full):
    portions = [(1 << 20) // math.isqrt(standing ** lean) + 1 for standing in range(1, number_of + 1)]
    largest = limit if full else min(limit, max(-(-total // number_of), total * portions[0] // sum(portions)))
    least = 1 if total - largest >= number_of - 1 else 0
    counts, rest = [largest] + [least] * (number_of - 1), total - largest - least * (number_of - 1)
    while rest > 0:
        movable = [i for i in range(1, number_of) if counts[i] < largest] or [i for i in range(1, number_of) if counts[i] < limit]
        mass, budget = sum([portions[i] for i in movable]), rest
        for i in movable:
            addition = min(limit - counts[i], max(1, budget * portions[i] // mass), rest)
            counts[i] = counts[i] + addition
            rest = rest - addition
    return np.array(counts)


def bell_draw(rng, shape, spread, reach, split=(), kind=jnp.bfloat16):
    values = spread * jax.random.normal(rng, shape, jnp.float32)
    if split:
        values = values * levels(rng, shape, split, -0.22, 0.18)
    return jnp.clip(values, -reach, reach).astype(kind)


def setup_inputs(seed: int = 0) -> dict:
    splits = jax.random.split(jax.random.key(seed), 14)
    tokens = bell_draw(splits[0], (TOKENS, MODEL_DIMENSION), 1.0, 6.0, ((0, 32),))
    routes_keys = jax.random.split(jax.random.fold_in(splits[1], 1), TOKENS // T_DEV)
    routes_turns = jax.random.permutation(jax.random.fold_in(splits[1], 3), TOKENS // T_DEV)
    routes = jax.vmap(lambda own, number: deal_out(jax.random.fold_in(splits[1], 2), own, number, T_DEV, EXPERTS, TOP, CAP, 2))(routes_keys, routes_turns).reshape((TOKENS, TOP))
    w_query = bell_draw(splits[2], (MODEL_DIMENSION, QUERY_HEAD_COUNT * HEAD_DIMENSION), MODEL_DIMENSION ** -0.5, 0.15625, ((0, 8), (1, 4)))
    key_projection = bell_draw(splits[3], (MODEL_DIMENSION, KEY_VALUE_HEADS * HEAD_DIMENSION), MODEL_DIMENSION ** -0.5, 0.15625, ((0, 8), (1, 4)))
    value_projection = bell_draw(splits[4], (MODEL_DIMENSION, KEY_VALUE_HEADS * HEAD_DIMENSION), MODEL_DIMENSION ** -0.5, 0.15625, ((0, 8), (1, 4)))
    w_out = bell_draw(splits[5], (QUERY_HEAD_COUNT * HEAD_DIMENSION, MODEL_DIMENSION), (max(1, QUERY_HEAD_COUNT * HEAD_DIMENSION // 256)) ** -0.5, 2.5, ((0, 4), (1, 8)))
    gain_attn = jnp.clip(1.0 + 0.1 * jax.random.normal(splits[6], (MODEL_DIMENSION,), jnp.float32), 0.5, 1.5).astype(jnp.bfloat16)
    gain_ffn = jnp.clip(1.0 + 0.1 * jax.random.normal(splits[7], (MODEL_DIMENSION,), jnp.float32), 0.5, 1.5).astype(jnp.bfloat16)
    w_router = bell_draw(splits[8], (MODEL_DIMENSION, EXPERTS), (4 * MODEL_DIMENSION) ** -0.5, 0.078125, ((0, 32),))
    w_gate = bell_draw(splits[9], (EXPERTS, MODEL_DIMENSION, F), MODEL_DIMENSION ** -0.5, 0.15625, ((0, 8),))
    w_up = bell_draw(splits[10], (EXPERTS, MODEL_DIMENSION, F), MODEL_DIMENSION ** -0.5, 0.15625, ((0, 8),))
    w_down = bell_draw(splits[11], (EXPERTS, F, MODEL_DIMENSION), (F // 4) ** -0.5, 0.5, ((0, 8),))
    out_grad = bell_draw(splits[12], (TOKENS, MODEL_DIMENSION), 1.0, 6.0, ((0, 32),))
    return dict(tokens=tokens, routes=routes, w_query=w_query, key_projection=key_projection, value_projection=value_projection, w_out=w_out, gain_attn=gain_attn, gain_ffn=gain_ffn, w_router=w_router, w_gate=w_gate, w_up=w_up, w_down=w_down, out_grad=out_grad)


norm_eps = 1e-05
negative = -1e+30
rope_base = 10000.0
highest = lax.Precision.HIGHEST

@jax.custom_vjp
def low(v):
    return lax.optimization_barrier(v.astype(jnp.bfloat16)).astype(jnp.float32)

@jax.custom_vjp
def low_back(v):
    return v

def low_keep(v):
    return (low(v), None)

def low_pass(kept, grad):
    return (grad,)

def back_keep(v):
    return (v, None)

def back_low(kept, grad):
    return (low(grad),)
low.defvjp(low_keep, low_pass)
low_back.defvjp(back_keep, back_low)

def rms_norm(values, scaling):
    factor = lax.rsqrt(lax.optimization_barrier(jnp.mean(values * values, axis=-1, keepdims=True)) + norm_eps)
    return values * factor * scaling

def rotary_tables(places, head_size):
    half_size = head_size // 2
    frequency = jnp.exp(jnp.arange(half_size, dtype=jnp.float32) * (-2.0 * jnp.log(rope_base) / head_size))
    angles = places.astype(jnp.float32)[:, None] * frequency[None, :]
    return (jnp.cos(angles)[:, None, :], jnp.sin(angles)[:, None, :])

def rotate(values, cosine, sine, head_size):
    total_row_count = values.shape[0]
    by_head = values.reshape(total_row_count, -1, head_size)
    half_size = head_size // 2
    first_half = by_head[..., :half_size]
    second_half = by_head[..., half_size:]
    turned = jnp.concatenate([first_half * cosine - second_half * sine, second_half * cosine + first_half * sine], axis=-1)
    return turned.reshape(total_row_count, -1)

def place_of(within, block_index, prompt_len):
    return jnp.where(within < PROMPT_BLK, block_index * PROMPT_BLK + within, prompt_len + (within - PROMPT_BLK) % CONT_LEN)

def attend(query_matrix, key_matrix_rows, value_matrix_rows, allowed):
    total_row_count = query_matrix.shape[0]
    grouped_heads = query_matrix.reshape(total_row_count, KEY_VALUE_HEADS, QUERY_HEAD_COUNT // KEY_VALUE_HEADS, HEAD_DIMENSION)
    key_head_split = key_matrix_rows.reshape(-1, KEY_VALUE_HEADS, HEAD_DIMENSION)
    value_heads_split = value_matrix_rows.reshape(-1, KEY_VALUE_HEADS, HEAD_DIMENSION)
    scores = jnp.einsum('rhgd,khd->hgrk', grouped_heads, key_head_split, precision=highest) * HEAD_DIMENSION ** (-0.5)
    scores = jnp.where(allowed, low_back(scores), negative)
    probs_low = low(jax.nn.softmax(scores, axis=-1))
    mixed_out = jnp.einsum('hgrk,khd->rhgd', probs_low, value_heads_split, precision=highest)
    return mixed_out.reshape(total_row_count, -1)

def attention(query_rows, key_matrix_rows, value_matrix_rows):

    def blocks(values):
        return values.reshape(N_SHARD, BLOCK, -1)
    prompt_q = blocks(query_rows)[:, :PROMPT_BLK]
    prompt_k = blocks(key_matrix_rows)[:, :PROMPT_BLK].reshape(PROMPT, -1)
    prompt_v = blocks(value_matrix_rows)[:, :PROMPT_BLK].reshape(PROMPT, -1)
    cont_q = blocks(query_rows)[:, PROMPT_BLK:].reshape(N_SHARD * CONTS, CONT_LEN, -1)
    cont_k = blocks(key_matrix_rows)[:, PROMPT_BLK:].reshape(N_SHARD * CONTS, CONT_LEN, -1)
    cont_v = blocks(value_matrix_rows)[:, PROMPT_BLK:].reshape(N_SHARD * CONTS, CONT_LEN, -1)
    key_places = jnp.arange(PROMPT, dtype=jnp.int32)

    def prompt_part(pieces):
        query_matrix, first_place = pieces
        allowed = key_places[None, :] <= first_place + jnp.arange(PROMPT_BLK, dtype=jnp.int32)[:, None]
        return attend(query_matrix, prompt_k, prompt_v, allowed)
    firsts = jnp.arange(N_SHARD, dtype=jnp.int32) * PROMPT_BLK
    prompt_out = lax.map(jax.checkpoint(prompt_part), (prompt_q, firsts))
    wide_places = jnp.arange(PROMPT + CONT_LEN, dtype=jnp.int32)
    cont_allowed = (wide_places[None, :] < PROMPT) | (wide_places[None, :] - PROMPT <= jnp.arange(CONT_LEN, dtype=jnp.int32)[:, None])

    def cont_part(pieces):
        query_matrix, own_keys, own_values = pieces
        return attend(query_matrix, jnp.concatenate([prompt_k, own_keys], axis=0), jnp.concatenate([prompt_v, own_values], axis=0), cont_allowed)
    cont_out = lax.map(jax.checkpoint(cont_part), (cont_q, cont_k, cont_v))
    joined = jnp.concatenate([prompt_out, cont_out.reshape(N_SHARD, CONTS * CONT_LEN, -1)], axis=1)
    return joined.reshape(TOKENS, -1)

def slot_table(routes):
    flat_routes = routes.reshape(TOKENS // T_DEV, T_DEV * TOP)
    expert_hits = (flat_routes[:, :, None] == jnp.arange(EXPERTS, dtype=jnp.int32)[None, None, :]).astype(jnp.int32)
    before = jnp.cumsum(expert_hits, axis=1) - expert_hits
    order_in_expert = lax.optimization_barrier(jnp.sum(before * expert_hits, axis=2))
    return flat_routes * CAP + order_in_expert

def expert_block(gate_weight, up_weight, down_weight, pieces):
    normed_rows, slots, gate_weights = pieces
    slot_rows = jnp.zeros((EXPERTS * CAP, MODEL_DIMENSION), jnp.float32).at[slots].set(jnp.repeat(normed_rows, TOP, axis=0))
    slot_rows = low_back(slot_rows).reshape(EXPERTS, CAP, MODEL_DIMENSION)
    gate_pre = low_back(jnp.einsum('ecd,edf->ecf', slot_rows, gate_weight, precision=highest))
    up_pre = low_back(jnp.einsum('ecd,edf->ecf', slot_rows, up_weight, precision=highest))
    hidden = low(jax.nn.silu(gate_pre) * up_pre)
    result = jnp.einsum('ecf,efd->ecd', hidden, down_weight, precision=highest)
    result = low(low_back(result)).reshape(EXPERTS * CAP, MODEL_DIMENSION)
    taken_rows = result[slots].reshape(T_DEV, TOP, MODEL_DIMENSION)
    return lax.optimization_barrier(jnp.sum(gate_weights[:, :, None] * taken_rows, axis=1))

def reference(tokens, routes, w_query, key_projection, value_projection, w_out, gain_attn, gain_ffn, w_router, w_gate, w_up, w_down, out_grad):
    token_index = jnp.arange(TOKENS, dtype=jnp.int32)
    places = place_of(token_index % BLOCK, token_index // BLOCK, PROMPT)
    cosine, sine = rotary_tables(places, HEAD_DIMENSION)
    slots = slot_table(routes)
    route_mask = (routes[:, :, None] == jnp.arange(EXPERTS, dtype=jnp.int32)[None, None, :]).astype(jnp.float32)

    def forward(inputs, query_weight, key_weight, value_weight, out_weight, first_gain, second_gain, router_weight, gate_weight, up_weight, down_weight):
        normed = low(rms_norm(inputs, first_gain))
        query_rows = low(low_back(rotate(low_back(jnp.dot(normed, query_weight, precision=highest)), cosine, sine, HEAD_DIMENSION)))
        key_matrix_rows = low(low_back(rotate(low_back(jnp.dot(normed, key_weight, precision=highest)), cosine, sine, HEAD_DIMENSION)))
        value_matrix_rows = low(low_back(jnp.dot(normed, value_weight, precision=highest)))
        mixed_out = low(low_back(attention(query_rows, key_matrix_rows, value_matrix_rows)))
        residual = inputs + low_back(jnp.dot(mixed_out, out_weight, precision=highest))
        second_normed = low(rms_norm(residual, second_gain))
        logits = jnp.dot(second_normed, router_weight, precision=highest)
        gate_weights = jax.nn.softmax(lax.optimization_barrier(jnp.sum(route_mask * logits[:, None, :], axis=-1)), axis=-1)
        expert_sum = lax.map(jax.checkpoint(partial(expert_block, gate_weight, up_weight, down_weight)), (second_normed.reshape(-1, T_DEV, MODEL_DIMENSION), slots, gate_weights.reshape(-1, T_DEV, TOP)))
        return residual + expert_sum.reshape(TOKENS, MODEL_DIMENSION)
    output, pullback = jax.vjp(forward, tokens.astype(jnp.float32), w_query.astype(jnp.float32), key_projection.astype(jnp.float32), value_projection.astype(jnp.float32), w_out.astype(jnp.float32), gain_attn.astype(jnp.float32), gain_ffn.astype(jnp.float32), w_router.astype(jnp.float32), w_gate.astype(jnp.float32), w_up.astype(jnp.float32), w_down.astype(jnp.float32))
    grads = pullback(out_grad.astype(jnp.float32))
    return (output.astype(jnp.bfloat16), grads[0], grads[1], grads[2], grads[3], grads[4], grads[5], grads[6], grads[7], grads[8], grads[9], grads[10])
```

```python
import jax
import jax.numpy as jnp
from jax import lax
from jax.sharding import PartitionSpec as P

HEAD_DIMENSION = 64
CONT_LEN = 512
PROMPT_BLK = 128


norm_eps = 1e-05
negative = -1e30
rope_base = 10000.0
highest = lax.Precision.HIGHEST


def rms_norm(values, scaling):
    factor = lax.rsqrt(jnp.mean(values * values, axis=-1, keepdims=True) + norm_eps)
    return values * factor * scaling


def swiglu(gate_pre, up_pre):
    return jax.nn.silu(gate_pre) * up_pre


def softmax_last(values):
    return jax.nn.softmax(values, axis=-1)


def rotary_tables(places, head_size):
    half_size = head_size // 2
    frequency = jnp.exp(
        jnp.arange(half_size, dtype=jnp.float32) * (-2.0 * jnp.log(rope_base) / head_size)
    )
    angles = places.astype(jnp.float32)[:, None] * frequency[None, :]
    return (jnp.cos(angles)[:, None, :], jnp.sin(angles)[:, None, :])


def rotate(values, cosine, sine, head_size):
    total_row_count = values.shape[0]
    by_head = values.reshape(total_row_count, -1, head_size)
    half_size = head_size // 2
    first_half = by_head[..., :half_size]
    second_half = by_head[..., half_size:]
    turned = jnp.concatenate(
        [first_half * cosine - second_half * sine, second_half * cosine + first_half * sine],
        axis=-1,
    )
    return turned.reshape(total_row_count, -1)


def place_of(within, block_index, prompt_len):
    return jnp.where(
        within < PROMPT_BLK,
        block_index * PROMPT_BLK + within,
        prompt_len + (within - PROMPT_BLK) % CONT_LEN,
    )


def times_transposed(left_side, right_side, precision=None):
    return lax.dot_general(
        left_side,
        right_side,
        (((1,), (1,)), ((), ())),
        precision=precision,
        preferred_element_type=jnp.float32,
    )


def transposed_times(left_side, right_side, precision=None):
    return lax.dot_general(
        left_side,
        right_side,
        (((0,), (0,)), ((), ())),
        precision=precision,
        preferred_element_type=jnp.float32,
    )


def head_scores(query_matrix, key_matrix_rows, allowed, head_size):
    total_row_count = query_matrix.shape[0]
    kv_heads = key_matrix_rows.shape[1] // head_size
    grouped_heads = query_matrix.reshape(total_row_count, kv_heads, -1, head_size)
    key_head_split = key_matrix_rows.reshape(key_matrix_rows.shape[0], kv_heads, head_size)
    scores = jnp.einsum(
        "rhgd,khd->hgrk", grouped_heads, key_head_split, preferred_element_type=jnp.float32
    ) * head_size ** (-0.5)
    return jnp.where(allowed, scores, negative)


def attend_forward(query_matrix, key_matrix_rows, value_matrix_rows, allowed, head_size):
    scores = head_scores(query_matrix, key_matrix_rows, allowed, head_size)
    row_max = jnp.max(scores, axis=-1, keepdims=True)
    weights = jnp.exp(scores - row_max)
    row_total = jnp.sum(weights, axis=-1, keepdims=True)
    probs_low = (weights / row_total).astype(jnp.bfloat16)
    kv_heads = key_matrix_rows.shape[1] // head_size
    value_heads_split = value_matrix_rows.reshape(value_matrix_rows.shape[0], kv_heads, head_size)
    mixed_out = jnp.einsum(
        "hgrk,khd->rhgd", probs_low, value_heads_split, preferred_element_type=jnp.float32
    )
    return (mixed_out.reshape(query_matrix.shape[0], -1), row_max + jnp.log(row_total))


def attend_backward(
    query_matrix, key_matrix_rows, value_matrix_rows, allowed, log_total, mixed_grad, head_size
):
    total_row_count = query_matrix.shape[0]
    kv_heads = key_matrix_rows.shape[1] // head_size
    scores = head_scores(query_matrix, key_matrix_rows, allowed, head_size)
    probs = jnp.exp(scores - log_total)
    value_heads_split = value_matrix_rows.reshape(-1, kv_heads, head_size)
    key_head_split = key_matrix_rows.reshape(-1, kv_heads, head_size)
    grouped_heads = query_matrix.reshape(total_row_count, kv_heads, -1, head_size)
    grad_grouped = mixed_grad.reshape(total_row_count, kv_heads, -1, head_size)
    prob_grad = jnp.einsum(
        "rhgd,khd->hgrk", grad_grouped, value_heads_split, preferred_element_type=jnp.float32
    )
    inner_sum = jnp.sum(probs * prob_grad, axis=-1, keepdims=True)
    score_grad = (probs * (prob_grad - inner_sum)).astype(jnp.bfloat16)
    score_scale = head_size ** (-0.5)
    query_grad = (
        jnp.einsum("hgrk,khd->rhgd", score_grad, key_head_split, preferred_element_type=jnp.float32)
        * score_scale
    )
    key_grad = (
        jnp.einsum("hgrk,rhgd->khd", score_grad, grouped_heads, preferred_element_type=jnp.float32)
        * score_scale
    )
    value_grad = jnp.einsum(
        "hgrk,rhgd->khd",
        probs.astype(jnp.bfloat16),
        grad_grouped,
        preferred_element_type=jnp.float32,
    )
    return (
        query_grad.reshape(total_row_count, -1),
        key_grad.reshape(key_matrix_rows.shape[0], -1),
        value_grad.reshape(value_matrix_rows.shape[0], -1),
    )


def rms_parts(values):
    return lax.rsqrt(jnp.mean(values * values, axis=-1, keepdims=True) + norm_eps)


def rms_backward(values, factor, scaling, normed_grad):
    scaled = scaling * normed_grad
    inner = jnp.mean(scaled * values, axis=-1, keepdims=True)
    values_grad = factor * scaled - values * (factor * factor * factor) * inner
    gain_grad = jnp.sum(normed_grad * values * factor, axis=0)
    return values_grad, gain_grad


def matmul(left_side, right_side):
    return jnp.dot(left_side, right_side, preferred_element_type=jnp.float32)


def on_device(
    tokens,
    routes,
    w_query,
    key_projection,
    value_projection,
    w_out,
    gain_attn,
    gain_ffn,
    w_router,
    w_gate,
    w_up,
    w_down,
    out_grad,
):
    bf16 = jnp.bfloat16
    shard_count = lax.axis_size("shard")
    seq_count = lax.axis_size("seq")
    shard_index = lax.axis_index("shard")
    seq_index = lax.axis_index("seq")
    tok_count, model_width = tokens.shape
    top_count = routes.shape[1]
    experts_all = w_router.shape[1]
    local_experts = w_gate.shape[0]
    block_len = tok_count * seq_count
    prompt_len = PROMPT_BLK * shard_count
    query_width = w_query.shape[1]
    key_width = key_projection.shape[1]

    small = jnp.concatenate([w_router, gain_attn[:, None], gain_ffn[:, None]], axis=1)
    small = lax.all_gather(small, "seq", axis=0, tiled=True)
    small = lax.all_gather(small, "shard", axis=0, tiled=True)
    router_weight = small[:, :experts_all]
    first_gain = small[:, experts_all].astype(jnp.float32)
    second_gain = small[:, experts_all + 1].astype(jnp.float32)
    block_tokens = lax.all_gather(tokens, "seq", axis=0, tiled=True)
    qkv_weight = lax.all_gather(
        jnp.concatenate([w_query, key_projection, value_projection], axis=1),
        "shard",
        axis=0,
        tiled=True,
    )
    out_weight = lax.all_gather(w_out, "seq", axis=0, tiled=True)
    out_weight = lax.all_gather(out_weight, "shard", axis=1, tiled=True)
    plane_grads = lax.all_gather(out_grad, "shard", axis=0, tiled=True)

    block_rows = jnp.arange(block_len, dtype=jnp.int32)
    cos_table, sin_table = rotary_tables(
        place_of(block_rows, shard_index, prompt_len), HEAD_DIMENSION
    )
    inputs = block_tokens.astype(jnp.float32)
    first_factor = rms_parts(inputs)
    normed_low = (inputs * first_factor * first_gain).astype(bf16)
    lin = matmul(normed_low, qkv_weight)
    query_heads = rotate(lin[:, :query_width], cos_table, sin_table, HEAD_DIMENSION).astype(bf16)
    key_heads = rotate(
        lin[:, query_width : query_width + key_width], cos_table, sin_table, HEAD_DIMENSION
    ).astype(bf16)
    value_heads = lin[:, query_width + key_width :].astype(bf16)
    prompt_both = lax.all_gather(
        jnp.concatenate([key_heads[:PROMPT_BLK], value_heads[:PROMPT_BLK]], axis=1),
        "shard",
        axis=0,
        tiled=True,
    )
    prompt_keys = prompt_both[:, :key_width]
    prompt_values = prompt_both[:, key_width:]
    key_places = jnp.arange(prompt_len, dtype=jnp.int32)
    prompt_allowed = (
        key_places[None, :]
        <= shard_index * PROMPT_BLK + jnp.arange(PROMPT_BLK, dtype=jnp.int32)[:, None]
    )
    wide_places = jnp.arange(prompt_len + CONT_LEN, dtype=jnp.int32)
    cont_allowed = (wide_places[None, :] < prompt_len) | (
        wide_places[None, :] - prompt_len <= jnp.arange(CONT_LEN, dtype=jnp.int32)[:, None]
    )
    cont_count = (block_len - PROMPT_BLK) // CONT_LEN
    mixed_piece, prompt_level = attend_forward(
        query_heads[:PROMPT_BLK], prompt_keys, prompt_values, prompt_allowed, HEAD_DIMENSION
    )
    mixed_parts = [mixed_piece]
    cont_levels = []
    cont_keys = []
    cont_values = []
    for number in range(cont_count):
        first_row = PROMPT_BLK + number * CONT_LEN
        last_row = first_row + CONT_LEN
        keys_all = jnp.concatenate([prompt_keys, key_heads[first_row:last_row]], axis=0)
        values_all = jnp.concatenate([prompt_values, value_heads[first_row:last_row]], axis=0)
        mixed_piece, cont_level = attend_forward(
            query_heads[first_row:last_row], keys_all, values_all, cont_allowed, HEAD_DIMENSION
        )
        mixed_parts.append(mixed_piece)
        cont_levels.append(cont_level)
        cont_keys.append(keys_all)
        cont_values.append(values_all)
    mixed_heads = jnp.concatenate(mixed_parts, axis=0).astype(bf16)
    mixed_tokens = lax.all_to_all(mixed_heads, "seq", split_axis=0, concat_axis=1, tiled=True)

    own_inputs = tokens.astype(jnp.float32)
    upstream = out_grad.astype(jnp.float32)
    residual = own_inputs + matmul(mixed_tokens, out_weight)
    second_factor = rms_parts(residual)
    second_low = (residual * second_factor * second_gain).astype(bf16)
    logits = matmul(second_low, router_weight)
    chosen = routes[:, :, None] == jnp.arange(experts_all, dtype=jnp.int32)[None, None, :]
    named = jnp.any(chosen, axis=1)
    gate_dense = jax.nn.softmax(jnp.where(named, logits, negative), axis=-1)
    gate_dense = jnp.where(named, gate_dense, 0.0)

    plane_rows = lax.all_gather(second_low, "shard", axis=0, tiled=True)
    plane_gates = lax.all_gather(gate_dense, "shard", axis=0, tiled=True)
    local_gates = lax.dynamic_slice_in_dim(
        plane_gates, shard_index * local_experts, local_experts, axis=1
    )
    expert_gates = local_gates.T[:, :, None]
    gate_pre = jnp.einsum("td,edf->etf", plane_rows, w_gate, preferred_element_type=jnp.float32)
    up_pre = jnp.einsum("td,edf->etf", plane_rows, w_up, preferred_element_type=jnp.float32)
    down_grad = jnp.einsum("td,efd->etf", plane_grads, w_down, preferred_element_type=jnp.float32)
    sigmoid = jax.nn.sigmoid(gate_pre)
    silu = gate_pre * sigmoid
    hidden = silu * up_pre
    gate_grad = jnp.sum(hidden * down_grad, axis=-1)
    hidden_low = (expert_gates * hidden).astype(bf16)
    hidden_grad = expert_gates * down_grad
    gate_pre_low = (hidden_grad * up_pre * sigmoid * (1.0 + gate_pre * (1.0 - sigmoid))).astype(bf16)
    up_pre_low = (hidden_grad * silu).astype(bf16)
    grad_down = jnp.einsum(
        "td,etf->edf", plane_grads, hidden_low, preferred_element_type=jnp.float32
    ).astype(bf16)
    grad_gate = jnp.einsum(
        "td,etf->edf", plane_rows, gate_pre_low, preferred_element_type=jnp.float32
    ).astype(bf16)
    grad_up = jnp.einsum(
        "td,etf->edf", plane_rows, up_pre_low, preferred_element_type=jnp.float32
    ).astype(bf16)
    row_part = (
        jnp.einsum("etf,edf->td", gate_pre_low, w_gate, preferred_element_type=jnp.float32)
        + jnp.einsum("etf,edf->td", up_pre_low, w_up, preferred_element_type=jnp.float32)
    ).astype(bf16)
    out_part = jnp.einsum(
        "etf,efd->td", hidden_low, w_down, preferred_element_type=jnp.float32
    ).astype(bf16)
    row_grad = lax.psum_scatter(row_part, "shard", scatter_dimension=0, tiled=True)
    gate_back = lax.all_to_all(
        gate_grad.reshape(local_experts, shard_count, tok_count).transpose(1, 0, 2),
        "shard",
        split_axis=0,
        concat_axis=0,
        tiled=True,
    )
    expert_sum = lax.psum_scatter(out_part, "shard", scatter_dimension=0, tiled=True)
    output = (residual + expert_sum.astype(jnp.float32)).astype(bf16)
    gate_grad_dense = gate_back.reshape(experts_all, tok_count).T
    weighted = gate_dense * gate_grad_dense
    logit_grad = weighted - gate_dense * jnp.sum(weighted, axis=-1, keepdims=True)
    grad_router = transposed_times(second_low.astype(jnp.float32), logit_grad, highest)
    second_grad = row_grad.astype(jnp.float32) + times_transposed(
        logit_grad, router_weight.astype(jnp.float32), highest
    )
    residual_part, grad_gain_ffn = rms_backward(residual, second_factor, second_gain, second_grad)
    residual_grad = upstream + residual_part
    residual_low = residual_grad.astype(bf16)
    mixed_grad_tokens = times_transposed(residual_low, out_weight).astype(bf16)
    mixed_grad = lax.all_to_all(mixed_grad_tokens, "seq", split_axis=1, concat_axis=0, tiled=True)
    whole_out = transposed_times(residual_low, mixed_tokens).astype(bf16)
    grad_out = lax.psum_scatter(whole_out, "shard", scatter_dimension=0, tiled=True)
    grad_out = lax.psum_scatter(grad_out, "seq", scatter_dimension=1, tiled=True)
    grad_out = grad_out.T.astype(jnp.float32)

    query_piece, prompt_key_grad, prompt_value_grad = attend_backward(
        query_heads[:PROMPT_BLK],
        prompt_keys,
        prompt_values,
        prompt_allowed,
        prompt_level,
        mixed_grad[:PROMPT_BLK],
        HEAD_DIMENSION,
    )
    query_parts = [query_piece]
    self_key_grads = []
    self_value_grads = []
    for number in range(cont_count):
        first_row = PROMPT_BLK + number * CONT_LEN
        last_row = first_row + CONT_LEN
        query_piece, key_piece, value_piece = attend_backward(
            query_heads[first_row:last_row],
            cont_keys[number],
            cont_values[number],
            cont_allowed,
            cont_levels[number],
            mixed_grad[first_row:last_row],
            HEAD_DIMENSION,
        )
        query_parts.append(query_piece)
        prompt_key_grad = prompt_key_grad + key_piece[:prompt_len]
        prompt_value_grad = prompt_value_grad + value_piece[:prompt_len]
        self_key_grads.append(key_piece[prompt_len:])
        self_value_grads.append(value_piece[prompt_len:])
    own_prompt = lax.psum_scatter(
        jnp.concatenate([prompt_key_grad, prompt_value_grad], axis=1).astype(bf16),
        "shard",
        scatter_dimension=0,
        tiled=True,
    ).astype(jnp.float32)
    query_grad = jnp.concatenate(query_parts, axis=0)
    key_grad = jnp.concatenate([own_prompt[:, :key_width]] + self_key_grads, axis=0)
    value_low = jnp.concatenate([own_prompt[:, key_width:]] + self_value_grads, axis=0).astype(bf16)
    lin_query = rotate(query_grad, cos_table, -sin_table, HEAD_DIMENSION).astype(bf16)
    lin_key = rotate(key_grad, cos_table, -sin_table, HEAD_DIMENSION).astype(bf16)
    lin_all = jnp.concatenate([lin_query, lin_key, value_low], axis=1)
    normed_part = times_transposed(lin_all, qkv_weight)
    normed_grad = lax.psum_scatter(
        normed_part.astype(bf16), "seq", scatter_dimension=0, tiled=True
    ).astype(jnp.float32)
    grad_qkv = lax.psum_scatter(
        transposed_times(normed_low, lin_all).astype(bf16),
        "shard",
        scatter_dimension=0,
        tiled=True,
    ).astype(jnp.float32)
    grad_query = grad_qkv[:, :query_width]
    grad_key = grad_qkv[:, query_width : query_width + key_width]
    grad_value = grad_qkv[:, query_width + key_width :]
    gain_part = jnp.sum(normed_part * inputs * first_factor, axis=0)
    own_factor = rms_parts(own_inputs)
    input_part, _ = rms_backward(own_inputs, own_factor, first_gain, normed_grad)
    tokens_grad = residual_grad + input_part
    small_grad = jnp.concatenate(
        [grad_router, gain_part[:, None], grad_gain_ffn[:, None]], axis=1
    ).astype(bf16)
    small_grad = lax.psum_scatter(small_grad, "shard", scatter_dimension=0, tiled=True)
    small_grad = lax.psum_scatter(small_grad, "seq", scatter_dimension=0, tiled=True)
    small_grad = small_grad.astype(jnp.float32)
    grad_gate = lax.psum_scatter(grad_gate, "seq", scatter_dimension=1, tiled=True)
    grad_up = lax.psum_scatter(grad_up, "seq", scatter_dimension=1, tiled=True)
    grad_down = lax.psum_scatter(grad_down, "seq", scatter_dimension=1, tiled=True)
    return (
        output,
        tokens_grad,
        grad_query,
        grad_key,
        grad_value,
        grad_out,
        small_grad[:, experts_all],
        small_grad[:, experts_all + 1],
        small_grad[:, :experts_all],
        grad_gate.astype(jnp.float32),
        grad_up.astype(jnp.float32),
        grad_down.transpose(0, 2, 1).astype(jnp.float32),
    )


def solution(mesh):
    return jax.shard_map(
        on_device,
        mesh=mesh,
        in_specs=(
            P(("shard", "seq"), None),
            P(("shard", "seq"), None),
            P("shard", "seq"),
            P("shard", "seq"),
            P("shard", "seq"),
            P("seq", "shard"),
            P(("shard", "seq")),
            P(("shard", "seq")),
            P(("shard", "seq"), None),
            P("shard", None, None),
            P("shard", None, None),
            P("shard", None, None),
            P(("shard", "seq"), None),
        ),
        out_specs=(
            P(("shard", "seq"), None),
            P(("shard", "seq"), None),
            P("shard", "seq"),
            P("shard", "seq"),
            P("shard", "seq"),
            P("seq", "shard"),
            P(("shard", "seq")),
            P(("shard", "seq")),
            P(("shard", "seq"), None),
            P("shard", "seq", None),
            P("shard", "seq", None),
            P("shard", None, "seq"),
        ),
        check_vma=False,
    )
```

```python
from functools import partial

import jax
import jax.numpy as jnp
from jax import lax
from jax.experimental import pallas as pl
from jax.experimental.pallas import tpu as pltpu
from jax.sharding import PartitionSpec as P

HEAD_DIMENSION = 64
CONT_LEN = 512
PROMPT_BLK = 128


norm_eps = 1e-05
negative = -1e30
rope_base = 10000.0
highest = lax.Precision.HIGHEST


def rms_norm(values, scaling):
    factor = lax.rsqrt(jnp.mean(values * values, axis=-1, keepdims=True) + norm_eps)
    return values * factor * scaling


def swiglu(gate_pre, up_pre):
    return jax.nn.silu(gate_pre) * up_pre


def softmax_last(values):
    return jax.nn.softmax(values, axis=-1)


def rotary_tables(places, head_size):
    half_size = head_size // 2
    frequency = jnp.exp(
        jnp.arange(half_size, dtype=jnp.float32) * (-2.0 * jnp.log(rope_base) / head_size)
    )
    angles = places.astype(jnp.float32)[:, None] * frequency[None, :]
    return (jnp.cos(angles)[:, None, :], jnp.sin(angles)[:, None, :])


def rotate(values, cosine, sine, head_size):
    total_row_count = values.shape[0]
    by_head = values.reshape(total_row_count, -1, head_size)
    half_size = head_size // 2
    first_half = by_head[..., :half_size]
    second_half = by_head[..., half_size:]
    turned = jnp.concatenate(
        [first_half * cosine - second_half * sine, second_half * cosine + first_half * sine],
        axis=-1,
    )
    return turned.reshape(total_row_count, -1)


def place_of(within, block_index, prompt_len):
    return jnp.where(
        within < PROMPT_BLK,
        block_index * PROMPT_BLK + within,
        prompt_len + (within - PROMPT_BLK) % CONT_LEN,
    )


def times_transposed(left_side, right_side, precision=None):
    return lax.dot_general(
        left_side,
        right_side,
        (((1,), (1,)), ((), ())),
        precision=precision,
        preferred_element_type=jnp.float32,
    )


def transposed_times(left_side, right_side, precision=None):
    return lax.dot_general(
        left_side,
        right_side,
        (((0,), (0,)), ((), ())),
        precision=precision,
        preferred_element_type=jnp.float32,
    )


def head_scores(query_matrix, key_matrix_rows, allowed, head_size):
    total_row_count = query_matrix.shape[0]
    kv_heads = key_matrix_rows.shape[1] // head_size
    grouped_heads = query_matrix.reshape(total_row_count, kv_heads, -1, head_size)
    key_head_split = key_matrix_rows.reshape(key_matrix_rows.shape[0], kv_heads, head_size)
    scores = jnp.einsum(
        "rhgd,khd->hgrk", grouped_heads, key_head_split, preferred_element_type=jnp.float32
    ) * head_size ** (-0.5)
    return jnp.where(allowed, scores, negative)


def attend_forward(query_matrix, key_matrix_rows, value_matrix_rows, allowed, head_size):
    scores = head_scores(query_matrix, key_matrix_rows, allowed, head_size)
    row_max = jnp.max(scores, axis=-1, keepdims=True)
    weights = jnp.exp(scores - row_max)
    row_total = jnp.sum(weights, axis=-1, keepdims=True)
    probs_low = (weights / row_total).astype(jnp.bfloat16)
    kv_heads = key_matrix_rows.shape[1] // head_size
    value_heads_split = value_matrix_rows.reshape(value_matrix_rows.shape[0], kv_heads, head_size)
    mixed_out = jnp.einsum(
        "hgrk,khd->rhgd", probs_low, value_heads_split, preferred_element_type=jnp.float32
    )
    return (mixed_out.reshape(query_matrix.shape[0], -1), row_max + jnp.log(row_total))


def attend_backward(
    query_matrix, key_matrix_rows, value_matrix_rows, allowed, log_total, mixed_grad, head_size
):
    total_row_count = query_matrix.shape[0]
    kv_heads = key_matrix_rows.shape[1] // head_size
    scores = head_scores(query_matrix, key_matrix_rows, allowed, head_size)
    probs = jnp.exp(scores - log_total)
    value_heads_split = value_matrix_rows.reshape(-1, kv_heads, head_size)
    key_head_split = key_matrix_rows.reshape(-1, kv_heads, head_size)
    grouped_heads = query_matrix.reshape(total_row_count, kv_heads, -1, head_size)
    grad_grouped = mixed_grad.reshape(total_row_count, kv_heads, -1, head_size)
    prob_grad = jnp.einsum(
        "rhgd,khd->hgrk", grad_grouped, value_heads_split, preferred_element_type=jnp.float32
    )
    inner_sum = jnp.sum(probs * prob_grad, axis=-1, keepdims=True)
    score_grad = (probs * (prob_grad - inner_sum)).astype(jnp.bfloat16)
    score_scale = head_size ** (-0.5)
    query_grad = (
        jnp.einsum("hgrk,khd->rhgd", score_grad, key_head_split, preferred_element_type=jnp.float32)
        * score_scale
    )
    key_grad = (
        jnp.einsum("hgrk,rhgd->khd", score_grad, grouped_heads, preferred_element_type=jnp.float32)
        * score_scale
    )
    value_grad = jnp.einsum(
        "hgrk,rhgd->khd",
        probs.astype(jnp.bfloat16),
        grad_grouped,
        preferred_element_type=jnp.float32,
    )
    return (
        query_grad.reshape(total_row_count, -1),
        key_grad.reshape(key_matrix_rows.shape[0], -1),
        value_grad.reshape(value_matrix_rows.shape[0], -1),
    )


def rms_parts(values):
    return lax.rsqrt(jnp.mean(values * values, axis=-1, keepdims=True) + norm_eps)


def rms_backward(values, factor, scaling, normed_grad):
    scaled = scaling * normed_grad
    inner = jnp.mean(scaled * values, axis=-1, keepdims=True)
    values_grad = factor * scaled - values * (factor * factor * factor) * inner
    gain_grad = jnp.sum(normed_grad * values * factor, axis=0)
    return values_grad, gain_grad


def matmul(left_side, right_side):
    return jnp.dot(left_side, right_side, preferred_element_type=jnp.float32)


LANES = 128


def exchange(values, axis_name, bit):
    count = lax.axis_size(axis_name)
    return lax.ppermute(values, axis_name, [(i, i ^ bit) for i in range(count)])


def bits_of(number):
    return [1 << k for k in range(number.bit_length()) if number >> k & 1]


def gather_blocks(own, axis_name):
    count = lax.axis_size(axis_name)
    half = own.shape[0] // 2
    blocks = {0: own}
    even = sorted(range(2, count, 2), key=lambda j: (len(bits_of(j)), j))
    if count > 1:
        blocks[1] = exchange(own, axis_name, 1)
    for j in even:
        bits = bits_of(j)
        if len(bits) == 1:
            blocks[j] = exchange(own, axis_name, j)
        else:
            low_bit, high_bit = bits[0], bits[-1]
            top = exchange(blocks[j ^ low_bit][:half], axis_name, low_bit)
            bottom = exchange(blocks[j ^ high_bit][half:], axis_name, high_bit)
            blocks[j] = jnp.concatenate([top, bottom], axis=0)
        blocks[j + 1] = exchange(blocks[j], axis_name, 1)
    return [blocks[j] for j in range(count)]


def add_rounded(left_side, right_side):
    return (left_side.astype(jnp.float32) + right_side.astype(jnp.float32)).astype(jnp.bfloat16)


def reduce_blocks(blocks, axis_name):
    count = lax.axis_size(axis_name)
    half = blocks[0].shape[0] // 2
    sums = {}
    for j in sorted(range(0, count, 2), key=lambda j: (-len(bits_of(j)), j)):
        arrived = exchange(blocks[j + 1], axis_name, 1)
        sums[j] = [
            add_rounded(blocks[j][:half], arrived[:half]),
            add_rounded(blocks[j][half:], arrived[half:]),
        ]
    extra = [[], []]
    for j in sorted(range(2, count, 2), key=lambda j: (-len(bits_of(j)), j)):
        bits = bits_of(j)
        if len(bits) > 1:
            low_bit, high_bit = bits[0], bits[-1]
            top = exchange(sums[j][0], axis_name, low_bit)
            bottom = exchange(sums[j][1], axis_name, high_bit)
            sums[j ^ low_bit][0] = add_rounded(sums[j ^ low_bit][0], top)
            sums[j ^ high_bit][1] = add_rounded(sums[j ^ high_bit][1], bottom)
        else:
            extra[0].append(exchange(sums[j][0], axis_name, j))
            extra[1].append(exchange(sums[j][1], axis_name, j))
    halves = []
    for part in range(2):
        total = sums[0][part].astype(jnp.float32)
        for piece in extra[part]:
            total = total + piece.astype(jnp.float32)
        halves.append(total)
    return jnp.concatenate(halves, axis=0)


def in_order(blocks, index):
    stacked = jnp.stack(blocks)
    return jnp.concatenate(
        [lax.dynamic_index_in_dim(stacked, j ^ index, 0, keepdims=True) for j in range(len(blocks))],
        axis=0,
    )


def relative_blocks(values, index, count):
    rows = values.shape[0] // count
    return [
        lax.dynamic_slice_in_dim(values, (index ^ j) * rows, rows, axis=0) for j in range(count)
    ]


def scatter_direct(pieces, axis_name):
    count = lax.axis_size(axis_name)
    index = lax.axis_index(axis_name)
    total = lax.dynamic_index_in_dim(pieces, index, 0, keepdims=False).astype(jnp.float32)
    for step in range(1, count):
        piece = lax.dynamic_index_in_dim(pieces, (index + step) % count, 0, keepdims=False)
        arrived = lax.ppermute(piece, axis_name, [(i, (i + step) % count) for i in range(count)])
        total = total + arrived.astype(jnp.float32)
    return total


def expert_body(
    experts_all, index_ref, x_even, x_odd, og_even, og_odd, gate_w, up_w, down_w, *rest
):
    (x_all, og_all, pre_all, hid_all, row_even, row_odd, out_even, out_odd) = rest[-12:-4]
    (row_acc, out_acc, back_acc, _) = rest[-4:]
    expert = pl.program_id(0)
    last = pl.num_programs(0) - 1
    rows = x_even.shape[0]
    width = x_all.shape[1]
    hidden_units = gate_w.shape[2]
    nt_dims = (((1,), (1,)), ((), ()))

    @pl.when(expert == 0)
    def _():
        x_all[:rows, :] = x_even[:, :width]
        x_all[rows:, :] = x_odd[:, :width]
        og_all[:rows, :] = og_even[...]
        og_all[rows:, :] = og_odd[...]

    column = index_ref[0] + expert
    lane = lax.broadcasted_iota(jnp.int32, (2 * rows, LANES), 1)
    coded = jnp.concatenate([x_even[:, width:], x_odd[:, width:]], axis=0).astype(jnp.float32)
    gate = jnp.sum(
        jnp.where((lane == column) | (lane == column + experts_all), coded, 0.0),
        axis=1,
        keepdims=True,
    )
    x_rows = x_all[...]
    og_rows = og_all[...]
    gate_pre = jnp.dot(x_rows, gate_w[0], preferred_element_type=jnp.float32)
    up_pre = jnp.dot(x_rows, up_w[0], preferred_element_type=jnp.float32)
    down_grad = lax.dot_general(og_rows, down_w[0], nt_dims, preferred_element_type=jnp.float32)
    sigmoid = 1.0 / (1.0 + jnp.exp(-gate_pre))
    silu = gate_pre * sigmoid
    hidden = silu * up_pre
    gate_back = jnp.sum(hidden * down_grad, axis=1, keepdims=True)
    hidden_low = (gate * hidden).astype(jnp.bfloat16)
    hidden_grad = gate * down_grad
    gate_pre_low = (
        hidden_grad * up_pre * sigmoid * (1.0 + gate_pre * (1.0 - sigmoid))
    ).astype(jnp.bfloat16)
    up_pre_low = (hidden_grad * silu).astype(jnp.bfloat16)
    hid_all[...] = hidden_low
    pre_all[0, :, :hidden_units] = gate_pre_low
    pre_all[0, :, hidden_units:] = up_pre_low
    row = lax.dot_general(
        gate_pre_low, gate_w[0], nt_dims, preferred_element_type=jnp.float32
    ) + lax.dot_general(up_pre_low, up_w[0], nt_dims, preferred_element_type=jnp.float32)
    out = jnp.dot(hidden_low, down_w[0], preferred_element_type=jnp.float32)
    high = gate_back.astype(jnp.bfloat16).astype(jnp.float32)
    back = jnp.where(lane == column, high, 0.0) + jnp.where(
        lane == column + experts_all, gate_back - high, 0.0
    )

    @pl.when(expert == 0)
    def _():
        row_acc[...] = row
        out_acc[...] = out
        back_acc[...] = back

    @pl.when(expert > 0)
    def _():
        row_acc[...] += row
        out_acc[...] += out
        back_acc[...] += back

    @pl.when(expert == last)
    def _():
        for ref, first in ((row_even, 0), (row_odd, rows)):
            ref[:, :width] = row_acc[first : first + rows, :].astype(jnp.bfloat16)
            ref[:, width:] = back_acc[first : first + rows, :].astype(jnp.bfloat16)
        out_even[...] = out_acc[:rows, :].astype(jnp.bfloat16)
        out_odd[...] = out_acc[rows:, :].astype(jnp.bfloat16)


def expert_pair(position, pairs, first_expert, experts_all, x_pair, og_pair, weights, carried):
    w_gate, w_up, w_down = weights
    rows, coded_width = x_pair[0].shape
    width = coded_width - LANES
    local_experts, _, hidden_units = w_gate.shape
    bf16 = jnp.bfloat16
    whole = 2 * rows
    fixed = lambda e, i: (0, 0)
    once = pl.Buffered(1)
    in_specs = (
        [pl.BlockSpec((rows, coded_width), fixed, pipeline_mode=once)] * 2
        + [pl.BlockSpec((rows, width), fixed, pipeline_mode=once)] * 2
        + [pl.BlockSpec((1, width, hidden_units), lambda e, i: (e, 0, 0))] * 2
        + [pl.BlockSpec((1, hidden_units, width), lambda e, i: (e, 0, 0))]
    )
    operands = [*x_pair, *og_pair, w_gate, w_up, w_down]
    aliases = {}
    if carried is not None:
        in_specs = in_specs + [pl.BlockSpec(memory_space=pl.ANY)] * 4
        aliases = {1 + len(operands) + k: k for k in range(4)}
        operands = operands + list(carried)
    out_shape = [
        jax.ShapeDtypeStruct((pairs * whole, width), bf16),
        jax.ShapeDtypeStruct((pairs * whole, width), bf16),
        jax.ShapeDtypeStruct((local_experts, pairs * whole, 2 * hidden_units), bf16),
        jax.ShapeDtypeStruct((pairs * whole, local_experts * hidden_units), bf16),
        jax.ShapeDtypeStruct((rows, coded_width), bf16),
        jax.ShapeDtypeStruct((rows, coded_width), bf16),
        jax.ShapeDtypeStruct((rows, width), bf16),
        jax.ShapeDtypeStruct((rows, width), bf16),
    ]
    out_specs = [
        pl.BlockSpec((whole, width), lambda e, i: (position, 0)),
        pl.BlockSpec((whole, width), lambda e, i: (position, 0)),
        pl.BlockSpec((1, whole, 2 * hidden_units), lambda e, i: (e, position, 0)),
        pl.BlockSpec((whole, hidden_units), lambda e, i: (position, e)),
        pl.BlockSpec((rows, coded_width), fixed),
        pl.BlockSpec((rows, coded_width), fixed),
        pl.BlockSpec((rows, width), fixed),
        pl.BlockSpec((rows, width), fixed),
    ]
    products = 2 * whole * width * hidden_units * local_experts
    results = pl.pallas_call(
        partial(expert_body, experts_all),
        out_shape=out_shape,
        grid_spec=pltpu.PrefetchScalarGridSpec(
            num_scalar_prefetch=1,
            grid=(local_experts,),
            in_specs=in_specs,
            out_specs=out_specs,
            scratch_shapes=[
                pltpu.VMEM((whole, width), jnp.float32),
                pltpu.VMEM((whole, width), jnp.float32),
                pltpu.VMEM((whole, LANES), jnp.float32),
                pltpu.VMEM((8, LANES), jnp.float32),
            ],
        ),
        input_output_aliases=aliases,
        compiler_params=pltpu.CompilerParams(
            dimension_semantics=("arbitrary",), vmem_limit_bytes=60 * 1024 * 1024
        ),
        cost_estimate=pl.CostEstimate(
            flops=6 * products,
            bytes_accessed=3 * 2 * local_experts * width * hidden_units + 20 * whole * width,
            transcendentals=whole * hidden_units * local_experts,
        ),
        name="experts",
    )(first_expert, *operands)
    return results[:4], results[4:]


def on_device(
    tokens,
    routes,
    w_query,
    key_projection,
    value_projection,
    w_out,
    gain_attn,
    gain_ffn,
    w_router,
    w_gate,
    w_up,
    w_down,
    out_grad,
):
    bf16 = jnp.bfloat16
    shard_count = lax.axis_size("shard")
    seq_count = lax.axis_size("seq")
    shard_index = lax.axis_index("shard")
    seq_index = lax.axis_index("seq")
    tok_count, model_width = tokens.shape
    top_count = routes.shape[1]
    experts_all = w_router.shape[1]
    local_experts = w_gate.shape[0]
    block_len = tok_count * seq_count
    prompt_len = PROMPT_BLK * shard_count
    query_width = w_query.shape[1]
    key_width = key_projection.shape[1]

    small = jnp.concatenate([w_router, gain_attn[:, None], gain_ffn[:, None]], axis=1)
    small = lax.all_gather(small, "seq", axis=0, tiled=True)
    small = lax.all_gather(small, "shard", axis=0, tiled=True)
    router_weight = small[:, :experts_all]
    first_gain = small[:, experts_all].astype(jnp.float32)
    second_gain = small[:, experts_all + 1].astype(jnp.float32)
    block_tokens = lax.all_gather(tokens, "seq", axis=0, tiled=True)
    qkv_blocks = gather_blocks(
        jnp.concatenate([w_query, key_projection, value_projection], axis=1), "shard"
    )
    qkv_weight = in_order(qkv_blocks, shard_index).reshape(model_width, -1)
    out_weight = lax.all_gather(w_out, "seq", axis=0, tiled=True)
    out_weight = lax.all_gather(out_weight, "shard", axis=1, tiled=True)
    grad_blocks = gather_blocks(lax.optimization_barrier((out_grad, qkv_weight))[0], "shard")

    block_rows = jnp.arange(block_len, dtype=jnp.int32)
    cos_table, sin_table = rotary_tables(
        place_of(block_rows, shard_index, prompt_len), HEAD_DIMENSION
    )
    inputs = block_tokens.astype(jnp.float32)
    first_factor = rms_parts(inputs)
    normed_low = (inputs * first_factor * first_gain).astype(bf16)
    lin = matmul(normed_low, qkv_weight)
    query_heads = rotate(lin[:, :query_width], cos_table, sin_table, HEAD_DIMENSION).astype(bf16)
    key_heads = rotate(
        lin[:, query_width : query_width + key_width], cos_table, sin_table, HEAD_DIMENSION
    ).astype(bf16)
    value_heads = lin[:, query_width + key_width :].astype(bf16)
    prompt_both = lax.all_gather(
        jnp.concatenate([key_heads[:PROMPT_BLK], value_heads[:PROMPT_BLK]], axis=1),
        "shard",
        axis=0,
        tiled=True,
    )
    prompt_keys = prompt_both[:, :key_width]
    prompt_values = prompt_both[:, key_width:]
    key_places = jnp.arange(prompt_len, dtype=jnp.int32)
    prompt_allowed = (
        key_places[None, :]
        <= shard_index * PROMPT_BLK + jnp.arange(PROMPT_BLK, dtype=jnp.int32)[:, None]
    )
    wide_places = jnp.arange(prompt_len + CONT_LEN, dtype=jnp.int32)
    cont_allowed = (wide_places[None, :] < prompt_len) | (
        wide_places[None, :] - prompt_len <= jnp.arange(CONT_LEN, dtype=jnp.int32)[:, None]
    )
    cont_count = (block_len - PROMPT_BLK) // CONT_LEN
    mixed_piece, prompt_level = attend_forward(
        query_heads[:PROMPT_BLK], prompt_keys, prompt_values, prompt_allowed, HEAD_DIMENSION
    )
    mixed_parts = [mixed_piece]
    cont_levels = []
    cont_keys = []
    cont_values = []
    for number in range(cont_count):
        first_row = PROMPT_BLK + number * CONT_LEN
        last_row = first_row + CONT_LEN
        keys_all = jnp.concatenate([prompt_keys, key_heads[first_row:last_row]], axis=0)
        values_all = jnp.concatenate([prompt_values, value_heads[first_row:last_row]], axis=0)
        mixed_piece, cont_level = attend_forward(
            query_heads[first_row:last_row], keys_all, values_all, cont_allowed, HEAD_DIMENSION
        )
        mixed_parts.append(mixed_piece)
        cont_levels.append(cont_level)
        cont_keys.append(keys_all)
        cont_values.append(values_all)
    mixed_heads = jnp.concatenate(mixed_parts, axis=0).astype(bf16)
    mixed_tokens = lax.all_to_all(mixed_heads, "seq", split_axis=0, concat_axis=1, tiled=True)

    own_inputs = tokens.astype(jnp.float32)
    upstream = out_grad.astype(jnp.float32)
    residual = own_inputs + matmul(mixed_tokens, out_weight)
    second_factor = rms_parts(residual)
    second_low = (residual * second_factor * second_gain).astype(bf16)
    logits = matmul(second_low, router_weight)
    chosen = routes[:, :, None] == jnp.arange(experts_all, dtype=jnp.int32)[None, None, :]
    named = jnp.any(chosen, axis=1)
    gate_dense = jax.nn.softmax(jnp.where(named, logits, negative), axis=-1)
    gate_dense = jnp.where(named, gate_dense, 0.0)

    gate_high = lax.reduce_precision(gate_dense, 8, 7)
    coded = jnp.concatenate(
        [
            second_low,
            gate_high.astype(bf16),
            (gate_dense - gate_high).astype(bf16),
            jnp.zeros((tok_count, LANES - 2 * experts_all), bf16),
        ],
        axis=1,
    )
    row_blocks = gather_blocks(coded, "shard")
    order = sorted(range(0, shard_count, 2), key=lambda j: (len(bits_of(j)), j))
    first_expert = (shard_index * local_experts).astype(jnp.int32).reshape(1)
    carried = None
    row_parts = [None] * shard_count
    out_parts = [None] * shard_count
    for position, j in enumerate(order):
        carried, pieces = expert_pair(
            position,
            len(order),
            first_expert,
            experts_all,
            row_blocks[j : j + 2],
            grad_blocks[j : j + 2],
            (w_gate, w_up, w_down),
            carried,
        )
        row_parts[j], row_parts[j + 1], out_parts[j], out_parts[j + 1] = pieces
    all_rows, all_grads, all_pre, all_hidden = carried
    down_sum = transposed_times(all_grads, all_hidden).astype(bf16)
    pre_sums = [transposed_times(all_rows, all_pre[e]).astype(bf16) for e in range(local_experts)]
    row_total = reduce_blocks(row_parts, "shard")
    row_total = lax.optimization_barrier((row_total, down_sum, *pre_sums))[0]
    row_grad = row_total[:, :model_width]
    gate_grad_dense = (
        row_total[:, model_width : model_width + experts_all]
        + row_total[:, model_width + experts_all : model_width + 2 * experts_all]
    )
    weighted = gate_dense * gate_grad_dense
    logit_grad = weighted - gate_dense * jnp.sum(weighted, axis=-1, keepdims=True)
    grad_router = transposed_times(second_low.astype(jnp.float32), logit_grad, highest)
    second_grad = row_grad + times_transposed(
        logit_grad, router_weight.astype(jnp.float32), highest
    )
    residual_part, grad_gain_ffn = rms_backward(residual, second_factor, second_gain, second_grad)
    residual_grad = upstream + residual_part
    residual_low = residual_grad.astype(bf16)
    mixed_grad_tokens = times_transposed(residual_low, out_weight).astype(bf16)
    mixed_grad = lax.all_to_all(mixed_grad_tokens, "seq", split_axis=1, concat_axis=0, tiled=True)
    out_parts = lax.optimization_barrier((out_parts, mixed_grad_tokens))[0]
    expert_sum = reduce_blocks(out_parts, "shard")
    output = (residual + expert_sum).astype(bf16)
    columns = [
        lax.dynamic_slice_in_dim(
            residual_low,
            (shard_index ^ j) * (model_width // shard_count),
            model_width // shard_count,
            axis=1,
        )
        for j in range(shard_count)
    ]
    whole_out = [transposed_times(part, mixed_tokens).astype(bf16) for part in columns]
    grad_out = reduce_blocks(whole_out, "shard").astype(bf16)
    grad_out = grad_out.reshape(grad_out.shape[0], seq_count, -1).transpose(1, 0, 2)
    grad_out = scatter_direct(grad_out, "seq").T

    query_piece, prompt_key_grad, prompt_value_grad = attend_backward(
        query_heads[:PROMPT_BLK],
        prompt_keys,
        prompt_values,
        prompt_allowed,
        prompt_level,
        mixed_grad[:PROMPT_BLK],
        HEAD_DIMENSION,
    )
    query_parts = [query_piece]
    self_key_grads = []
    self_value_grads = []
    for number in range(cont_count):
        first_row = PROMPT_BLK + number * CONT_LEN
        last_row = first_row + CONT_LEN
        query_piece, key_piece, value_piece = attend_backward(
            query_heads[first_row:last_row],
            cont_keys[number],
            cont_values[number],
            cont_allowed,
            cont_levels[number],
            mixed_grad[first_row:last_row],
            HEAD_DIMENSION,
        )
        query_parts.append(query_piece)
        prompt_key_grad = prompt_key_grad + key_piece[:prompt_len]
        prompt_value_grad = prompt_value_grad + value_piece[:prompt_len]
        self_key_grads.append(key_piece[prompt_len:])
        self_value_grads.append(value_piece[prompt_len:])
    own_prompt = reduce_blocks(
        relative_blocks(
            jnp.concatenate([prompt_key_grad, prompt_value_grad], axis=1).astype(bf16),
            shard_index,
            shard_count,
        ),
        "shard",
    )
    query_grad = jnp.concatenate(query_parts, axis=0)
    key_grad = jnp.concatenate([own_prompt[:, :key_width]] + self_key_grads, axis=0)
    value_low = jnp.concatenate([own_prompt[:, key_width:]] + self_value_grads, axis=0).astype(bf16)
    lin_query = rotate(query_grad, cos_table, -sin_table, HEAD_DIMENSION).astype(bf16)
    lin_key = rotate(key_grad, cos_table, -sin_table, HEAD_DIMENSION).astype(bf16)
    lin_all = jnp.concatenate([lin_query, lin_key, value_low], axis=1)
    normed_part = times_transposed(lin_all, qkv_weight)
    normed_grad = lax.psum_scatter(
        normed_part.astype(bf16), "seq", scatter_dimension=0, tiled=True
    ).astype(jnp.float32)
    gain_part = jnp.sum(normed_part * inputs * first_factor, axis=0)
    small_grad = jnp.concatenate(
        [grad_router, gain_part[:, None], grad_gain_ffn[:, None]], axis=1
    )
    grad_qkv = jnp.concatenate([transposed_times(normed_low, lin_all), small_grad], axis=1)
    grad_qkv = reduce_blocks(
        relative_blocks(grad_qkv.astype(bf16), shard_index, shard_count), "shard"
    )
    grad_query = grad_qkv[:, :query_width]
    grad_key = grad_qkv[:, query_width : query_width + key_width]
    grad_value = grad_qkv[:, query_width + key_width : query_width + 2 * key_width]
    small_grad = grad_qkv[:, query_width + 2 * key_width :].astype(bf16)
    small_grad = scatter_direct(
        small_grad.reshape(seq_count, -1, small_grad.shape[1]), "seq"
    )
    own_factor = rms_parts(own_inputs)
    input_part, _ = rms_backward(own_inputs, own_factor, first_gain, normed_grad)
    tokens_grad = residual_grad + input_part
    grad_down = lax.psum_scatter(down_sum, "seq", scatter_dimension=0, tiled=True)
    pre_grads = [
        lax.psum_scatter(part, "seq", scatter_dimension=0, tiled=True) for part in pre_sums
    ]
    hidden_units = w_gate.shape[2]
    grad_down = grad_down.T.reshape(local_experts, hidden_units, -1)
    grad_gate = jnp.stack([part[:, :hidden_units] for part in pre_grads])
    grad_up = jnp.stack([part[:, hidden_units:] for part in pre_grads])
    return (
        output,
        tokens_grad,
        grad_query,
        grad_key,
        grad_value,
        grad_out,
        small_grad[:, experts_all],
        small_grad[:, experts_all + 1],
        small_grad[:, :experts_all],
        grad_gate.astype(jnp.float32),
        grad_up.astype(jnp.float32),
        grad_down.astype(jnp.float32),
    )


def solution(mesh):
    return jax.shard_map(
        on_device,
        mesh=mesh,
        in_specs=(
            P(("shard", "seq"), None),
            P(("shard", "seq"), None),
            P("shard", "seq"),
            P("shard", "seq"),
            P("shard", "seq"),
            P("seq", "shard"),
            P(("shard", "seq")),
            P(("shard", "seq")),
            P(("shard", "seq"), None),
            P("shard", None, None),
            P("shard", None, None),
            P("shard", None, None),
            P(("shard", "seq"), None),
        ),
        out_specs=(
            P(("shard", "seq"), None),
            P(("shard", "seq"), None),
            P("shard", "seq"),
            P("shard", "seq"),
            P("shard", "seq"),
            P("seq", "shard"),
            P(("shard", "seq")),
            P(("shard", "seq")),
            P(("shard", "seq"), None),
            P("shard", "seq", None),
            P("shard", "seq", None),
            P("shard", None, "seq"),
        ),
        check_vma=False,
    )
```

```python
from functools import partial

import jax
import jax.numpy as jnp
from jax import lax
from jax.experimental import pallas as pl
from jax.experimental.pallas import tpu as pltpu
from jax.sharding import PartitionSpec as P

HEAD_DIMENSION = 64
CONT_LEN = 512
PROMPT_BLK = 128


norm_eps = 1e-05
negative = -1e30
rope_base = 10000.0
highest = lax.Precision.HIGHEST


def rms_norm(values, scaling):
    factor = lax.rsqrt(jnp.mean(values * values, axis=-1, keepdims=True) + norm_eps)
    return values * factor * scaling


def swiglu(gate_pre, up_pre):
    return jax.nn.silu(gate_pre) * up_pre


def rotary_tables(places, head_size):
    half_size = head_size // 2
    frequency = jnp.exp(
        jnp.arange(half_size, dtype=jnp.float32) * (-2.0 * jnp.log(rope_base) / head_size)
    )
    angles = places.astype(jnp.float32)[:, None] * frequency[None, :]
    return (jnp.cos(angles)[:, None, :], jnp.sin(angles)[:, None, :])


def rotate(values, cosine, sine, head_size):
    total_row_count = values.shape[0]
    by_head = values.reshape(total_row_count, -1, head_size)
    half_size = head_size // 2
    first_half = by_head[..., :half_size]
    second_half = by_head[..., half_size:]
    turned = jnp.concatenate(
        [first_half * cosine - second_half * sine, second_half * cosine + first_half * sine],
        axis=-1,
    )
    return turned.reshape(total_row_count, -1)


def place_of(within, block_index, prompt_len):
    return jnp.where(
        within < PROMPT_BLK,
        block_index * PROMPT_BLK + within,
        prompt_len + (within - PROMPT_BLK) % CONT_LEN,
    )


def times_transposed(left_side, right_side, precision=None):
    return lax.dot_general(
        left_side,
        right_side,
        (((1,), (1,)), ((), ())),
        precision=precision,
        preferred_element_type=jnp.float32,
    )


def transposed_times(left_side, right_side, precision=None):
    return lax.dot_general(
        left_side,
        right_side,
        (((0,), (0,)), ((), ())),
        precision=precision,
        preferred_element_type=jnp.float32,
    )


def rms_parts(values):
    return lax.rsqrt(jnp.mean(values * values, axis=-1, keepdims=True) + norm_eps)


def rms_backward(values, factor, scaling, normed_grad):
    scaled = scaling * normed_grad
    inner = jnp.mean(scaled * values, axis=-1, keepdims=True)
    values_grad = factor * scaled - values * (factor * factor * factor) * inner
    gain_grad = jnp.sum(normed_grad * values * factor, axis=0)
    return values_grad, gain_grad


def matmul(left_side, right_side):
    return jnp.dot(left_side, right_side, preferred_element_type=jnp.float32)


LANES = 128


def relane(values, source, target):
    lane = lax.broadcasted_iota(jnp.int32, values.shape, 1)
    swapped = jnp.where(source != target, pltpu.roll(values, HEAD_DIMENSION, 1), values)
    return jnp.where(lane // HEAD_DIMENSION == target, swapped, 0.0)


def head_rows(ref, first, count, source, target):
    values = ref[pl.ds(first, count), :].astype(jnp.float32)
    return relane(values, source, target).astype(jnp.bfloat16)


def nt_dot(left_side, right_side):
    return lax.dot_general(
        left_side, right_side, (((1,), (1,)), ((), ())), preferred_element_type=jnp.float32
    )


def nn_dot(left_side, right_side):
    return jnp.dot(left_side, right_side, preferred_element_type=jnp.float32)


def below_diagonal(scores):
    key_row = lax.broadcasted_iota(jnp.int32, scores.shape, 0)
    query_column = lax.broadcasted_iota(jnp.int32, scores.shape, 1)
    return jnp.where(key_row <= query_column, scores, negative)


def seen_prompt(scores, first_key, shard_index):
    key_row = lax.broadcasted_iota(jnp.int32, scores.shape, 0) + first_key
    query_column = lax.broadcasted_iota(jnp.int32, scores.shape, 1) % PROMPT_BLK
    return jnp.where(key_row <= query_column + shard_index * PROMPT_BLK, scores, negative)


def transposed(values):
    return values.astype(jnp.float32).T


QUERY_CHUNK = 512
KEY_CHUNK = 1024
FORWARD_CHUNK = 256


def attend_forward_body(
    group, kv_heads, index_ref, q_ref, kp_ref, vp_ref, ko_ref, vo_ref, mixed_ref, level_ref, vt_all, acc
):
    pair = pl.program_id(0)
    prompt_len = kp_ref.shape[0]
    block_len = ko_ref.shape[0]
    conts = (block_len - PROMPT_BLK) // CONT_LEN
    shard_index = index_ref[0]

    @pl.when(pair == 0)
    def _():
        vt_all[:, :prompt_len] = transposed(vp_ref[...]).astype(jnp.bfloat16)
        vt_all[:, prompt_len:] = transposed(vo_ref[...]).astype(jnp.bfloat16)

    acc[...] = jnp.zeros_like(acc)
    size = min(FORWARD_CHUNK, prompt_len)
    prompt_keys = [slice(first, first + size) for first in range(0, prompt_len, size)]

    def kv_half(side):
        return jnp.minimum((2 * pair + side) // group, kv_heads - 1)

    def finish(scores, value_columns):
        level = jnp.max(scores[0], axis=0, keepdims=True)
        for part in scores[1:]:
            level = jnp.maximum(level, jnp.max(part, axis=0, keepdims=True))
        total = None
        mixed = None
        for part, columns in zip(scores, value_columns):
            weights = jnp.exp(part - level)
            part_total = jnp.sum(weights, axis=0, keepdims=True)
            part_mixed = nn_dot(columns, weights.astype(jnp.bfloat16))
            total = part_total if total is None else total + part_total
            mixed = part_mixed if mixed is None else mixed + part_mixed
        return mixed / total, level + jnp.log(total)

    both = jnp.concatenate(
        [head_rows(q_ref, 0, PROMPT_BLK, side, kv_half(side)) for side in range(2)], axis=0
    )
    mixed, level = finish(
        [
            seen_prompt(nt_dot(kp_ref[keys, :], both), keys.start, shard_index)
            for keys in prompt_keys
        ],
        [vt_all[:, keys] for keys in prompt_keys],
    )
    mixed = mixed.T
    for side in range(2):
        rows = slice(side * PROMPT_BLK, (side + 1) * PROMPT_BLK)
        acc[:PROMPT_BLK, :] += relane(mixed[rows], kv_half(side), side)
        level_ref[side, :, :PROMPT_BLK] = level[:, rows]

    def step(turn, _):
        side = turn // conts
        number = turn % conts
        half = kv_half(side)
        first_own = PROMPT_BLK + number * CONT_LEN
        for chunk in range(CONT_LEN // QUERY_CHUNK):
            before = chunk * QUERY_CHUNK
            first_row = pl.multiple_of(first_own + before, PROMPT_BLK)
            queries = head_rows(q_ref, first_row, QUERY_CHUNK, side, half)
            scores = [nt_dot(kp_ref[keys, :], queries) for keys in prompt_keys]
            columns = [vt_all[:, keys] for keys in prompt_keys]
            if before:
                start = pl.multiple_of(first_own, PROMPT_BLK)
                scores.append(nt_dot(ko_ref[pl.ds(start, before), :], queries))
                columns.append(
                    vt_all[:, pl.ds(pl.multiple_of(prompt_len + start, PROMPT_BLK), before)]
                )
            scores.append(below_diagonal(nt_dot(ko_ref[pl.ds(first_row, QUERY_CHUNK), :], queries)))
            columns.append(
                vt_all[:, pl.ds(pl.multiple_of(prompt_len + first_row, PROMPT_BLK), QUERY_CHUNK)]
            )
            mixed, level = finish(scores, columns)
            acc[pl.ds(first_row, QUERY_CHUNK), :] += relane(mixed.T, half, side)
            level_ref[side, :, pl.ds(first_row, QUERY_CHUNK)] = level
        return 0

    lax.fori_loop(0, 2 * conts, step, 0)
    mixed_ref[...] = acc[...].astype(jnp.bfloat16)


def attend_backward_body(
    group,
    kv_heads,
    index_ref,
    q_ref,
    grad_ref,
    mixed_ref,
    level_ref,
    kp_ref,
    vp_ref,
    ko_ref,
    vo_ref,
    dq_ref,
    dprompt_ref,
    down_ref,
    kt_all,
    acc,
    prompt_acc,
):
    pair = pl.program_id(0)
    last = pl.num_programs(0) - 1
    prompt_len = kp_ref.shape[0]
    block_len = ko_ref.shape[0]
    conts = (block_len - PROMPT_BLK) // CONT_LEN
    shard_index = index_ref[0]
    bf16 = jnp.bfloat16

    @pl.when(pair == 0)
    def _():
        kt_all[:, :prompt_len] = transposed(kp_ref[...]).astype(bf16)
        kt_all[:, prompt_len:] = transposed(ko_ref[...]).astype(bf16)
        prompt_acc[...] = jnp.zeros_like(prompt_acc)
        down_ref[...] = jnp.zeros_like(down_ref)

    acc[...] = jnp.zeros_like(acc)

    def kv_half(side):
        return jnp.minimum((2 * pair + side) // group, kv_heads - 1)

    def inner_sums(first_row, count, side):
        rows = pl.ds(first_row, count)
        product = mixed_ref[rows, :].astype(jnp.float32) * grad_ref[rows, :].astype(jnp.float32)
        return jnp.sum(relane(product, side, side).T, axis=0, keepdims=True)

    def part(keys, values, key_columns, queries, grads, level, inner, mask, sums, first_key):
        scores = nt_dot(keys, queries)
        if mask is not None:
            scores = mask(scores)
        probs = jnp.exp(scores - level)
        score_grad = (probs * (nt_dot(values, grads) - inner)).astype(bf16)
        rows = pl.ds(first_key, keys.shape[0])
        sums[rows, :LANES] += nn_dot(score_grad, queries)
        sums[rows, LANES:] += nn_dot(probs.astype(bf16), grads)
        return nn_dot(key_columns, score_grad)

    def prompt_parts(queries, grads, level, inner, masked):
        total = None
        size = min(KEY_CHUNK, prompt_len)
        for first_key in range(0, prompt_len, size):
            rows = slice(first_key, first_key + size)
            mask = (lambda s, f=first_key: seen_prompt(s, f, shard_index)) if masked else None
            piece = part(
                kp_ref[rows, :], vp_ref[rows, :], kt_all[:, rows], queries, grads, level, inner,
                mask, prompt_acc, first_key,
            )
            total = piece if total is None else total + piece
        return total

    both_q, both_g, both_level, both_inner = [], [], [], []
    for side in range(2):
        both_q.append(head_rows(q_ref, 0, PROMPT_BLK, side, kv_half(side)))
        both_g.append(head_rows(grad_ref, 0, PROMPT_BLK, side, kv_half(side)))
        both_level.append(level_ref[side, :, :PROMPT_BLK])
        both_inner.append(inner_sums(0, PROMPT_BLK, side))
    grad_q = prompt_parts(
        jnp.concatenate(both_q, axis=0),
        jnp.concatenate(both_g, axis=0),
        jnp.concatenate(both_level, axis=1),
        jnp.concatenate(both_inner, axis=1),
        True,
    ).T
    for side in range(2):
        rows = slice(side * PROMPT_BLK, (side + 1) * PROMPT_BLK)
        acc[:PROMPT_BLK, :] += relane(grad_q[rows], kv_half(side), side)

    def step(turn, _):
        side = turn // conts
        number = turn % conts
        half = kv_half(side)
        first_own = PROMPT_BLK + number * CONT_LEN
        for chunk in range(CONT_LEN // QUERY_CHUNK):
            before = chunk * QUERY_CHUNK
            first_row = pl.multiple_of(first_own + before, PROMPT_BLK)
            queries = head_rows(q_ref, first_row, QUERY_CHUNK, side, half)
            grads = head_rows(grad_ref, first_row, QUERY_CHUNK, side, half)
            level = level_ref[side, :, pl.ds(first_row, QUERY_CHUNK)]
            inner = inner_sums(first_row, QUERY_CHUNK, side)
            grad_q = prompt_parts(queries, grads, level, inner, False)
            own = [(first_row, QUERY_CHUNK, below_diagonal)]
            if before:
                own.append((pl.multiple_of(first_own, PROMPT_BLK), before, None))
            for start, size, mask in own:
                rows = pl.ds(start, size)
                columns = pl.ds(pl.multiple_of(prompt_len + start, PROMPT_BLK), size)
                grad_q += part(
                    ko_ref[rows, :], vo_ref[rows, :], kt_all[:, columns], queries, grads, level,
                    inner, mask, down_ref, start,
                )
            acc[pl.ds(first_row, QUERY_CHUNK), :] += relane(grad_q.T, half, side)
        return 0

    lax.fori_loop(0, 2 * conts, step, 0)
    dq_ref[...] = acc[...] * HEAD_DIMENSION ** (-0.5)

    @pl.when(pair == last)
    def _():
        dprompt_ref[...] = prompt_acc[...].astype(bf16)


def pair_specs(block_len, prompt_len):
    by_pair = pl.BlockSpec((block_len, LANES), lambda b, i: (0, b))
    levels = pl.BlockSpec((2, 1, block_len), lambda b, i: (b, 0, 0))
    sources = [
        pl.BlockSpec((prompt_len, LANES), lambda b, i: (0, 0)),
        pl.BlockSpec((prompt_len, LANES), lambda b, i: (0, 1)),
        pl.BlockSpec((block_len, LANES), lambda b, i: (0, 0)),
        pl.BlockSpec((block_len, LANES), lambda b, i: (0, 1)),
    ]
    return by_pair, levels, sources


def attention_cost(block_len, prompt_len, width, products):
    pairs = (block_len * prompt_len + block_len * CONT_LEN // 2) * (width // HEAD_DIMENSION)
    return pl.CostEstimate(
        flops=products * 2 * pairs * 2 * LANES,
        bytes_accessed=8 * block_len * width,
        transcendentals=pairs,
    )


def attend_forward(index, queries, kv_prompt, kv_own, group, kv_heads):
    block_len, width = queries.shape
    prompt_len = kv_prompt.shape[0]
    by_pair, levels, sources = pair_specs(block_len, prompt_len)
    return pl.pallas_call(
        partial(attend_forward_body, group, kv_heads),
        out_shape=[
            jax.ShapeDtypeStruct((block_len, width), jnp.bfloat16),
            jax.ShapeDtypeStruct((width // HEAD_DIMENSION, 1, block_len), jnp.float32),
        ],
        grid_spec=pltpu.PrefetchScalarGridSpec(
            num_scalar_prefetch=1,
            grid=(width // LANES,),
            in_specs=[by_pair] + sources,
            out_specs=[by_pair, levels],
            scratch_shapes=[
                pltpu.VMEM((LANES, prompt_len + block_len), jnp.bfloat16),
                pltpu.VMEM((block_len, LANES), jnp.float32),
            ],
        ),
        compiler_params=pltpu.CompilerParams(
            dimension_semantics=("arbitrary",), vmem_limit_bytes=56 * 1024 * 1024
        ),
        cost_estimate=attention_cost(block_len, prompt_len, width, 2),
        name="attend_forward",
    )(index, queries, kv_prompt, kv_prompt, kv_own, kv_own)


def attend_backward(index, queries, grads, mixed, level, kv_prompt, kv_own, group, kv_heads):
    block_len, width = queries.shape
    prompt_len = kv_prompt.shape[0]
    by_pair, levels, sources = pair_specs(block_len, prompt_len)
    return pl.pallas_call(
        partial(attend_backward_body, group, kv_heads),
        out_shape=[
            jax.ShapeDtypeStruct((block_len, width), jnp.float32),
            jax.ShapeDtypeStruct((prompt_len, 2 * LANES), jnp.bfloat16),
            jax.ShapeDtypeStruct((block_len, 2 * LANES), jnp.float32),
        ],
        grid_spec=pltpu.PrefetchScalarGridSpec(
            num_scalar_prefetch=1,
            grid=(width // LANES,),
            in_specs=[by_pair, by_pair, by_pair, levels] + sources,
            out_specs=[
                by_pair,
                pl.BlockSpec((prompt_len, 2 * LANES), lambda b, i: (0, 0)),
                pl.BlockSpec((block_len, 2 * LANES), lambda b, i: (0, 0)),
            ],
            scratch_shapes=[
                pltpu.VMEM((LANES, prompt_len + block_len), jnp.bfloat16),
                pltpu.VMEM((block_len, LANES), jnp.float32),
                pltpu.VMEM((prompt_len, 2 * LANES), jnp.float32),
            ],
        ),
        compiler_params=pltpu.CompilerParams(
            dimension_semantics=("arbitrary",), vmem_limit_bytes=56 * 1024 * 1024
        ),
        cost_estimate=attention_cost(block_len, prompt_len, width, 5),
        name="attend_backward",
    )(index, queries, grads, mixed, level, kv_prompt, kv_prompt, kv_own, kv_own)


def to_lanes(values):
    extra = -values.shape[1] % LANES
    return jnp.pad(values, ((0, 0), (0, extra))) if extra else values


def exchange(values, axis_name, bit):
    count = lax.axis_size(axis_name)
    return lax.ppermute(values, axis_name, [(i, i ^ bit) for i in range(count)])


def bits_of(number):
    return [1 << k for k in range(number.bit_length()) if number >> k & 1]


def gather_blocks(own, axis_name):
    count = lax.axis_size(axis_name)
    half = own.shape[0] // 2
    blocks = {0: own}
    even = sorted(range(2, count, 2), key=lambda j: (len(bits_of(j)), j))
    if count > 1:
        blocks[1] = exchange(own, axis_name, 1)
    for j in even:
        bits = bits_of(j)
        if len(bits) == 1:
            blocks[j] = exchange(own, axis_name, j)
        else:
            low_bit, high_bit = bits[0], bits[-1]
            top = exchange(blocks[j ^ low_bit][:half], axis_name, low_bit)
            bottom = exchange(blocks[j ^ high_bit][half:], axis_name, high_bit)
            blocks[j] = jnp.concatenate([top, bottom], axis=0)
        blocks[j + 1] = exchange(blocks[j], axis_name, 1)
    return [blocks[j] for j in range(count)]


def add_rounded(left_side, right_side):
    return (left_side.astype(jnp.float32) + right_side.astype(jnp.float32)).astype(jnp.bfloat16)


def reduce_blocks(blocks, axis_name):
    count = lax.axis_size(axis_name)
    half = blocks[0].shape[0] // 2
    sums = {}
    for j in sorted(range(0, count, 2), key=lambda j: (-len(bits_of(j)), j)):
        arrived = exchange(blocks[j + 1], axis_name, 1)
        sums[j] = [
            add_rounded(blocks[j][:half], arrived[:half]),
            add_rounded(blocks[j][half:], arrived[half:]),
        ]
    extra = [[], []]
    for j in sorted(range(2, count, 2), key=lambda j: (-len(bits_of(j)), j)):
        bits = bits_of(j)
        if len(bits) > 1:
            low_bit, high_bit = bits[0], bits[-1]
            top = exchange(sums[j][0], axis_name, low_bit)
            bottom = exchange(sums[j][1], axis_name, high_bit)
            sums[j ^ low_bit][0] = add_rounded(sums[j ^ low_bit][0], top)
            sums[j ^ high_bit][1] = add_rounded(sums[j ^ high_bit][1], bottom)
        else:
            extra[0].append(exchange(sums[j][0], axis_name, j))
            extra[1].append(exchange(sums[j][1], axis_name, j))
    halves = []
    for part in range(2):
        total = sums[0][part].astype(jnp.float32)
        for piece in extra[part]:
            total = total + piece.astype(jnp.float32)
        halves.append(total)
    return jnp.concatenate(halves, axis=0)


def in_order(blocks, index):
    stacked = jnp.stack(blocks)
    return jnp.concatenate(
        [lax.dynamic_index_in_dim(stacked, j ^ index, 0, keepdims=True) for j in range(len(blocks))],
        axis=0,
    )


def relative_blocks(values, index, count):
    rows = values.shape[0] // count
    return [
        lax.dynamic_slice_in_dim(values, (index ^ j) * rows, rows, axis=0) for j in range(count)
    ]


def scatter_direct(pieces, axis_name):
    count = lax.axis_size(axis_name)
    index = lax.axis_index(axis_name)
    total = lax.dynamic_index_in_dim(pieces, index, 0, keepdims=False).astype(jnp.float32)
    for step in range(1, count):
        piece = lax.dynamic_index_in_dim(pieces, (index + step) % count, 0, keepdims=False)
        arrived = lax.ppermute(piece, axis_name, [(i, (i + step) % count) for i in range(count)])
        total = total + arrived.astype(jnp.float32)
    return total


def expert_body(
    experts_all, index_ref, x_even, x_odd, og_even, og_odd, gate_w, up_w, down_w, *rest
):
    (x_all, og_all, pre_all, hid_all, row_even, row_odd, out_even, out_odd) = rest[-12:-4]
    (row_acc, out_acc, back_acc, _) = rest[-4:]
    expert = pl.program_id(0)
    last = pl.num_programs(0) - 1
    rows = x_even.shape[0]
    width = x_all.shape[1]
    hidden_units = gate_w.shape[2]
    nt_dims = (((1,), (1,)), ((), ()))

    @pl.when(expert == 0)
    def _():
        x_all[:rows, :] = x_even[:, :width]
        x_all[rows:, :] = x_odd[:, :width]
        og_all[:rows, :] = og_even[...]
        og_all[rows:, :] = og_odd[...]

    column = index_ref[0] + expert
    lane = lax.broadcasted_iota(jnp.int32, (2 * rows, LANES), 1)
    coded = jnp.concatenate([x_even[:, width:], x_odd[:, width:]], axis=0).astype(jnp.float32)
    gate = jnp.sum(
        jnp.where((lane == column) | (lane == column + experts_all), coded, 0.0),
        axis=1,
        keepdims=True,
    )
    x_rows = x_all[...]
    og_rows = og_all[...]
    gate_pre = jnp.dot(x_rows, gate_w[0], preferred_element_type=jnp.float32)
    up_pre = jnp.dot(x_rows, up_w[0], preferred_element_type=jnp.float32)
    down_grad = lax.dot_general(og_rows, down_w[0], nt_dims, preferred_element_type=jnp.float32)
    sigmoid = 1.0 / (1.0 + jnp.exp(-gate_pre))
    silu = gate_pre * sigmoid
    hidden = silu * up_pre
    gate_back = jnp.sum(hidden * down_grad, axis=1, keepdims=True)
    hidden_low = (gate * hidden).astype(jnp.bfloat16)
    hidden_grad = gate * down_grad
    gate_pre_low = (
        hidden_grad * up_pre * sigmoid * (1.0 + gate_pre * (1.0 - sigmoid))
    ).astype(jnp.bfloat16)
    up_pre_low = (hidden_grad * silu).astype(jnp.bfloat16)
    hid_all[...] = hidden_low
    pre_all[0, :, :hidden_units] = gate_pre_low
    pre_all[0, :, hidden_units:] = up_pre_low
    row = lax.dot_general(
        gate_pre_low, gate_w[0], nt_dims, preferred_element_type=jnp.float32
    ) + lax.dot_general(up_pre_low, up_w[0], nt_dims, preferred_element_type=jnp.float32)
    out = jnp.dot(hidden_low, down_w[0], preferred_element_type=jnp.float32)
    high = gate_back.astype(jnp.bfloat16).astype(jnp.float32)
    back = jnp.where(lane == column, high, 0.0) + jnp.where(
        lane == column + experts_all, gate_back - high, 0.0
    )

    @pl.when(expert == 0)
    def _():
        row_acc[...] = row
        out_acc[...] = out
        back_acc[...] = back

    @pl.when(expert > 0)
    def _():
        row_acc[...] += row
        out_acc[...] += out
        back_acc[...] += back

    @pl.when(expert == last)
    def _():
        for ref, first in ((row_even, 0), (row_odd, rows)):
            ref[:, :width] = row_acc[first : first + rows, :].astype(jnp.bfloat16)
            ref[:, width:] = back_acc[first : first + rows, :].astype(jnp.bfloat16)
        out_even[...] = out_acc[:rows, :].astype(jnp.bfloat16)
        out_odd[...] = out_acc[rows:, :].astype(jnp.bfloat16)


def expert_pair(position, pairs, first_expert, experts_all, x_pair, og_pair, weights, carried):
    w_gate, w_up, w_down = weights
    rows, coded_width = x_pair[0].shape
    width = coded_width - LANES
    local_experts, _, hidden_units = w_gate.shape
    bf16 = jnp.bfloat16
    whole = 2 * rows
    fixed = lambda e, i: (0, 0)
    once = pl.Buffered(1)
    in_specs = (
        [pl.BlockSpec((rows, coded_width), fixed, pipeline_mode=once)] * 2
        + [pl.BlockSpec((rows, width), fixed, pipeline_mode=once)] * 2
        + [pl.BlockSpec((1, width, hidden_units), lambda e, i: (e, 0, 0))] * 2
        + [pl.BlockSpec((1, hidden_units, width), lambda e, i: (e, 0, 0))]
    )
    operands = [*x_pair, *og_pair, w_gate, w_up, w_down]
    aliases = {}
    if carried is not None:
        in_specs = in_specs + [pl.BlockSpec(memory_space=pl.ANY)] * 4
        aliases = {1 + len(operands) + k: k for k in range(4)}
        operands = operands + list(carried)
    out_shape = [
        jax.ShapeDtypeStruct((pairs * whole, width), bf16),
        jax.ShapeDtypeStruct((pairs * whole, width), bf16),
        jax.ShapeDtypeStruct((local_experts, pairs * whole, 2 * hidden_units), bf16),
        jax.ShapeDtypeStruct((pairs * whole, local_experts * hidden_units), bf16),
        jax.ShapeDtypeStruct((rows, coded_width), bf16),
        jax.ShapeDtypeStruct((rows, coded_width), bf16),
        jax.ShapeDtypeStruct((rows, width), bf16),
        jax.ShapeDtypeStruct((rows, width), bf16),
    ]
    out_specs = [
        pl.BlockSpec((whole, width), lambda e, i: (position, 0)),
        pl.BlockSpec((whole, width), lambda e, i: (position, 0)),
        pl.BlockSpec((1, whole, 2 * hidden_units), lambda e, i: (e, position, 0)),
        pl.BlockSpec((whole, hidden_units), lambda e, i: (position, e)),
        pl.BlockSpec((rows, coded_width), fixed),
        pl.BlockSpec((rows, coded_width), fixed),
        pl.BlockSpec((rows, width), fixed),
        pl.BlockSpec((rows, width), fixed),
    ]
    products = 2 * whole * width * hidden_units * local_experts
    results = pl.pallas_call(
        partial(expert_body, experts_all),
        out_shape=out_shape,
        grid_spec=pltpu.PrefetchScalarGridSpec(
            num_scalar_prefetch=1,
            grid=(local_experts,),
            in_specs=in_specs,
            out_specs=out_specs,
            scratch_shapes=[
                pltpu.VMEM((whole, width), jnp.float32),
                pltpu.VMEM((whole, width), jnp.float32),
                pltpu.VMEM((whole, LANES), jnp.float32),
                pltpu.VMEM((8, LANES), jnp.float32),
            ],
        ),
        input_output_aliases=aliases,
        compiler_params=pltpu.CompilerParams(
            dimension_semantics=("arbitrary",), vmem_limit_bytes=60 * 1024 * 1024
        ),
        cost_estimate=pl.CostEstimate(
            flops=6 * products,
            bytes_accessed=3 * 2 * local_experts * width * hidden_units + 20 * whole * width,
            transcendentals=whole * hidden_units * local_experts,
        ),
        name="experts",
    )(first_expert, *operands)
    return results[:4], results[4:]


def on_device(
    tokens,
    routes,
    w_query,
    key_projection,
    value_projection,
    w_out,
    gain_attn,
    gain_ffn,
    w_router,
    w_gate,
    w_up,
    w_down,
    out_grad,
):
    bf16 = jnp.bfloat16
    shard_count = lax.axis_size("shard")
    seq_count = lax.axis_size("seq")
    shard_index = lax.axis_index("shard")
    seq_index = lax.axis_index("seq")
    tok_count, model_width = tokens.shape
    top_count = routes.shape[1]
    experts_all = w_router.shape[1]
    local_experts = w_gate.shape[0]
    block_len = tok_count * seq_count
    prompt_len = PROMPT_BLK * shard_count
    query_width = w_query.shape[1]
    key_width = key_projection.shape[1]

    small = jnp.concatenate([w_router, gain_attn[:, None], gain_ffn[:, None]], axis=1)
    small = lax.all_gather(small, "seq", axis=0, tiled=True)
    small = lax.all_gather(small, "shard", axis=0, tiled=True)
    router_weight = small[:, :experts_all]
    first_gain = small[:, experts_all].astype(jnp.float32)
    second_gain = small[:, experts_all + 1].astype(jnp.float32)
    block_tokens = lax.all_gather(tokens, "seq", axis=0, tiled=True)
    qkv_blocks = gather_blocks(
        jnp.concatenate([w_query, key_projection, value_projection], axis=1), "shard"
    )
    qkv_weight = in_order(qkv_blocks, shard_index).reshape(model_width, -1)
    out_weight = lax.all_gather(w_out, "seq", axis=0, tiled=True)
    out_weight = lax.all_gather(out_weight, "shard", axis=1, tiled=True)
    grad_blocks = gather_blocks(lax.optimization_barrier((out_grad, qkv_weight))[0], "shard")

    block_rows = jnp.arange(block_len, dtype=jnp.int32)
    cos_table, sin_table = rotary_tables(
        place_of(block_rows, shard_index, prompt_len), HEAD_DIMENSION
    )
    inputs = block_tokens.astype(jnp.float32)
    first_factor = rms_parts(inputs)
    normed_low = (inputs * first_factor * first_gain).astype(bf16)
    lin = matmul(normed_low, qkv_weight)
    kv_heads = key_width // HEAD_DIMENSION
    group = query_width // key_width
    queries = rotate(lin[:, :query_width], cos_table, sin_table, HEAD_DIMENSION)
    queries = to_lanes((queries * HEAD_DIMENSION ** (-0.5)).astype(bf16))
    key_heads = rotate(
        lin[:, query_width : query_width + key_width], cos_table, sin_table, HEAD_DIMENSION
    ).astype(bf16)
    value_heads = lin[:, query_width + key_width :].astype(bf16)
    kv_own = jnp.concatenate([to_lanes(key_heads), to_lanes(value_heads)], axis=1)
    kv_prompt = lax.all_gather(kv_own[:PROMPT_BLK], "shard", axis=0, tiled=True)
    block_number = shard_index.astype(jnp.int32).reshape(1)
    mixed_own, levels = attend_forward(block_number, queries, kv_prompt, kv_own, group, kv_heads)
    mixed_heads = mixed_own[:, :query_width]
    mixed_tokens = lax.all_to_all(mixed_heads, "seq", split_axis=0, concat_axis=1, tiled=True)

    own_inputs = tokens.astype(jnp.float32)
    upstream = out_grad.astype(jnp.float32)
    residual = own_inputs + matmul(mixed_tokens, out_weight)
    second_factor = rms_parts(residual)
    second_low = (residual * second_factor * second_gain).astype(bf16)
    logits = matmul(second_low, router_weight)
    chosen = routes[:, :, None] == jnp.arange(experts_all, dtype=jnp.int32)[None, None, :]
    named = jnp.any(chosen, axis=1)
    gate_dense = jax.nn.softmax(jnp.where(named, logits, negative), axis=-1)
    gate_dense = jnp.where(named, gate_dense, 0.0)

    gate_high = lax.reduce_precision(gate_dense, 8, 7)
    coded = jnp.concatenate(
        [
            second_low,
            gate_high.astype(bf16),
            (gate_dense - gate_high).astype(bf16),
            jnp.zeros((tok_count, LANES - 2 * experts_all), bf16),
        ],
        axis=1,
    )
    row_blocks = gather_blocks(coded, "shard")
    order = sorted(range(0, shard_count, 2), key=lambda j: (len(bits_of(j)), j))
    first_expert = (shard_index * local_experts).astype(jnp.int32).reshape(1)
    carried = None
    row_parts = [None] * shard_count
    out_parts = [None] * shard_count
    for position, j in enumerate(order):
        carried, pieces = expert_pair(
            position,
            len(order),
            first_expert,
            experts_all,
            row_blocks[j : j + 2],
            grad_blocks[j : j + 2],
            (w_gate, w_up, w_down),
            carried,
        )
        row_parts[j], row_parts[j + 1], out_parts[j], out_parts[j + 1] = pieces
    all_rows, all_grads, all_pre, all_hidden = carried
    down_sum = transposed_times(all_grads, all_hidden).astype(bf16)
    pre_sums = [transposed_times(all_rows, all_pre[e]).astype(bf16) for e in range(local_experts)]
    row_total = reduce_blocks(row_parts, "shard")
    row_total = lax.optimization_barrier((row_total, down_sum, *pre_sums))[0]
    row_grad = row_total[:, :model_width]
    gate_grad_dense = (
        row_total[:, model_width : model_width + experts_all]
        + row_total[:, model_width + experts_all : model_width + 2 * experts_all]
    )
    weighted = gate_dense * gate_grad_dense
    logit_grad = weighted - gate_dense * jnp.sum(weighted, axis=-1, keepdims=True)
    grad_router = transposed_times(second_low.astype(jnp.float32), logit_grad, highest)
    second_grad = row_grad + times_transposed(
        logit_grad, router_weight.astype(jnp.float32), highest
    )
    residual_part, grad_gain_ffn = rms_backward(residual, second_factor, second_gain, second_grad)
    residual_grad = upstream + residual_part
    residual_low = residual_grad.astype(bf16)
    mixed_grad_tokens = times_transposed(residual_low, out_weight).astype(bf16)
    mixed_grad = lax.all_to_all(mixed_grad_tokens, "seq", split_axis=1, concat_axis=0, tiled=True)
    out_parts = lax.optimization_barrier((out_parts, mixed_grad_tokens))[0]
    expert_sum = reduce_blocks(out_parts, "shard")
    output = (residual + expert_sum).astype(bf16)
    columns = [
        lax.dynamic_slice_in_dim(
            residual_low,
            (shard_index ^ j) * (model_width // shard_count),
            model_width // shard_count,
            axis=1,
        )
        for j in range(shard_count)
    ]
    whole_out = [transposed_times(part, mixed_tokens).astype(bf16) for part in columns]
    grad_out = reduce_blocks(whole_out, "shard").astype(bf16)
    grad_out = grad_out.reshape(grad_out.shape[0], seq_count, -1).transpose(1, 0, 2)
    grad_out = scatter_direct(grad_out, "seq").T

    query_grad, prompt_grad, self_grad = attend_backward(
        block_number,
        queries,
        to_lanes(mixed_grad),
        mixed_own,
        levels,
        kv_prompt,
        kv_own,
        group,
        kv_heads,
    )
    query_grad = query_grad[:, :query_width]
    own_prompt = reduce_blocks(relative_blocks(prompt_grad, shard_index, shard_count), "shard")
    key_grad = jnp.concatenate(
        [own_prompt[:, :key_width], self_grad[PROMPT_BLK:, :key_width]], axis=0
    )
    value_low = jnp.concatenate(
        [own_prompt[:, LANES : LANES + key_width], self_grad[PROMPT_BLK:, LANES : LANES + key_width]],
        axis=0,
    ).astype(bf16)
    lin_query = rotate(query_grad, cos_table, -sin_table, HEAD_DIMENSION).astype(bf16)
    lin_key = rotate(key_grad, cos_table, -sin_table, HEAD_DIMENSION).astype(bf16)
    lin_all = jnp.concatenate([lin_query, lin_key, value_low], axis=1)
    normed_part = times_transposed(lin_all, qkv_weight)
    normed_grad = lax.psum_scatter(
        normed_part.astype(bf16), "seq", scatter_dimension=0, tiled=True
    ).astype(jnp.float32)
    gain_part = jnp.sum(normed_part * inputs * first_factor, axis=0)
    small_grad = jnp.concatenate(
        [grad_router, gain_part[:, None], grad_gain_ffn[:, None]], axis=1
    )
    grad_qkv = jnp.concatenate([transposed_times(normed_low, lin_all), small_grad], axis=1)
    grad_qkv = reduce_blocks(
        relative_blocks(grad_qkv.astype(bf16), shard_index, shard_count), "shard"
    )
    grad_query = grad_qkv[:, :query_width]
    grad_key = grad_qkv[:, query_width : query_width + key_width]
    grad_value = grad_qkv[:, query_width + key_width : query_width + 2 * key_width]
    small_grad = grad_qkv[:, query_width + 2 * key_width :].astype(bf16)
    small_grad = scatter_direct(
        small_grad.reshape(seq_count, -1, small_grad.shape[1]), "seq"
    )
    own_factor = rms_parts(own_inputs)
    input_part, _ = rms_backward(own_inputs, own_factor, first_gain, normed_grad)
    tokens_grad = residual_grad + input_part
    grad_down = lax.psum_scatter(down_sum, "seq", scatter_dimension=0, tiled=True)
    pre_grads = [
        lax.psum_scatter(part, "seq", scatter_dimension=0, tiled=True) for part in pre_sums
    ]
    hidden_units = w_gate.shape[2]
    grad_down = grad_down.T.reshape(local_experts, hidden_units, -1)
    grad_gate = jnp.stack([part[:, :hidden_units] for part in pre_grads])
    grad_up = jnp.stack([part[:, hidden_units:] for part in pre_grads])
    return (
        output,
        tokens_grad,
        grad_query,
        grad_key,
        grad_value,
        grad_out,
        small_grad[:, experts_all],
        small_grad[:, experts_all + 1],
        small_grad[:, :experts_all],
        grad_gate.astype(jnp.float32),
        grad_up.astype(jnp.float32),
        grad_down.astype(jnp.float32),
    )


def solution(mesh):
    return jax.shard_map(
        on_device,
        mesh=mesh,
        in_specs=(
            P(("shard", "seq"), None),
            P(("shard", "seq"), None),
            P("shard", "seq"),
            P("shard", "seq"),
            P("shard", "seq"),
            P("seq", "shard"),
            P(("shard", "seq")),
            P(("shard", "seq")),
            P(("shard", "seq"), None),
            P("shard", None, None),
            P("shard", None, None),
            P("shard", None, None),
            P(("shard", "seq"), None),
        ),
        out_specs=(
            P(("shard", "seq"), None),
            P(("shard", "seq"), None),
            P("shard", "seq"),
            P("shard", "seq"),
            P("shard", "seq"),
            P("seq", "shard"),
            P(("shard", "seq")),
            P(("shard", "seq")),
            P(("shard", "seq"), None),
            P("shard", "seq", None),
            P("shard", "seq", None),
            P("shard", None, "seq"),
        ),
        check_vma=False,
    )
```

```python
from functools import partial

import jax
import jax.numpy as jnp
from jax import lax
from jax.experimental import pallas as pl
from jax.experimental.pallas import tpu as pltpu
from jax.sharding import PartitionSpec as P

HEAD_DIMENSION = 64
CONT_LEN = 512
PROMPT_BLK = 128


norm_eps = 1e-05
negative = -1e30
rope_base = 10000.0
highest = lax.Precision.HIGHEST


def rms_norm(values, scaling):
    factor = lax.rsqrt(jnp.mean(values * values, axis=-1, keepdims=True) + norm_eps)
    return values * factor * scaling


def swiglu(gate_pre, up_pre):
    return jax.nn.silu(gate_pre) * up_pre


def rotary_tables(places, head_size):
    half_size = head_size // 2
    frequency = jnp.exp(
        jnp.arange(half_size, dtype=jnp.float32) * (-2.0 * jnp.log(rope_base) / head_size)
    )
    angles = places.astype(jnp.float32)[:, None] * frequency[None, :]
    return (jnp.cos(angles)[:, None, :], jnp.sin(angles)[:, None, :])


def rotate(values, cosine, sine, head_size):
    total_row_count = values.shape[0]
    by_head = values.reshape(total_row_count, -1, head_size)
    half_size = head_size // 2
    first_half = by_head[..., :half_size]
    second_half = by_head[..., half_size:]
    turned = jnp.concatenate(
        [first_half * cosine - second_half * sine, second_half * cosine + first_half * sine],
        axis=-1,
    )
    return turned.reshape(total_row_count, -1)


def place_of(within, block_index, prompt_len):
    return jnp.where(
        within < PROMPT_BLK,
        block_index * PROMPT_BLK + within,
        prompt_len + (within - PROMPT_BLK) % CONT_LEN,
    )


def times_transposed(left_side, right_side, precision=None):
    return lax.dot_general(
        left_side,
        right_side,
        (((1,), (1,)), ((), ())),
        precision=precision,
        preferred_element_type=jnp.float32,
    )


def transposed_times(left_side, right_side, precision=None):
    return lax.dot_general(
        left_side,
        right_side,
        (((0,), (0,)), ((), ())),
        precision=precision,
        preferred_element_type=jnp.float32,
    )


def rms_parts(values):
    return lax.rsqrt(jnp.mean(values * values, axis=-1, keepdims=True) + norm_eps)


def rms_backward(values, factor, scaling, normed_grad):
    scaled = scaling * normed_grad
    inner = jnp.mean(scaled * values, axis=-1, keepdims=True)
    values_grad = factor * scaled - values * (factor * factor * factor) * inner
    gain_grad = jnp.sum(normed_grad * values * factor, axis=0)
    return values_grad, gain_grad


def matmul(left_side, right_side):
    return jnp.dot(left_side, right_side, preferred_element_type=jnp.float32)


LANES = 128


def relane(values, source, target):
    lane = lax.broadcasted_iota(jnp.int32, values.shape, 1)
    swapped = jnp.where(source != target, pltpu.roll(values, HEAD_DIMENSION, 1), values)
    return jnp.where(lane // HEAD_DIMENSION == target, swapped, 0.0)


def head_rows(ref, first, count, source, target):
    values = ref[pl.ds(first, count), :].astype(jnp.float32)
    return relane(values, source, target).astype(jnp.bfloat16)


def nt_dot(left_side, right_side):
    return lax.dot_general(
        left_side, right_side, (((1,), (1,)), ((), ())), preferred_element_type=jnp.float32
    )


def nn_dot(left_side, right_side):
    return jnp.dot(left_side, right_side, preferred_element_type=jnp.float32)


def below_diagonal(scores):
    key_row = lax.broadcasted_iota(jnp.int32, scores.shape, 0)
    query_column = lax.broadcasted_iota(jnp.int32, scores.shape, 1)
    return jnp.where(key_row <= query_column, scores, negative)


def seen_prompt(scores, first_key, shard_index):
    key_row = lax.broadcasted_iota(jnp.int32, scores.shape, 0) + first_key
    query_column = lax.broadcasted_iota(jnp.int32, scores.shape, 1) % PROMPT_BLK
    return jnp.where(key_row <= query_column + shard_index * PROMPT_BLK, scores, negative)


def transposed(values):
    return values.astype(jnp.float32).T


QUERY_CHUNK = 512
KEY_CHUNK = 1024
FORWARD_CHUNK = 256


def attend_forward_body(
    group, kv_heads, index_ref, q_ref, kp_ref, vp_ref, ko_ref, vo_ref, mixed_ref, level_ref, vt_all, acc
):
    pair = pl.program_id(0)
    prompt_len = kp_ref.shape[0]
    block_len = ko_ref.shape[0]
    conts = (block_len - PROMPT_BLK) // CONT_LEN
    shard_index = index_ref[0]

    @pl.when(pair == 0)
    def _():
        vt_all[:, :prompt_len] = transposed(vp_ref[...]).astype(jnp.bfloat16)
        vt_all[:, prompt_len:] = transposed(vo_ref[...]).astype(jnp.bfloat16)

    acc[...] = jnp.zeros_like(acc)
    size = min(FORWARD_CHUNK, prompt_len)
    prompt_keys = [slice(first, first + size) for first in range(0, prompt_len, size)]

    def kv_half(side):
        return jnp.minimum((2 * pair + side) // group, kv_heads - 1)

    def finish(scores, value_columns):
        level = jnp.max(scores[0], axis=0, keepdims=True)
        for part in scores[1:]:
            level = jnp.maximum(level, jnp.max(part, axis=0, keepdims=True))
        total = None
        mixed = None
        for part, columns in zip(scores, value_columns):
            weights = jnp.exp(part - level)
            part_total = jnp.sum(weights, axis=0, keepdims=True)
            part_mixed = nn_dot(columns, weights.astype(jnp.bfloat16))
            total = part_total if total is None else total + part_total
            mixed = part_mixed if mixed is None else mixed + part_mixed
        return mixed / total, level + jnp.log(total)

    both = jnp.concatenate(
        [head_rows(q_ref, 0, PROMPT_BLK, side, kv_half(side)) for side in range(2)], axis=0
    )
    mixed, level = finish(
        [
            seen_prompt(nt_dot(kp_ref[keys, :], both), keys.start, shard_index)
            for keys in prompt_keys
        ],
        [vt_all[:, keys] for keys in prompt_keys],
    )
    mixed = mixed.T
    for side in range(2):
        rows = slice(side * PROMPT_BLK, (side + 1) * PROMPT_BLK)
        acc[:PROMPT_BLK, :] += relane(mixed[rows], kv_half(side), side)
        level_ref[side, :, :PROMPT_BLK] = level[:, rows]

    def step(turn, _):
        side = turn // conts
        number = turn % conts
        half = kv_half(side)
        first_own = PROMPT_BLK + number * CONT_LEN
        for chunk in range(CONT_LEN // QUERY_CHUNK):
            before = chunk * QUERY_CHUNK
            first_row = pl.multiple_of(first_own + before, PROMPT_BLK)
            queries = head_rows(q_ref, first_row, QUERY_CHUNK, side, half)
            scores = [nt_dot(kp_ref[keys, :], queries) for keys in prompt_keys]
            columns = [vt_all[:, keys] for keys in prompt_keys]
            if before:
                start = pl.multiple_of(first_own, PROMPT_BLK)
                scores.append(nt_dot(ko_ref[pl.ds(start, before), :], queries))
                columns.append(
                    vt_all[:, pl.ds(pl.multiple_of(prompt_len + start, PROMPT_BLK), before)]
                )
            scores.append(below_diagonal(nt_dot(ko_ref[pl.ds(first_row, QUERY_CHUNK), :], queries)))
            columns.append(
                vt_all[:, pl.ds(pl.multiple_of(prompt_len + first_row, PROMPT_BLK), QUERY_CHUNK)]
            )
            mixed, level = finish(scores, columns)
            acc[pl.ds(first_row, QUERY_CHUNK), :] += relane(mixed.T, half, side)
            level_ref[side, :, pl.ds(first_row, QUERY_CHUNK)] = level
        return 0

    lax.fori_loop(0, 2 * conts, step, 0)
    mixed_ref[...] = acc[...].astype(jnp.bfloat16)


def attend_backward_body(
    group,
    kv_heads,
    index_ref,
    q_ref,
    grad_ref,
    mixed_ref,
    level_ref,
    kp_ref,
    vp_ref,
    ko_ref,
    vo_ref,
    dq_ref,
    dprompt_ref,
    down_ref,
    kt_all,
    acc,
    prompt_acc,
):
    pair = pl.program_id(0)
    last = pl.num_programs(0) - 1
    prompt_len = kp_ref.shape[0]
    block_len = ko_ref.shape[0]
    conts = (block_len - PROMPT_BLK) // CONT_LEN
    shard_index = index_ref[0]
    bf16 = jnp.bfloat16

    @pl.when(pair == 0)
    def _():
        kt_all[:, :prompt_len] = transposed(kp_ref[...]).astype(bf16)
        kt_all[:, prompt_len:] = transposed(ko_ref[...]).astype(bf16)
        prompt_acc[...] = jnp.zeros_like(prompt_acc)
        down_ref[...] = jnp.zeros_like(down_ref)

    acc[...] = jnp.zeros_like(acc)

    def kv_half(side):
        return jnp.minimum((2 * pair + side) // group, kv_heads - 1)

    def inner_sums(first_row, count, side):
        rows = pl.ds(first_row, count)
        product = mixed_ref[rows, :].astype(jnp.float32) * grad_ref[rows, :].astype(jnp.float32)
        return jnp.sum(relane(product, side, side).T, axis=0, keepdims=True)

    def part(keys, values, key_columns, queries, grads, level, inner, mask, sums, first_key):
        scores = nt_dot(keys, queries)
        if mask is not None:
            scores = mask(scores)
        probs = jnp.exp(scores - level)
        score_grad = (probs * (nt_dot(values, grads) - inner)).astype(bf16)
        rows = pl.ds(first_key, keys.shape[0])
        sums[rows, :LANES] += nn_dot(score_grad, queries)
        sums[rows, LANES:] += nn_dot(probs.astype(bf16), grads)
        return nn_dot(key_columns, score_grad)

    def prompt_parts(queries, grads, level, inner, masked):
        total = None
        size = min(KEY_CHUNK, prompt_len)
        for first_key in range(0, prompt_len, size):
            rows = slice(first_key, first_key + size)
            mask = (lambda s, f=first_key: seen_prompt(s, f, shard_index)) if masked else None
            piece = part(
                kp_ref[rows, :], vp_ref[rows, :], kt_all[:, rows], queries, grads, level, inner,
                mask, prompt_acc, first_key,
            )
            total = piece if total is None else total + piece
        return total

    both_q, both_g, both_level, both_inner = [], [], [], []
    for side in range(2):
        both_q.append(head_rows(q_ref, 0, PROMPT_BLK, side, kv_half(side)))
        both_g.append(head_rows(grad_ref, 0, PROMPT_BLK, side, kv_half(side)))
        both_level.append(level_ref[side, :, :PROMPT_BLK])
        both_inner.append(inner_sums(0, PROMPT_BLK, side))
    grad_q = prompt_parts(
        jnp.concatenate(both_q, axis=0),
        jnp.concatenate(both_g, axis=0),
        jnp.concatenate(both_level, axis=1),
        jnp.concatenate(both_inner, axis=1),
        True,
    ).T
    for side in range(2):
        rows = slice(side * PROMPT_BLK, (side + 1) * PROMPT_BLK)
        acc[:PROMPT_BLK, :] += relane(grad_q[rows], kv_half(side), side)

    def step(turn, _):
        side = turn // conts
        number = turn % conts
        half = kv_half(side)
        first_own = PROMPT_BLK + number * CONT_LEN
        for chunk in range(CONT_LEN // QUERY_CHUNK):
            before = chunk * QUERY_CHUNK
            first_row = pl.multiple_of(first_own + before, PROMPT_BLK)
            queries = head_rows(q_ref, first_row, QUERY_CHUNK, side, half)
            grads = head_rows(grad_ref, first_row, QUERY_CHUNK, side, half)
            level = level_ref[side, :, pl.ds(first_row, QUERY_CHUNK)]
            inner = inner_sums(first_row, QUERY_CHUNK, side)
            grad_q = prompt_parts(queries, grads, level, inner, False)
            own = [(first_row, QUERY_CHUNK, below_diagonal)]
            if before:
                own.append((pl.multiple_of(first_own, PROMPT_BLK), before, None))
            for start, size, mask in own:
                rows = pl.ds(start, size)
                columns = pl.ds(pl.multiple_of(prompt_len + start, PROMPT_BLK), size)
                grad_q += part(
                    ko_ref[rows, :], vo_ref[rows, :], kt_all[:, columns], queries, grads, level,
                    inner, mask, down_ref, start,
                )
            acc[pl.ds(first_row, QUERY_CHUNK), :] += relane(grad_q.T, half, side)
        return 0

    lax.fori_loop(0, 2 * conts, step, 0)
    dq_ref[...] = acc[...] * HEAD_DIMENSION ** (-0.5)

    @pl.when(pair == last)
    def _():
        dprompt_ref[...] = prompt_acc[...].astype(bf16)


def pair_specs(block_len, prompt_len):
    by_pair = pl.BlockSpec((block_len, LANES), lambda b, i: (0, b))
    levels = pl.BlockSpec((2, 1, block_len), lambda b, i: (b, 0, 0))
    sources = [
        pl.BlockSpec((prompt_len, LANES), lambda b, i: (0, 0)),
        pl.BlockSpec((prompt_len, LANES), lambda b, i: (0, 1)),
        pl.BlockSpec((block_len, LANES), lambda b, i: (0, 0)),
        pl.BlockSpec((block_len, LANES), lambda b, i: (0, 1)),
    ]
    return by_pair, levels, sources


def attention_cost(block_len, prompt_len, width, products):
    pairs = (block_len * prompt_len + block_len * CONT_LEN // 2) * (width // HEAD_DIMENSION)
    return pl.CostEstimate(
        flops=products * 2 * pairs * 2 * LANES,
        bytes_accessed=8 * block_len * width,
        transcendentals=pairs,
    )


def attend_forward(index, queries, kv_prompt, kv_own, group, kv_heads):
    block_len, width = queries.shape
    prompt_len = kv_prompt.shape[0]
    by_pair, levels, sources = pair_specs(block_len, prompt_len)
    return pl.pallas_call(
        partial(attend_forward_body, group, kv_heads),
        out_shape=[
            jax.ShapeDtypeStruct((block_len, width), jnp.bfloat16),
            jax.ShapeDtypeStruct((width // HEAD_DIMENSION, 1, block_len), jnp.float32),
        ],
        grid_spec=pltpu.PrefetchScalarGridSpec(
            num_scalar_prefetch=1,
            grid=(width // LANES,),
            in_specs=[by_pair] + sources,
            out_specs=[by_pair, levels],
            scratch_shapes=[
                pltpu.VMEM((LANES, prompt_len + block_len), jnp.bfloat16),
                pltpu.VMEM((block_len, LANES), jnp.float32),
            ],
        ),
        compiler_params=pltpu.CompilerParams(
            dimension_semantics=("arbitrary",), vmem_limit_bytes=56 * 1024 * 1024
        ),
        cost_estimate=attention_cost(block_len, prompt_len, width, 2),
        name="attend_forward",
    )(index, queries, kv_prompt, kv_prompt, kv_own, kv_own)


def attend_backward(index, queries, grads, mixed, level, kv_prompt, kv_own, group, kv_heads):
    block_len, width = queries.shape
    prompt_len = kv_prompt.shape[0]
    by_pair, levels, sources = pair_specs(block_len, prompt_len)
    return pl.pallas_call(
        partial(attend_backward_body, group, kv_heads),
        out_shape=[
            jax.ShapeDtypeStruct((block_len, width), jnp.float32),
            jax.ShapeDtypeStruct((prompt_len, 2 * LANES), jnp.bfloat16),
            jax.ShapeDtypeStruct((block_len, 2 * LANES), jnp.float32),
        ],
        grid_spec=pltpu.PrefetchScalarGridSpec(
            num_scalar_prefetch=1,
            grid=(width // LANES,),
            in_specs=[by_pair, by_pair, by_pair, levels] + sources,
            out_specs=[
                by_pair,
                pl.BlockSpec((prompt_len, 2 * LANES), lambda b, i: (0, 0)),
                pl.BlockSpec((block_len, 2 * LANES), lambda b, i: (0, 0)),
            ],
            scratch_shapes=[
                pltpu.VMEM((LANES, prompt_len + block_len), jnp.bfloat16),
                pltpu.VMEM((block_len, LANES), jnp.float32),
                pltpu.VMEM((prompt_len, 2 * LANES), jnp.float32),
            ],
        ),
        compiler_params=pltpu.CompilerParams(
            dimension_semantics=("arbitrary",), vmem_limit_bytes=56 * 1024 * 1024
        ),
        cost_estimate=attention_cost(block_len, prompt_len, width, 5),
        name="attend_backward",
    )(index, queries, grads, mixed, level, kv_prompt, kv_prompt, kv_own, kv_own)


def to_lanes(values):
    extra = -values.shape[1] % LANES
    return jnp.pad(values, ((0, 0), (0, extra))) if extra else values


def exchange(values, axis_name, bit):
    count = lax.axis_size(axis_name)
    return lax.ppermute(values, axis_name, [(i, i ^ bit) for i in range(count)])


def bits_of(number):
    return [1 << k for k in range(number.bit_length()) if number >> k & 1]


def gather_blocks(own, axis_name, after_first=None):
    count = lax.axis_size(axis_name)
    half = own.shape[0] // 2
    blocks = {0: own, 1: exchange(own, axis_name, 1)}
    even = sorted(range(2, count, 2), key=lambda j: (len(bits_of(j)), j))
    singles = [j for j in even if len(bits_of(j)) == 1]
    for j in singles:
        blocks[j] = exchange(own, axis_name, j)
    if after_first is not None:
        blocks.update(zip(singles, after_first([blocks[j] for j in singles])))
    for j in even:
        bits = bits_of(j)
        if len(bits) > 1:
            low_bit, high_bit = bits[0], bits[-1]
            top = exchange(blocks[j ^ low_bit][:half], axis_name, low_bit)
            bottom = exchange(blocks[j ^ high_bit][half:], axis_name, high_bit)
            blocks[j] = jnp.concatenate([top, bottom], axis=0)
        blocks[j + 1] = exchange(blocks[j], axis_name, 1)
    return [blocks[j] for j in range(count)]


def pass_on(values, axis_name, step, way):
    count = lax.axis_size(axis_name)
    if way > 0:
        pairs = [(i, i + 1) for i in range(step - 1, count - 1)]
    else:
        pairs = [(i, i - 1) for i in range(1, count - step + 1)]
    return lax.ppermute(values, axis_name, pairs)


def gather_line(own, rising, falling, axis_name):
    count = lax.axis_size(axis_name)
    index = lax.axis_index(axis_name)
    rows = own.shape[0]
    buffer = jnp.zeros(((count + 1) * rows, own.shape[1]), own.dtype)
    buffer = lax.dynamic_update_slice_in_dim(buffer, own, index * rows, axis=0)
    for step in range(1, count):
        if step > 1:
            rising = pass_on(rising, axis_name, step, 1)
            falling = pass_on(falling, axis_name, step, -1)
        slot = jnp.where(index >= step, index - step, count)
        buffer = lax.dynamic_update_slice_in_dim(buffer, rising, slot * rows, axis=0)
        slot = jnp.where(index + step < count, index + step, count)
        buffer = lax.dynamic_update_slice_in_dim(buffer, falling, slot * rows, axis=0)
    return buffer[: count * rows]


def add_rounded(left_side, right_side):
    return (left_side.astype(jnp.float32) + right_side.astype(jnp.float32)).astype(jnp.bfloat16)


def fold(even, odd, axis_name):
    arrived = exchange(odd, axis_name, 1)
    half = even.shape[0] // 2
    return [add_rounded(even[:half], arrived[:half]), add_rounded(even[half:], arrived[half:])]


def reduce_blocks(blocks, axis_name):
    count = len(blocks)
    sums = {}
    for j in sorted(range(0, count, 2), key=lambda j: (-len(bits_of(j)), j)):
        sums[j] = fold(blocks[j], blocks[j + 1], axis_name)
    return reduce_singles(sums, reduce_several(sums, axis_name), axis_name)


def reduce_several(sums, axis_name):
    sums = {j: list(halves) for j, halves in sums.items()}
    pending = []
    for j in sorted((j for j in sums if len(bits_of(j)) > 1), key=lambda j: (-len(bits_of(j)), j)):
        low_bit, high_bit = bits_of(j)[0], bits_of(j)[-1]
        for part, bit in ((0, low_bit), (1, high_bit)):
            piece = exchange(sums[j][part], axis_name, bit)
            if len(bits_of(j ^ bit)) > 1:
                sums[j ^ bit][part] = add_rounded(sums[j ^ bit][part], piece)
            else:
                pending.append((j ^ bit, part, piece))
    return pending


def reduce_singles(sums, pending, axis_name):
    sums = {j: list(halves) for j, halves in sums.items()}
    for j, part, piece in pending:
        sums[j][part] = add_rounded(sums[j][part], piece)
    halves = []
    for part in range(2):
        total = sums[0][part].astype(jnp.float32)
        for j in sums:
            if len(bits_of(j)) == 1:
                total = total + exchange(sums[j][part], axis_name, j).astype(jnp.float32)
        halves.append(total)
    return jnp.concatenate(halves, axis=0)


def in_order(blocks, index):
    stacked = jnp.stack(blocks)
    return jnp.concatenate(
        [lax.dynamic_index_in_dim(stacked, j ^ index, 0, keepdims=True) for j in range(len(blocks))],
        axis=0,
    )


def relative_blocks(values, index, count):
    rows = values.shape[0] // count
    return [
        lax.dynamic_slice_in_dim(values, (index ^ j) * rows, rows, axis=0) for j in range(count)
    ]


def scatter_direct(pieces, axis_name):
    count = lax.axis_size(axis_name)
    index = lax.axis_index(axis_name)
    total = lax.dynamic_index_in_dim(pieces, index, 0, keepdims=False).astype(jnp.float32)
    for step in range(1, count):
        piece = lax.dynamic_index_in_dim(pieces, (index + step) % count, 0, keepdims=False)
        arrived = lax.ppermute(piece, axis_name, [(i, (i + step) % count) for i in range(count)])
        total = total + arrived.astype(jnp.float32)
    return total


def expert_body(
    experts_all, index_ref, x_even, x_odd, og_even, og_odd, gate_w, up_w, down_w, *rest
):
    (x_all, og_all, pre_all, hid_all, row_even, row_odd, out_even, out_odd) = rest[-12:-4]
    (row_acc, out_acc, back_acc, _) = rest[-4:]
    expert = pl.program_id(0)
    last = pl.num_programs(0) - 1
    rows = x_even.shape[0]
    width = x_all.shape[1]
    hidden_units = gate_w.shape[2]
    nt_dims = (((1,), (1,)), ((), ()))

    @pl.when(expert == 0)
    def _():
        x_all[:rows, :] = x_even[:, :width]
        x_all[rows:, :] = x_odd[:, :width]
        og_all[:rows, :] = og_even[...]
        og_all[rows:, :] = og_odd[...]

    column = index_ref[0] + expert
    lane = lax.broadcasted_iota(jnp.int32, (2 * rows, LANES), 1)
    coded = jnp.concatenate([x_even[:, width:], x_odd[:, width:]], axis=0).astype(jnp.float32)
    gate = jnp.sum(
        jnp.where((lane == column) | (lane == column + experts_all), coded, 0.0),
        axis=1,
        keepdims=True,
    )
    x_rows = x_all[...]
    og_rows = og_all[...]
    gate_pre = jnp.dot(x_rows, gate_w[0], preferred_element_type=jnp.float32)
    up_pre = jnp.dot(x_rows, up_w[0], preferred_element_type=jnp.float32)
    down_grad = lax.dot_general(og_rows, down_w[0], nt_dims, preferred_element_type=jnp.float32)
    sigmoid = 1.0 / (1.0 + jnp.exp(-gate_pre))
    silu = gate_pre * sigmoid
    hidden = silu * up_pre
    gate_back = jnp.sum(hidden * down_grad, axis=1, keepdims=True)
    hidden_low = (gate * hidden).astype(jnp.bfloat16)
    hidden_grad = gate * down_grad
    gate_pre_low = (
        hidden_grad * up_pre * sigmoid * (1.0 + gate_pre * (1.0 - sigmoid))
    ).astype(jnp.bfloat16)
    up_pre_low = (hidden_grad * silu).astype(jnp.bfloat16)
    hid_all[...] = hidden_low
    pre_all[0, :, :hidden_units] = gate_pre_low
    pre_all[0, :, hidden_units:] = up_pre_low
    row = lax.dot_general(
        gate_pre_low, gate_w[0], nt_dims, preferred_element_type=jnp.float32
    ) + lax.dot_general(up_pre_low, up_w[0], nt_dims, preferred_element_type=jnp.float32)
    out = jnp.dot(hidden_low, down_w[0], preferred_element_type=jnp.float32)
    high = gate_back.astype(jnp.bfloat16).astype(jnp.float32)
    back = jnp.where(lane == column, high, 0.0) + jnp.where(
        lane == column + experts_all, gate_back - high, 0.0
    )

    @pl.when(expert == 0)
    def _():
        row_acc[...] = row
        out_acc[...] = out
        back_acc[...] = back

    @pl.when(expert > 0)
    def _():
        row_acc[...] += row
        out_acc[...] += out
        back_acc[...] += back

    @pl.when(expert == last)
    def _():
        for ref, first in ((row_even, 0), (row_odd, rows)):
            ref[:, :width] = row_acc[first : first + rows, :].astype(jnp.bfloat16)
            ref[:, width:] = back_acc[first : first + rows, :].astype(jnp.bfloat16)
        out_even[...] = out_acc[:rows, :].astype(jnp.bfloat16)
        out_odd[...] = out_acc[rows:, :].astype(jnp.bfloat16)


def expert_pair(position, pairs, first_expert, experts_all, x_pair, og_pair, weights, carried):
    w_gate, w_up, w_down = weights
    rows, coded_width = x_pair[0].shape
    width = coded_width - LANES
    local_experts, _, hidden_units = w_gate.shape
    bf16 = jnp.bfloat16
    whole = 2 * rows
    fixed = lambda e, i: (0, 0)
    once = pl.Buffered(1)
    in_specs = (
        [pl.BlockSpec((rows, coded_width), fixed, pipeline_mode=once)] * 2
        + [pl.BlockSpec((rows, width), fixed, pipeline_mode=once)] * 2
        + [pl.BlockSpec((1, width, hidden_units), lambda e, i: (e, 0, 0))] * 2
        + [pl.BlockSpec((1, hidden_units, width), lambda e, i: (e, 0, 0))]
    )
    operands = [*x_pair, *og_pair, w_gate, w_up, w_down]
    aliases = {}
    if carried is not None:
        in_specs = in_specs + [pl.BlockSpec(memory_space=pl.ANY)] * 4
        aliases = {1 + len(operands) + k: k for k in range(4)}
        operands = operands + list(carried)
    out_shape = [
        jax.ShapeDtypeStruct((pairs * whole, width), bf16),
        jax.ShapeDtypeStruct((pairs * whole, width), bf16),
        jax.ShapeDtypeStruct((local_experts, pairs * whole, 2 * hidden_units), bf16),
        jax.ShapeDtypeStruct((pairs * whole, local_experts * hidden_units), bf16),
        jax.ShapeDtypeStruct((rows, coded_width), bf16),
        jax.ShapeDtypeStruct((rows, coded_width), bf16),
        jax.ShapeDtypeStruct((rows, width), bf16),
        jax.ShapeDtypeStruct((rows, width), bf16),
    ]
    out_specs = [
        pl.BlockSpec((whole, width), lambda e, i: (position, 0)),
        pl.BlockSpec((whole, width), lambda e, i: (position, 0)),
        pl.BlockSpec((1, whole, 2 * hidden_units), lambda e, i: (e, position, 0)),
        pl.BlockSpec((whole, hidden_units), lambda e, i: (position, e)),
        pl.BlockSpec((rows, coded_width), fixed),
        pl.BlockSpec((rows, coded_width), fixed),
        pl.BlockSpec((rows, width), fixed),
        pl.BlockSpec((rows, width), fixed),
    ]
    products = 2 * whole * width * hidden_units * local_experts
    results = pl.pallas_call(
        partial(expert_body, experts_all),
        out_shape=out_shape,
        grid_spec=pltpu.PrefetchScalarGridSpec(
            num_scalar_prefetch=1,
            grid=(local_experts,),
            in_specs=in_specs,
            out_specs=out_specs,
            scratch_shapes=[
                pltpu.VMEM((whole, width), jnp.float32),
                pltpu.VMEM((whole, width), jnp.float32),
                pltpu.VMEM((whole, LANES), jnp.float32),
                pltpu.VMEM((8, LANES), jnp.float32),
            ],
        ),
        input_output_aliases=aliases,
        compiler_params=pltpu.CompilerParams(
            dimension_semantics=("arbitrary",), vmem_limit_bytes=60 * 1024 * 1024
        ),
        cost_estimate=pl.CostEstimate(
            flops=6 * products,
            bytes_accessed=3 * 2 * local_experts * width * hidden_units + 20 * whole * width,
            transcendentals=whole * hidden_units * local_experts,
        ),
        name="experts",
    )(first_expert, *operands)
    return results[:4], results[4:]


def on_device(
    tokens,
    routes,
    w_query,
    key_projection,
    value_projection,
    w_out,
    gain_attn,
    gain_ffn,
    w_router,
    w_gate,
    w_up,
    w_down,
    out_grad,
):
    bf16 = jnp.bfloat16
    shard_count = lax.axis_size("shard")
    seq_count = lax.axis_size("seq")
    shard_index = lax.axis_index("shard")
    seq_index = lax.axis_index("seq")
    tok_count, model_width = tokens.shape
    top_count = routes.shape[1]
    experts_all = w_router.shape[1]
    local_experts = w_gate.shape[0]
    block_len = tok_count * seq_count
    prompt_len = PROMPT_BLK * shard_count
    query_width = w_query.shape[1]
    key_width = key_projection.shape[1]

    line = [pass_on(tokens, "seq", 1, 1), pass_on(tokens, "seq", 1, -1)]
    small = jnp.concatenate([w_router, gain_attn[:, None], gain_ffn[:, None]], axis=1)
    small = lax.all_gather(small, ("shard", "seq"), axis=0, tiled=True)
    router_weight = small[:, :experts_all]
    first_gain = small[:, experts_all].astype(jnp.float32)
    second_gain = small[:, experts_all + 1].astype(jnp.float32)
    own_weight = jnp.concatenate([w_query, key_projection, value_projection], axis=1)

    def after_tokens(blocks):
        blocks, line[:] = lax.optimization_barrier((blocks, line))
        return blocks

    qkv_weight = in_order(gather_blocks(own_weight, "shard", after_tokens), shard_index)
    block_tokens = gather_line(tokens, line[0], line[1], "seq")
    qkv_weight = qkv_weight.reshape(model_width, -1)
    out_weight = lax.all_gather(w_out, ("shard", "seq"), axis=0, tiled=False)
    out_weight = out_weight.reshape(shard_count, seq_count, *w_out.shape)
    out_weight = out_weight.transpose(1, 2, 0, 3).reshape(model_width, model_width)
    out_grad_late, qkv_weight = lax.optimization_barrier((out_grad, qkv_weight))
    grad_blocks = gather_blocks(out_grad_late, "shard")

    block_rows = jnp.arange(block_len, dtype=jnp.int32)
    cos_table, sin_table = rotary_tables(
        place_of(block_rows, shard_index, prompt_len), HEAD_DIMENSION
    )
    inputs = block_tokens.astype(jnp.float32)
    first_factor = rms_parts(inputs)
    normed_low = (inputs * first_factor * first_gain).astype(bf16)
    lin = matmul(normed_low, qkv_weight)
    kv_heads = key_width // HEAD_DIMENSION
    group = query_width // key_width
    queries = rotate(lin[:, :query_width], cos_table, sin_table, HEAD_DIMENSION)
    queries = to_lanes((queries * HEAD_DIMENSION ** (-0.5)).astype(bf16))
    key_heads = rotate(
        lin[:, query_width : query_width + key_width], cos_table, sin_table, HEAD_DIMENSION
    ).astype(bf16)
    value_heads = lin[:, query_width + key_width :].astype(bf16)
    kv_own = jnp.concatenate([to_lanes(key_heads), to_lanes(value_heads)], axis=1)
    kv_prompt = lax.all_gather(kv_own[:PROMPT_BLK], "shard", axis=0, tiled=True)
    block_number = shard_index.astype(jnp.int32).reshape(1)
    singles = [1 << k for k in range(1, (shard_count - 1).bit_length())]
    queries, grad_blocks[::2] = lax.optimization_barrier((queries, grad_blocks[::2]))
    mixed_own, levels = attend_forward(block_number, queries, kv_prompt, kv_own, group, kv_heads)
    mixed_own, grad_blocks = lax.optimization_barrier((mixed_own, grad_blocks))
    mixed_heads = mixed_own[:, :query_width]
    mixed_tokens = lax.all_to_all(mixed_heads, "seq", split_axis=0, concat_axis=1, tiled=True)

    half_features = model_width // 2
    core_bit = shard_index % 2
    half_weight, mixed_tokens = lax.optimization_barrier(
        (
            lax.dynamic_slice_in_dim(qkv_weight, core_bit * half_features, half_features, axis=0),
            mixed_tokens,
        )
    )
    wide_half = lax.all_gather(half_weight, "seq", axis=0, tiled=False)

    own_inputs = tokens.astype(jnp.float32)
    upstream = out_grad.astype(jnp.float32)
    residual = own_inputs + matmul(mixed_tokens, out_weight)
    second_factor = rms_parts(residual)
    second_low = (residual * second_factor * second_gain).astype(bf16)
    logits = matmul(second_low, router_weight)
    chosen = routes[:, :, None] == jnp.arange(experts_all, dtype=jnp.int32)[None, None, :]
    named = jnp.any(chosen, axis=1)
    gate_dense = jax.nn.softmax(jnp.where(named, logits, negative), axis=-1)
    gate_dense = jnp.where(named, gate_dense, 0.0)

    gate_high = lax.reduce_precision(gate_dense, 8, 7)
    coded = jnp.concatenate(
        [
            second_low,
            gate_high.astype(bf16),
            (gate_dense - gate_high).astype(bf16),
            jnp.zeros((tok_count, LANES - 2 * experts_all), bf16),
        ],
        axis=1,
    )
    row_blocks = {0: coded, 1: exchange(coded, "shard", 1)}
    for bit in singles:
        row_blocks[bit] = exchange(coded, "shard", bit)
    several = sorted(
        (j for j in range(0, shard_count, 2) if len(bits_of(j)) > 1),
        key=lambda j: (len(bits_of(j)), j),
    )
    order = [0] + singles[:-1] + several + singles[-1:]
    first_expert = (shard_index * local_experts).astype(jnp.int32).reshape(1)
    carried = None
    row_sums = {}
    out_parts = [None] * shard_count
    for position, j in enumerate(order):
        row_pair = [row_blocks[j], row_blocks[j + 1]]
        if j == order[-1]:
            row_pair, row_sums = lax.optimization_barrier((row_pair, row_sums))
            pending = reduce_several(row_sums, "shard")
        carried, pieces = expert_pair(
            position,
            len(order),
            first_expert,
            experts_all,
            row_pair,
            grad_blocks[j : j + 2],
            (w_gate, w_up, w_down),
            carried,
        )
        pieces = list(pieces)
        if j == 0:
            arrived, pieces[2] = lax.optimization_barrier(
                ([row_blocks[bit] for bit in singles], pieces[2])
            )
            row_blocks.update(zip(singles, arrived))
            half = tok_count // 2
            for k in singles + several:
                if k in several:
                    low_bit, high_bit = bits_of(k)[0], bits_of(k)[-1]
                    top = exchange(row_blocks[k ^ low_bit][:half], "shard", low_bit)
                    bottom = exchange(row_blocks[k ^ high_bit][half:], "shard", high_bit)
                    row_blocks[k] = jnp.concatenate([top, bottom], axis=0)
                row_blocks[k + 1] = exchange(row_blocks[k], "shard", 1)
        row_sums[j] = fold(pieces[0], pieces[1], "shard")
        out_parts[j], out_parts[j + 1] = pieces[2], pieces[3]
    all_rows, all_grads, all_pre, all_hidden = carried
    arrived = [piece for _, _, piece in pending]
    row_sums, all_grads, arrived = lax.optimization_barrier((row_sums, all_grads, arrived))
    pending = [(j, part, piece) for (j, part, _), piece in zip(pending, arrived)]
    down_sum = transposed_times(all_grads, all_hidden).astype(bf16)
    row_total = reduce_singles(row_sums, pending, "shard")
    row_total, down_sum = lax.optimization_barrier((row_total, down_sum))
    row_grad = row_total[:, :model_width]
    gate_grad_dense = (
        row_total[:, model_width : model_width + experts_all]
        + row_total[:, model_width + experts_all : model_width + 2 * experts_all]
    )
    weighted = gate_dense * gate_grad_dense
    logit_grad = weighted - gate_dense * jnp.sum(weighted, axis=-1, keepdims=True)
    grad_router = transposed_times(second_low.astype(jnp.float32), logit_grad, highest)
    second_grad = row_grad + times_transposed(
        logit_grad, router_weight.astype(jnp.float32), highest
    )
    residual_part, grad_gain_ffn = rms_backward(residual, second_factor, second_gain, second_grad)
    residual_grad = upstream + residual_part
    residual_low = residual_grad.astype(bf16)
    mixed_grad_tokens = times_transposed(residual_low, out_weight).astype(bf16)
    other_half = exchange(wide_half, "shard", 1)
    mixed_grad_tokens, out_parts, all_rows, other_half, mixed_late = lax.optimization_barrier(
        (mixed_grad_tokens, out_parts, all_rows, other_half, mixed_tokens)
    )
    mixed_grad = lax.all_to_all(mixed_grad_tokens, "seq", split_axis=1, concat_axis=0, tiled=True)
    pre_sums = [transposed_times(all_rows, all_pre[e]).astype(bf16) for e in range(local_experts)]
    mixed_grad, pre_sums = lax.optimization_barrier((mixed_grad, pre_sums))
    expert_sum = reduce_blocks(out_parts, "shard")
    output = (residual + expert_sum).astype(bf16)
    columns = [
        lax.dynamic_slice_in_dim(
            residual_low,
            (shard_index ^ j) * (model_width // shard_count),
            model_width // shard_count,
            axis=1,
        )
        for j in range(shard_count)
    ]
    whole_out = [transposed_times(part, mixed_late).astype(bf16) for part in columns]
    grad_out = reduce_blocks(whole_out, "shard").astype(bf16)
    grad_out = grad_out.reshape(grad_out.shape[0], seq_count, -1).transpose(1, 0, 2)
    grad_out = scatter_direct(grad_out, "seq").T

    query_grad, prompt_grad, self_grad = attend_backward(
        block_number,
        queries,
        to_lanes(mixed_grad),
        mixed_own,
        levels,
        kv_prompt,
        kv_own,
        group,
        kv_heads,
    )
    query_grad = query_grad[:, :query_width]
    own_prompt = reduce_blocks(relative_blocks(prompt_grad, shard_index, shard_count), "shard")
    key_grad = jnp.concatenate(
        [own_prompt[:, :key_width], self_grad[PROMPT_BLK:, :key_width]], axis=0
    )
    value_low = jnp.concatenate(
        [own_prompt[:, LANES : LANES + key_width], self_grad[PROMPT_BLK:, LANES : LANES + key_width]],
        axis=0,
    ).astype(bf16)
    lin_query = rotate(query_grad, cos_table, -sin_table, HEAD_DIMENSION).astype(bf16)
    lin_key = rotate(key_grad, cos_table, -sin_table, HEAD_DIMENSION).astype(bf16)
    lin_both = jnp.concatenate([lin_key, value_low], axis=1)
    query_tokens = lax.all_to_all(lin_query, "seq", split_axis=0, concat_axis=1, tiled=True)
    lin_both, query_tokens = lax.optimization_barrier((lin_both, query_tokens))
    both_tokens = lax.all_to_all(lin_both, "seq", split_axis=0, concat_axis=1, tiled=True)
    parts = [0.0, 0.0]
    for lin, first, last in (
        (query_tokens, 0, query_width),
        (both_tokens, query_width, query_width + 2 * key_width),
    ):
        for k, weight in enumerate((wide_half, other_half)):
            for group_index in range(seq_count):
                columns = slice(group_index * (last - first), (group_index + 1) * (last - first))
                parts[k] = parts[k] + times_transposed(
                    lin[:, columns], weight[group_index, :, first:last]
                )
    normed_grad = jnp.concatenate(
        [
            jnp.where(core_bit == 0, parts[0], parts[1]),
            jnp.where(core_bit == 0, parts[1], parts[0]),
        ],
        axis=1,
    )
    small_grad = jnp.concatenate([grad_router, grad_gain_ffn[:, None]], axis=1)
    grad_qkv = jnp.concatenate(
        [
            transposed_times(normed_low, lin_query),
            transposed_times(normed_low, lin_both),
            small_grad,
        ],
        axis=1,
    )
    grad_qkv = reduce_blocks(
        relative_blocks(grad_qkv.astype(bf16), shard_index, shard_count), "shard"
    )
    own_features = own_weight.shape[0]
    gain_own = lax.dynamic_slice_in_dim(first_gain, shard_index * own_features, own_features)
    all_columns = own_weight.shape[1]
    gain_part = (
        jnp.sum(own_weight.astype(jnp.float32) * grad_qkv[:, :all_columns], axis=1) / gain_own
    )
    grad_query = grad_qkv[:, :query_width]
    grad_key = grad_qkv[:, query_width : query_width + key_width]
    grad_value = grad_qkv[:, query_width + key_width : query_width + 2 * key_width]
    small_grad = jnp.concatenate([grad_qkv[:, all_columns:], gain_part[:, None]], axis=1).astype(bf16)
    small_grad = scatter_direct(
        small_grad.reshape(seq_count, -1, small_grad.shape[1]), "seq"
    )
    own_factor = rms_parts(own_inputs)
    input_part, _ = rms_backward(own_inputs, own_factor, first_gain, normed_grad)
    tokens_grad = residual_grad + input_part
    grad_down = lax.psum_scatter(down_sum, "seq", scatter_dimension=0, tiled=True)
    pre_grads = [
        lax.psum_scatter(part, "seq", scatter_dimension=0, tiled=True) for part in pre_sums
    ]
    hidden_units = w_gate.shape[2]
    grad_down = grad_down.T.reshape(local_experts, hidden_units, -1)
    grad_gate = jnp.stack([part[:, :hidden_units] for part in pre_grads])
    grad_up = jnp.stack([part[:, hidden_units:] for part in pre_grads])
    return (
        output,
        tokens_grad,
        grad_query,
        grad_key,
        grad_value,
        grad_out,
        small_grad[:, experts_all + 1],
        small_grad[:, experts_all],
        small_grad[:, :experts_all],
        grad_gate.astype(jnp.float32),
        grad_up.astype(jnp.float32),
        grad_down.astype(jnp.float32),
    )


def solution(mesh):
    return jax.shard_map(
        on_device,
        mesh=mesh,
        in_specs=(
            P(("shard", "seq"), None),
            P(("shard", "seq"), None),
            P("shard", "seq"),
            P("shard", "seq"),
            P("shard", "seq"),
            P("seq", "shard"),
            P(("shard", "seq")),
            P(("shard", "seq")),
            P(("shard", "seq"), None),
            P("shard", None, None),
            P("shard", None, None),
            P("shard", None, None),
            P(("shard", "seq"), None),
        ),
        out_specs=(
            P(("shard", "seq"), None),
            P(("shard", "seq"), None),
            P("shard", "seq"),
            P("shard", "seq"),
            P("shard", "seq"),
            P("seq", "shard"),
            P(("shard", "seq")),
            P(("shard", "seq")),
            P(("shard", "seq"), None),
            P("shard", "seq", None),
            P("shard", "seq", None),
            P("shard", None, "seq"),
        ),
        check_vma=False,
    )
```

```python
from functools import partial

import jax
import jax.numpy as jnp
from jax import lax
from jax.experimental import pallas as pl
from jax.experimental.pallas import tpu as pltpu
from jax.sharding import PartitionSpec as P

HEAD_DIMENSION = 64
CONT_LEN = 512
PROMPT_BLK = 128


norm_eps = 1e-05
negative = -1e30
rope_base = 10000.0
highest = lax.Precision.HIGHEST


def rms_norm(values, scaling):
    factor = lax.rsqrt(jnp.mean(values * values, axis=-1, keepdims=True) + norm_eps)
    return values * factor * scaling


def swiglu(gate_pre, up_pre):
    return jax.nn.silu(gate_pre) * up_pre


def rotary_tables(places, head_size):
    half_size = head_size // 2
    frequency = jnp.exp(
        jnp.arange(half_size, dtype=jnp.float32) * (-2.0 * jnp.log(rope_base) / head_size)
    )
    angles = places.astype(jnp.float32)[:, None] * frequency[None, :]
    return (jnp.cos(angles)[:, None, :], jnp.sin(angles)[:, None, :])


def rotate(values, cosine, sine, head_size):
    total_row_count = values.shape[0]
    by_head = values.reshape(total_row_count, -1, head_size)
    half_size = head_size // 2
    first_half = by_head[..., :half_size]
    second_half = by_head[..., half_size:]
    turned = jnp.concatenate(
        [first_half * cosine - second_half * sine, second_half * cosine + first_half * sine],
        axis=-1,
    )
    return turned.reshape(total_row_count, -1)


def place_of(within, block_index, prompt_len):
    return jnp.where(
        within < PROMPT_BLK,
        block_index * PROMPT_BLK + within,
        prompt_len + (within - PROMPT_BLK) % CONT_LEN,
    )


def times_transposed(left_side, right_side, precision=None):
    return lax.dot_general(
        left_side,
        right_side,
        (((1,), (1,)), ((), ())),
        precision=precision,
        preferred_element_type=jnp.float32,
    )


def transposed_times(left_side, right_side, precision=None):
    return lax.dot_general(
        left_side,
        right_side,
        (((0,), (0,)), ((), ())),
        precision=precision,
        preferred_element_type=jnp.float32,
    )


def rms_parts(values):
    return lax.rsqrt(jnp.mean(values * values, axis=-1, keepdims=True) + norm_eps)


def rms_backward(values, factor, scaling, normed_grad):
    scaled = scaling * normed_grad
    inner = jnp.mean(scaled * values, axis=-1, keepdims=True)
    values_grad = factor * scaled - values * (factor * factor * factor) * inner
    gain_grad = jnp.sum(normed_grad * values * factor, axis=0)
    return values_grad, gain_grad


def matmul(left_side, right_side):
    return jnp.dot(left_side, right_side, preferred_element_type=jnp.float32)


LANES = 128


def relane(values, source, target):
    lane = lax.broadcasted_iota(jnp.int32, values.shape, 1)
    swapped = jnp.where(source != target, pltpu.roll(values, HEAD_DIMENSION, 1), values)
    return jnp.where(lane // HEAD_DIMENSION == target, swapped, 0.0)


def head_rows(ref, first, count, source, target):
    values = ref[pl.ds(first, count), :].astype(jnp.float32)
    return relane(values, source, target).astype(jnp.bfloat16)


def nt_dot(left_side, right_side):
    return lax.dot_general(
        left_side, right_side, (((1,), (1,)), ((), ())), preferred_element_type=jnp.float32
    )


def nn_dot(left_side, right_side):
    return jnp.dot(left_side, right_side, preferred_element_type=jnp.float32)


def below_diagonal(scores):
    key_row = lax.broadcasted_iota(jnp.int32, scores.shape, 0)
    query_column = lax.broadcasted_iota(jnp.int32, scores.shape, 1)
    return jnp.where(key_row <= query_column, scores, negative)


def seen_prompt(scores, first_key, shard_index):
    key_row = lax.broadcasted_iota(jnp.int32, scores.shape, 0) + first_key
    query_column = lax.broadcasted_iota(jnp.int32, scores.shape, 1) % PROMPT_BLK
    return jnp.where(key_row <= query_column + shard_index * PROMPT_BLK, scores, negative)


def transposed(values):
    return values.astype(jnp.float32).T


QUERY_CHUNK = 512
KEY_CHUNK = 1024
FORWARD_CHUNK = 256


def attend_forward_body(
    group, kv_heads, index_ref, q_ref, kp_ref, vp_ref, ko_ref, vo_ref, mixed_ref, level_ref, vt_all, acc
):
    pair = pl.program_id(0)
    prompt_len = kp_ref.shape[0]
    block_len = ko_ref.shape[0]
    conts = (block_len - PROMPT_BLK) // CONT_LEN
    shard_index = index_ref[0]

    @pl.when(pair == 0)
    def _():
        vt_all[:, :prompt_len] = transposed(vp_ref[...]).astype(jnp.bfloat16)
        vt_all[:, prompt_len:] = transposed(vo_ref[...]).astype(jnp.bfloat16)

    acc[...] = jnp.zeros_like(acc)
    size = min(FORWARD_CHUNK, prompt_len)
    prompt_keys = [slice(first, first + size) for first in range(0, prompt_len, size)]

    def kv_half(side):
        return jnp.minimum((2 * pair + side) // group, kv_heads - 1)

    def finish(scores, value_columns):
        level = jnp.max(scores[0], axis=0, keepdims=True)
        for part in scores[1:]:
            level = jnp.maximum(level, jnp.max(part, axis=0, keepdims=True))
        total = None
        mixed = None
        for part, columns in zip(scores, value_columns):
            weights = jnp.exp(part - level)
            part_total = jnp.sum(weights, axis=0, keepdims=True)
            part_mixed = nn_dot(columns, weights.astype(jnp.bfloat16))
            total = part_total if total is None else total + part_total
            mixed = part_mixed if mixed is None else mixed + part_mixed
        return mixed / total, level + jnp.log(total)

    both = jnp.concatenate(
        [head_rows(q_ref, 0, PROMPT_BLK, side, kv_half(side)) for side in range(2)], axis=0
    )
    mixed, level = finish(
        [
            seen_prompt(nt_dot(kp_ref[keys, :], both), keys.start, shard_index)
            for keys in prompt_keys
        ],
        [vt_all[:, keys] for keys in prompt_keys],
    )
    mixed = mixed.T
    for side in range(2):
        rows = slice(side * PROMPT_BLK, (side + 1) * PROMPT_BLK)
        acc[:PROMPT_BLK, :] += relane(mixed[rows], kv_half(side), side)
        level_ref[side, :, :PROMPT_BLK] = level[:, rows]

    def step(turn, _):
        side = turn // conts
        number = turn % conts
        half = kv_half(side)
        first_own = PROMPT_BLK + number * CONT_LEN
        for chunk in range(CONT_LEN // QUERY_CHUNK):
            before = chunk * QUERY_CHUNK
            first_row = pl.multiple_of(first_own + before, PROMPT_BLK)
            queries = head_rows(q_ref, first_row, QUERY_CHUNK, side, half)
            scores = [nt_dot(kp_ref[keys, :], queries) for keys in prompt_keys]
            columns = [vt_all[:, keys] for keys in prompt_keys]
            if before:
                start = pl.multiple_of(first_own, PROMPT_BLK)
                scores.append(nt_dot(ko_ref[pl.ds(start, before), :], queries))
                columns.append(
                    vt_all[:, pl.ds(pl.multiple_of(prompt_len + start, PROMPT_BLK), before)]
                )
            scores.append(below_diagonal(nt_dot(ko_ref[pl.ds(first_row, QUERY_CHUNK), :], queries)))
            columns.append(
                vt_all[:, pl.ds(pl.multiple_of(prompt_len + first_row, PROMPT_BLK), QUERY_CHUNK)]
            )
            mixed, level = finish(scores, columns)
            acc[pl.ds(first_row, QUERY_CHUNK), :] += relane(mixed.T, half, side)
            level_ref[side, :, pl.ds(first_row, QUERY_CHUNK)] = level
        return 0

    lax.fori_loop(0, 2 * conts, step, 0)
    mixed_ref[...] = acc[...].astype(jnp.bfloat16)


def attend_backward_body(
    group,
    kv_heads,
    index_ref,
    q_ref,
    grad_ref,
    mixed_ref,
    level_ref,
    kp_ref,
    vp_ref,
    ko_ref,
    vo_ref,
    dq_ref,
    dprompt_ref,
    down_ref,
    kt_all,
    acc,
    prompt_acc,
):
    pair = pl.program_id(0)
    last = pl.num_programs(0) - 1
    prompt_len = kp_ref.shape[0]
    block_len = ko_ref.shape[0]
    conts = (block_len - PROMPT_BLK) // CONT_LEN
    shard_index = index_ref[0]
    bf16 = jnp.bfloat16

    @pl.when(pair == 0)
    def _():
        kt_all[:, :prompt_len] = transposed(kp_ref[...]).astype(bf16)
        kt_all[:, prompt_len:] = transposed(ko_ref[...]).astype(bf16)
        prompt_acc[...] = jnp.zeros_like(prompt_acc)
        down_ref[...] = jnp.zeros_like(down_ref)

    acc[...] = jnp.zeros_like(acc)

    def kv_half(side):
        return jnp.minimum((2 * pair + side) // group, kv_heads - 1)

    def inner_sums(first_row, count, side):
        rows = pl.ds(first_row, count)
        product = mixed_ref[rows, :].astype(jnp.float32) * grad_ref[rows, :].astype(jnp.float32)
        return jnp.sum(relane(product, side, side).T, axis=0, keepdims=True)

    def part(keys, values, key_columns, queries, grads, level, inner, mask, sums, first_key):
        scores = nt_dot(keys, queries)
        if mask is not None:
            scores = mask(scores)
        probs = jnp.exp(scores - level)
        score_grad = (probs * (nt_dot(values, grads) - inner)).astype(bf16)
        rows = pl.ds(first_key, keys.shape[0])
        sums[rows, :LANES] += nn_dot(score_grad, queries)
        sums[rows, LANES:] += nn_dot(probs.astype(bf16), grads)
        return nn_dot(key_columns, score_grad)

    def prompt_parts(queries, grads, level, inner, masked):
        total = None
        size = min(KEY_CHUNK, prompt_len)
        for first_key in range(0, prompt_len, size):
            rows = slice(first_key, first_key + size)
            mask = (lambda s, f=first_key: seen_prompt(s, f, shard_index)) if masked else None
            piece = part(
                kp_ref[rows, :], vp_ref[rows, :], kt_all[:, rows], queries, grads, level, inner,
                mask, prompt_acc, first_key,
            )
            total = piece if total is None else total + piece
        return total

    both_q, both_g, both_level, both_inner = [], [], [], []
    for side in range(2):
        both_q.append(head_rows(q_ref, 0, PROMPT_BLK, side, kv_half(side)))
        both_g.append(head_rows(grad_ref, 0, PROMPT_BLK, side, kv_half(side)))
        both_level.append(level_ref[side, :, :PROMPT_BLK])
        both_inner.append(inner_sums(0, PROMPT_BLK, side))
    grad_q = prompt_parts(
        jnp.concatenate(both_q, axis=0),
        jnp.concatenate(both_g, axis=0),
        jnp.concatenate(both_level, axis=1),
        jnp.concatenate(both_inner, axis=1),
        True,
    ).T
    for side in range(2):
        rows = slice(side * PROMPT_BLK, (side + 1) * PROMPT_BLK)
        acc[:PROMPT_BLK, :] += relane(grad_q[rows], kv_half(side), side)

    def step(turn, _):
        side = turn // conts
        number = turn % conts
        half = kv_half(side)
        first_own = PROMPT_BLK + number * CONT_LEN
        for chunk in range(CONT_LEN // QUERY_CHUNK):
            before = chunk * QUERY_CHUNK
            first_row = pl.multiple_of(first_own + before, PROMPT_BLK)
            queries = head_rows(q_ref, first_row, QUERY_CHUNK, side, half)
            grads = head_rows(grad_ref, first_row, QUERY_CHUNK, side, half)
            level = level_ref[side, :, pl.ds(first_row, QUERY_CHUNK)]
            inner = inner_sums(first_row, QUERY_CHUNK, side)
            grad_q = prompt_parts(queries, grads, level, inner, False)
            own = [(first_row, QUERY_CHUNK, below_diagonal)]
            if before:
                own.append((pl.multiple_of(first_own, PROMPT_BLK), before, None))
            for start, size, mask in own:
                rows = pl.ds(start, size)
                columns = pl.ds(pl.multiple_of(prompt_len + start, PROMPT_BLK), size)
                grad_q += part(
                    ko_ref[rows, :], vo_ref[rows, :], kt_all[:, columns], queries, grads, level,
                    inner, mask, down_ref, start,
                )
            acc[pl.ds(first_row, QUERY_CHUNK), :] += relane(grad_q.T, half, side)
        return 0

    lax.fori_loop(0, 2 * conts, step, 0)
    dq_ref[...] = acc[...] * HEAD_DIMENSION ** (-0.5)

    @pl.when(pair == last)
    def _():
        dprompt_ref[...] = prompt_acc[...].astype(bf16)


def pair_specs(block_len, prompt_len):
    by_pair = pl.BlockSpec((block_len, LANES), lambda b, i: (0, b))
    levels = pl.BlockSpec((2, 1, block_len), lambda b, i: (b, 0, 0))
    sources = [
        pl.BlockSpec((prompt_len, LANES), lambda b, i: (0, 0)),
        pl.BlockSpec((prompt_len, LANES), lambda b, i: (0, 1)),
        pl.BlockSpec((block_len, LANES), lambda b, i: (0, 0)),
        pl.BlockSpec((block_len, LANES), lambda b, i: (0, 1)),
    ]
    return by_pair, levels, sources


def attention_cost(block_len, prompt_len, width, products):
    pairs = (block_len * prompt_len + block_len * CONT_LEN // 2) * (width // HEAD_DIMENSION)
    return pl.CostEstimate(
        flops=products * 2 * pairs * 2 * LANES,
        bytes_accessed=8 * block_len * width,
        transcendentals=pairs,
    )


def attend_forward(index, queries, kv_prompt, kv_own, group, kv_heads):
    block_len, width = queries.shape
    prompt_len = kv_prompt.shape[0]
    by_pair, levels, sources = pair_specs(block_len, prompt_len)
    return pl.pallas_call(
        partial(attend_forward_body, group, kv_heads),
        out_shape=[
            jax.ShapeDtypeStruct((block_len, width), jnp.bfloat16),
            jax.ShapeDtypeStruct((width // HEAD_DIMENSION, 1, block_len), jnp.float32),
        ],
        grid_spec=pltpu.PrefetchScalarGridSpec(
            num_scalar_prefetch=1,
            grid=(width // LANES,),
            in_specs=[by_pair] + sources,
            out_specs=[by_pair, levels],
            scratch_shapes=[
                pltpu.VMEM((LANES, prompt_len + block_len), jnp.bfloat16),
                pltpu.VMEM((block_len, LANES), jnp.float32),
            ],
        ),
        compiler_params=pltpu.CompilerParams(
            dimension_semantics=("arbitrary",), vmem_limit_bytes=56 * 1024 * 1024
        ),
        cost_estimate=attention_cost(block_len, prompt_len, width, 2),
        name="attend_forward",
    )(index, queries, kv_prompt, kv_prompt, kv_own, kv_own)


def attend_backward(index, queries, grads, mixed, level, kv_prompt, kv_own, group, kv_heads):
    block_len, width = queries.shape
    prompt_len = kv_prompt.shape[0]
    by_pair, levels, sources = pair_specs(block_len, prompt_len)
    return pl.pallas_call(
        partial(attend_backward_body, group, kv_heads),
        out_shape=[
            jax.ShapeDtypeStruct((block_len, width), jnp.float32),
            jax.ShapeDtypeStruct((prompt_len, 2 * LANES), jnp.bfloat16),
            jax.ShapeDtypeStruct((block_len, 2 * LANES), jnp.float32),
        ],
        grid_spec=pltpu.PrefetchScalarGridSpec(
            num_scalar_prefetch=1,
            grid=(width // LANES,),
            in_specs=[by_pair, by_pair, by_pair, levels] + sources,
            out_specs=[
                by_pair,
                pl.BlockSpec((prompt_len, 2 * LANES), lambda b, i: (0, 0)),
                pl.BlockSpec((block_len, 2 * LANES), lambda b, i: (0, 0)),
            ],
            scratch_shapes=[
                pltpu.VMEM((LANES, prompt_len + block_len), jnp.bfloat16),
                pltpu.VMEM((block_len, LANES), jnp.float32),
                pltpu.VMEM((prompt_len, 2 * LANES), jnp.float32),
            ],
        ),
        compiler_params=pltpu.CompilerParams(
            dimension_semantics=("arbitrary",), vmem_limit_bytes=56 * 1024 * 1024
        ),
        cost_estimate=attention_cost(block_len, prompt_len, width, 5),
        name="attend_backward",
    )(index, queries, grads, mixed, level, kv_prompt, kv_prompt, kv_own, kv_own)


def to_lanes(values):
    extra = -values.shape[1] % LANES
    return jnp.pad(values, ((0, 0), (0, extra))) if extra else values


def exchange(values, axis_name, bit):
    count = lax.axis_size(axis_name)
    return lax.ppermute(values, axis_name, [(i, i ^ bit) for i in range(count)])


def bits_of(number):
    return [1 << k for k in range(number.bit_length()) if number >> k & 1]


def even_blocks(count):
    even = sorted(range(2, count, 2), key=lambda j: (len(bits_of(j)), j))
    singles = [j for j in even if len(bits_of(j)) == 1]
    return singles, even[len(singles) :]


def gather_blocks(own, axis_name, after_first=None):
    count = lax.axis_size(axis_name)
    singles, several = even_blocks(count)
    blocks = {0: own, 1: exchange(own, axis_name, 1)}
    for j in singles:
        blocks[j] = exchange(own, axis_name, j)
    if after_first is not None:
        blocks.update(zip(singles, after_first([blocks[j] for j in singles])))
    for j in several:
        low_bit = bits_of(j)[0]
        blocks[j] = exchange(blocks[j ^ low_bit], axis_name, low_bit)
    for j in singles + several:
        blocks[j + 1] = exchange(blocks[j], axis_name, 1)
    return [blocks[j] for j in range(count)]


def pass_on(values, axis_name, step, way):
    count = lax.axis_size(axis_name)
    if way > 0:
        pairs = [(i, i + 1) for i in range(step - 1, count - 1)]
    else:
        pairs = [(i, i - 1) for i in range(1, count - step + 1)]
    return lax.ppermute(values, axis_name, pairs)


def gather_line(owns, axis_name, after_first, after_last):
    count = lax.axis_size(axis_name)
    index = lax.axis_index(axis_name)
    rising, falling = list(owns), list(owns)
    arrived = []
    for step in range(1, count):
        rising = [pass_on(own, axis_name, step, 1) for own in rising]
        falling = [pass_on(own, axis_name, step, -1) for own in falling]
        if step == 1:
            rising, falling = after_first((rising, falling))
        if step == count - 1:
            rising, falling = after_last((rising, falling))
        arrived.append((rising, falling))
    results = []
    for k, own in enumerate(owns):
        rows = own.shape[0]
        buffer = jnp.zeros(((count + 1) * rows, own.shape[1]), own.dtype)
        buffer = lax.dynamic_update_slice_in_dim(buffer, own, index * rows, axis=0)
        for step, (rising, falling) in enumerate(arrived, 1):
            slot = jnp.where(index >= step, index - step, count)
            buffer = lax.dynamic_update_slice_in_dim(buffer, rising[k], slot * rows, axis=0)
            slot = jnp.where(index + step < count, index + step, count)
            buffer = lax.dynamic_update_slice_in_dim(buffer, falling[k], slot * rows, axis=0)
        results.append(buffer[: count * rows])
    return results


def add_rounded(left_side, right_side):
    return (left_side.astype(jnp.float32) + right_side.astype(jnp.float32)).astype(jnp.bfloat16)


def reduce_several(sums, axis_name):
    sums = dict(sums)
    pending = []
    for j in sorted((j for j in sums if len(bits_of(j)) > 1), key=lambda j: (-len(bits_of(j)), j)):
        bit = bits_of(j)[-1]
        piece = exchange(sums[j], axis_name, bit)
        if len(bits_of(j ^ bit)) > 1:
            sums[j ^ bit] = add_rounded(sums[j ^ bit], piece)
        else:
            pending.append((j ^ bit, piece))
    return pending


def reduce_singles(sums, pending, axis_name):
    sums = dict(sums)
    for j, piece in pending:
        sums[j] = add_rounded(sums[j], piece)
    return [sums[0]] + [exchange(sums[j], axis_name, j) for j in sums if len(bits_of(j)) == 1]


def add_all(pieces):
    total = pieces[0].astype(jnp.float32)
    for piece in pieces[1:]:
        total = total + piece.astype(jnp.float32)
    return total


def reduce_blocks(blocks, axis_name):
    singles, several = even_blocks(len(blocks))
    sums = {
        j: add_rounded(blocks[j], exchange(blocks[j + 1], axis_name, 1))
        for j in several[::-1] + singles + [0]
    }
    return add_all(reduce_singles(sums, reduce_several(sums, axis_name), axis_name))


def in_order(blocks, index):
    stacked = jnp.stack(blocks)
    return jnp.concatenate(
        [lax.dynamic_index_in_dim(stacked, j ^ index, 0, keepdims=True) for j in range(len(blocks))],
        axis=0,
    )


def relative_blocks(values, index, count):
    rows = values.shape[0] // count
    return [
        lax.dynamic_slice_in_dim(values, (index ^ j) * rows, rows, axis=0) for j in range(count)
    ]


def scatter_direct(pieces, axis_name):
    count = lax.axis_size(axis_name)
    index = lax.axis_index(axis_name)
    total = lax.dynamic_index_in_dim(pieces, index, 0, keepdims=False).astype(jnp.float32)
    for step in range(1, count):
        piece = lax.dynamic_index_in_dim(pieces, (index + step) % count, 0, keepdims=False)
        arrived = lax.ppermute(piece, axis_name, [(i, (i + step) % count) for i in range(count)])
        total = total + arrived.astype(jnp.float32)
    return total


def expert_body(
    experts_all, index_ref, x_even, x_odd, og_even, og_odd, gate_w, up_w, down_w, *rest
):
    (x_all, og_all, pre_all, hid_all, row_even, row_odd, out_even, out_odd) = rest[-12:-4]
    (row_acc, out_acc, back_acc, _) = rest[-4:]
    expert = pl.program_id(0)
    last = pl.num_programs(0) - 1
    rows = x_even.shape[0]
    width = x_all.shape[1]
    hidden_units = gate_w.shape[2]
    nt_dims = (((1,), (1,)), ((), ()))

    @pl.when(expert == 0)
    def _():
        x_all[:rows, :] = x_even[:, :width]
        x_all[rows:, :] = x_odd[:, :width]
        og_all[:rows, :] = og_even[...]
        og_all[rows:, :] = og_odd[...]

    column = index_ref[0] + expert
    lane = lax.broadcasted_iota(jnp.int32, (2 * rows, LANES), 1)
    coded = jnp.concatenate([x_even[:, width:], x_odd[:, width:]], axis=0).astype(jnp.float32)
    gate = jnp.sum(
        jnp.where((lane == column) | (lane == column + experts_all), coded, 0.0),
        axis=1,
        keepdims=True,
    )
    x_rows = x_all[...]
    og_rows = og_all[...]
    gate_pre = jnp.dot(x_rows, gate_w[0], preferred_element_type=jnp.float32)
    up_pre = jnp.dot(x_rows, up_w[0], preferred_element_type=jnp.float32)
    down_grad = lax.dot_general(og_rows, down_w[0], nt_dims, preferred_element_type=jnp.float32)
    sigmoid = 1.0 / (1.0 + jnp.exp(-gate_pre))
    silu = gate_pre * sigmoid
    hidden = silu * up_pre
    gate_back = jnp.sum(hidden * down_grad, axis=1, keepdims=True)
    hidden_low = (gate * hidden).astype(jnp.bfloat16)
    hidden_grad = gate * down_grad
    gate_pre_low = (
        hidden_grad * up_pre * sigmoid * (1.0 + gate_pre * (1.0 - sigmoid))
    ).astype(jnp.bfloat16)
    up_pre_low = (hidden_grad * silu).astype(jnp.bfloat16)
    hid_all[...] = hidden_low
    pre_all[0, :, :hidden_units] = gate_pre_low
    pre_all[0, :, hidden_units:] = up_pre_low
    row = lax.dot_general(
        gate_pre_low, gate_w[0], nt_dims, preferred_element_type=jnp.float32
    ) + lax.dot_general(up_pre_low, up_w[0], nt_dims, preferred_element_type=jnp.float32)
    out = jnp.dot(hidden_low, down_w[0], preferred_element_type=jnp.float32)
    high = gate_back.astype(jnp.bfloat16).astype(jnp.float32)
    back = jnp.where(lane == column, high, 0.0) + jnp.where(
        lane == column + experts_all, gate_back - high, 0.0
    )

    @pl.when(expert == 0)
    def _():
        row_acc[...] = row
        out_acc[...] = out
        back_acc[...] = back

    @pl.when(expert > 0)
    def _():
        row_acc[...] += row
        out_acc[...] += out
        back_acc[...] += back

    @pl.when(expert == last)
    def _():
        for ref, first in ((row_even, 0), (row_odd, rows)):
            ref[:, :width] = row_acc[first : first + rows, :].astype(jnp.bfloat16)
            ref[:, width:] = back_acc[first : first + rows, :].astype(jnp.bfloat16)
        out_even[...] = out_acc[:rows, :].astype(jnp.bfloat16)
        out_odd[...] = out_acc[rows:, :].astype(jnp.bfloat16)


def expert_pair(position, pairs, first_expert, experts_all, x_pair, og_pair, weights, carried):
    w_gate, w_up, w_down = weights
    rows, coded_width = x_pair[0].shape
    width = coded_width - LANES
    local_experts, _, hidden_units = w_gate.shape
    bf16 = jnp.bfloat16
    whole = 2 * rows
    fixed = lambda e, i: (0, 0)
    once = pl.Buffered(1)
    in_specs = (
        [pl.BlockSpec((rows, coded_width), fixed, pipeline_mode=once)] * 2
        + [pl.BlockSpec((rows, width), fixed, pipeline_mode=once)] * 2
        + [pl.BlockSpec((1, width, hidden_units), lambda e, i: (e, 0, 0))] * 2
        + [pl.BlockSpec((1, hidden_units, width), lambda e, i: (e, 0, 0))]
    )
    operands = [*x_pair, *og_pair, w_gate, w_up, w_down]
    aliases = {}
    if carried is not None:
        in_specs = in_specs + [pl.BlockSpec(memory_space=pl.ANY)] * 4
        aliases = {1 + len(operands) + k: k for k in range(4)}
        operands = operands + list(carried)
    out_shape = [
        jax.ShapeDtypeStruct((pairs * whole, width), bf16),
        jax.ShapeDtypeStruct((pairs * whole, width), bf16),
        jax.ShapeDtypeStruct((local_experts, pairs * whole, 2 * hidden_units), bf16),
        jax.ShapeDtypeStruct((pairs * whole, local_experts * hidden_units), bf16),
        jax.ShapeDtypeStruct((rows, coded_width), bf16),
        jax.ShapeDtypeStruct((rows, coded_width), bf16),
        jax.ShapeDtypeStruct((rows, width), bf16),
        jax.ShapeDtypeStruct((rows, width), bf16),
    ]
    out_specs = [
        pl.BlockSpec((whole, width), lambda e, i: (position, 0)),
        pl.BlockSpec((whole, width), lambda e, i: (position, 0)),
        pl.BlockSpec((1, whole, 2 * hidden_units), lambda e, i: (e, position, 0)),
        pl.BlockSpec((whole, hidden_units), lambda e, i: (position, e)),
        pl.BlockSpec((rows, coded_width), fixed),
        pl.BlockSpec((rows, coded_width), fixed),
        pl.BlockSpec((rows, width), fixed),
        pl.BlockSpec((rows, width), fixed),
    ]
    products = 2 * whole * width * hidden_units * local_experts
    results = pl.pallas_call(
        partial(expert_body, experts_all),
        out_shape=out_shape,
        grid_spec=pltpu.PrefetchScalarGridSpec(
            num_scalar_prefetch=1,
            grid=(local_experts,),
            in_specs=in_specs,
            out_specs=out_specs,
            scratch_shapes=[
                pltpu.VMEM((whole, width), jnp.float32),
                pltpu.VMEM((whole, width), jnp.float32),
                pltpu.VMEM((whole, LANES), jnp.float32),
                pltpu.VMEM((8, LANES), jnp.float32),
            ],
        ),
        input_output_aliases=aliases,
        compiler_params=pltpu.CompilerParams(
            dimension_semantics=("arbitrary",), vmem_limit_bytes=60 * 1024 * 1024
        ),
        cost_estimate=pl.CostEstimate(
            flops=6 * products,
            bytes_accessed=3 * 2 * local_experts * width * hidden_units + 20 * whole * width,
            transcendentals=whole * hidden_units * local_experts,
        ),
        name="experts",
    )(first_expert, *operands)
    return results[:4], results[4:]


def on_device(
    tokens,
    routes,
    w_query,
    key_projection,
    value_projection,
    w_out,
    gain_attn,
    gain_ffn,
    w_router,
    w_gate,
    w_up,
    w_down,
    out_grad,
):
    bf16 = jnp.bfloat16
    shard_count = lax.axis_size("shard")
    seq_count = lax.axis_size("seq")
    shard_index = lax.axis_index("shard")
    seq_index = lax.axis_index("seq")
    tok_count, model_width = tokens.shape
    top_count = routes.shape[1]
    experts_all = w_router.shape[1]
    local_experts = w_gate.shape[0]
    block_len = tok_count * seq_count
    prompt_len = PROMPT_BLK * shard_count
    query_width = w_query.shape[1]
    key_width = key_projection.shape[1]

    singles, several = even_blocks(shard_count)
    own_weight = jnp.concatenate([w_query, key_projection, value_projection], axis=1)
    held = {}

    def after_first(line):
        small = jnp.concatenate([w_router, gain_attn[:, None], gain_ffn[:, None]], axis=1)
        small = lax.all_gather(small, "seq", axis=0, tiled=True)
        small = lax.all_gather(small, "shard", axis=0, tiled=True)

        def tie(blocks):
            blocks, held["line"], held["small"] = lax.optimization_barrier((blocks, line, small))
            return blocks

        blocks = gather_blocks(own_weight, "shard", tie)
        late = lax.optimization_barrier(([blocks[k] for k in several], out_grad))[1]
        held["weights"] = blocks
        held["grads"] = gather_blocks(late, "shard")
        return held["line"]

    def after_last(line):
        near = [held["grads"][k] for k in singles]
        line, near = lax.optimization_barrier((line, near))
        for k, block in zip(singles, near):
            held["grads"][k] = block
        return line

    block_tokens, out_weight = gather_line([tokens, w_out], "seq", after_first, after_last)
    out_weight = lax.all_gather(out_weight, "shard", axis=1, tiled=True)
    small = held["small"]
    router_weight = small[:, :experts_all]
    first_gain = small[:, experts_all].astype(jnp.float32)
    second_gain = small[:, experts_all + 1].astype(jnp.float32)
    qkv_weight = in_order(held["weights"], shard_index).reshape(model_width, -1)
    grad_blocks = held["grads"]

    block_rows = jnp.arange(block_len, dtype=jnp.int32)
    cos_table, sin_table = rotary_tables(
        place_of(block_rows, shard_index, prompt_len), HEAD_DIMENSION
    )
    inputs = block_tokens.astype(jnp.float32)
    first_factor = rms_parts(inputs)
    normed_low = (inputs * first_factor * first_gain).astype(bf16)
    lin = matmul(normed_low, qkv_weight)
    kv_heads = key_width // HEAD_DIMENSION
    group = query_width // key_width
    queries = rotate(lin[:, :query_width], cos_table, sin_table, HEAD_DIMENSION)
    queries = to_lanes((queries * HEAD_DIMENSION ** (-0.5)).astype(bf16))
    key_heads = rotate(
        lin[:, query_width : query_width + key_width], cos_table, sin_table, HEAD_DIMENSION
    ).astype(bf16)
    value_heads = lin[:, query_width + key_width :].astype(bf16)
    kv_own = jnp.concatenate([to_lanes(key_heads), to_lanes(value_heads)], axis=1)
    kv_prompt = lax.all_gather(kv_own[:PROMPT_BLK], "shard", axis=0, tiled=True)
    block_number = shard_index.astype(jnp.int32).reshape(1)
    mixed_own, levels = attend_forward(block_number, queries, kv_prompt, kv_own, group, kv_heads)
    sooner = [j for j in range(1, shard_count) if j - 1 not in several]
    mixed_own, held_blocks = lax.optimization_barrier((mixed_own, [grad_blocks[j] for j in sooner]))
    for j, block in zip(sooner, held_blocks):
        grad_blocks[j] = block
    for j in several:
        grad_blocks[j + 1] = exchange(grad_blocks[j], "shard", 1)
    mixed_heads = mixed_own[:, :query_width]
    mixed_tokens = lax.all_to_all(mixed_heads, "seq", split_axis=0, concat_axis=1, tiled=True)

    half_features = model_width // 2
    core_bit = shard_index % 2
    half_weight, mixed_tokens = lax.optimization_barrier(
        (
            lax.dynamic_slice_in_dim(qkv_weight, core_bit * half_features, half_features, axis=0),
            mixed_tokens,
        )
    )
    wide_half = lax.all_gather(half_weight, "seq", axis=0, tiled=False)

    own_inputs = tokens.astype(jnp.float32)
    upstream = out_grad.astype(jnp.float32)
    residual = own_inputs + matmul(mixed_tokens, out_weight)
    second_factor = rms_parts(residual)
    second_low = (residual * second_factor * second_gain).astype(bf16)
    logits = matmul(second_low, router_weight)
    chosen = routes[:, :, None] == jnp.arange(experts_all, dtype=jnp.int32)[None, None, :]
    named = jnp.any(chosen, axis=1)
    gate_dense = jax.nn.softmax(jnp.where(named, logits, negative), axis=-1)
    gate_dense = jnp.where(named, gate_dense, 0.0)

    gate_high = lax.reduce_precision(gate_dense, 8, 7)
    coded = jnp.concatenate(
        [
            second_low,
            gate_high.astype(bf16),
            (gate_dense - gate_high).astype(bf16),
            jnp.zeros((tok_count, LANES - 2 * experts_all), bf16),
        ],
        axis=1,
    )
    row_blocks = {0: coded, 1: exchange(coded, "shard", 1)}
    for bit in singles:
        row_blocks[bit] = exchange(coded, "shard", bit)
    order = [0] + singles[:-1] + several + singles[-1:]
    first_expert = (shard_index * local_experts).astype(jnp.int32).reshape(1)
    carried = None
    pending = []
    row_sums = {}
    out_parts = [None] * shard_count
    for position, j in enumerate(order):
        row_pair = [row_blocks[j], row_blocks[j + 1]]
        if j == order[-1]:
            row_pair, row_sums = lax.optimization_barrier((row_pair, row_sums))
            pending = reduce_several(row_sums, "shard")
        carried, pieces = expert_pair(
            position,
            len(order),
            first_expert,
            experts_all,
            row_pair,
            grad_blocks[j : j + 2],
            (w_gate, w_up, w_down),
            carried,
        )
        if position == 0:
            arrived, pieces = lax.optimization_barrier(
                ([row_blocks[bit] for bit in singles], pieces)
            )
            row_blocks.update(zip(singles, arrived))
            for bit in singles:
                row_blocks[bit + 1] = exchange(row_blocks[bit], "shard", 1)
            for k in several:
                low_bit = bits_of(k)[0]
                row_blocks[k] = exchange(row_blocks[k ^ low_bit], "shard", low_bit)
        elif position == 1:
            arrived, pieces = lax.optimization_barrier(([row_blocks[k] for k in several], pieces))
            row_blocks.update(zip(several, arrived))
            for k in several:
                row_blocks[k + 1] = exchange(row_blocks[k], "shard", 1)
        elif j == order[-1]:
            arrived, pieces = lax.optimization_barrier(([piece for _, piece in pending], pieces))
            pending = [(k, piece) for (k, _), piece in zip(pending, arrived)]
        row_sums[j] = add_rounded(pieces[0], exchange(pieces[1], "shard", 1))
        out_parts[j], out_parts[j + 1] = pieces[2], pieces[3]
    all_rows, all_grads, all_pre, all_hidden = carried
    row_sums, all_grads = lax.optimization_barrier((row_sums, all_grads))
    down_sum = transposed_times(all_grads, all_hidden).astype(bf16)
    grad_down = lax.psum_scatter(down_sum, "seq", scatter_dimension=0, tiled=True)
    row_pieces = reduce_singles(row_sums, pending, "shard")
    row_pieces, down_sum = lax.optimization_barrier((row_pieces, down_sum))
    row_total = add_all(row_pieces)
    row_grad = row_total[:, :model_width]
    gate_grad_dense = (
        row_total[:, model_width : model_width + experts_all]
        + row_total[:, model_width + experts_all : model_width + 2 * experts_all]
    )
    weighted = gate_dense * gate_grad_dense
    logit_grad = weighted - gate_dense * jnp.sum(weighted, axis=-1, keepdims=True)
    grad_router = transposed_times(second_low.astype(jnp.float32), logit_grad, highest)
    second_grad = row_grad + times_transposed(
        logit_grad, router_weight.astype(jnp.float32), highest
    )
    residual_part, grad_gain_ffn = rms_backward(residual, second_factor, second_gain, second_grad)
    residual_grad = upstream + residual_part
    residual_low = residual_grad.astype(bf16)
    mixed_grad_tokens = times_transposed(residual_low, out_weight).astype(bf16)
    other_half = exchange(wide_half, "shard", 1)
    mixed_grad_tokens, out_parts, all_rows, other_half, mixed_late = lax.optimization_barrier(
        (mixed_grad_tokens, out_parts, all_rows, other_half, mixed_tokens)
    )
    mixed_grad = lax.all_to_all(mixed_grad_tokens, "seq", split_axis=1, concat_axis=0, tiled=True)
    odd = [exchange(out_parts[j + 1], "shard", 1) for j in order]
    pre_sums = [transposed_times(all_rows, all_pre[0]).astype(bf16)]
    odd, pre_sums[0], all_rows = lax.optimization_barrier((odd, pre_sums[0], all_rows))
    out_sums = {j: add_rounded(out_parts[j], piece) for j, piece in zip(order, odd)}
    out_pending = reduce_several(out_sums, "shard")
    pre_sums += [
        transposed_times(all_rows, all_pre[e]).astype(bf16) for e in range(1, local_experts)
    ]
    arrived, pre_sums = lax.optimization_barrier(([piece for _, piece in out_pending], pre_sums))
    out_pending = [(j, piece) for (j, _), piece in zip(out_pending, arrived)]
    out_pieces = reduce_singles(out_sums, out_pending, "shard")
    columns = [
        lax.dynamic_slice_in_dim(
            residual_low,
            (shard_index ^ j) * (model_width // shard_count),
            model_width // shard_count,
            axis=1,
        )
        for j in range(shard_count)
    ]
    whole_out = [transposed_times(part, mixed_late).astype(bf16) for part in columns]
    first_odd = [exchange(whole_out[j + 1], "shard", 1) for j in order[:2]]
    mixed_grad, pre_sums, whole_out, first_odd = lax.optimization_barrier(
        (mixed_grad, pre_sums, whole_out, first_odd)
    )
    whole_odd = first_odd + [exchange(whole_out[j + 1], "shard", 1) for j in order[2:]]

    query_grad, prompt_grad, self_grad = attend_backward(
        block_number,
        queries,
        to_lanes(mixed_grad),
        mixed_own,
        levels,
        kv_prompt,
        kv_own,
        group,
        kv_heads,
    )
    query_grad, prompt_grad, self_grad, out_pieces, whole_odd = lax.optimization_barrier(
        (query_grad, prompt_grad, self_grad, out_pieces, whole_odd)
    )
    query_grad = query_grad[:, :query_width]
    own_prompt = reduce_blocks(relative_blocks(prompt_grad, shard_index, shard_count), "shard")
    key_grad = jnp.concatenate(
        [own_prompt[:, :key_width], self_grad[PROMPT_BLK:, :key_width]], axis=0
    )
    value_low = jnp.concatenate(
        [own_prompt[:, LANES : LANES + key_width], self_grad[PROMPT_BLK:, LANES : LANES + key_width]],
        axis=0,
    ).astype(bf16)
    lin_query = rotate(query_grad, cos_table, -sin_table, HEAD_DIMENSION).astype(bf16)
    lin_key = rotate(key_grad, cos_table, -sin_table, HEAD_DIMENSION).astype(bf16)
    lin_both = jnp.concatenate([lin_key, value_low], axis=1)
    query_tokens = lax.all_to_all(lin_query, "seq", split_axis=0, concat_axis=1, tiled=True)
    lin_both, query_tokens = lax.optimization_barrier((lin_both, query_tokens))
    both_tokens = lax.all_to_all(lin_both, "seq", split_axis=0, concat_axis=1, tiled=True)
    whole_sums = {j: add_rounded(whole_out[j], piece) for j, piece in zip(order, whole_odd)}
    grad_out = add_all(
        reduce_singles(whole_sums, reduce_several(whole_sums, "shard"), "shard")
    ).astype(bf16)
    grad_out, output_sum, both_tokens = lax.optimization_barrier(
        (grad_out, add_all(out_pieces), both_tokens)
    )
    output = (residual + output_sum).astype(bf16)
    grad_out = grad_out.reshape(grad_out.shape[0], seq_count, -1).transpose(1, 0, 2)
    grad_out = scatter_direct(grad_out, "seq").T
    parts = [0.0, 0.0]
    for lin, first, last in (
        (query_tokens, 0, query_width),
        (both_tokens, query_width, query_width + 2 * key_width),
    ):
        for k, weight in enumerate((wide_half, other_half)):
            for group_index in range(seq_count):
                columns = slice(group_index * (last - first), (group_index + 1) * (last - first))
                parts[k] = parts[k] + times_transposed(
                    lin[:, columns], weight[group_index, :, first:last]
                )
    normed_grad = jnp.concatenate(
        [
            jnp.where(core_bit == 0, parts[0], parts[1]),
            jnp.where(core_bit == 0, parts[1], parts[0]),
        ],
        axis=1,
    )
    small_grad = jnp.concatenate([grad_router, grad_gain_ffn[:, None]], axis=1)
    grad_qkv = jnp.concatenate(
        [
            transposed_times(normed_low, lin_query),
            transposed_times(normed_low, lin_both),
            small_grad,
        ],
        axis=1,
    )
    grad_qkv = reduce_blocks(
        relative_blocks(grad_qkv.astype(bf16), shard_index, shard_count), "shard"
    )
    own_features = own_weight.shape[0]
    gain_own = lax.dynamic_slice_in_dim(first_gain, shard_index * own_features, own_features)
    all_columns = own_weight.shape[1]
    gain_part = (
        jnp.sum(own_weight.astype(jnp.float32) * grad_qkv[:, :all_columns], axis=1) / gain_own
    )
    grad_query = grad_qkv[:, :query_width]
    grad_key = grad_qkv[:, query_width : query_width + key_width]
    grad_value = grad_qkv[:, query_width + key_width : query_width + 2 * key_width]
    small_grad = jnp.concatenate([grad_qkv[:, all_columns:], gain_part[:, None]], axis=1).astype(bf16)
    small_grad = scatter_direct(
        small_grad.reshape(seq_count, -1, small_grad.shape[1]), "seq"
    )
    own_factor = rms_parts(own_inputs)
    input_part, _ = rms_backward(own_inputs, own_factor, first_gain, normed_grad)
    tokens_grad = residual_grad + input_part
    pre_grads = [
        lax.psum_scatter(part, "seq", scatter_dimension=0, tiled=True) for part in pre_sums
    ]
    hidden_units = w_gate.shape[2]
    grad_down = grad_down.T.reshape(local_experts, hidden_units, -1)
    grad_gate = jnp.stack([part[:, :hidden_units] for part in pre_grads])
    grad_up = jnp.stack([part[:, hidden_units:] for part in pre_grads])
    return (
        output,
        tokens_grad,
        grad_query,
        grad_key,
        grad_value,
        grad_out,
        small_grad[:, experts_all + 1],
        small_grad[:, experts_all],
        small_grad[:, :experts_all],
        grad_gate.astype(jnp.float32),
        grad_up.astype(jnp.float32),
        grad_down.astype(jnp.float32),
    )


def solution(mesh):
    return jax.shard_map(
        on_device,
        mesh=mesh,
        in_specs=(
            P(("shard", "seq"), None),
            P(("shard", "seq"), None),
            P("shard", "seq"),
            P("shard", "seq"),
            P("shard", "seq"),
            P("seq", "shard"),
            P(("shard", "seq")),
            P(("shard", "seq")),
            P(("shard", "seq"), None),
            P("shard", None, None),
            P("shard", None, None),
            P("shard", None, None),
            P(("shard", "seq"), None),
        ),
        out_specs=(
            P(("shard", "seq"), None),
            P(("shard", "seq"), None),
            P("shard", "seq"),
            P("shard", "seq"),
            P("shard", "seq"),
            P("seq", "shard"),
            P(("shard", "seq")),
            P(("shard", "seq")),
            P(("shard", "seq"), None),
            P("shard", "seq", None),
            P("shard", "seq", None),
            P("shard", None, "seq"),
        ),
        check_vma=False,
    )
```

```python
from functools import partial

import jax
import jax.numpy as jnp
from jax import lax
from jax.experimental import pallas as pl
from jax.experimental.pallas import tpu as pltpu
from jax.sharding import PartitionSpec as P

HEAD_DIMENSION = 64
CONT_LEN = 512
PROMPT_BLK = 128


norm_eps = 1e-05
negative = -1e30
rope_base = 10000.0
highest = lax.Precision.HIGHEST


def rms_norm(values, scaling):
    factor = lax.rsqrt(jnp.mean(values * values, axis=-1, keepdims=True) + norm_eps)
    return values * factor * scaling


def swiglu(gate_pre, up_pre):
    return jax.nn.silu(gate_pre) * up_pre


def rotary_tables(places, head_size):
    half_size = head_size // 2
    frequency = jnp.exp(
        jnp.arange(half_size, dtype=jnp.float32) * (-2.0 * jnp.log(rope_base) / head_size)
    )
    angles = places.astype(jnp.float32)[:, None] * frequency[None, :]
    return (jnp.cos(angles)[:, None, :], jnp.sin(angles)[:, None, :])


def rotate(values, cosine, sine, head_size):
    total_row_count = values.shape[0]
    by_head = values.reshape(total_row_count, -1, head_size)
    half_size = head_size // 2
    first_half = by_head[..., :half_size]
    second_half = by_head[..., half_size:]
    turned = jnp.concatenate(
        [first_half * cosine - second_half * sine, second_half * cosine + first_half * sine],
        axis=-1,
    )
    return turned.reshape(total_row_count, -1)


def place_of(within, block_index, prompt_len):
    return jnp.where(
        within < PROMPT_BLK,
        block_index * PROMPT_BLK + within,
        prompt_len + (within - PROMPT_BLK) % CONT_LEN,
    )


def times_transposed(left_side, right_side, precision=None):
    return lax.dot_general(
        left_side,
        right_side,
        (((1,), (1,)), ((), ())),
        precision=precision,
        preferred_element_type=jnp.float32,
    )


def transposed_times(left_side, right_side, precision=None):
    return lax.dot_general(
        left_side,
        right_side,
        (((0,), (0,)), ((), ())),
        precision=precision,
        preferred_element_type=jnp.float32,
    )


def rms_parts(values):
    return lax.rsqrt(jnp.mean(values * values, axis=-1, keepdims=True) + norm_eps)


def rms_backward(values, factor, scaling, normed_grad):
    scaled = scaling * normed_grad
    inner = jnp.mean(scaled * values, axis=-1, keepdims=True)
    values_grad = factor * scaled - values * (factor * factor * factor) * inner
    gain_grad = jnp.sum(normed_grad * values * factor, axis=0)
    return values_grad, gain_grad


def matmul(left_side, right_side):
    return jnp.dot(left_side, right_side, preferred_element_type=jnp.float32)


LANES = 128


def relane(values, source, target):
    lane = lax.broadcasted_iota(jnp.int32, values.shape, 1)
    swapped = jnp.where(source != target, pltpu.roll(values, HEAD_DIMENSION, 1), values)
    return jnp.where(lane // HEAD_DIMENSION == target, swapped, 0.0)


def head_rows(ref, first, count, source, target):
    values = ref[pl.ds(first, count), :].astype(jnp.float32)
    return relane(values, source, target).astype(jnp.bfloat16)


def nt_dot(left_side, right_side):
    return lax.dot_general(
        left_side, right_side, (((1,), (1,)), ((), ())), preferred_element_type=jnp.float32
    )


def nn_dot(left_side, right_side):
    return jnp.dot(left_side, right_side, preferred_element_type=jnp.float32)


def below_diagonal(scores):
    key_row = lax.broadcasted_iota(jnp.int32, scores.shape, 0)
    query_column = lax.broadcasted_iota(jnp.int32, scores.shape, 1)
    return jnp.where(key_row <= query_column, scores, negative)


def seen_prompt(scores, first_key, shard_index):
    key_row = lax.broadcasted_iota(jnp.int32, scores.shape, 0) + first_key
    query_column = lax.broadcasted_iota(jnp.int32, scores.shape, 1) % PROMPT_BLK
    return jnp.where(key_row <= query_column + shard_index * PROMPT_BLK, scores, negative)


def transposed(values):
    return values.astype(jnp.float32).T


QUERY_CHUNK = 512
KEY_CHUNK = 1024
FORWARD_CHUNK = 256


def attend_forward_body(
    group, kv_heads, index_ref, q_ref, kp_ref, vp_ref, ko_ref, vo_ref, mixed_ref, level_ref, vt_all, acc
):
    pair = pl.program_id(0)
    prompt_len = kp_ref.shape[0]
    block_len = ko_ref.shape[0]
    conts = (block_len - PROMPT_BLK) // CONT_LEN
    shard_index = index_ref[0]

    @pl.when(pair == 0)
    def _():
        vt_all[:, :prompt_len] = transposed(vp_ref[...]).astype(jnp.bfloat16)
        vt_all[:, prompt_len:] = transposed(vo_ref[...]).astype(jnp.bfloat16)

    acc[...] = jnp.zeros_like(acc)
    size = min(FORWARD_CHUNK, prompt_len)
    prompt_keys = [slice(first, first + size) for first in range(0, prompt_len, size)]

    def kv_half(side):
        return jnp.minimum((2 * pair + side) // group, kv_heads - 1)

    def finish(scores, value_columns):
        level = jnp.max(scores[0], axis=0, keepdims=True)
        for part in scores[1:]:
            level = jnp.maximum(level, jnp.max(part, axis=0, keepdims=True))
        total = None
        mixed = None
        for part, columns in zip(scores, value_columns):
            weights = jnp.exp(part - level)
            part_total = jnp.sum(weights, axis=0, keepdims=True)
            part_mixed = nn_dot(columns, weights.astype(jnp.bfloat16))
            total = part_total if total is None else total + part_total
            mixed = part_mixed if mixed is None else mixed + part_mixed
        return mixed / total, level + jnp.log(total)

    both = jnp.concatenate(
        [head_rows(q_ref, 0, PROMPT_BLK, side, kv_half(side)) for side in range(2)], axis=0
    )
    mixed, level = finish(
        [
            seen_prompt(nt_dot(kp_ref[keys, :], both), keys.start, shard_index)
            for keys in prompt_keys
        ],
        [vt_all[:, keys] for keys in prompt_keys],
    )
    mixed = mixed.T
    for side in range(2):
        rows = slice(side * PROMPT_BLK, (side + 1) * PROMPT_BLK)
        acc[:PROMPT_BLK, :] += relane(mixed[rows], kv_half(side), side)
        level_ref[side, :, :PROMPT_BLK] = level[:, rows]

    def step(turn, _):
        side = turn // conts
        number = turn % conts
        half = kv_half(side)
        first_own = PROMPT_BLK + number * CONT_LEN
        for chunk in range(CONT_LEN // QUERY_CHUNK):
            before = chunk * QUERY_CHUNK
            first_row = pl.multiple_of(first_own + before, PROMPT_BLK)
            queries = head_rows(q_ref, first_row, QUERY_CHUNK, side, half)
            scores = [nt_dot(kp_ref[keys, :], queries) for keys in prompt_keys]
            columns = [vt_all[:, keys] for keys in prompt_keys]
            if before:
                start = pl.multiple_of(first_own, PROMPT_BLK)
                scores.append(nt_dot(ko_ref[pl.ds(start, before), :], queries))
                columns.append(
                    vt_all[:, pl.ds(pl.multiple_of(prompt_len + start, PROMPT_BLK), before)]
                )
            scores.append(below_diagonal(nt_dot(ko_ref[pl.ds(first_row, QUERY_CHUNK), :], queries)))
            columns.append(
                vt_all[:, pl.ds(pl.multiple_of(prompt_len + first_row, PROMPT_BLK), QUERY_CHUNK)]
            )
            mixed, level = finish(scores, columns)
            acc[pl.ds(first_row, QUERY_CHUNK), :] += relane(mixed.T, half, side)
            level_ref[side, :, pl.ds(first_row, QUERY_CHUNK)] = level
        return 0

    lax.fori_loop(0, 2 * conts, step, 0)
    mixed_ref[...] = acc[...].astype(jnp.bfloat16)


def attend_backward_body(
    group,
    kv_heads,
    index_ref,
    q_ref,
    grad_ref,
    mixed_ref,
    level_ref,
    cos_ref,
    sin_ref,
    kp_ref,
    vp_ref,
    ko_ref,
    vo_ref,
    dq_ref,
    dprompt_ref,
    down_ref,
    kt_all,
    acc,
    prompt_acc,
):
    pair = pl.program_id(0)
    last = pl.num_programs(0) - 1
    prompt_len = kp_ref.shape[0]
    block_len = ko_ref.shape[0]
    conts = (block_len - PROMPT_BLK) // CONT_LEN
    shard_index = index_ref[0]
    bf16 = jnp.bfloat16

    @pl.when(pair == 0)
    def _():
        kt_all[:, :prompt_len] = transposed(kp_ref[...]).astype(bf16)
        kt_all[:, prompt_len:] = transposed(ko_ref[...]).astype(bf16)
        prompt_acc[...] = jnp.zeros_like(prompt_acc)
        down_ref[...] = jnp.zeros_like(down_ref)

    acc[...] = jnp.zeros_like(acc)

    def kv_half(side):
        return jnp.minimum((2 * pair + side) // group, kv_heads - 1)

    def inner_sums(first_row, count, side):
        rows = pl.ds(first_row, count)
        product = mixed_ref[rows, :].astype(jnp.float32) * grad_ref[rows, :].astype(jnp.float32)
        return jnp.sum(relane(product, side, side).T, axis=0, keepdims=True)

    def part(keys, values, key_columns, queries, grads, level, inner, mask, sums, first_key):
        scores = nt_dot(keys, queries)
        if mask is not None:
            scores = mask(scores)
        probs = jnp.exp(scores - level)
        score_grad = (probs * (nt_dot(values, grads) - inner)).astype(bf16)
        rows = pl.ds(first_key, keys.shape[0])
        sums[rows, :LANES] += nn_dot(score_grad, queries)
        sums[rows, LANES:] += nn_dot(probs.astype(bf16), grads)
        return nn_dot(key_columns, score_grad)

    def prompt_parts(queries, grads, level, inner, masked):
        total = None
        size = min(KEY_CHUNK, prompt_len)
        for first_key in range(0, prompt_len, size):
            rows = slice(first_key, first_key + size)
            mask = (lambda s, f=first_key: seen_prompt(s, f, shard_index)) if masked else None
            piece = part(
                kp_ref[rows, :], vp_ref[rows, :], kt_all[:, rows], queries, grads, level, inner,
                mask, prompt_acc, first_key,
            )
            total = piece if total is None else total + piece
        return total

    both_q, both_g, both_level, both_inner = [], [], [], []
    for side in range(2):
        both_q.append(head_rows(q_ref, 0, PROMPT_BLK, side, kv_half(side)))
        both_g.append(head_rows(grad_ref, 0, PROMPT_BLK, side, kv_half(side)))
        both_level.append(level_ref[side, :, :PROMPT_BLK])
        both_inner.append(inner_sums(0, PROMPT_BLK, side))
    grad_q = prompt_parts(
        jnp.concatenate(both_q, axis=0),
        jnp.concatenate(both_g, axis=0),
        jnp.concatenate(both_level, axis=1),
        jnp.concatenate(both_inner, axis=1),
        True,
    ).T
    for side in range(2):
        rows = slice(side * PROMPT_BLK, (side + 1) * PROMPT_BLK)
        acc[:PROMPT_BLK, :] += relane(grad_q[rows], kv_half(side), side)

    def step(turn, _):
        side = turn // conts
        number = turn % conts
        half = kv_half(side)
        first_own = PROMPT_BLK + number * CONT_LEN
        for chunk in range(CONT_LEN // QUERY_CHUNK):
            before = chunk * QUERY_CHUNK
            first_row = pl.multiple_of(first_own + before, PROMPT_BLK)
            queries = head_rows(q_ref, first_row, QUERY_CHUNK, side, half)
            grads = head_rows(grad_ref, first_row, QUERY_CHUNK, side, half)
            level = level_ref[side, :, pl.ds(first_row, QUERY_CHUNK)]
            inner = inner_sums(first_row, QUERY_CHUNK, side)
            grad_q = prompt_parts(queries, grads, level, inner, False)
            own = [(first_row, QUERY_CHUNK, below_diagonal)]
            if before:
                own.append((pl.multiple_of(first_own, PROMPT_BLK), before, None))
            for start, size, mask in own:
                rows = pl.ds(start, size)
                columns = pl.ds(pl.multiple_of(prompt_len + start, PROMPT_BLK), size)
                grad_q += part(
                    ko_ref[rows, :], vo_ref[rows, :], kt_all[:, columns], queries, grads, level,
                    inner, mask, down_ref, start,
                )
            acc[pl.ds(first_row, QUERY_CHUNK), :] += relane(grad_q.T, half, side)
        return 0

    lax.fori_loop(0, 2 * conts, step, 0)
    grads = acc[...] * HEAD_DIMENSION ** (-0.5)
    half = HEAD_DIMENSION // 2
    lane = lax.broadcasted_iota(jnp.int32, grads.shape, 1)
    swapped = jnp.where(
        lane % HEAD_DIMENSION < half,
        pltpu.roll(grads, LANES - half, 1),
        pltpu.roll(grads, half, 1),
    )
    dq_ref[...] = (grads * cos_ref[...] + swapped * sin_ref[...]).astype(bf16)

    @pl.when(pair == last)
    def _():
        dprompt_ref[...] = prompt_acc[...].astype(bf16)


def pair_specs(block_len, prompt_len):
    by_pair = pl.BlockSpec((block_len, LANES), lambda b, i: (0, b))
    levels = pl.BlockSpec((2, 1, block_len), lambda b, i: (b, 0, 0))
    sources = [
        pl.BlockSpec((prompt_len, LANES), lambda b, i: (0, 0)),
        pl.BlockSpec((prompt_len, LANES), lambda b, i: (0, 1)),
        pl.BlockSpec((block_len, LANES), lambda b, i: (0, 0)),
        pl.BlockSpec((block_len, LANES), lambda b, i: (0, 1)),
    ]
    return by_pair, levels, sources


def attention_cost(block_len, prompt_len, width, products):
    pairs = (block_len * prompt_len + block_len * CONT_LEN // 2) * (width // HEAD_DIMENSION)
    return pl.CostEstimate(
        flops=products * 2 * pairs * 2 * LANES,
        bytes_accessed=8 * block_len * width,
        transcendentals=pairs,
    )


def attend_forward(index, queries, kv_prompt, kv_own, group, kv_heads):
    block_len, width = queries.shape
    prompt_len = kv_prompt.shape[0]
    by_pair, levels, sources = pair_specs(block_len, prompt_len)
    return pl.pallas_call(
        partial(attend_forward_body, group, kv_heads),
        out_shape=[
            jax.ShapeDtypeStruct((block_len, width), jnp.bfloat16),
            jax.ShapeDtypeStruct((width // HEAD_DIMENSION, 1, block_len), jnp.float32),
        ],
        grid_spec=pltpu.PrefetchScalarGridSpec(
            num_scalar_prefetch=1,
            grid=(width // LANES,),
            in_specs=[by_pair] + sources,
            out_specs=[by_pair, levels],
            scratch_shapes=[
                pltpu.VMEM((LANES, prompt_len + block_len), jnp.bfloat16),
                pltpu.VMEM((block_len, LANES), jnp.float32),
            ],
        ),
        compiler_params=pltpu.CompilerParams(
            dimension_semantics=("arbitrary",), vmem_limit_bytes=56 * 1024 * 1024
        ),
        cost_estimate=attention_cost(block_len, prompt_len, width, 2),
        name="attend_forward",
    )(index, queries, kv_prompt, kv_prompt, kv_own, kv_own)


def attend_backward(
    index, queries, grads, mixed, level, tables, kv_prompt, kv_own, group, kv_heads
):
    block_len, width = queries.shape
    prompt_len = kv_prompt.shape[0]
    by_pair, levels, sources = pair_specs(block_len, prompt_len)
    return pl.pallas_call(
        partial(attend_backward_body, group, kv_heads),
        out_shape=[
            jax.ShapeDtypeStruct((block_len, width), jnp.bfloat16),
            jax.ShapeDtypeStruct((prompt_len, 2 * LANES), jnp.bfloat16),
            jax.ShapeDtypeStruct((block_len, 2 * LANES), jnp.float32),
        ],
        grid_spec=pltpu.PrefetchScalarGridSpec(
            num_scalar_prefetch=1,
            grid=(width // LANES,),
            in_specs=[by_pair, by_pair, by_pair, levels]
            + [pl.BlockSpec((block_len, LANES), lambda b, i: (0, 0))] * 2
            + sources,
            out_specs=[
                by_pair,
                pl.BlockSpec((prompt_len, 2 * LANES), lambda b, i: (0, 0)),
                pl.BlockSpec((block_len, 2 * LANES), lambda b, i: (0, 0)),
            ],
            scratch_shapes=[
                pltpu.VMEM((LANES, prompt_len + block_len), jnp.bfloat16),
                pltpu.VMEM((block_len, LANES), jnp.float32),
                pltpu.VMEM((prompt_len, 2 * LANES), jnp.float32),
            ],
        ),
        compiler_params=pltpu.CompilerParams(
            dimension_semantics=("arbitrary",), vmem_limit_bytes=56 * 1024 * 1024
        ),
        cost_estimate=attention_cost(block_len, prompt_len, width, 5),
        name="attend_backward",
    )(index, queries, grads, mixed, level, *tables, kv_prompt, kv_prompt, kv_own, kv_own)


def to_lanes(values):
    extra = -values.shape[1] % LANES
    return jnp.pad(values, ((0, 0), (0, extra))) if extra else values


def exchange(values, axis_name, bit):
    count = lax.axis_size(axis_name)
    return lax.ppermute(values, axis_name, [(i, i ^ bit) for i in range(count)])


def bits_of(number):
    return [1 << k for k in range(number.bit_length()) if number >> k & 1]


def even_blocks(count):
    even = sorted(range(2, count, 2), key=lambda j: (len(bits_of(j)), j))
    singles = [j for j in even if len(bits_of(j)) == 1]
    return singles, even[len(singles) :]


def gather_blocks(own, axis_name, after_first=None):
    count = lax.axis_size(axis_name)
    singles, several = even_blocks(count)
    blocks = {0: own, 1: exchange(own, axis_name, 1)}
    for j in singles:
        blocks[j] = exchange(own, axis_name, j)
    if after_first is not None:
        blocks.update(zip(singles, after_first([blocks[j] for j in singles])))
    for j in several:
        low_bit = bits_of(j)[0]
        blocks[j] = exchange(blocks[j ^ low_bit], axis_name, low_bit)
    for j in singles + several:
        blocks[j + 1] = exchange(blocks[j], axis_name, 1)
    return [blocks[j] for j in range(count)]


def add_rounded(left_side, right_side):
    return (left_side.astype(jnp.float32) + right_side.astype(jnp.float32)).astype(jnp.bfloat16)


def reduce_several(sums, axis_name):
    sums = dict(sums)
    pending = []
    for j in sorted((j for j in sums if len(bits_of(j)) > 1), key=lambda j: (-len(bits_of(j)), j)):
        bit = bits_of(j)[-1]
        piece = exchange(sums[j], axis_name, bit)
        if len(bits_of(j ^ bit)) > 1:
            sums[j ^ bit] = add_rounded(sums[j ^ bit], piece)
        else:
            pending.append((j ^ bit, piece))
    return pending


def reduce_singles(sums, pending, axis_name):
    sums = dict(sums)
    for j, piece in pending:
        sums[j] = add_rounded(sums[j], piece)
    return [sums[0]] + [exchange(sums[j], axis_name, j) for j in sums if len(bits_of(j)) == 1]


def add_all(pieces):
    total = pieces[0].astype(jnp.float32)
    for piece in pieces[1:]:
        total = total + piece.astype(jnp.float32)
    return total


def halves_by_core(values, axis_name):
    count = lax.axis_size(axis_name)
    parity = lax.axis_index(axis_name) % 2
    paired = values.reshape(count // 2, 2, values.shape[0] // count, values.shape[1])
    keep = lax.dynamic_index_in_dim(paired, parity, 1, keepdims=False)
    give = lax.dynamic_index_in_dim(paired, 1 - parity, 1, keepdims=False)
    return keep, give


def chip_sums(keep, arrived, axis_name):
    index = lax.axis_index(axis_name)
    total = add_rounded(keep, arrived)
    return {
        2 * k: lax.dynamic_index_in_dim(total, (index // 2) ^ k, 0, keepdims=False)
        for k in range(total.shape[0])
    }


def reduce_rows(values, axis_name):
    keep, give = halves_by_core(values, axis_name)
    sums = chip_sums(keep, exchange(give, axis_name, 1), axis_name)
    return add_all(reduce_singles(sums, reduce_several(sums, axis_name), axis_name))


def in_order(blocks, index):
    stacked = jnp.stack(blocks)
    return jnp.concatenate(
        [lax.dynamic_index_in_dim(stacked, j ^ index, 0, keepdims=True) for j in range(len(blocks))],
        axis=0,
    )


def scatter_direct(pieces, axis_name):
    count = lax.axis_size(axis_name)
    index = lax.axis_index(axis_name)
    total = lax.dynamic_index_in_dim(pieces, index, 0, keepdims=False).astype(jnp.float32)
    for step in range(1, count):
        piece = lax.dynamic_index_in_dim(pieces, (index + step) % count, 0, keepdims=False)
        arrived = lax.ppermute(piece, axis_name, [(i, (i + step) % count) for i in range(count)])
        total = total + arrived.astype(jnp.float32)
    return total


def expert_body(
    experts_all, index_ref, x_even, x_odd, og_even, og_odd, gate_w, up_w, down_w, *rest
):
    (x_all, og_all, pre_all, hid_all, row_even, row_odd, out_even, out_odd) = rest[-12:-4]
    (row_acc, out_acc, back_acc, _) = rest[-4:]
    expert = pl.program_id(0)
    last = pl.num_programs(0) - 1
    rows = x_even.shape[0]
    width = x_all.shape[1]
    hidden_units = gate_w.shape[2]
    nt_dims = (((1,), (1,)), ((), ()))

    @pl.when(expert == 0)
    def _():
        x_all[:rows, :] = x_even[:, :width]
        x_all[rows:, :] = x_odd[:, :width]
        og_all[:rows, :] = og_even[...]
        og_all[rows:, :] = og_odd[...]

    column = index_ref[0] + expert
    lane = lax.broadcasted_iota(jnp.int32, (2 * rows, LANES), 1)
    coded = jnp.concatenate([x_even[:, width:], x_odd[:, width:]], axis=0).astype(jnp.float32)
    gate = jnp.sum(
        jnp.where((lane == column) | (lane == column + experts_all), coded, 0.0),
        axis=1,
        keepdims=True,
    )
    x_rows = x_all[...]
    og_rows = og_all[...]
    gate_pre = jnp.dot(x_rows, gate_w[0], preferred_element_type=jnp.float32)
    up_pre = jnp.dot(x_rows, up_w[0], preferred_element_type=jnp.float32)
    down_grad = lax.dot_general(og_rows, down_w[0], nt_dims, preferred_element_type=jnp.float32)
    sigmoid = 1.0 / (1.0 + jnp.exp(-gate_pre))
    silu = gate_pre * sigmoid
    hidden = silu * up_pre
    gate_back = jnp.sum(hidden * down_grad, axis=1, keepdims=True)
    hidden_low = (gate * hidden).astype(jnp.bfloat16)
    hidden_grad = gate * down_grad
    gate_pre_low = (
        hidden_grad * up_pre * sigmoid * (1.0 + gate_pre * (1.0 - sigmoid))
    ).astype(jnp.bfloat16)
    up_pre_low = (hidden_grad * silu).astype(jnp.bfloat16)
    hid_all[...] = hidden_low
    pre_all[0, :, :hidden_units] = gate_pre_low
    pre_all[0, :, hidden_units:] = up_pre_low
    row = lax.dot_general(
        gate_pre_low, gate_w[0], nt_dims, preferred_element_type=jnp.float32
    ) + lax.dot_general(up_pre_low, up_w[0], nt_dims, preferred_element_type=jnp.float32)
    out = jnp.dot(hidden_low, down_w[0], preferred_element_type=jnp.float32)
    high = gate_back.astype(jnp.bfloat16).astype(jnp.float32)
    back = jnp.where(lane == column, high, 0.0) + jnp.where(
        lane == column + experts_all, gate_back - high, 0.0
    )

    @pl.when(expert == 0)
    def _():
        row_acc[...] = row
        out_acc[...] = out
        back_acc[...] = back

    @pl.when(expert > 0)
    def _():
        row_acc[...] += row
        out_acc[...] += out
        back_acc[...] += back

    @pl.when(expert == last)
    def _():
        for ref, first in ((row_even, 0), (row_odd, rows)):
            ref[:, :width] = row_acc[first : first + rows, :].astype(jnp.bfloat16)
            ref[:, width:] = back_acc[first : first + rows, :].astype(jnp.bfloat16)
        out_even[...] = out_acc[:rows, :].astype(jnp.bfloat16)
        out_odd[...] = out_acc[rows:, :].astype(jnp.bfloat16)


def expert_pair(position, pairs, first_expert, experts_all, x_pair, og_pair, weights, carried):
    w_gate, w_up, w_down = weights
    rows, coded_width = x_pair[0].shape
    width = coded_width - LANES
    local_experts, _, hidden_units = w_gate.shape
    bf16 = jnp.bfloat16
    whole = 2 * rows
    fixed = lambda e, i: (0, 0)
    once = pl.Buffered(1)
    in_specs = (
        [pl.BlockSpec((rows, coded_width), fixed, pipeline_mode=once)] * 2
        + [pl.BlockSpec((rows, width), fixed, pipeline_mode=once)] * 2
        + [pl.BlockSpec((1, width, hidden_units), lambda e, i: (e, 0, 0))] * 2
        + [pl.BlockSpec((1, hidden_units, width), lambda e, i: (e, 0, 0))]
    )
    operands = [*x_pair, *og_pair, w_gate, w_up, w_down]
    aliases = {}
    if carried is not None:
        in_specs = in_specs + [pl.BlockSpec(memory_space=pl.ANY)] * 4
        aliases = {1 + len(operands) + k: k for k in range(4)}
        operands = operands + list(carried)
    out_shape = [
        jax.ShapeDtypeStruct((pairs * whole, width), bf16),
        jax.ShapeDtypeStruct((pairs * whole, width), bf16),
        jax.ShapeDtypeStruct((local_experts, pairs * whole, 2 * hidden_units), bf16),
        jax.ShapeDtypeStruct((pairs * whole, local_experts * hidden_units), bf16),
        jax.ShapeDtypeStruct((rows, coded_width), bf16),
        jax.ShapeDtypeStruct((rows, coded_width), bf16),
        jax.ShapeDtypeStruct((rows, width), bf16),
        jax.ShapeDtypeStruct((rows, width), bf16),
    ]
    out_specs = [
        pl.BlockSpec((whole, width), lambda e, i: (position, 0)),
        pl.BlockSpec((whole, width), lambda e, i: (position, 0)),
        pl.BlockSpec((1, whole, 2 * hidden_units), lambda e, i: (e, position, 0)),
        pl.BlockSpec((whole, hidden_units), lambda e, i: (position, e)),
        pl.BlockSpec((rows, coded_width), fixed),
        pl.BlockSpec((rows, coded_width), fixed),
        pl.BlockSpec((rows, width), fixed),
        pl.BlockSpec((rows, width), fixed),
    ]
    products = 2 * whole * width * hidden_units * local_experts
    results = pl.pallas_call(
        partial(expert_body, experts_all),
        out_shape=out_shape,
        grid_spec=pltpu.PrefetchScalarGridSpec(
            num_scalar_prefetch=1,
            grid=(local_experts,),
            in_specs=in_specs,
            out_specs=out_specs,
            scratch_shapes=[
                pltpu.VMEM((whole, width), jnp.float32),
                pltpu.VMEM((whole, width), jnp.float32),
                pltpu.VMEM((whole, LANES), jnp.float32),
                pltpu.VMEM((8, LANES), jnp.float32),
            ],
        ),
        input_output_aliases=aliases,
        compiler_params=pltpu.CompilerParams(
            dimension_semantics=("arbitrary",), vmem_limit_bytes=60 * 1024 * 1024
        ),
        cost_estimate=pl.CostEstimate(
            flops=6 * products,
            bytes_accessed=3 * 2 * local_experts * width * hidden_units + 20 * whole * width,
            transcendentals=whole * hidden_units * local_experts,
        ),
        name="experts",
    )(first_expert, *operands)
    return results[:4], results[4:]


def on_device(
    tokens,
    routes,
    w_query,
    key_projection,
    value_projection,
    w_out,
    gain_attn,
    gain_ffn,
    w_router,
    w_gate,
    w_up,
    w_down,
    out_grad,
):
    bf16 = jnp.bfloat16
    shard_count = lax.axis_size("shard")
    seq_count = lax.axis_size("seq")
    shard_index = lax.axis_index("shard")
    seq_index = lax.axis_index("seq")
    tok_count, model_width = tokens.shape
    top_count = routes.shape[1]
    experts_all = w_router.shape[1]
    local_experts = w_gate.shape[0]
    block_len = tok_count * seq_count
    prompt_len = PROMPT_BLK * shard_count
    query_width = w_query.shape[1]
    key_width = key_projection.shape[1]

    singles, several = even_blocks(shard_count)
    small = jnp.concatenate([w_router, gain_attn[:, None], gain_ffn[:, None]], axis=1)
    small = lax.all_gather(small, "seq", axis=0, tiled=True)
    small = lax.all_gather(small, "shard", axis=0, tiled=True)
    router_weight = small[:, :experts_all]
    first_gain = small[:, experts_all].astype(jnp.float32)
    second_gain = small[:, experts_all + 1].astype(jnp.float32)
    block_tokens = lax.all_gather(tokens, "seq", axis=0, tiled=True)
    own_weight = jnp.concatenate([w_query, key_projection, value_projection], axis=1)
    weight_blocks = gather_blocks(own_weight, "shard")
    out_weight = lax.all_gather(w_out, "seq", axis=0, tiled=True)
    out_weight = lax.all_gather(out_weight, "shard", axis=1, tiled=True)
    late = lax.optimization_barrier(([weight_blocks[k] for k in several], out_grad))[1]
    grad_blocks = gather_blocks(late, "shard")
    qkv_weight = in_order(weight_blocks, shard_index).reshape(model_width, -1)
    block_tokens, near = lax.optimization_barrier((block_tokens, [grad_blocks[k] for k in singles]))
    for k, block in zip(singles, near):
        grad_blocks[k] = block

    block_rows = jnp.arange(block_len, dtype=jnp.int32)
    cos_table, sin_table = rotary_tables(
        place_of(block_rows, shard_index, prompt_len), HEAD_DIMENSION
    )
    inputs = block_tokens.astype(jnp.float32)
    first_factor = rms_parts(inputs)
    normed_low = (inputs * first_factor * first_gain).astype(bf16)
    lin = matmul(normed_low, qkv_weight)
    kv_heads = key_width // HEAD_DIMENSION
    group = query_width // key_width
    queries = rotate(lin[:, :query_width], cos_table, sin_table, HEAD_DIMENSION)
    queries = to_lanes((queries * HEAD_DIMENSION ** (-0.5)).astype(bf16))
    key_heads = rotate(
        lin[:, query_width : query_width + key_width], cos_table, sin_table, HEAD_DIMENSION
    ).astype(bf16)
    value_heads = lin[:, query_width + key_width :].astype(bf16)
    kv_own = jnp.concatenate([to_lanes(key_heads), to_lanes(value_heads)], axis=1)
    kv_prompt = lax.all_gather(kv_own[:PROMPT_BLK], "shard", axis=0, tiled=True)
    block_number = shard_index.astype(jnp.int32).reshape(1)
    mixed_own, levels = attend_forward(block_number, queries, kv_prompt, kv_own, group, kv_heads)
    sooner = [j for j in range(1, shard_count) if j - 1 not in several]
    mixed_own, held_blocks = lax.optimization_barrier((mixed_own, [grad_blocks[j] for j in sooner]))
    for j, block in zip(sooner, held_blocks):
        grad_blocks[j] = block
    for j in several:
        grad_blocks[j + 1] = exchange(grad_blocks[j], "shard", 1)
    mixed_heads = mixed_own[:, :query_width]
    mixed_tokens = lax.all_to_all(mixed_heads, "seq", split_axis=0, concat_axis=1, tiled=True)

    half_features = model_width // 2
    core_bit = shard_index % 2
    half_weight, mixed_tokens = lax.optimization_barrier(
        (
            lax.dynamic_slice_in_dim(qkv_weight, core_bit * half_features, half_features, axis=0),
            mixed_tokens,
        )
    )
    wide_half = lax.all_gather(half_weight, "seq", axis=0, tiled=False)

    own_inputs = tokens.astype(jnp.float32)
    upstream = out_grad.astype(jnp.float32)
    residual = own_inputs + matmul(mixed_tokens, out_weight)
    second_factor = rms_parts(residual)
    second_low = (residual * second_factor * second_gain).astype(bf16)
    logits = matmul(second_low, router_weight)
    chosen = routes[:, :, None] == jnp.arange(experts_all, dtype=jnp.int32)[None, None, :]
    named = jnp.any(chosen, axis=1)
    gate_dense = jax.nn.softmax(jnp.where(named, logits, negative), axis=-1)
    gate_dense = jnp.where(named, gate_dense, 0.0)

    gate_high = lax.reduce_precision(gate_dense, 8, 7)
    coded = jnp.concatenate(
        [
            second_low,
            gate_high.astype(bf16),
            (gate_dense - gate_high).astype(bf16),
            jnp.zeros((tok_count, LANES - 2 * experts_all), bf16),
        ],
        axis=1,
    )
    row_blocks = {0: coded, 1: exchange(coded, "shard", 1)}
    for bit in singles:
        row_blocks[bit] = exchange(coded, "shard", bit)
    order = [0] + singles[:-1] + several + singles[-1:]
    first_expert = (shard_index * local_experts).astype(jnp.int32).reshape(1)
    carried = None
    pending = []
    row_sums = {}
    out_parts = [None] * shard_count
    for position, j in enumerate(order):
        row_pair = [row_blocks[j], row_blocks[j + 1]]
        if j == order[-1]:
            row_pair, row_sums = lax.optimization_barrier((row_pair, row_sums))
            pending = reduce_several(row_sums, "shard")
        carried, pieces = expert_pair(
            position,
            len(order),
            first_expert,
            experts_all,
            row_pair,
            grad_blocks[j : j + 2],
            (w_gate, w_up, w_down),
            carried,
        )
        if position == 0:
            arrived, pieces = lax.optimization_barrier(
                ([row_blocks[bit] for bit in singles], pieces)
            )
            row_blocks.update(zip(singles, arrived))
            for bit in singles:
                row_blocks[bit + 1] = exchange(row_blocks[bit], "shard", 1)
            for k in several:
                low_bit = bits_of(k)[0]
                row_blocks[k] = exchange(row_blocks[k ^ low_bit], "shard", low_bit)
        elif position == 1:
            arrived, pieces = lax.optimization_barrier(([row_blocks[k] for k in several], pieces))
            row_blocks.update(zip(several, arrived))
            for k in several:
                row_blocks[k + 1] = exchange(row_blocks[k], "shard", 1)
        elif j == order[-1]:
            arrived, pieces = lax.optimization_barrier(([piece for _, piece in pending], pieces))
            pending = [(k, piece) for (k, _), piece in zip(pending, arrived)]
        row_sums[j] = add_rounded(pieces[0], exchange(pieces[1], "shard", 1))
        out_parts[j], out_parts[j + 1] = pieces[2], pieces[3]
    all_rows, all_grads, all_pre, all_hidden = carried
    row_sums, all_grads = lax.optimization_barrier((row_sums, all_grads))
    down_sum = transposed_times(all_grads, all_hidden).astype(bf16)
    grad_down = lax.psum_scatter(down_sum, "seq", scatter_dimension=0, tiled=True)
    all_rows = lax.optimization_barrier((all_rows, down_sum))[0]
    pre_sums = [transposed_times(all_rows, all_pre[0]).astype(bf16)]
    row_pieces = reduce_singles(row_sums, pending, "shard")
    row_pieces, pre_sums[0] = lax.optimization_barrier((row_pieces, pre_sums[0]))
    row_total = add_all(row_pieces)
    row_grad = row_total[:, :model_width]
    gate_grad_dense = (
        row_total[:, model_width : model_width + experts_all]
        + row_total[:, model_width + experts_all : model_width + 2 * experts_all]
    )
    weighted = gate_dense * gate_grad_dense
    logit_grad = weighted - gate_dense * jnp.sum(weighted, axis=-1, keepdims=True)
    grad_router = transposed_times(second_low.astype(jnp.float32), logit_grad, highest)
    second_grad = row_grad + times_transposed(
        logit_grad, router_weight.astype(jnp.float32), highest
    )
    residual_part, grad_gain_ffn = rms_backward(residual, second_factor, second_gain, second_grad)
    residual_grad = upstream + residual_part
    residual_low = residual_grad.astype(bf16)
    mixed_grad_tokens = times_transposed(residual_low, out_weight).astype(bf16)
    other_half = exchange(wide_half, "shard", 1)
    mixed_grad_tokens, out_parts, all_rows, other_half, mixed_late = lax.optimization_barrier(
        (mixed_grad_tokens, out_parts, all_rows, other_half, mixed_tokens)
    )
    mixed_grad = lax.all_to_all(mixed_grad_tokens, "seq", split_axis=1, concat_axis=0, tiled=True)
    odd = [exchange(out_parts[j + 1], "shard", 1) for j in order]
    pre_sums += [
        transposed_times(all_rows, all_pre[e]).astype(bf16) for e in range(1, local_experts)
    ]
    odd, pre_sums = lax.optimization_barrier((odd, pre_sums))
    out_sums = {j: add_rounded(out_parts[j], piece) for j, piece in zip(order, odd)}
    out_pending = reduce_several(out_sums, "shard")
    whole_out = transposed_times(residual_low, mixed_late).astype(bf16)
    whole_keep, whole_give = halves_by_core(whole_out, "shard")
    whole_arrived = exchange(whole_give, "shard", 1)
    mixed_grad, pre_sums, arrived, whole_arrived = lax.optimization_barrier(
        (mixed_grad, pre_sums, [piece for _, piece in out_pending], whole_arrived)
    )
    out_pending = [(j, piece) for (j, _), piece in zip(out_pending, arrived)]
    out_pieces = reduce_singles(out_sums, out_pending, "shard")
    whole_sums = chip_sums(whole_keep, whole_arrived, "shard")
    whole_pending = reduce_several(whole_sums, "shard")
    pre_grads = [
        lax.psum_scatter(part, "seq", scatter_dimension=0, tiled=True) for part in pre_sums
    ]

    query_grad, prompt_grad, self_grad = attend_backward(
        block_number,
        queries,
        to_lanes(mixed_grad),
        mixed_own,
        levels,
        [
            jnp.tile(cos_table[:, 0, :], (1, LANES // cos_table.shape[2])),
            jnp.tile(
                jnp.concatenate([sin_table, -sin_table], axis=2)[:, 0, :],
                (1, LANES // HEAD_DIMENSION),
            ),
        ],
        kv_prompt,
        kv_own,
        group,
        kv_heads,
    )
    query_grad, prompt_grad, self_grad, out_pieces, arrived = lax.optimization_barrier(
        (query_grad, prompt_grad, self_grad, out_pieces, [piece for _, piece in whole_pending])
    )
    whole_pending = [(j, piece) for (j, _), piece in zip(whole_pending, arrived)]
    lin_query = query_grad[:, :query_width]
    own_prompt = reduce_rows(prompt_grad, "shard")
    key_grad = jnp.concatenate(
        [own_prompt[:, :key_width], self_grad[PROMPT_BLK:, :key_width]], axis=0
    )
    value_low = jnp.concatenate(
        [own_prompt[:, LANES : LANES + key_width], self_grad[PROMPT_BLK:, LANES : LANES + key_width]],
        axis=0,
    ).astype(bf16)
    lin_key = rotate(key_grad, cos_table, -sin_table, HEAD_DIMENSION).astype(bf16)
    lin_all = jnp.concatenate([lin_query, lin_key, value_low], axis=1)
    all_columns = lin_all.shape[1]
    lin_all, out_pieces, whole_sums = lax.optimization_barrier((lin_all, out_pieces, whole_sums))
    lin_tokens = lax.all_to_all(lin_all, "seq", split_axis=0, concat_axis=1, tiled=True)

    small_grad = jnp.concatenate([grad_router, grad_gain_ffn[:, None]], axis=1)
    grad_qkv = jnp.concatenate([transposed_times(normed_low, lin_all), small_grad], axis=1)
    grad_qkv = reduce_rows(grad_qkv.astype(bf16), "shard")
    output = (residual + add_all(out_pieces)).astype(bf16)
    grad_out = add_all(reduce_singles(whole_sums, whole_pending, "shard")).astype(bf16)
    grad_out = grad_out.reshape(grad_out.shape[0], seq_count, -1).transpose(1, 0, 2)
    grad_out = scatter_direct(grad_out, "seq").T
    hidden_units = w_gate.shape[2]
    grad_down = grad_down.T.reshape(local_experts, hidden_units, -1).astype(jnp.float32)
    first_grads = pre_grads[0].astype(jnp.float32)
    lin_tokens, grad_out, output, grad_down, first_grads = lax.optimization_barrier(
        (lin_tokens, grad_out, output, grad_down, first_grads)
    )
    pre_grads = [first_grads] + [part.astype(jnp.float32) for part in pre_grads[1:]]
    parts = [0.0, 0.0]
    for k, weight in enumerate((wide_half, other_half)):
        for group_index in range(seq_count):
            columns = slice(group_index * all_columns, (group_index + 1) * all_columns)
            parts[k] = parts[k] + times_transposed(lin_tokens[:, columns], weight[group_index])
    normed_grad = jnp.concatenate(
        [
            jnp.where(core_bit == 0, parts[0], parts[1]),
            jnp.where(core_bit == 0, parts[1], parts[0]),
        ],
        axis=1,
    )
    own_features = own_weight.shape[0]
    gain_own = lax.dynamic_slice_in_dim(first_gain, shard_index * own_features, own_features)
    gain_part = (
        jnp.sum(own_weight.astype(jnp.float32) * grad_qkv[:, :all_columns], axis=1) / gain_own
    )
    grad_query = grad_qkv[:, :query_width]
    grad_key = grad_qkv[:, query_width : query_width + key_width]
    grad_value = grad_qkv[:, query_width + key_width : query_width + 2 * key_width]
    small_grad = jnp.concatenate([grad_qkv[:, all_columns:], gain_part[:, None]], axis=1).astype(bf16)
    small_grad = scatter_direct(
        small_grad.reshape(seq_count, -1, small_grad.shape[1]), "seq"
    )
    own_factor = rms_parts(own_inputs)
    input_part, _ = rms_backward(own_inputs, own_factor, first_gain, normed_grad)
    tokens_grad = residual_grad + input_part
    grad_gate = jnp.stack([part[:, :hidden_units] for part in pre_grads])
    grad_up = jnp.stack([part[:, hidden_units:] for part in pre_grads])
    return (
        output,
        tokens_grad,
        grad_query,
        grad_key,
        grad_value,
        grad_out,
        small_grad[:, experts_all + 1],
        small_grad[:, experts_all],
        small_grad[:, :experts_all],
        grad_gate,
        grad_up,
        grad_down,
    )


def solution(mesh):
    return jax.shard_map(
        on_device,
        mesh=mesh,
        in_specs=(
            P(("shard", "seq"), None),
            P(("shard", "seq"), None),
            P("shard", "seq"),
            P("shard", "seq"),
            P("shard", "seq"),
            P("seq", "shard"),
            P(("shard", "seq")),
            P(("shard", "seq")),
            P(("shard", "seq"), None),
            P("shard", None, None),
            P("shard", None, None),
            P("shard", None, None),
            P(("shard", "seq"), None),
        ),
        out_specs=(
            P(("shard", "seq"), None),
            P(("shard", "seq"), None),
            P("shard", "seq"),
            P("shard", "seq"),
            P("shard", "seq"),
            P("seq", "shard"),
            P(("shard", "seq")),
            P(("shard", "seq")),
            P(("shard", "seq"), None),
            P("shard", "seq", None),
            P("shard", "seq", None),
            P("shard", None, "seq"),
        ),
        check_vma=False,
    )
```

```python
from functools import partial

import jax
import jax.numpy as jnp
from jax import lax
from jax.experimental import pallas as pl
from jax.experimental.pallas import tpu as pltpu
from jax.sharding import PartitionSpec as P

HEAD_DIMENSION = 64
CONT_LEN = 512
PROMPT_BLK = 128


norm_eps = 1e-05
negative = -1e30
rope_base = 10000.0
highest = lax.Precision.HIGHEST


def rms_norm(values, scaling):
    factor = lax.rsqrt(jnp.mean(values * values, axis=-1, keepdims=True) + norm_eps)
    return values * factor * scaling


def swiglu(gate_pre, up_pre):
    return jax.nn.silu(gate_pre) * up_pre


def rotary_tables(places, head_size):
    half_size = head_size // 2
    frequency = jnp.exp(
        jnp.arange(half_size, dtype=jnp.float32) * (-2.0 * jnp.log(rope_base) / head_size)
    )
    angles = places.astype(jnp.float32)[:, None] * frequency[None, :]
    return (jnp.cos(angles)[:, None, :], jnp.sin(angles)[:, None, :])


def rotate(values, cosine, sine, head_size):
    total_row_count = values.shape[0]
    by_head = values.reshape(total_row_count, -1, head_size)
    half_size = head_size // 2
    first_half = by_head[..., :half_size]
    second_half = by_head[..., half_size:]
    turned = jnp.concatenate(
        [first_half * cosine - second_half * sine, second_half * cosine + first_half * sine],
        axis=-1,
    )
    return turned.reshape(total_row_count, -1)


def place_of(within, block_index, prompt_len):
    return jnp.where(
        within < PROMPT_BLK,
        block_index * PROMPT_BLK + within,
        prompt_len + (within - PROMPT_BLK) % CONT_LEN,
    )


def times_transposed(left_side, right_side, precision=None):
    return lax.dot_general(
        left_side,
        right_side,
        (((1,), (1,)), ((), ())),
        precision=precision,
        preferred_element_type=jnp.float32,
    )


def transposed_times(left_side, right_side, precision=None):
    return lax.dot_general(
        left_side,
        right_side,
        (((0,), (0,)), ((), ())),
        precision=precision,
        preferred_element_type=jnp.float32,
    )


def rms_parts(values):
    return lax.rsqrt(jnp.mean(values * values, axis=-1, keepdims=True) + norm_eps)


def rms_backward(values, factor, scaling, normed_grad):
    scaled = scaling * normed_grad
    inner = jnp.mean(scaled * values, axis=-1, keepdims=True)
    values_grad = factor * scaled - values * (factor * factor * factor) * inner
    gain_grad = jnp.sum(normed_grad * values * factor, axis=0)
    return values_grad, gain_grad


def matmul(left_side, right_side):
    return jnp.dot(left_side, right_side, preferred_element_type=jnp.float32)


LANES = 128


def relane(values, source, target):
    lane = lax.broadcasted_iota(jnp.int32, values.shape, 1)
    swapped = jnp.where(source != target, pltpu.roll(values, HEAD_DIMENSION, 1), values)
    return jnp.where(lane // HEAD_DIMENSION == target, swapped, 0.0)


def head_rows(ref, first, count, source, target):
    values = ref[pl.ds(first, count), :].astype(jnp.float32)
    return relane(values, source, target).astype(jnp.bfloat16)


def nt_dot(left_side, right_side):
    return lax.dot_general(
        left_side, right_side, (((1,), (1,)), ((), ())), preferred_element_type=jnp.float32
    )


def nn_dot(left_side, right_side):
    return jnp.dot(left_side, right_side, preferred_element_type=jnp.float32)


def below_diagonal(scores):
    key_row = lax.broadcasted_iota(jnp.int32, scores.shape, 0)
    query_column = lax.broadcasted_iota(jnp.int32, scores.shape, 1)
    return jnp.where(key_row <= query_column, scores, negative)


def seen_prompt(scores, first_key, shard_index):
    key_row = lax.broadcasted_iota(jnp.int32, scores.shape, 0) + first_key
    query_column = lax.broadcasted_iota(jnp.int32, scores.shape, 1) % PROMPT_BLK
    return jnp.where(key_row <= query_column + shard_index * PROMPT_BLK, scores, negative)


def transposed(values):
    return values.astype(jnp.float32).T


QUERY_CHUNK = 512
KEY_CHUNK = 1024
FORWARD_CHUNK = 256


def attend_forward_body(
    group, kv_heads, index_ref, q_ref, kp_ref, vp_ref, ko_ref, vo_ref, mixed_ref, level_ref, vt_all, acc
):
    pair = pl.program_id(0)
    prompt_len = kp_ref.shape[0]
    block_len = ko_ref.shape[0]
    conts = (block_len - PROMPT_BLK) // CONT_LEN
    shard_index = index_ref[0]

    @pl.when(pair == 0)
    def _():
        vt_all[:, :prompt_len] = transposed(vp_ref[...]).astype(jnp.bfloat16)
        vt_all[:, prompt_len:] = transposed(vo_ref[...]).astype(jnp.bfloat16)

    acc[...] = jnp.zeros_like(acc)
    size = min(FORWARD_CHUNK, prompt_len)
    prompt_keys = [slice(first, first + size) for first in range(0, prompt_len, size)]

    def kv_half(side):
        return jnp.minimum((2 * pair + side) // group, kv_heads - 1)

    def finish(scores, value_columns):
        level = jnp.max(scores[0], axis=0, keepdims=True)
        for part in scores[1:]:
            level = jnp.maximum(level, jnp.max(part, axis=0, keepdims=True))
        total = None
        mixed = None
        for part, columns in zip(scores, value_columns):
            weights = jnp.exp(part - level)
            part_total = jnp.sum(weights, axis=0, keepdims=True)
            part_mixed = nn_dot(columns, weights.astype(jnp.bfloat16))
            total = part_total if total is None else total + part_total
            mixed = part_mixed if mixed is None else mixed + part_mixed
        return mixed / total, level + jnp.log(total)

    both = jnp.concatenate(
        [head_rows(q_ref, 0, PROMPT_BLK, side, kv_half(side)) for side in range(2)], axis=0
    )
    mixed, level = finish(
        [
            seen_prompt(nt_dot(kp_ref[keys, :], both), keys.start, shard_index)
            for keys in prompt_keys
        ],
        [vt_all[:, keys] for keys in prompt_keys],
    )
    mixed = mixed.T
    for side in range(2):
        rows = slice(side * PROMPT_BLK, (side + 1) * PROMPT_BLK)
        acc[:PROMPT_BLK, :] += relane(mixed[rows], kv_half(side), side)
        level_ref[side, :, :PROMPT_BLK] = level[:, rows]

    def step(turn, _):
        side = turn // conts
        number = turn % conts
        half = kv_half(side)
        first_own = PROMPT_BLK + number * CONT_LEN
        for chunk in range(CONT_LEN // QUERY_CHUNK):
            before = chunk * QUERY_CHUNK
            first_row = pl.multiple_of(first_own + before, PROMPT_BLK)
            queries = head_rows(q_ref, first_row, QUERY_CHUNK, side, half)
            scores = [nt_dot(kp_ref[keys, :], queries) for keys in prompt_keys]
            columns = [vt_all[:, keys] for keys in prompt_keys]
            if before:
                start = pl.multiple_of(first_own, PROMPT_BLK)
                scores.append(nt_dot(ko_ref[pl.ds(start, before), :], queries))
                columns.append(
                    vt_all[:, pl.ds(pl.multiple_of(prompt_len + start, PROMPT_BLK), before)]
                )
            scores.append(below_diagonal(nt_dot(ko_ref[pl.ds(first_row, QUERY_CHUNK), :], queries)))
            columns.append(
                vt_all[:, pl.ds(pl.multiple_of(prompt_len + first_row, PROMPT_BLK), QUERY_CHUNK)]
            )
            mixed, level = finish(scores, columns)
            acc[pl.ds(first_row, QUERY_CHUNK), :] += relane(mixed.T, half, side)
            level_ref[side, :, pl.ds(first_row, QUERY_CHUNK)] = level
        return 0

    lax.fori_loop(0, 2 * conts, step, 0)
    mixed_ref[...] = acc[...].astype(jnp.bfloat16)


def attend_backward_body(
    group,
    kv_heads,
    index_ref,
    q_ref,
    grad_ref,
    mixed_ref,
    level_ref,
    cos_ref,
    sin_ref,
    kp_ref,
    vp_ref,
    ko_ref,
    vo_ref,
    dq_ref,
    dprompt_ref,
    down_ref,
    kt_all,
    acc,
    prompt_acc,
):
    pair = pl.program_id(0)
    last = pl.num_programs(0) - 1
    prompt_len = kp_ref.shape[0]
    block_len = ko_ref.shape[0]
    conts = (block_len - PROMPT_BLK) // CONT_LEN
    shard_index = index_ref[0]
    bf16 = jnp.bfloat16

    @pl.when(pair == 0)
    def _():
        kt_all[:, :prompt_len] = transposed(kp_ref[...]).astype(bf16)
        kt_all[:, prompt_len:] = transposed(ko_ref[...]).astype(bf16)
        prompt_acc[...] = jnp.zeros_like(prompt_acc)
        down_ref[...] = jnp.zeros_like(down_ref)

    acc[...] = jnp.zeros_like(acc)

    def kv_half(side):
        return jnp.minimum((2 * pair + side) // group, kv_heads - 1)

    def inner_sums(first_row, count, side):
        rows = pl.ds(first_row, count)
        product = mixed_ref[rows, :].astype(jnp.float32) * grad_ref[rows, :].astype(jnp.float32)
        return jnp.sum(relane(product, side, side).T, axis=0, keepdims=True)

    def part(keys, values, key_columns, queries, grads, level, inner, mask, sums, first_key):
        scores = nt_dot(keys, queries)
        if mask is not None:
            scores = mask(scores)
        probs = jnp.exp(scores - level)
        score_grad = (probs * (nt_dot(values, grads) - inner)).astype(bf16)
        rows = pl.ds(first_key, keys.shape[0])
        sums[rows, :LANES] += nn_dot(score_grad, queries)
        sums[rows, LANES:] += nn_dot(probs.astype(bf16), grads)
        return nn_dot(key_columns, score_grad)

    def prompt_parts(queries, grads, level, inner, masked):
        total = None
        size = min(KEY_CHUNK, prompt_len)
        for first_key in range(0, prompt_len, size):
            rows = slice(first_key, first_key + size)
            mask = (lambda s, f=first_key: seen_prompt(s, f, shard_index)) if masked else None
            piece = part(
                kp_ref[rows, :], vp_ref[rows, :], kt_all[:, rows], queries, grads, level, inner,
                mask, prompt_acc, first_key,
            )
            total = piece if total is None else total + piece
        return total

    both_q, both_g, both_level, both_inner = [], [], [], []
    for side in range(2):
        both_q.append(head_rows(q_ref, 0, PROMPT_BLK, side, kv_half(side)))
        both_g.append(head_rows(grad_ref, 0, PROMPT_BLK, side, kv_half(side)))
        both_level.append(level_ref[side, :, :PROMPT_BLK])
        both_inner.append(inner_sums(0, PROMPT_BLK, side))
    grad_q = prompt_parts(
        jnp.concatenate(both_q, axis=0),
        jnp.concatenate(both_g, axis=0),
        jnp.concatenate(both_level, axis=1),
        jnp.concatenate(both_inner, axis=1),
        True,
    ).T
    for side in range(2):
        rows = slice(side * PROMPT_BLK, (side + 1) * PROMPT_BLK)
        acc[:PROMPT_BLK, :] += relane(grad_q[rows], kv_half(side), side)

    def step(turn, _):
        side = turn // conts
        number = turn % conts
        half = kv_half(side)
        first_own = PROMPT_BLK + number * CONT_LEN
        for chunk in range(CONT_LEN // QUERY_CHUNK):
            before = chunk * QUERY_CHUNK
            first_row = pl.multiple_of(first_own + before, PROMPT_BLK)
            queries = head_rows(q_ref, first_row, QUERY_CHUNK, side, half)
            grads = head_rows(grad_ref, first_row, QUERY_CHUNK, side, half)
            level = level_ref[side, :, pl.ds(first_row, QUERY_CHUNK)]
            inner = inner_sums(first_row, QUERY_CHUNK, side)
            grad_q = prompt_parts(queries, grads, level, inner, False)
            own = [(first_row, QUERY_CHUNK, below_diagonal)]
            if before:
                own.append((pl.multiple_of(first_own, PROMPT_BLK), before, None))
            for start, size, mask in own:
                rows = pl.ds(start, size)
                columns = pl.ds(pl.multiple_of(prompt_len + start, PROMPT_BLK), size)
                grad_q += part(
                    ko_ref[rows, :], vo_ref[rows, :], kt_all[:, columns], queries, grads, level,
                    inner, mask, down_ref, start,
                )
            acc[pl.ds(first_row, QUERY_CHUNK), :] += relane(grad_q.T, half, side)
        return 0

    lax.fori_loop(0, 2 * conts, step, 0)
    grads = acc[...] * HEAD_DIMENSION ** (-0.5)
    half = HEAD_DIMENSION // 2
    lane = lax.broadcasted_iota(jnp.int32, grads.shape, 1)
    swapped = jnp.where(
        lane % HEAD_DIMENSION < half,
        pltpu.roll(grads, LANES - half, 1),
        pltpu.roll(grads, half, 1),
    )
    dq_ref[...] = (grads * cos_ref[...] + swapped * sin_ref[...]).astype(bf16)

    @pl.when(pair == last)
    def _():
        dprompt_ref[...] = prompt_acc[...].astype(bf16)


def pair_specs(block_len, prompt_len):
    by_pair = pl.BlockSpec((block_len, LANES), lambda b, i: (0, b))
    levels = pl.BlockSpec((2, 1, block_len), lambda b, i: (b, 0, 0))
    sources = [
        pl.BlockSpec((prompt_len, LANES), lambda b, i: (0, 0)),
        pl.BlockSpec((prompt_len, LANES), lambda b, i: (0, 1)),
        pl.BlockSpec((block_len, LANES), lambda b, i: (0, 0)),
        pl.BlockSpec((block_len, LANES), lambda b, i: (0, 1)),
    ]
    return by_pair, levels, sources


def attention_cost(block_len, prompt_len, width, products):
    pairs = (block_len * prompt_len + block_len * CONT_LEN // 2) * (width // HEAD_DIMENSION)
    return pl.CostEstimate(
        flops=products * 2 * pairs * 2 * LANES,
        bytes_accessed=8 * block_len * width,
        transcendentals=pairs,
    )


def attend_forward(index, queries, kv_prompt, kv_own, group, kv_heads):
    block_len, width = queries.shape
    prompt_len = kv_prompt.shape[0]
    by_pair, levels, sources = pair_specs(block_len, prompt_len)
    return pl.pallas_call(
        partial(attend_forward_body, group, kv_heads),
        out_shape=[
            jax.ShapeDtypeStruct((block_len, width), jnp.bfloat16),
            jax.ShapeDtypeStruct((width // HEAD_DIMENSION, 1, block_len), jnp.float32),
        ],
        grid_spec=pltpu.PrefetchScalarGridSpec(
            num_scalar_prefetch=1,
            grid=(width // LANES,),
            in_specs=[by_pair] + sources,
            out_specs=[by_pair, levels],
            scratch_shapes=[
                pltpu.VMEM((LANES, prompt_len + block_len), jnp.bfloat16),
                pltpu.VMEM((block_len, LANES), jnp.float32),
            ],
        ),
        compiler_params=pltpu.CompilerParams(
            dimension_semantics=("arbitrary",), vmem_limit_bytes=56 * 1024 * 1024
        ),
        cost_estimate=attention_cost(block_len, prompt_len, width, 2),
        name="attend_forward",
    )(index, queries, kv_prompt, kv_prompt, kv_own, kv_own)


def attend_backward(
    index, queries, grads, mixed, level, tables, kv_prompt, kv_own, group, kv_heads
):
    block_len, width = queries.shape
    prompt_len = kv_prompt.shape[0]
    by_pair, levels, sources = pair_specs(block_len, prompt_len)
    return pl.pallas_call(
        partial(attend_backward_body, group, kv_heads),
        out_shape=[
            jax.ShapeDtypeStruct((block_len, width), jnp.bfloat16),
            jax.ShapeDtypeStruct((prompt_len, 2 * LANES), jnp.bfloat16),
            jax.ShapeDtypeStruct((block_len, 2 * LANES), jnp.float32),
        ],
        grid_spec=pltpu.PrefetchScalarGridSpec(
            num_scalar_prefetch=1,
            grid=(width // LANES,),
            in_specs=[by_pair, by_pair, by_pair, levels]
            + [pl.BlockSpec((block_len, LANES), lambda b, i: (0, 0))] * 2
            + sources,
            out_specs=[
                by_pair,
                pl.BlockSpec((prompt_len, 2 * LANES), lambda b, i: (0, 0)),
                pl.BlockSpec((block_len, 2 * LANES), lambda b, i: (0, 0)),
            ],
            scratch_shapes=[
                pltpu.VMEM((LANES, prompt_len + block_len), jnp.bfloat16),
                pltpu.VMEM((block_len, LANES), jnp.float32),
                pltpu.VMEM((prompt_len, 2 * LANES), jnp.float32),
            ],
        ),
        compiler_params=pltpu.CompilerParams(
            dimension_semantics=("arbitrary",), vmem_limit_bytes=56 * 1024 * 1024
        ),
        cost_estimate=attention_cost(block_len, prompt_len, width, 5),
        name="attend_backward",
    )(index, queries, grads, mixed, level, *tables, kv_prompt, kv_prompt, kv_own, kv_own)


def to_lanes(values):
    extra = -values.shape[1] % LANES
    return jnp.pad(values, ((0, 0), (0, extra))) if extra else values


def exchange(values, axis_name, bit):
    count = lax.axis_size(axis_name)
    return lax.ppermute(values, axis_name, [(i, i ^ bit) for i in range(count)])


def bits_of(number):
    return [1 << k for k in range(number.bit_length()) if number >> k & 1]


def even_blocks(count):
    even = sorted(range(2, count, 2), key=lambda j: (len(bits_of(j)), j))
    singles = [j for j in even if len(bits_of(j)) == 1]
    return singles, even[len(singles) :]


def gather_blocks(own, axis_name, after_first=None):
    count = lax.axis_size(axis_name)
    singles, several = even_blocks(count)
    blocks = {0: own, 1: exchange(own, axis_name, 1)}
    for j in singles:
        blocks[j] = exchange(own, axis_name, j)
    if after_first is not None:
        blocks.update(zip(singles, after_first([blocks[j] for j in singles])))
    for j in several:
        low_bit = bits_of(j)[0]
        blocks[j] = exchange(blocks[j ^ low_bit], axis_name, low_bit)
    for j in singles + several:
        blocks[j + 1] = exchange(blocks[j], axis_name, 1)
    return [blocks[j] for j in range(count)]


def add_rounded(left_side, right_side):
    return (left_side.astype(jnp.float32) + right_side.astype(jnp.float32)).astype(jnp.bfloat16)


def reduce_several(sums, axis_name):
    sums = dict(sums)
    pending = []
    for j in sorted((j for j in sums if len(bits_of(j)) > 1), key=lambda j: (-len(bits_of(j)), j)):
        bit = bits_of(j)[-1]
        piece = exchange(sums[j], axis_name, bit)
        if len(bits_of(j ^ bit)) > 1:
            sums[j ^ bit] = add_rounded(sums[j ^ bit], piece)
        else:
            pending.append((j ^ bit, piece))
    return pending


def reduce_singles(sums, pending, axis_name):
    sums = dict(sums)
    for j, piece in pending:
        sums[j] = add_rounded(sums[j], piece)
    return [sums[0]] + [exchange(sums[j], axis_name, j) for j in sums if len(bits_of(j)) == 1]


def add_all(pieces):
    total = pieces[0].astype(jnp.float32)
    for piece in pieces[1:]:
        total = total + piece.astype(jnp.float32)
    return total


def halves_by_core(values, axis_name):
    count = lax.axis_size(axis_name)
    parity = lax.axis_index(axis_name) % 2
    paired = values.reshape(count // 2, 2, values.shape[0] // count, values.shape[1])
    keep = lax.dynamic_index_in_dim(paired, parity, 1, keepdims=False)
    give = lax.dynamic_index_in_dim(paired, 1 - parity, 1, keepdims=False)
    return keep, give


def chip_sums(keep, arrived, axis_name):
    index = lax.axis_index(axis_name)
    total = add_rounded(keep, arrived)
    return {
        2 * k: lax.dynamic_index_in_dim(total, (index // 2) ^ k, 0, keepdims=False)
        for k in range(total.shape[0])
    }


def reduce_rows(values, axis_name):
    keep, give = halves_by_core(values, axis_name)
    sums = chip_sums(keep, exchange(give, axis_name, 1), axis_name)
    return add_all(reduce_singles(sums, reduce_several(sums, axis_name), axis_name))


def in_order(blocks, index):
    stacked = jnp.stack(blocks)
    return jnp.concatenate(
        [lax.dynamic_index_in_dim(stacked, j ^ index, 0, keepdims=True) for j in range(len(blocks))],
        axis=0,
    )


def expert_body(
    experts_all, index_ref, x_even, x_odd, og_even, og_odd, gate_w, up_w, down_w, *rest
):
    (x_all, og_all, pre_all, hid_all, row_even, row_odd, out_even, out_odd) = rest[-12:-4]
    (row_acc, out_acc, back_acc, _) = rest[-4:]
    expert = pl.program_id(0)
    last = pl.num_programs(0) - 1
    rows = x_even.shape[0]
    width = x_all.shape[1]
    hidden_units = gate_w.shape[2]
    nt_dims = (((1,), (1,)), ((), ()))

    @pl.when(expert == 0)
    def _():
        x_all[:rows, :] = x_even[:, :width]
        x_all[rows:, :] = x_odd[:, :width]
        og_all[:rows, :] = og_even[...]
        og_all[rows:, :] = og_odd[...]

    column = index_ref[0] + expert
    lane = lax.broadcasted_iota(jnp.int32, (2 * rows, LANES), 1)
    coded = jnp.concatenate([x_even[:, width:], x_odd[:, width:]], axis=0).astype(jnp.float32)
    gate = jnp.sum(
        jnp.where((lane == column) | (lane == column + experts_all), coded, 0.0),
        axis=1,
        keepdims=True,
    )
    x_rows = x_all[...]
    og_rows = og_all[...]
    gate_pre = jnp.dot(x_rows, gate_w[0], preferred_element_type=jnp.float32)
    up_pre = jnp.dot(x_rows, up_w[0], preferred_element_type=jnp.float32)
    down_grad = lax.dot_general(og_rows, down_w[0], nt_dims, preferred_element_type=jnp.float32)
    sigmoid = 1.0 / (1.0 + jnp.exp(-gate_pre))
    silu = gate_pre * sigmoid
    hidden = silu * up_pre
    gate_back = jnp.sum(hidden * down_grad, axis=1, keepdims=True)
    hidden_low = (gate * hidden).astype(jnp.bfloat16)
    hidden_grad = gate * down_grad
    gate_pre_low = (
        hidden_grad * up_pre * sigmoid * (1.0 + gate_pre * (1.0 - sigmoid))
    ).astype(jnp.bfloat16)
    up_pre_low = (hidden_grad * silu).astype(jnp.bfloat16)
    hid_all[...] = hidden_low
    pre_all[0, :, :hidden_units] = gate_pre_low
    pre_all[0, :, hidden_units:] = up_pre_low
    row = lax.dot_general(
        gate_pre_low, gate_w[0], nt_dims, preferred_element_type=jnp.float32
    ) + lax.dot_general(up_pre_low, up_w[0], nt_dims, preferred_element_type=jnp.float32)
    out = jnp.dot(hidden_low, down_w[0], preferred_element_type=jnp.float32)
    high = gate_back.astype(jnp.bfloat16).astype(jnp.float32)
    back = jnp.where(lane == column, high, 0.0) + jnp.where(
        lane == column + experts_all, gate_back - high, 0.0
    )

    @pl.when(expert == 0)
    def _():
        row_acc[...] = row
        out_acc[...] = out
        back_acc[...] = back

    @pl.when(expert > 0)
    def _():
        row_acc[...] += row
        out_acc[...] += out
        back_acc[...] += back

    @pl.when(expert == last)
    def _():
        for ref, first in ((row_even, 0), (row_odd, rows)):
            ref[:, :width] = row_acc[first : first + rows, :].astype(jnp.bfloat16)
            ref[:, width:] = back_acc[first : first + rows, :].astype(jnp.bfloat16)
        out_even[...] = out_acc[:rows, :].astype(jnp.bfloat16)
        out_odd[...] = out_acc[rows:, :].astype(jnp.bfloat16)


def expert_pair(position, pairs, first_expert, experts_all, x_pair, og_pair, weights, carried):
    w_gate, w_up, w_down = weights
    rows, coded_width = x_pair[0].shape
    width = coded_width - LANES
    local_experts, _, hidden_units = w_gate.shape
    bf16 = jnp.bfloat16
    whole = 2 * rows
    fixed = lambda e, i: (0, 0)
    once = pl.Buffered(1)
    in_specs = (
        [pl.BlockSpec((rows, coded_width), fixed, pipeline_mode=once)] * 2
        + [pl.BlockSpec((rows, width), fixed, pipeline_mode=once)] * 2
        + [pl.BlockSpec((1, width, hidden_units), lambda e, i: (e, 0, 0))] * 2
        + [pl.BlockSpec((1, hidden_units, width), lambda e, i: (e, 0, 0))]
    )
    operands = [*x_pair, *og_pair, w_gate, w_up, w_down]
    aliases = {}
    if carried is not None:
        in_specs = in_specs + [pl.BlockSpec(memory_space=pl.ANY)] * 4
        aliases = {1 + len(operands) + k: k for k in range(4)}
        operands = operands + list(carried)
    out_shape = [
        jax.ShapeDtypeStruct((pairs * whole, width), bf16),
        jax.ShapeDtypeStruct((pairs * whole, width), bf16),
        jax.ShapeDtypeStruct((local_experts, pairs * whole, 2 * hidden_units), bf16),
        jax.ShapeDtypeStruct((pairs * whole, local_experts * hidden_units), bf16),
        jax.ShapeDtypeStruct((rows, coded_width), bf16),
        jax.ShapeDtypeStruct((rows, coded_width), bf16),
        jax.ShapeDtypeStruct((rows, width), bf16),
        jax.ShapeDtypeStruct((rows, width), bf16),
    ]
    out_specs = [
        pl.BlockSpec((whole, width), lambda e, i: (position, 0)),
        pl.BlockSpec((whole, width), lambda e, i: (position, 0)),
        pl.BlockSpec((1, whole, 2 * hidden_units), lambda e, i: (e, position, 0)),
        pl.BlockSpec((whole, hidden_units), lambda e, i: (position, e)),
        pl.BlockSpec((rows, coded_width), fixed),
        pl.BlockSpec((rows, coded_width), fixed),
        pl.BlockSpec((rows, width), fixed),
        pl.BlockSpec((rows, width), fixed),
    ]
    products = 2 * whole * width * hidden_units * local_experts
    results = pl.pallas_call(
        partial(expert_body, experts_all),
        out_shape=out_shape,
        grid_spec=pltpu.PrefetchScalarGridSpec(
            num_scalar_prefetch=1,
            grid=(local_experts,),
            in_specs=in_specs,
            out_specs=out_specs,
            scratch_shapes=[
                pltpu.VMEM((whole, width), jnp.float32),
                pltpu.VMEM((whole, width), jnp.float32),
                pltpu.VMEM((whole, LANES), jnp.float32),
                pltpu.VMEM((8, LANES), jnp.float32),
            ],
        ),
        input_output_aliases=aliases,
        compiler_params=pltpu.CompilerParams(
            dimension_semantics=("arbitrary",), vmem_limit_bytes=60 * 1024 * 1024
        ),
        cost_estimate=pl.CostEstimate(
            flops=6 * products,
            bytes_accessed=3 * 2 * local_experts * width * hidden_units + 20 * whole * width,
            transcendentals=whole * hidden_units * local_experts,
        ),
        name="experts",
    )(first_expert, *operands)
    return results[:4], results[4:]


def on_device(
    tokens,
    routes,
    w_query,
    key_projection,
    value_projection,
    w_out,
    gain_attn,
    gain_ffn,
    w_router,
    w_gate,
    w_up,
    w_down,
    out_grad,
):
    bf16 = jnp.bfloat16
    shard_count = lax.axis_size("shard")
    seq_count = lax.axis_size("seq")
    shard_index = lax.axis_index("shard")
    seq_index = lax.axis_index("seq")
    tok_count, model_width = tokens.shape
    top_count = routes.shape[1]
    experts_all = w_router.shape[1]
    local_experts = w_gate.shape[0]
    block_len = tok_count * seq_count
    prompt_len = PROMPT_BLK * shard_count
    query_width = w_query.shape[1]
    key_width = key_projection.shape[1]

    singles, several = even_blocks(shard_count)
    small = jnp.concatenate([w_router, gain_attn[:, None], gain_ffn[:, None]], axis=1)
    small = lax.all_gather(small, "seq", axis=0, tiled=True)
    small = lax.all_gather(small, "shard", axis=0, tiled=True)
    router_weight = small[:, :experts_all]
    first_gain = small[:, experts_all].astype(jnp.float32)
    second_gain = small[:, experts_all + 1].astype(jnp.float32)
    block_tokens = lax.all_gather(tokens, "seq", axis=0, tiled=True)
    own_weight = jnp.concatenate([w_query, key_projection, value_projection], axis=1)
    grad_blocks = {0: out_grad}
    near = [exchange(out_grad, "shard", bit) for bit in singles]

    def with_near(blocks):
        blocks, near[:] = lax.optimization_barrier((blocks, near))
        return blocks

    weight_blocks = gather_blocks(own_weight, "shard", with_near)
    grad_blocks.update(zip(singles, near))
    for j in [0] + singles:
        grad_blocks[j + 1] = exchange(grad_blocks[j], "shard", 1)
    out_weight = lax.all_gather(w_out, "seq", axis=0, tiled=True)
    qkv_weight = in_order(weight_blocks, shard_index).reshape(model_width, -1)

    block_rows = jnp.arange(block_len, dtype=jnp.int32)
    cos_table, sin_table = rotary_tables(
        place_of(block_rows, shard_index, prompt_len), HEAD_DIMENSION
    )
    inputs = block_tokens.astype(jnp.float32)
    first_factor = rms_parts(inputs)
    normed_low = (inputs * first_factor * first_gain).astype(bf16)
    lin = matmul(normed_low, qkv_weight)
    kv_heads = key_width // HEAD_DIMENSION
    group = query_width // key_width
    queries = rotate(lin[:, :query_width], cos_table, sin_table, HEAD_DIMENSION)
    queries = to_lanes((queries * HEAD_DIMENSION ** (-0.5)).astype(bf16))
    key_heads = rotate(
        lin[:, query_width : query_width + key_width], cos_table, sin_table, HEAD_DIMENSION
    ).astype(bf16)
    value_heads = lin[:, query_width + key_width :].astype(bf16)
    kv_own = jnp.concatenate([to_lanes(key_heads), to_lanes(value_heads)], axis=1)
    kv_prompt = lax.all_gather(kv_own[:PROMPT_BLK], "shard", axis=0, tiled=True)
    kv_prompt, out_weight, near = lax.optimization_barrier(
        (kv_prompt, out_weight, [grad_blocks[bit] for bit in singles])
    )
    grad_blocks.update(zip(singles, near))
    out_weight = lax.all_gather(out_weight, "shard", axis=1, tiled=True)
    for j in several:
        low_bit = bits_of(j)[0]
        grad_blocks[j] = exchange(grad_blocks[j ^ low_bit], "shard", low_bit)
    block_number = shard_index.astype(jnp.int32).reshape(1)
    mixed_own, levels = attend_forward(block_number, queries, kv_prompt, kv_own, group, kv_heads)
    sooner = [j for j in range(1, shard_count) if j - 1 not in several]
    mixed_own, held_blocks = lax.optimization_barrier((mixed_own, [grad_blocks[j] for j in sooner]))
    for j, block in zip(sooner, held_blocks):
        grad_blocks[j] = block
    for j in several:
        grad_blocks[j + 1] = exchange(grad_blocks[j], "shard", 1)
    mixed_heads = mixed_own[:, :query_width]
    mixed_tokens = lax.all_to_all(mixed_heads, "seq", split_axis=0, concat_axis=1, tiled=True)

    half_features = model_width // 2
    core_bit = shard_index % 2
    half_weight, mixed_tokens = lax.optimization_barrier(
        (
            lax.dynamic_slice_in_dim(qkv_weight, core_bit * half_features, half_features, axis=0),
            mixed_tokens,
        )
    )
    wide_half = lax.all_gather(half_weight, "seq", axis=0, tiled=False)

    own_inputs = tokens.astype(jnp.float32)
    upstream = out_grad.astype(jnp.float32)
    residual = own_inputs + matmul(mixed_tokens, out_weight)
    second_factor = rms_parts(residual)
    second_low = (residual * second_factor * second_gain).astype(bf16)
    logits = matmul(second_low, router_weight)
    chosen = routes[:, :, None] == jnp.arange(experts_all, dtype=jnp.int32)[None, None, :]
    named = jnp.any(chosen, axis=1)
    gate_dense = jax.nn.softmax(jnp.where(named, logits, negative), axis=-1)
    gate_dense = jnp.where(named, gate_dense, 0.0)

    gate_high = lax.reduce_precision(gate_dense, 8, 7)
    coded = jnp.concatenate(
        [
            second_low,
            gate_high.astype(bf16),
            (gate_dense - gate_high).astype(bf16),
            jnp.zeros((tok_count, LANES - 2 * experts_all), bf16),
        ],
        axis=1,
    )
    row_blocks = {0: coded, 1: exchange(coded, "shard", 1)}
    for bit in singles:
        row_blocks[bit] = exchange(coded, "shard", bit)
    order = [0] + singles[:-1] + several + singles[-1:]
    first_expert = (shard_index * local_experts).astype(jnp.int32).reshape(1)
    carried = None
    pending = []
    row_sums = {}
    out_parts = [None] * shard_count
    for position, j in enumerate(order):
        row_pair = [row_blocks[j], row_blocks[j + 1]]
        if j == order[-1]:
            row_pair, row_sums = lax.optimization_barrier((row_pair, row_sums))
            pending = reduce_several(row_sums, "shard")
        carried, pieces = expert_pair(
            position,
            len(order),
            first_expert,
            experts_all,
            row_pair,
            [grad_blocks[j], grad_blocks[j + 1]],
            (w_gate, w_up, w_down),
            carried,
        )
        if position == 0:
            arrived, pieces = lax.optimization_barrier(
                ([row_blocks[bit] for bit in singles], pieces)
            )
            row_blocks.update(zip(singles, arrived))
            for bit in singles:
                row_blocks[bit + 1] = exchange(row_blocks[bit], "shard", 1)
            for k in several:
                low_bit = bits_of(k)[0]
                row_blocks[k] = exchange(row_blocks[k ^ low_bit], "shard", low_bit)
        elif position == 1:
            arrived, pieces = lax.optimization_barrier(([row_blocks[k] for k in several], pieces))
            row_blocks.update(zip(several, arrived))
            for k in several:
                row_blocks[k + 1] = exchange(row_blocks[k], "shard", 1)
        elif j == order[-1]:
            arrived, pieces = lax.optimization_barrier(([piece for _, piece in pending], pieces))
            pending = [(k, piece) for (k, _), piece in zip(pending, arrived)]
        arrived = exchange(pieces[1], "shard", 1)
        if j != order[-1]:
            row_sums[j] = add_rounded(pieces[0], arrived)
        out_parts[j], out_parts[j + 1] = pieces[2], pieces[3]
    all_rows, all_grads, all_pre, all_hidden = carried
    down_sum = transposed_times(all_grads, all_hidden).astype(bf16)
    grad_down = lax.psum_scatter(down_sum, "seq", scatter_dimension=0, tiled=True)
    all_rows, arrived, down_sum = lax.optimization_barrier((all_rows, arrived, down_sum))
    row_sums[order[-1]] = add_rounded(pieces[0], arrived)
    pre_sums = [transposed_times(all_rows, all_pre[0]).astype(bf16)]
    row_pieces = reduce_singles(row_sums, pending, "shard")
    row_pieces, pre_sums[0] = lax.optimization_barrier((row_pieces, pre_sums[0]))
    row_total = add_all(row_pieces)
    row_grad = row_total[:, :model_width]
    gate_grad_dense = (
        row_total[:, model_width : model_width + experts_all]
        + row_total[:, model_width + experts_all : model_width + 2 * experts_all]
    )
    weighted = gate_dense * gate_grad_dense
    logit_grad = weighted - gate_dense * jnp.sum(weighted, axis=-1, keepdims=True)
    grad_router = transposed_times(second_low.astype(jnp.float32), logit_grad, highest)
    second_grad = row_grad + times_transposed(
        logit_grad, router_weight.astype(jnp.float32), highest
    )
    residual_part, grad_gain_ffn = rms_backward(residual, second_factor, second_gain, second_grad)
    residual_grad = upstream + residual_part
    residual_low = residual_grad.astype(bf16)
    mixed_grad_tokens = times_transposed(residual_low, out_weight).astype(bf16)
    other_half = exchange(wide_half, "shard", 1)
    mixed_grad_tokens, out_parts, all_rows, other_half, mixed_late = lax.optimization_barrier(
        (mixed_grad_tokens, out_parts, all_rows, other_half, mixed_tokens)
    )
    mixed_grad = lax.all_to_all(mixed_grad_tokens, "seq", split_axis=1, concat_axis=0, tiled=True)
    odd = [exchange(out_parts[j + 1], "shard", 1) for j in order]
    hidden_units = w_gate.shape[2]
    for e in range(1, local_experts):
        for first in (0, hidden_units):
            columns = all_pre[e, :, first : first + hidden_units]
            pre_sums.append(transposed_times(all_rows, columns).astype(bf16))
    odd, pre_sums = lax.optimization_barrier((odd, pre_sums))
    out_sums = {j: add_rounded(out_parts[j], piece) for j, piece in zip(order, odd)}
    out_pending = reduce_several(out_sums, "shard")
    whole_out = transposed_times(residual_low, mixed_late).astype(bf16)
    whole_keep, whole_give = halves_by_core(whole_out, "shard")
    whole_arrived = exchange(whole_give, "shard", 1)
    mixed_grad, pre_sums, arrived, whole_arrived = lax.optimization_barrier(
        (mixed_grad, pre_sums, [piece for _, piece in out_pending], whole_arrived)
    )
    out_pending = [(j, piece) for (j, _), piece in zip(out_pending, arrived)]
    out_pieces = reduce_singles(out_sums, out_pending, "shard")
    whole_sums = chip_sums(whole_keep, whole_arrived, "shard")
    whole_pending = reduce_several(whole_sums, "shard")
    pre_grads = [
        lax.psum_scatter(part, "seq", scatter_dimension=0, tiled=True) for part in pre_sums[:-1]
    ]

    query_grad, prompt_grad, self_grad = attend_backward(
        block_number,
        queries,
        to_lanes(mixed_grad),
        mixed_own,
        levels,
        [
            jnp.tile(cos_table[:, 0, :], (1, LANES // cos_table.shape[2])),
            jnp.tile(
                jnp.concatenate([sin_table, -sin_table], axis=2)[:, 0, :],
                (1, LANES // HEAD_DIMENSION),
            ),
        ],
        kv_prompt,
        kv_own,
        group,
        kv_heads,
    )
    query_grad, prompt_grad, self_grad, out_pieces, arrived = lax.optimization_barrier(
        (query_grad, prompt_grad, self_grad, out_pieces, [piece for _, piece in whole_pending])
    )
    whole_pending = [(j, piece) for (j, _), piece in zip(whole_pending, arrived)]
    lin_query = query_grad[:, :query_width]
    own_prompt = reduce_rows(prompt_grad, "shard")
    key_grad = jnp.concatenate(
        [own_prompt[:, :key_width], self_grad[PROMPT_BLK:, :key_width]], axis=0
    )
    value_low = jnp.concatenate(
        [own_prompt[:, LANES : LANES + key_width], self_grad[PROMPT_BLK:, LANES : LANES + key_width]],
        axis=0,
    ).astype(bf16)
    lin_key = rotate(key_grad, cos_table, -sin_table, HEAD_DIMENSION).astype(bf16)
    lin_all = jnp.concatenate([lin_query, lin_key, value_low], axis=1)
    all_columns = lin_all.shape[1]
    lin_all, out_pieces, whole_sums = lax.optimization_barrier((lin_all, out_pieces, whole_sums))
    lin_tokens = lax.all_to_all(lin_all, "seq", split_axis=0, concat_axis=1, tiled=True)

    small_grad = jnp.concatenate([grad_router, grad_gain_ffn[:, None]], axis=1)
    grad_qkv = jnp.concatenate([transposed_times(normed_low, lin_all), small_grad], axis=1)
    grad_qkv = reduce_rows(grad_qkv.astype(bf16), "shard")
    output = (residual + add_all(out_pieces)).astype(bf16)
    grad_out = add_all(reduce_singles(whole_sums, whole_pending, "shard")).astype(bf16).T
    grad_down = grad_down.T.reshape(local_experts, hidden_units, -1).astype(jnp.float32)
    first_grads = pre_grads[0].astype(jnp.float32)
    lin_tokens, grad_out, output, grad_down, first_grads = lax.optimization_barrier(
        (lin_tokens, grad_out, output, grad_down, first_grads)
    )
    parts = [0.0, 0.0]
    for k, weight in enumerate((wide_half, other_half)):
        for group_index in range(seq_count):
            columns = slice(group_index * all_columns, (group_index + 1) * all_columns)
            parts[k] = parts[k] + times_transposed(lin_tokens[:, columns], weight[group_index])
    normed_grad = jnp.concatenate(
        [
            jnp.where(core_bit == 0, parts[0], parts[1]),
            jnp.where(core_bit == 0, parts[1], parts[0]),
        ],
        axis=1,
    )
    own_features = own_weight.shape[0]
    gain_own = lax.dynamic_slice_in_dim(first_gain, shard_index * own_features, own_features)
    gain_part = (
        jnp.sum(own_weight.astype(jnp.float32) * grad_qkv[:, :all_columns], axis=1) / gain_own
    )
    grad_query = grad_qkv[:, :query_width]
    grad_key = grad_qkv[:, query_width : query_width + key_width]
    grad_value = grad_qkv[:, query_width + key_width : query_width + 2 * key_width]
    small_grad = jnp.concatenate([grad_qkv[:, all_columns:], gain_part[:, None]], axis=1)
    own_small = own_features // seq_count
    small_grad = small_grad.astype(bf16).reshape(seq_count, own_small, -1)
    small_grad = jnp.pad(small_grad, ((0, 0), (0, model_width // seq_count - own_small), (0, 0)))
    last_sum = jnp.concatenate(
        [pre_sums[-1], grad_out, small_grad.reshape(model_width, -1)], axis=1
    )
    last_sum = lax.psum_scatter(last_sum, "seq", scatter_dimension=0, tiled=True)
    last_sum = last_sum.astype(jnp.float32)
    grad_out = last_sum[:, hidden_units : hidden_units + w_out.shape[1]]
    small_grad = last_sum[:own_small, hidden_units + w_out.shape[1] :]
    own_factor = rms_parts(own_inputs)
    input_part, _ = rms_backward(own_inputs, own_factor, first_gain, normed_grad)
    tokens_grad = residual_grad + input_part
    halves = [first_grads[:, :hidden_units], first_grads[:, hidden_units:]]
    halves += [part.astype(jnp.float32) for part in pre_grads[1:]] + [last_sum[:, :hidden_units]]
    grad_gate = jnp.stack(halves[0::2])
    grad_up = jnp.stack(halves[1::2])
    return (
        output,
        tokens_grad,
        grad_query,
        grad_key,
        grad_value,
        grad_out,
        small_grad[:, experts_all + 1],
        small_grad[:, experts_all],
        small_grad[:, :experts_all],
        grad_gate,
        grad_up,
        grad_down,
    )


def solution(mesh):
    return jax.shard_map(
        on_device,
        mesh=mesh,
        in_specs=(
            P(("shard", "seq"), None),
            P(("shard", "seq"), None),
            P("shard", "seq"),
            P("shard", "seq"),
            P("shard", "seq"),
            P("seq", "shard"),
            P(("shard", "seq")),
            P(("shard", "seq")),
            P(("shard", "seq"), None),
            P("shard", None, None),
            P("shard", None, None),
            P("shard", None, None),
            P(("shard", "seq"), None),
        ),
        out_specs=(
            P(("shard", "seq"), None),
            P(("shard", "seq"), None),
            P("shard", "seq"),
            P("shard", "seq"),
            P("shard", "seq"),
            P("seq", "shard"),
            P(("shard", "seq")),
            P(("shard", "seq")),
            P(("shard", "seq"), None),
            P("shard", "seq", None),
            P("shard", "seq", None),
            P("shard", None, "seq"),
        ),
        check_vma=False,
    )
```

```python
from functools import partial

import jax
import jax.numpy as jnp
from jax import lax
from jax.experimental import pallas as pl
from jax.experimental.pallas import tpu as pltpu
from jax.sharding import PartitionSpec as P

HEAD_DIMENSION = 64
CONT_LEN = 512
PROMPT_BLK = 128


norm_eps = 1e-05
negative = -1e30
rope_base = 10000.0
highest = lax.Precision.HIGHEST


def rms_norm(values, scaling):
    factor = lax.rsqrt(jnp.mean(values * values, axis=-1, keepdims=True) + norm_eps)
    return values * factor * scaling


def swiglu(gate_pre, up_pre):
    return jax.nn.silu(gate_pre) * up_pre


def rotary_tables(places, head_size):
    half_size = head_size // 2
    frequency = jnp.exp(
        jnp.arange(half_size, dtype=jnp.float32) * (-2.0 * jnp.log(rope_base) / head_size)
    )
    angles = places.astype(jnp.float32)[:, None] * frequency[None, :]
    return (jnp.cos(angles)[:, None, :], jnp.sin(angles)[:, None, :])


def rotate(values, cosine, sine, head_size):
    total_row_count = values.shape[0]
    by_head = values.reshape(total_row_count, -1, head_size)
    half_size = head_size // 2
    first_half = by_head[..., :half_size]
    second_half = by_head[..., half_size:]
    turned = jnp.concatenate(
        [first_half * cosine - second_half * sine, second_half * cosine + first_half * sine],
        axis=-1,
    )
    return turned.reshape(total_row_count, -1)


def place_of(within, block_index, prompt_len):
    return jnp.where(
        within < PROMPT_BLK,
        block_index * PROMPT_BLK + within,
        prompt_len + (within - PROMPT_BLK) % CONT_LEN,
    )


def times_transposed(left_side, right_side, precision=None):
    return lax.dot_general(
        left_side,
        right_side,
        (((1,), (1,)), ((), ())),
        precision=precision,
        preferred_element_type=jnp.float32,
    )


def transposed_times(left_side, right_side, precision=None):
    return lax.dot_general(
        left_side,
        right_side,
        (((0,), (0,)), ((), ())),
        precision=precision,
        preferred_element_type=jnp.float32,
    )


def rms_parts(values):
    return lax.rsqrt(jnp.mean(values * values, axis=-1, keepdims=True) + norm_eps)


def rms_backward(values, factor, scaling, normed_grad):
    scaled = scaling * normed_grad
    inner = jnp.mean(scaled * values, axis=-1, keepdims=True)
    values_grad = factor * scaled - values * (factor * factor * factor) * inner
    gain_grad = jnp.sum(normed_grad * values * factor, axis=0)
    return values_grad, gain_grad


def matmul(left_side, right_side):
    return jnp.dot(left_side, right_side, preferred_element_type=jnp.float32)


LANES = 128


def relane(values, source, target):
    lane = lax.broadcasted_iota(jnp.int32, values.shape, 1)
    swapped = jnp.where(source != target, pltpu.roll(values, HEAD_DIMENSION, 1), values)
    return jnp.where(lane // HEAD_DIMENSION == target, swapped, 0.0)


def head_rows(ref, first, count, source, target):
    values = ref[pl.ds(first, count), :].astype(jnp.float32)
    return relane(values, source, target).astype(jnp.bfloat16)


def nt_dot(left_side, right_side):
    return lax.dot_general(
        left_side, right_side, (((1,), (1,)), ((), ())), preferred_element_type=jnp.float32
    )


def nn_dot(left_side, right_side):
    return jnp.dot(left_side, right_side, preferred_element_type=jnp.float32)


def below_diagonal(scores):
    key_row = lax.broadcasted_iota(jnp.int32, scores.shape, 0)
    query_column = lax.broadcasted_iota(jnp.int32, scores.shape, 1)
    return jnp.where(key_row <= query_column, scores, negative)


def seen_prompt(scores, first_key, shard_index):
    key_row = lax.broadcasted_iota(jnp.int32, scores.shape, 0) + first_key
    query_column = lax.broadcasted_iota(jnp.int32, scores.shape, 1) % PROMPT_BLK
    return jnp.where(key_row <= query_column + shard_index * PROMPT_BLK, scores, negative)


def transposed(values):
    return values.astype(jnp.float32).T


QUERY_CHUNK = 512
KEY_CHUNK = 1024
FORWARD_CHUNK = 256


def attend_forward_body(
    group, kv_heads, index_ref, q_ref, kp_ref, vp_ref, ko_ref, vo_ref, mixed_ref, level_ref, vt_all, acc
):
    pair = pl.program_id(0)
    prompt_len = kp_ref.shape[0]
    block_len = ko_ref.shape[0]
    conts = (block_len - PROMPT_BLK) // CONT_LEN
    shard_index = index_ref[0]

    @pl.when(pair == 0)
    def _():
        vt_all[:, :prompt_len] = transposed(vp_ref[...]).astype(jnp.bfloat16)
        vt_all[:, prompt_len:] = transposed(vo_ref[...]).astype(jnp.bfloat16)

    acc[...] = jnp.zeros_like(acc)
    size = min(FORWARD_CHUNK, prompt_len)
    prompt_keys = [slice(first, first + size) for first in range(0, prompt_len, size)]

    def kv_half(side):
        return jnp.minimum((2 * pair + side) // group, kv_heads - 1)

    def finish(scores, value_columns):
        level = jnp.max(scores[0], axis=0, keepdims=True)
        for part in scores[1:]:
            level = jnp.maximum(level, jnp.max(part, axis=0, keepdims=True))
        total = None
        mixed = None
        for part, columns in zip(scores, value_columns):
            weights = jnp.exp(part - level)
            part_total = jnp.sum(weights, axis=0, keepdims=True)
            part_mixed = nn_dot(columns, weights.astype(jnp.bfloat16))
            total = part_total if total is None else total + part_total
            mixed = part_mixed if mixed is None else mixed + part_mixed
        return mixed / total, level + jnp.log(total)

    both = jnp.concatenate(
        [head_rows(q_ref, 0, PROMPT_BLK, side, kv_half(side)) for side in range(2)], axis=0
    )
    mixed, level = finish(
        [
            seen_prompt(nt_dot(kp_ref[keys, :], both), keys.start, shard_index)
            for keys in prompt_keys
        ],
        [vt_all[:, keys] for keys in prompt_keys],
    )
    mixed = mixed.T
    for side in range(2):
        rows = slice(side * PROMPT_BLK, (side + 1) * PROMPT_BLK)
        acc[:PROMPT_BLK, :] += relane(mixed[rows], kv_half(side), side)
        level_ref[side, :, :PROMPT_BLK] = level[:, rows]

    def step(turn, _):
        side = turn // conts
        number = turn % conts
        half = kv_half(side)
        first_own = PROMPT_BLK + number * CONT_LEN
        for chunk in range(CONT_LEN // QUERY_CHUNK):
            before = chunk * QUERY_CHUNK
            first_row = pl.multiple_of(first_own + before, PROMPT_BLK)
            queries = head_rows(q_ref, first_row, QUERY_CHUNK, side, half)
            scores = [nt_dot(kp_ref[keys, :], queries) for keys in prompt_keys]
            columns = [vt_all[:, keys] for keys in prompt_keys]
            if before:
                start = pl.multiple_of(first_own, PROMPT_BLK)
                scores.append(nt_dot(ko_ref[pl.ds(start, before), :], queries))
                columns.append(
                    vt_all[:, pl.ds(pl.multiple_of(prompt_len + start, PROMPT_BLK), before)]
                )
            scores.append(below_diagonal(nt_dot(ko_ref[pl.ds(first_row, QUERY_CHUNK), :], queries)))
            columns.append(
                vt_all[:, pl.ds(pl.multiple_of(prompt_len + first_row, PROMPT_BLK), QUERY_CHUNK)]
            )
            mixed, level = finish(scores, columns)
            acc[pl.ds(first_row, QUERY_CHUNK), :] += relane(mixed.T, half, side)
            level_ref[side, :, pl.ds(first_row, QUERY_CHUNK)] = level
        return 0

    lax.fori_loop(0, 2 * conts, step, 0)
    mixed_ref[...] = acc[...].astype(jnp.bfloat16)


def attend_backward_body(
    group,
    kv_heads,
    index_ref,
    q_ref,
    grad_ref,
    mixed_ref,
    level_ref,
    cos_ref,
    sin_ref,
    kp_ref,
    vp_ref,
    ko_ref,
    vo_ref,
    dq_ref,
    dprompt_ref,
    down_ref,
    kt_all,
    acc,
    prompt_acc,
):
    pair = pl.program_id(0)
    last = pl.num_programs(0) - 1
    prompt_len = kp_ref.shape[0]
    block_len = ko_ref.shape[0]
    conts = (block_len - PROMPT_BLK) // CONT_LEN
    shard_index = index_ref[0]
    bf16 = jnp.bfloat16

    @pl.when(pair == 0)
    def _():
        kt_all[:, :prompt_len] = transposed(kp_ref[...]).astype(bf16)
        kt_all[:, prompt_len:] = transposed(ko_ref[...]).astype(bf16)
        prompt_acc[...] = jnp.zeros_like(prompt_acc)
        down_ref[...] = jnp.zeros_like(down_ref)

    acc[...] = jnp.zeros_like(acc)

    def kv_half(side):
        return jnp.minimum((2 * pair + side) // group, kv_heads - 1)

    def inner_sums(first_row, count, side):
        rows = pl.ds(first_row, count)
        product = mixed_ref[rows, :].astype(jnp.float32) * grad_ref[rows, :].astype(jnp.float32)
        return jnp.sum(relane(product, side, side).T, axis=0, keepdims=True)

    def part(keys, values, key_columns, queries, grads, level, inner, mask, sums, first_key):
        scores = nt_dot(keys, queries)
        if mask is not None:
            scores = mask(scores)
        probs = jnp.exp(scores - level)
        score_grad = (probs * (nt_dot(values, grads) - inner)).astype(bf16)
        rows = pl.ds(first_key, keys.shape[0])
        sums[rows, :LANES] += nn_dot(score_grad, queries)
        sums[rows, LANES:] += nn_dot(probs.astype(bf16), grads)
        return nn_dot(key_columns, score_grad)

    def prompt_parts(queries, grads, level, inner, masked):
        total = None
        size = min(KEY_CHUNK, prompt_len)
        for first_key in range(0, prompt_len, size):
            rows = slice(first_key, first_key + size)
            mask = (lambda s, f=first_key: seen_prompt(s, f, shard_index)) if masked else None
            piece = part(
                kp_ref[rows, :], vp_ref[rows, :], kt_all[:, rows], queries, grads, level, inner,
                mask, prompt_acc, first_key,
            )
            total = piece if total is None else total + piece
        return total

    both_q, both_g, both_level, both_inner = [], [], [], []
    for side in range(2):
        both_q.append(head_rows(q_ref, 0, PROMPT_BLK, side, kv_half(side)))
        both_g.append(head_rows(grad_ref, 0, PROMPT_BLK, side, kv_half(side)))
        both_level.append(level_ref[side, :, :PROMPT_BLK])
        both_inner.append(inner_sums(0, PROMPT_BLK, side))
    grad_q = prompt_parts(
        jnp.concatenate(both_q, axis=0),
        jnp.concatenate(both_g, axis=0),
        jnp.concatenate(both_level, axis=1),
        jnp.concatenate(both_inner, axis=1),
        True,
    ).T
    for side in range(2):
        rows = slice(side * PROMPT_BLK, (side + 1) * PROMPT_BLK)
        acc[:PROMPT_BLK, :] += relane(grad_q[rows], kv_half(side), side)

    def step(turn, _):
        side = turn // conts
        number = turn % conts
        half = kv_half(side)
        first_own = PROMPT_BLK + number * CONT_LEN
        for chunk in range(CONT_LEN // QUERY_CHUNK):
            before = chunk * QUERY_CHUNK
            first_row = pl.multiple_of(first_own + before, PROMPT_BLK)
            queries = head_rows(q_ref, first_row, QUERY_CHUNK, side, half)
            grads = head_rows(grad_ref, first_row, QUERY_CHUNK, side, half)
            level = level_ref[side, :, pl.ds(first_row, QUERY_CHUNK)]
            inner = inner_sums(first_row, QUERY_CHUNK, side)
            grad_q = prompt_parts(queries, grads, level, inner, False)
            own = [(first_row, QUERY_CHUNK, below_diagonal)]
            if before:
                own.append((pl.multiple_of(first_own, PROMPT_BLK), before, None))
            for start, size, mask in own:
                rows = pl.ds(start, size)
                columns = pl.ds(pl.multiple_of(prompt_len + start, PROMPT_BLK), size)
                grad_q += part(
                    ko_ref[rows, :], vo_ref[rows, :], kt_all[:, columns], queries, grads, level,
                    inner, mask, down_ref, start,
                )
            acc[pl.ds(first_row, QUERY_CHUNK), :] += relane(grad_q.T, half, side)
        return 0

    lax.fori_loop(0, 2 * conts, step, 0)
    grads = acc[...] * HEAD_DIMENSION ** (-0.5)
    half = HEAD_DIMENSION // 2
    lane = lax.broadcasted_iota(jnp.int32, grads.shape, 1)
    swapped = jnp.where(
        lane % HEAD_DIMENSION < half,
        pltpu.roll(grads, LANES - half, 1),
        pltpu.roll(grads, half, 1),
    )
    dq_ref[...] = (grads * cos_ref[...] + swapped * sin_ref[...]).astype(bf16)

    @pl.when(pair == last)
    def _():
        dprompt_ref[...] = prompt_acc[...].astype(bf16)


def pair_specs(block_len, prompt_len):
    by_pair = pl.BlockSpec((block_len, LANES), lambda b, i: (0, b))
    levels = pl.BlockSpec((2, 1, block_len), lambda b, i: (b, 0, 0))
    sources = [
        pl.BlockSpec((prompt_len, LANES), lambda b, i: (0, 0)),
        pl.BlockSpec((prompt_len, LANES), lambda b, i: (0, 1)),
        pl.BlockSpec((block_len, LANES), lambda b, i: (0, 0)),
        pl.BlockSpec((block_len, LANES), lambda b, i: (0, 1)),
    ]
    return by_pair, levels, sources


def attention_cost(block_len, prompt_len, width, products):
    pairs = (block_len * prompt_len + block_len * CONT_LEN // 2) * (width // HEAD_DIMENSION)
    return pl.CostEstimate(
        flops=products * 2 * pairs * 2 * LANES,
        bytes_accessed=8 * block_len * width,
        transcendentals=pairs,
    )


def attend_forward(index, queries, kv_prompt, kv_own, group, kv_heads):
    block_len, width = queries.shape
    prompt_len = kv_prompt.shape[0]
    by_pair, levels, sources = pair_specs(block_len, prompt_len)
    return pl.pallas_call(
        partial(attend_forward_body, group, kv_heads),
        out_shape=[
            jax.ShapeDtypeStruct((block_len, width), jnp.bfloat16),
            jax.ShapeDtypeStruct((width // HEAD_DIMENSION, 1, block_len), jnp.float32),
        ],
        grid_spec=pltpu.PrefetchScalarGridSpec(
            num_scalar_prefetch=1,
            grid=(width // LANES,),
            in_specs=[by_pair] + sources,
            out_specs=[by_pair, levels],
            scratch_shapes=[
                pltpu.VMEM((LANES, prompt_len + block_len), jnp.bfloat16),
                pltpu.VMEM((block_len, LANES), jnp.float32),
            ],
        ),
        compiler_params=pltpu.CompilerParams(
            dimension_semantics=("arbitrary",), vmem_limit_bytes=56 * 1024 * 1024
        ),
        cost_estimate=attention_cost(block_len, prompt_len, width, 2),
        name="attend_forward",
    )(index, queries, kv_prompt, kv_prompt, kv_own, kv_own)


def attend_backward(
    index, queries, grads, mixed, level, tables, kv_prompt, kv_own, group, kv_heads
):
    block_len, width = queries.shape
    prompt_len = kv_prompt.shape[0]
    by_pair, levels, sources = pair_specs(block_len, prompt_len)
    return pl.pallas_call(
        partial(attend_backward_body, group, kv_heads),
        out_shape=[
            jax.ShapeDtypeStruct((block_len, width), jnp.bfloat16),
            jax.ShapeDtypeStruct((prompt_len, 2 * LANES), jnp.bfloat16),
            jax.ShapeDtypeStruct((block_len, 2 * LANES), jnp.float32),
        ],
        grid_spec=pltpu.PrefetchScalarGridSpec(
            num_scalar_prefetch=1,
            grid=(width // LANES,),
            in_specs=[by_pair, by_pair, by_pair, levels]
            + [pl.BlockSpec((block_len, LANES), lambda b, i: (0, 0))] * 2
            + sources,
            out_specs=[
                by_pair,
                pl.BlockSpec((prompt_len, 2 * LANES), lambda b, i: (0, 0)),
                pl.BlockSpec((block_len, 2 * LANES), lambda b, i: (0, 0)),
            ],
            scratch_shapes=[
                pltpu.VMEM((LANES, prompt_len + block_len), jnp.bfloat16),
                pltpu.VMEM((block_len, LANES), jnp.float32),
                pltpu.VMEM((prompt_len, 2 * LANES), jnp.float32),
            ],
        ),
        compiler_params=pltpu.CompilerParams(
            dimension_semantics=("arbitrary",), vmem_limit_bytes=56 * 1024 * 1024
        ),
        cost_estimate=attention_cost(block_len, prompt_len, width, 5),
        name="attend_backward",
    )(index, queries, grads, mixed, level, *tables, kv_prompt, kv_prompt, kv_own, kv_own)


def to_lanes(values):
    extra = -values.shape[1] % LANES
    return jnp.pad(values, ((0, 0), (0, extra))) if extra else values


def exchange(values, axis_name, bit):
    count = lax.axis_size(axis_name)
    return lax.ppermute(values, axis_name, [(i, i ^ bit) for i in range(count)])


def bits_of(number):
    return [1 << k for k in range(number.bit_length()) if number >> k & 1]


def even_blocks(count):
    even = sorted(range(2, count, 2), key=lambda j: (len(bits_of(j)), j))
    singles = [j for j in even if len(bits_of(j)) == 1]
    return singles, even[len(singles) :]


def gather_blocks(own, axis_name, after_first=None):
    count = lax.axis_size(axis_name)
    singles, several = even_blocks(count)
    blocks = {0: own, 1: exchange(own, axis_name, 1)}
    for j in singles:
        blocks[j] = exchange(own, axis_name, j)
    if after_first is not None:
        blocks.update(zip(singles, after_first([blocks[j] for j in singles])))
    for j in several:
        low_bit = bits_of(j)[0]
        blocks[j] = exchange(blocks[j ^ low_bit], axis_name, low_bit)
    for j in singles + several:
        blocks[j + 1] = exchange(blocks[j], axis_name, 1)
    return [blocks[j] for j in range(count)]


def add_rounded(left_side, right_side):
    return (left_side.astype(jnp.float32) + right_side.astype(jnp.float32)).astype(jnp.bfloat16)


def reduce_several(sums, axis_name):
    sums = dict(sums)
    pending = []
    for j in sorted((j for j in sums if len(bits_of(j)) > 1), key=lambda j: (-len(bits_of(j)), j)):
        bit = bits_of(j)[-1]
        piece = exchange(sums[j], axis_name, bit)
        if len(bits_of(j ^ bit)) > 1:
            sums[j ^ bit] = add_rounded(sums[j ^ bit], piece)
        else:
            pending.append((j ^ bit, piece))
    return pending


def reduce_singles(sums, pending, axis_name):
    sums = dict(sums)
    for j, piece in pending:
        sums[j] = add_rounded(sums[j], piece)
    return [sums[0]] + [exchange(sums[j], axis_name, j) for j in sums if len(bits_of(j)) == 1]


def add_all(pieces):
    total = pieces[0].astype(jnp.float32)
    for piece in pieces[1:]:
        total = total + piece.astype(jnp.float32)
    return total


def halves_by_core(values, axis_name):
    count = lax.axis_size(axis_name)
    parity = lax.axis_index(axis_name) % 2
    paired = values.reshape(count // 2, 2, values.shape[0] // count, values.shape[1])
    keep = lax.dynamic_index_in_dim(paired, parity, 1, keepdims=False)
    give = lax.dynamic_index_in_dim(paired, 1 - parity, 1, keepdims=False)
    return keep, give


def chip_sums(keep, arrived, axis_name):
    index = lax.axis_index(axis_name)
    total = add_rounded(keep, arrived)
    return {
        2 * k: lax.dynamic_index_in_dim(total, (index // 2) ^ k, 0, keepdims=False)
        for k in range(total.shape[0])
    }


def reduce_rows(values, axis_name):
    keep, give = halves_by_core(values, axis_name)
    sums = chip_sums(keep, exchange(give, axis_name, 1), axis_name)
    return add_all(reduce_singles(sums, reduce_several(sums, axis_name), axis_name))


def in_order(blocks, index):
    stacked = jnp.stack(blocks)
    return jnp.concatenate(
        [lax.dynamic_index_in_dim(stacked, j ^ index, 0, keepdims=True) for j in range(len(blocks))],
        axis=0,
    )


def expert_body(
    experts_all, index_ref, x_even, x_odd, og_even, og_odd, gate_w, up_w, down_w, *rest
):
    (x_all, og_all, pre_all, hid_all, row_even, row_odd, out_even, out_odd) = rest[-12:-4]
    (row_acc, out_acc, back_acc, _) = rest[-4:]
    expert = pl.program_id(0)
    last = pl.num_programs(0) - 1
    rows = x_even.shape[0]
    width = x_all.shape[1]
    hidden_units = gate_w.shape[2]
    nt_dims = (((1,), (1,)), ((), ()))

    @pl.when(expert == 0)
    def _():
        x_all[:rows, :] = x_even[:, :width]
        x_all[rows:, :] = x_odd[:, :width]
        og_all[:rows, :] = og_even[...]
        og_all[rows:, :] = og_odd[...]

    column = index_ref[0] + expert
    lane = lax.broadcasted_iota(jnp.int32, (2 * rows, LANES), 1)
    coded = jnp.concatenate([x_even[:, width:], x_odd[:, width:]], axis=0).astype(jnp.float32)
    gate = jnp.sum(
        jnp.where((lane == column) | (lane == column + experts_all), coded, 0.0),
        axis=1,
        keepdims=True,
    )
    x_rows = x_all[...]
    og_rows = og_all[...]
    gate_pre = jnp.dot(x_rows, gate_w[0], preferred_element_type=jnp.float32)
    up_pre = jnp.dot(x_rows, up_w[0], preferred_element_type=jnp.float32)
    down_grad = lax.dot_general(og_rows, down_w[0], nt_dims, preferred_element_type=jnp.float32)
    sigmoid = 1.0 / (1.0 + jnp.exp(-gate_pre))
    silu = gate_pre * sigmoid
    hidden = silu * up_pre
    gate_back = jnp.sum(hidden * down_grad, axis=1, keepdims=True)
    hidden_low = (gate * hidden).astype(jnp.bfloat16)
    hidden_grad = gate * down_grad
    gate_pre_low = (
        hidden_grad * up_pre * sigmoid * (1.0 + gate_pre * (1.0 - sigmoid))
    ).astype(jnp.bfloat16)
    up_pre_low = (hidden_grad * silu).astype(jnp.bfloat16)
    hid_all[...] = hidden_low
    pre_all[0, :, :hidden_units] = gate_pre_low
    pre_all[0, :, hidden_units:] = up_pre_low
    row = lax.dot_general(
        gate_pre_low, gate_w[0], nt_dims, preferred_element_type=jnp.float32
    ) + lax.dot_general(up_pre_low, up_w[0], nt_dims, preferred_element_type=jnp.float32)
    out = jnp.dot(hidden_low, down_w[0], preferred_element_type=jnp.float32)
    high = gate_back.astype(jnp.bfloat16).astype(jnp.float32)
    back = jnp.where(lane == column, high, 0.0) + jnp.where(
        lane == column + experts_all, gate_back - high, 0.0
    )

    @pl.when(expert == 0)
    def _():
        row_acc[...] = row
        out_acc[...] = out
        back_acc[...] = back

    @pl.when(expert > 0)
    def _():
        row_acc[...] += row
        out_acc[...] += out
        back_acc[...] += back

    @pl.when(expert == last)
    def _():
        for ref, first in ((row_even, 0), (row_odd, rows)):
            ref[:, :width] = row_acc[first : first + rows, :].astype(jnp.bfloat16)
            ref[:, width:] = back_acc[first : first + rows, :].astype(jnp.bfloat16)
        out_even[...] = out_acc[:rows, :].astype(jnp.bfloat16)
        out_odd[...] = out_acc[rows:, :].astype(jnp.bfloat16)


def expert_pair(position, pairs, first_expert, experts_all, x_pair, og_pair, weights, carried):
    w_gate, w_up, w_down = weights
    rows, coded_width = x_pair[0].shape
    width = coded_width - LANES
    local_experts, _, hidden_units = w_gate.shape
    bf16 = jnp.bfloat16
    whole = 2 * rows
    fixed = lambda e, i: (0, 0)
    once = pl.Buffered(1)
    in_specs = (
        [pl.BlockSpec((rows, coded_width), fixed, pipeline_mode=once)] * 2
        + [pl.BlockSpec((rows, width), fixed, pipeline_mode=once)] * 2
        + [pl.BlockSpec((1, width, hidden_units), lambda e, i: (e, 0, 0))] * 2
        + [pl.BlockSpec((1, hidden_units, width), lambda e, i: (e, 0, 0))]
    )
    operands = [*x_pair, *og_pair, w_gate, w_up, w_down]
    aliases = {}
    if carried is not None:
        in_specs = in_specs + [pl.BlockSpec(memory_space=pl.ANY)] * 4
        aliases = {1 + len(operands) + k: k for k in range(4)}
        operands = operands + list(carried)
    out_shape = [
        jax.ShapeDtypeStruct((pairs * whole, width), bf16),
        jax.ShapeDtypeStruct((pairs * whole, width), bf16),
        jax.ShapeDtypeStruct((local_experts, pairs * whole, 2 * hidden_units), bf16),
        jax.ShapeDtypeStruct((pairs * whole, local_experts * hidden_units), bf16),
        jax.ShapeDtypeStruct((rows, coded_width), bf16),
        jax.ShapeDtypeStruct((rows, coded_width), bf16),
        jax.ShapeDtypeStruct((rows, width), bf16),
        jax.ShapeDtypeStruct((rows, width), bf16),
    ]
    out_specs = [
        pl.BlockSpec((whole, width), lambda e, i: (position, 0)),
        pl.BlockSpec((whole, width), lambda e, i: (position, 0)),
        pl.BlockSpec((1, whole, 2 * hidden_units), lambda e, i: (e, position, 0)),
        pl.BlockSpec((whole, hidden_units), lambda e, i: (position, e)),
        pl.BlockSpec((rows, coded_width), fixed),
        pl.BlockSpec((rows, coded_width), fixed),
        pl.BlockSpec((rows, width), fixed),
        pl.BlockSpec((rows, width), fixed),
    ]
    products = 2 * whole * width * hidden_units * local_experts
    results = pl.pallas_call(
        partial(expert_body, experts_all),
        out_shape=out_shape,
        grid_spec=pltpu.PrefetchScalarGridSpec(
            num_scalar_prefetch=1,
            grid=(local_experts,),
            in_specs=in_specs,
            out_specs=out_specs,
            scratch_shapes=[
                pltpu.VMEM((whole, width), jnp.float32),
                pltpu.VMEM((whole, width), jnp.float32),
                pltpu.VMEM((whole, LANES), jnp.float32),
                pltpu.VMEM((8, LANES), jnp.float32),
            ],
        ),
        input_output_aliases=aliases,
        compiler_params=pltpu.CompilerParams(
            dimension_semantics=("arbitrary",), vmem_limit_bytes=60 * 1024 * 1024
        ),
        cost_estimate=pl.CostEstimate(
            flops=6 * products,
            bytes_accessed=3 * 2 * local_experts * width * hidden_units + 20 * whole * width,
            transcendentals=whole * hidden_units * local_experts,
        ),
        name="experts",
    )(first_expert, *operands)
    return results[:4], results[4:]


def on_device(
    tokens,
    routes,
    w_query,
    key_projection,
    value_projection,
    w_out,
    gain_attn,
    gain_ffn,
    w_router,
    w_gate,
    w_up,
    w_down,
    out_grad,
):
    bf16 = jnp.bfloat16
    shard_count = lax.axis_size("shard")
    seq_count = lax.axis_size("seq")
    shard_index = lax.axis_index("shard")
    seq_index = lax.axis_index("seq")
    tok_count, model_width = tokens.shape
    top_count = routes.shape[1]
    experts_all = w_router.shape[1]
    local_experts = w_gate.shape[0]
    block_len = tok_count * seq_count
    prompt_len = PROMPT_BLK * shard_count
    query_width = w_query.shape[1]
    key_width = key_projection.shape[1]

    singles, several = even_blocks(shard_count)
    small = jnp.concatenate([w_router, gain_attn[:, None], gain_ffn[:, None]], axis=1)
    small = lax.all_gather(small, "seq", axis=0, tiled=True)
    small = lax.all_gather(small, "shard", axis=0, tiled=True)
    router_weight = small[:, :experts_all]
    first_gain = small[:, experts_all].astype(jnp.float32)
    second_gain = small[:, experts_all + 1].astype(jnp.float32)
    block_tokens = lax.all_gather(tokens, "seq", axis=0, tiled=True)
    own_weight = jnp.concatenate([w_query, key_projection, value_projection], axis=1)
    grad_blocks = {0: out_grad}
    near = [exchange(out_grad, "shard", bit) for bit in singles]

    def with_near(blocks):
        blocks, near[:] = lax.optimization_barrier((blocks, near))
        return blocks

    weight_blocks = gather_blocks(own_weight, "shard", with_near)
    grad_blocks.update(zip(singles, near))
    for j in [0] + singles:
        grad_blocks[j + 1] = exchange(grad_blocks[j], "shard", 1)
    out_weight = lax.all_gather(w_out, "seq", axis=0, tiled=True)
    qkv_weight = in_order(weight_blocks, shard_index).reshape(model_width, -1)

    block_rows = jnp.arange(block_len, dtype=jnp.int32)
    cos_table, sin_table = rotary_tables(
        place_of(block_rows, shard_index, prompt_len), HEAD_DIMENSION
    )
    inputs = block_tokens.astype(jnp.float32)
    first_factor = rms_parts(inputs)
    normed_low = (inputs * first_factor * first_gain).astype(bf16)
    lin = matmul(normed_low, qkv_weight)
    kv_heads = key_width // HEAD_DIMENSION
    group = query_width // key_width
    queries = rotate(lin[:, :query_width], cos_table, sin_table, HEAD_DIMENSION)
    queries = to_lanes((queries * HEAD_DIMENSION ** (-0.5)).astype(bf16))
    key_heads = rotate(
        lin[:, query_width : query_width + key_width], cos_table, sin_table, HEAD_DIMENSION
    ).astype(bf16)
    value_heads = lin[:, query_width + key_width :].astype(bf16)
    kv_own = jnp.concatenate([to_lanes(key_heads), to_lanes(value_heads)], axis=1)
    kv_prompt = lax.all_gather(kv_own[:PROMPT_BLK], "shard", axis=0, tiled=True)
    kv_prompt, out_weight, near = lax.optimization_barrier(
        (kv_prompt, out_weight, [grad_blocks[bit] for bit in singles])
    )
    grad_blocks.update(zip(singles, near))
    out_weight = lax.all_gather(out_weight, "shard", axis=1, tiled=True)
    for j in several:
        low_bit = bits_of(j)[0]
        grad_blocks[j] = exchange(grad_blocks[j ^ low_bit], "shard", low_bit)
    block_number = shard_index.astype(jnp.int32).reshape(1)
    mixed_own, levels = attend_forward(block_number, queries, kv_prompt, kv_own, group, kv_heads)
    sooner = [j for j in range(1, shard_count) if j - 1 not in several]
    mixed_own, held_blocks = lax.optimization_barrier((mixed_own, [grad_blocks[j] for j in sooner]))
    for j, block in zip(sooner, held_blocks):
        grad_blocks[j] = block
    for j in several:
        grad_blocks[j + 1] = exchange(grad_blocks[j], "shard", 1)
    mixed_heads = mixed_own[:, :query_width]
    mixed_tokens = lax.all_to_all(mixed_heads, "seq", split_axis=0, concat_axis=1, tiled=True)

    half_features = model_width // 2
    core_bit = shard_index % 2
    half_weight, mixed_tokens = lax.optimization_barrier(
        (
            lax.dynamic_slice_in_dim(qkv_weight, core_bit * half_features, half_features, axis=0),
            mixed_tokens,
        )
    )
    wide_half = lax.all_gather(half_weight, "seq", axis=0, tiled=False)

    own_inputs = tokens.astype(jnp.float32)
    upstream = out_grad.astype(jnp.float32)
    residual = own_inputs + matmul(mixed_tokens, out_weight)
    second_factor = rms_parts(residual)
    second_low = (residual * second_factor * second_gain).astype(bf16)
    logits = matmul(second_low, router_weight)
    chosen = routes[:, :, None] == jnp.arange(experts_all, dtype=jnp.int32)[None, None, :]
    named = jnp.any(chosen, axis=1)
    gate_dense = jax.nn.softmax(jnp.where(named, logits, negative), axis=-1)
    gate_dense = jnp.where(named, gate_dense, 0.0)

    gate_high = lax.reduce_precision(gate_dense, 8, 7)
    coded = jnp.concatenate(
        [
            second_low,
            gate_high.astype(bf16),
            (gate_dense - gate_high).astype(bf16),
            jnp.zeros((tok_count, LANES - 2 * experts_all), bf16),
        ],
        axis=1,
    )
    row_blocks = {0: coded, 1: exchange(coded, "shard", 1)}
    for bit in singles:
        row_blocks[bit] = exchange(coded, "shard", bit)
    order = [0] + singles[:-1] + several + singles[-1:]
    first_expert = (shard_index * local_experts).astype(jnp.int32).reshape(1)
    carried = None
    pending = []
    row_sums = {}
    out_parts = [None] * shard_count
    for position, j in enumerate(order):
        row_pair = [row_blocks[j], row_blocks[j + 1]]
        if j == order[-1]:
            row_pair, row_sums = lax.optimization_barrier((row_pair, row_sums))
            pending = reduce_several(row_sums, "shard")
        carried, pieces = expert_pair(
            position,
            len(order),
            first_expert,
            experts_all,
            row_pair,
            [grad_blocks[j], grad_blocks[j + 1]],
            (w_gate, w_up, w_down),
            carried,
        )
        if position == 0:
            arrived, pieces = lax.optimization_barrier(
                ([row_blocks[bit] for bit in singles], pieces)
            )
            row_blocks.update(zip(singles, arrived))
            for bit in singles:
                row_blocks[bit + 1] = exchange(row_blocks[bit], "shard", 1)
            for k in several:
                low_bit = bits_of(k)[0]
                row_blocks[k] = exchange(row_blocks[k ^ low_bit], "shard", low_bit)
        elif position == 1:
            arrived, pieces = lax.optimization_barrier(([row_blocks[k] for k in several], pieces))
            row_blocks.update(zip(several, arrived))
            for k in several:
                row_blocks[k + 1] = exchange(row_blocks[k], "shard", 1)
        elif j == order[-1]:
            arrived, pieces, carried = lax.optimization_barrier(
                ([piece for _, piece in pending], pieces, carried)
            )
            pending = [(k, piece) for (k, _), piece in zip(pending, arrived)]
        arrived = exchange(pieces[1], "shard", 1)
        if j != order[-1]:
            row_sums[j] = add_rounded(pieces[0], arrived)
        out_parts[j], out_parts[j + 1] = pieces[2], pieces[3]
    carried, wide_half = lax.optimization_barrier((carried, wide_half))
    all_rows, all_grads, all_pre, all_hidden = carried
    down_sum = transposed_times(all_grads, all_hidden).astype(bf16)
    grad_down = lax.psum_scatter(down_sum, "seq", scatter_dimension=0, tiled=True)
    all_rows, arrived, down_sum = lax.optimization_barrier((all_rows, arrived, down_sum))
    row_sums[order[-1]] = add_rounded(pieces[0], arrived)
    pre_sums = [transposed_times(all_rows, all_pre[0]).astype(bf16)]
    pre_grads = [lax.psum_scatter(pre_sums[0], "seq", scatter_dimension=0, tiled=True)]
    row_pieces = reduce_singles(row_sums, pending, "shard")
    row_pieces, pre_sums[0] = lax.optimization_barrier((row_pieces, pre_sums[0]))
    row_total = add_all(row_pieces)
    row_grad = row_total[:, :model_width]
    gate_grad_dense = (
        row_total[:, model_width : model_width + experts_all]
        + row_total[:, model_width + experts_all : model_width + 2 * experts_all]
    )
    weighted = gate_dense * gate_grad_dense
    logit_grad = weighted - gate_dense * jnp.sum(weighted, axis=-1, keepdims=True)
    second_grad = row_grad + times_transposed(
        logit_grad, router_weight.astype(jnp.float32), highest
    )
    residual_part, grad_gain_ffn = rms_backward(residual, second_factor, second_gain, second_grad)
    residual_grad = upstream + residual_part
    residual_low = residual_grad.astype(bf16)
    mixed_grad_tokens = times_transposed(residual_low, out_weight).astype(bf16)
    other_half = exchange(wide_half, "shard", 1)
    mixed_grad_tokens, out_parts, all_rows, other_half, mixed_late = lax.optimization_barrier(
        (mixed_grad_tokens, out_parts, all_rows, other_half, mixed_tokens)
    )
    mixed_grad = lax.all_to_all(mixed_grad_tokens, "seq", split_axis=1, concat_axis=0, tiled=True)
    odd = [exchange(out_parts[j + 1], "shard", 1) for j in order]
    pre_sums += [
        transposed_times(all_rows, all_pre[e]).astype(bf16) for e in range(1, local_experts)
    ]
    pre_grads += [
        lax.psum_scatter(part, "seq", scatter_dimension=0, tiled=True) for part in pre_sums[1:]
    ]
    odd, pre_sums = lax.optimization_barrier((odd, pre_sums))
    odd = dict(zip(order, odd))
    out_sums = {j: add_rounded(out_parts[j], odd[j]) for j in several}
    whole_out = transposed_times(residual_low, mixed_late).astype(bf16)
    whole_keep, whole_give = halves_by_core(whole_out, "shard")
    whole_arrived = exchange(whole_give, "shard", 1)
    mixed_grad, pre_sums, out_sums, whole_arrived, odd = lax.optimization_barrier(
        (mixed_grad, pre_sums, out_sums, whole_arrived, odd)
    )
    out_pending = reduce_several(out_sums, "shard")
    whole_sums = chip_sums(whole_keep, whole_arrived, "shard")
    whole_pending = reduce_several(whole_sums, "shard")

    query_grad, prompt_grad, self_grad = attend_backward(
        block_number,
        queries,
        to_lanes(mixed_grad),
        mixed_own,
        levels,
        [
            jnp.tile(cos_table[:, 0, :], (1, LANES // cos_table.shape[2])),
            jnp.tile(
                jnp.concatenate([sin_table, -sin_table], axis=2)[:, 0, :],
                (1, LANES // HEAD_DIMENSION),
            ),
        ],
        kv_prompt,
        kv_own,
        group,
        kv_heads,
    )
    query_grad, prompt_grad, self_grad, arrived, out_arrived = lax.optimization_barrier(
        (
            query_grad,
            prompt_grad,
            self_grad,
            [piece for _, piece in whole_pending],
            [piece for _, piece in out_pending],
        )
    )
    whole_pending = [(j, piece) for (j, _), piece in zip(whole_pending, arrived)]
    out_pending = [(j, piece) for (j, _), piece in zip(out_pending, out_arrived)]
    lin_query = query_grad[:, :query_width]
    own_prompt = reduce_rows(prompt_grad, "shard")
    key_grad = jnp.concatenate(
        [own_prompt[:, :key_width], self_grad[PROMPT_BLK:, :key_width]], axis=0
    )
    value_low = jnp.concatenate(
        [own_prompt[:, LANES : LANES + key_width], self_grad[PROMPT_BLK:, LANES : LANES + key_width]],
        axis=0,
    ).astype(bf16)
    lin_key = rotate(key_grad, cos_table, -sin_table, HEAD_DIMENSION).astype(bf16)
    lin_all = jnp.concatenate([lin_query, lin_key, value_low], axis=1)
    all_columns = lin_all.shape[1]
    lin_all, whole_sums = lax.optimization_barrier((lin_all, whole_sums))
    lin_tokens = lax.all_to_all(lin_all, "seq", split_axis=0, concat_axis=1, tiled=True)

    keep, give = halves_by_core(transposed_times(normed_low, lin_all).astype(bf16), "shard")
    arrived, odd, logit_grad = lax.optimization_barrier(
        (exchange(give, "shard", 1), odd, logit_grad)
    )
    qkv_sums = chip_sums(keep, arrived, "shard")
    grad_qkv = add_all(reduce_singles(qkv_sums, reduce_several(qkv_sums, "shard"), "shard"))
    grad_router = transposed_times(second_low.astype(jnp.float32), logit_grad, highest)
    small_grad = jnp.concatenate([grad_router, grad_gain_ffn[:, None]], axis=1)
    small_grad = reduce_rows(small_grad.astype(bf16), "shard")
    for j in [0] + singles:
        out_sums[j] = add_rounded(out_parts[j], odd[j])
    out_sums = {j: out_sums[j] for j in [0] + singles}
    output = (residual + add_all(reduce_singles(out_sums, out_pending, "shard"))).astype(bf16)
    grad_out = add_all(reduce_singles(whole_sums, whole_pending, "shard")).astype(bf16).T
    hidden_units = w_gate.shape[2]
    lin_tokens, grad_down, pre_grads[0] = lax.optimization_barrier(
        (lin_tokens, grad_down, pre_grads[0])
    )
    grad_down = grad_down.T.reshape(local_experts, hidden_units, -1).astype(jnp.float32)
    parts = [0.0, 0.0]
    for k, weight in enumerate((wide_half, other_half)):
        for group_index in range(seq_count):
            columns = slice(group_index * all_columns, (group_index + 1) * all_columns)
            parts[k] = parts[k] + times_transposed(lin_tokens[:, columns], weight[group_index])
    normed_grad = jnp.concatenate(
        [
            jnp.where(core_bit == 0, parts[0], parts[1]),
            jnp.where(core_bit == 0, parts[1], parts[0]),
        ],
        axis=1,
    )
    own_features = own_weight.shape[0]
    gain_own = lax.dynamic_slice_in_dim(first_gain, shard_index * own_features, own_features)
    gain_part = (
        jnp.sum(own_weight.astype(jnp.float32) * grad_qkv[:, :all_columns], axis=1) / gain_own
    )
    grad_query = grad_qkv[:, :query_width]
    grad_key = grad_qkv[:, query_width : query_width + key_width]
    grad_value = grad_qkv[:, query_width + key_width : query_width + 2 * key_width]
    small_grad = jnp.concatenate([small_grad, gain_part[:, None]], axis=1)
    own_small = own_features // seq_count
    small_grad = small_grad.astype(bf16).reshape(seq_count, own_small, -1)
    small_grad = jnp.pad(small_grad, ((0, 0), (0, model_width // seq_count - own_small), (0, 0)))
    last_sum = jnp.concatenate([grad_out, small_grad.reshape(model_width, -1)], axis=1)
    last_sum = lax.psum_scatter(last_sum, "seq", scatter_dimension=0, tiled=True)
    last_sum = last_sum.astype(jnp.float32)
    grad_out = last_sum[:, : w_out.shape[1]]
    small_grad = last_sum[:own_small, w_out.shape[1] :]
    own_factor = rms_parts(own_inputs)
    input_part, _ = rms_backward(own_inputs, own_factor, first_gain, normed_grad)
    tokens_grad = residual_grad + input_part
    pre_grads = [part.astype(jnp.float32) for part in pre_grads]
    grad_gate = jnp.stack([part[:, :hidden_units] for part in pre_grads])
    grad_up = jnp.stack([part[:, hidden_units:] for part in pre_grads])
    return (
        output,
        tokens_grad,
        grad_query,
        grad_key,
        grad_value,
        grad_out,
        small_grad[:, experts_all + 1],
        small_grad[:, experts_all],
        small_grad[:, :experts_all],
        grad_gate,
        grad_up,
        grad_down,
    )


def solution(mesh):
    return jax.shard_map(
        on_device,
        mesh=mesh,
        in_specs=(
            P(("shard", "seq"), None),
            P(("shard", "seq"), None),
            P("shard", "seq"),
            P("shard", "seq"),
            P("shard", "seq"),
            P("seq", "shard"),
            P(("shard", "seq")),
            P(("shard", "seq")),
            P(("shard", "seq"), None),
            P("shard", None, None),
            P("shard", None, None),
            P("shard", None, None),
            P(("shard", "seq"), None),
        ),
        out_specs=(
            P(("shard", "seq"), None),
            P(("shard", "seq"), None),
            P("shard", "seq"),
            P("shard", "seq"),
            P("shard", "seq"),
            P("seq", "shard"),
            P(("shard", "seq")),
            P(("shard", "seq")),
            P(("shard", "seq"), None),
            P("shard", "seq", None),
            P("shard", "seq", None),
            P("shard", None, "seq"),
        ),
        check_vma=False,
    )
```

```python
from functools import partial

import jax
import jax.numpy as jnp
from jax import lax
from jax.experimental import pallas as pl
from jax.experimental.pallas import tpu as pltpu
from jax.sharding import PartitionSpec as P

HEAD_DIMENSION = 64
CONT_LEN = 512
PROMPT_BLK = 128


norm_eps = 1e-05
negative = -1e30
rope_base = 10000.0
highest = lax.Precision.HIGHEST


def rms_norm(values, scaling):
    factor = lax.rsqrt(jnp.mean(values * values, axis=-1, keepdims=True) + norm_eps)
    return values * factor * scaling


def swiglu(gate_pre, up_pre):
    return jax.nn.silu(gate_pre) * up_pre


def rotary_tables(places, head_size):
    half_size = head_size // 2
    frequency = jnp.exp(
        jnp.arange(half_size, dtype=jnp.float32) * (-2.0 * jnp.log(rope_base) / head_size)
    )
    angles = places.astype(jnp.float32)[:, None] * frequency[None, :]
    return (jnp.cos(angles)[:, None, :], jnp.sin(angles)[:, None, :])


def rotate(values, cosine, sine, head_size):
    total_row_count = values.shape[0]
    by_head = values.reshape(total_row_count, -1, head_size)
    half_size = head_size // 2
    first_half = by_head[..., :half_size]
    second_half = by_head[..., half_size:]
    turned = jnp.concatenate(
        [first_half * cosine - second_half * sine, second_half * cosine + first_half * sine],
        axis=-1,
    )
    return turned.reshape(total_row_count, -1)


def place_of(within, block_index, prompt_len):
    return jnp.where(
        within < PROMPT_BLK,
        block_index * PROMPT_BLK + within,
        prompt_len + (within - PROMPT_BLK) % CONT_LEN,
    )


def times_transposed(left_side, right_side, precision=None):
    return lax.dot_general(
        left_side,
        right_side,
        (((1,), (1,)), ((), ())),
        precision=precision,
        preferred_element_type=jnp.float32,
    )


def transposed_times(left_side, right_side, precision=None):
    return lax.dot_general(
        left_side,
        right_side,
        (((0,), (0,)), ((), ())),
        precision=precision,
        preferred_element_type=jnp.float32,
    )


def rms_parts(values):
    return lax.rsqrt(jnp.mean(values * values, axis=-1, keepdims=True) + norm_eps)


def rms_backward(values, factor, scaling, normed_grad):
    scaled = scaling * normed_grad
    inner = jnp.mean(scaled * values, axis=-1, keepdims=True)
    values_grad = factor * scaled - values * (factor * factor * factor) * inner
    gain_grad = jnp.sum(normed_grad * values * factor, axis=0)
    return values_grad, gain_grad


def matmul(left_side, right_side):
    return jnp.dot(left_side, right_side, preferred_element_type=jnp.float32)


LANES = 128


def relane(values, source, target):
    lane = lax.broadcasted_iota(jnp.int32, values.shape, 1)
    swapped = jnp.where(source != target, pltpu.roll(values, HEAD_DIMENSION, 1), values)
    return jnp.where(lane // HEAD_DIMENSION == target, swapped, 0.0)


def head_rows(ref, first, count, source, target):
    values = ref[pl.ds(first, count), :].astype(jnp.float32)
    return relane(values, source, target).astype(jnp.bfloat16)


def nt_dot(left_side, right_side):
    return lax.dot_general(
        left_side, right_side, (((1,), (1,)), ((), ())), preferred_element_type=jnp.float32
    )


def nn_dot(left_side, right_side):
    return jnp.dot(left_side, right_side, preferred_element_type=jnp.float32)


def below_diagonal(scores):
    key_row = lax.broadcasted_iota(jnp.int32, scores.shape, 0)
    query_column = lax.broadcasted_iota(jnp.int32, scores.shape, 1)
    return jnp.where(key_row <= query_column, scores, negative)


def seen_prompt(scores, first_key, shard_index):
    key_row = lax.broadcasted_iota(jnp.int32, scores.shape, 0) + first_key
    query_column = lax.broadcasted_iota(jnp.int32, scores.shape, 1) % PROMPT_BLK
    return jnp.where(key_row <= query_column + shard_index * PROMPT_BLK, scores, negative)


def transposed(values):
    return values.astype(jnp.float32).T


QUERY_CHUNK = 512
KEY_CHUNK = 1024
FORWARD_CHUNK = 256


def attend_forward_body(
    group, kv_heads, index_ref, q_ref, kp_ref, vp_ref, ko_ref, vo_ref, mixed_ref, level_ref, vt_all, acc
):
    pair = pl.program_id(0)
    prompt_len = kp_ref.shape[0]
    block_len = ko_ref.shape[0]
    conts = (block_len - PROMPT_BLK) // CONT_LEN
    shard_index = index_ref[0]

    @pl.when(pair == 0)
    def _():
        vt_all[:, :prompt_len] = transposed(vp_ref[...]).astype(jnp.bfloat16)
        vt_all[:, prompt_len:] = transposed(vo_ref[...]).astype(jnp.bfloat16)

    acc[...] = jnp.zeros_like(acc)
    size = min(FORWARD_CHUNK, prompt_len)
    prompt_keys = [slice(first, first + size) for first in range(0, prompt_len, size)]

    def kv_half(side):
        return jnp.minimum((2 * pair + side) // group, kv_heads - 1)

    def finish(scores, value_columns):
        level = jnp.max(scores[0], axis=0, keepdims=True)
        for part in scores[1:]:
            level = jnp.maximum(level, jnp.max(part, axis=0, keepdims=True))
        total = None
        mixed = None
        for part, columns in zip(scores, value_columns):
            weights = jnp.exp(part - level)
            part_total = jnp.sum(weights, axis=0, keepdims=True)
            part_mixed = nn_dot(columns, weights.astype(jnp.bfloat16))
            total = part_total if total is None else total + part_total
            mixed = part_mixed if mixed is None else mixed + part_mixed
        return mixed / total, level + jnp.log(total)

    both = jnp.concatenate(
        [head_rows(q_ref, 0, PROMPT_BLK, side, kv_half(side)) for side in range(2)], axis=0
    )
    mixed, level = finish(
        [
            seen_prompt(nt_dot(kp_ref[keys, :], both), keys.start, shard_index)
            for keys in prompt_keys
        ],
        [vt_all[:, keys] for keys in prompt_keys],
    )
    mixed = mixed.T
    for side in range(2):
        rows = slice(side * PROMPT_BLK, (side + 1) * PROMPT_BLK)
        acc[:PROMPT_BLK, :] += relane(mixed[rows], kv_half(side), side)
        level_ref[side, :, :PROMPT_BLK] = level[:, rows]

    def step(turn, _):
        side = turn // conts
        number = turn % conts
        half = kv_half(side)
        first_own = PROMPT_BLK + number * CONT_LEN
        for chunk in range(CONT_LEN // QUERY_CHUNK):
            before = chunk * QUERY_CHUNK
            first_row = pl.multiple_of(first_own + before, PROMPT_BLK)
            queries = head_rows(q_ref, first_row, QUERY_CHUNK, side, half)
            scores = [nt_dot(kp_ref[keys, :], queries) for keys in prompt_keys]
            columns = [vt_all[:, keys] for keys in prompt_keys]
            if before:
                start = pl.multiple_of(first_own, PROMPT_BLK)
                scores.append(nt_dot(ko_ref[pl.ds(start, before), :], queries))
                columns.append(
                    vt_all[:, pl.ds(pl.multiple_of(prompt_len + start, PROMPT_BLK), before)]
                )
            scores.append(below_diagonal(nt_dot(ko_ref[pl.ds(first_row, QUERY_CHUNK), :], queries)))
            columns.append(
                vt_all[:, pl.ds(pl.multiple_of(prompt_len + first_row, PROMPT_BLK), QUERY_CHUNK)]
            )
            mixed, level = finish(scores, columns)
            acc[pl.ds(first_row, QUERY_CHUNK), :] += relane(mixed.T, half, side)
            level_ref[side, :, pl.ds(first_row, QUERY_CHUNK)] = level
        return 0

    lax.fori_loop(0, 2 * conts, step, 0)
    mixed_ref[...] = acc[...].astype(jnp.bfloat16)


def attend_backward_body(
    group,
    kv_heads,
    index_ref,
    q_ref,
    grad_ref,
    mixed_ref,
    level_ref,
    cos_ref,
    sin_ref,
    kp_ref,
    vp_ref,
    ko_ref,
    vo_ref,
    dq_ref,
    dprompt_ref,
    down_ref,
    kt_all,
    acc,
    prompt_acc,
):
    pair = pl.program_id(0)
    last = pl.num_programs(0) - 1
    prompt_len = kp_ref.shape[0]
    block_len = ko_ref.shape[0]
    conts = (block_len - PROMPT_BLK) // CONT_LEN
    shard_index = index_ref[0]
    bf16 = jnp.bfloat16

    @pl.when(pair == 0)
    def _():
        kt_all[:, :prompt_len] = transposed(kp_ref[...]).astype(bf16)
        kt_all[:, prompt_len:] = transposed(ko_ref[...]).astype(bf16)
        prompt_acc[...] = jnp.zeros_like(prompt_acc)
        down_ref[...] = jnp.zeros_like(down_ref)

    acc[...] = jnp.zeros_like(acc)

    def kv_half(side):
        return jnp.minimum((2 * pair + side) // group, kv_heads - 1)

    def inner_sums(first_row, count, side):
        rows = pl.ds(first_row, count)
        product = mixed_ref[rows, :].astype(jnp.float32) * grad_ref[rows, :].astype(jnp.float32)
        return jnp.sum(relane(product, side, side).T, axis=0, keepdims=True)

    def part(keys, values, key_columns, queries, grads, level, inner, mask, sums, first_key):
        scores = nt_dot(keys, queries)
        if mask is not None:
            scores = mask(scores)
        probs = jnp.exp(scores - level)
        score_grad = (probs * (nt_dot(values, grads) - inner)).astype(bf16)
        rows = pl.ds(first_key, keys.shape[0])
        sums[rows, :LANES] += nn_dot(score_grad, queries)
        sums[rows, LANES:] += nn_dot(probs.astype(bf16), grads)
        return nn_dot(key_columns, score_grad)

    def prompt_parts(queries, grads, level, inner, masked):
        total = None
        size = min(KEY_CHUNK, prompt_len)
        for first_key in range(0, prompt_len, size):
            rows = slice(first_key, first_key + size)
            mask = (lambda s, f=first_key: seen_prompt(s, f, shard_index)) if masked else None
            piece = part(
                kp_ref[rows, :], vp_ref[rows, :], kt_all[:, rows], queries, grads, level, inner,
                mask, prompt_acc, first_key,
            )
            total = piece if total is None else total + piece
        return total

    both_q, both_g, both_level, both_inner = [], [], [], []
    for side in range(2):
        both_q.append(head_rows(q_ref, 0, PROMPT_BLK, side, kv_half(side)))
        both_g.append(head_rows(grad_ref, 0, PROMPT_BLK, side, kv_half(side)))
        both_level.append(level_ref[side, :, :PROMPT_BLK])
        both_inner.append(inner_sums(0, PROMPT_BLK, side))
    grad_q = prompt_parts(
        jnp.concatenate(both_q, axis=0),
        jnp.concatenate(both_g, axis=0),
        jnp.concatenate(both_level, axis=1),
        jnp.concatenate(both_inner, axis=1),
        True,
    ).T
    for side in range(2):
        rows = slice(side * PROMPT_BLK, (side + 1) * PROMPT_BLK)
        acc[:PROMPT_BLK, :] += relane(grad_q[rows], kv_half(side), side)

    def step(turn, _):
        side = turn // conts
        number = turn % conts
        half = kv_half(side)
        first_own = PROMPT_BLK + number * CONT_LEN
        for chunk in range(CONT_LEN // QUERY_CHUNK):
            before = chunk * QUERY_CHUNK
            first_row = pl.multiple_of(first_own + before, PROMPT_BLK)
            queries = head_rows(q_ref, first_row, QUERY_CHUNK, side, half)
            grads = head_rows(grad_ref, first_row, QUERY_CHUNK, side, half)
            level = level_ref[side, :, pl.ds(first_row, QUERY_CHUNK)]
            inner = inner_sums(first_row, QUERY_CHUNK, side)
            grad_q = prompt_parts(queries, grads, level, inner, False)
            own = [(first_row, QUERY_CHUNK, below_diagonal)]
            if before:
                own.append((pl.multiple_of(first_own, PROMPT_BLK), before, None))
            for start, size, mask in own:
                rows = pl.ds(start, size)
                columns = pl.ds(pl.multiple_of(prompt_len + start, PROMPT_BLK), size)
                grad_q += part(
                    ko_ref[rows, :], vo_ref[rows, :], kt_all[:, columns], queries, grads, level,
                    inner, mask, down_ref, start,
                )
            acc[pl.ds(first_row, QUERY_CHUNK), :] += relane(grad_q.T, half, side)
        return 0

    lax.fori_loop(0, 2 * conts, step, 0)
    grads = acc[...] * HEAD_DIMENSION ** (-0.5)
    half = HEAD_DIMENSION // 2
    lane = lax.broadcasted_iota(jnp.int32, grads.shape, 1)
    swapped = jnp.where(
        lane % HEAD_DIMENSION < half,
        pltpu.roll(grads, LANES - half, 1),
        pltpu.roll(grads, half, 1),
    )
    dq_ref[...] = (grads * cos_ref[...] + swapped * sin_ref[...]).astype(bf16)

    @pl.when(pair == last)
    def _():
        dprompt_ref[...] = prompt_acc[...].astype(bf16)


def pair_specs(block_len, prompt_len):
    by_pair = pl.BlockSpec((block_len, LANES), lambda b, i: (0, b))
    levels = pl.BlockSpec((2, 1, block_len), lambda b, i: (b, 0, 0))
    sources = [
        pl.BlockSpec((prompt_len, LANES), lambda b, i: (0, 0)),
        pl.BlockSpec((prompt_len, LANES), lambda b, i: (0, 1)),
        pl.BlockSpec((block_len, LANES), lambda b, i: (0, 0)),
        pl.BlockSpec((block_len, LANES), lambda b, i: (0, 1)),
    ]
    return by_pair, levels, sources


def attention_cost(block_len, prompt_len, width, products):
    pairs = (block_len * prompt_len + block_len * CONT_LEN // 2) * (width // HEAD_DIMENSION)
    return pl.CostEstimate(
        flops=products * 2 * pairs * 2 * LANES,
        bytes_accessed=8 * block_len * width,
        transcendentals=pairs,
    )


def attend_forward(index, queries, kv_prompt, kv_own, group, kv_heads):
    block_len, width = queries.shape
    prompt_len = kv_prompt.shape[0]
    by_pair, levels, sources = pair_specs(block_len, prompt_len)
    return pl.pallas_call(
        partial(attend_forward_body, group, kv_heads),
        out_shape=[
            jax.ShapeDtypeStruct((block_len, width), jnp.bfloat16),
            jax.ShapeDtypeStruct((width // HEAD_DIMENSION, 1, block_len), jnp.float32),
        ],
        grid_spec=pltpu.PrefetchScalarGridSpec(
            num_scalar_prefetch=1,
            grid=(width // LANES,),
            in_specs=[by_pair] + sources,
            out_specs=[by_pair, levels],
            scratch_shapes=[
                pltpu.VMEM((LANES, prompt_len + block_len), jnp.bfloat16),
                pltpu.VMEM((block_len, LANES), jnp.float32),
            ],
        ),
        compiler_params=pltpu.CompilerParams(
            dimension_semantics=("arbitrary",), vmem_limit_bytes=56 * 1024 * 1024
        ),
        cost_estimate=attention_cost(block_len, prompt_len, width, 2),
        name="attend_forward",
    )(index, queries, kv_prompt, kv_prompt, kv_own, kv_own)


def attend_backward(
    index, queries, grads, mixed, level, tables, kv_prompt, kv_own, group, kv_heads
):
    block_len, width = queries.shape
    prompt_len = kv_prompt.shape[0]
    by_pair, levels, sources = pair_specs(block_len, prompt_len)
    return pl.pallas_call(
        partial(attend_backward_body, group, kv_heads),
        out_shape=[
            jax.ShapeDtypeStruct((block_len, width), jnp.bfloat16),
            jax.ShapeDtypeStruct((prompt_len, 2 * LANES), jnp.bfloat16),
            jax.ShapeDtypeStruct((block_len, 2 * LANES), jnp.float32),
        ],
        grid_spec=pltpu.PrefetchScalarGridSpec(
            num_scalar_prefetch=1,
            grid=(width // LANES,),
            in_specs=[by_pair, by_pair, by_pair, levels]
            + [pl.BlockSpec((block_len, LANES), lambda b, i: (0, 0))] * 2
            + sources,
            out_specs=[
                by_pair,
                pl.BlockSpec((prompt_len, 2 * LANES), lambda b, i: (0, 0)),
                pl.BlockSpec((block_len, 2 * LANES), lambda b, i: (0, 0)),
            ],
            scratch_shapes=[
                pltpu.VMEM((LANES, prompt_len + block_len), jnp.bfloat16),
                pltpu.VMEM((block_len, LANES), jnp.float32),
                pltpu.VMEM((prompt_len, 2 * LANES), jnp.float32),
            ],
        ),
        compiler_params=pltpu.CompilerParams(
            dimension_semantics=("arbitrary",), vmem_limit_bytes=56 * 1024 * 1024
        ),
        cost_estimate=attention_cost(block_len, prompt_len, width, 5),
        name="attend_backward",
    )(index, queries, grads, mixed, level, *tables, kv_prompt, kv_prompt, kv_own, kv_own)


def to_lanes(values):
    extra = -values.shape[1] % LANES
    return jnp.pad(values, ((0, 0), (0, extra))) if extra else values


def exchange(values, axis_name, bit):
    count = lax.axis_size(axis_name)
    return lax.ppermute(values, axis_name, [(i, i ^ bit) for i in range(count)])


def bits_of(number):
    return [1 << k for k in range(number.bit_length()) if number >> k & 1]


def even_blocks(count):
    even = sorted(range(2, count, 2), key=lambda j: (len(bits_of(j)), j))
    singles = [j for j in even if len(bits_of(j)) == 1]
    return singles, even[len(singles) :]


def gather_blocks(own, axis_name, after_first=None):
    count = lax.axis_size(axis_name)
    singles, several = even_blocks(count)
    blocks = {0: own, 1: exchange(own, axis_name, 1)}
    for j in singles:
        blocks[j] = exchange(own, axis_name, j)
    if after_first is not None:
        blocks.update(zip(singles, after_first([blocks[j] for j in singles])))
    for j in several:
        low_bit = bits_of(j)[0]
        blocks[j] = exchange(blocks[j ^ low_bit], axis_name, low_bit)
    for j in singles + several:
        blocks[j + 1] = exchange(blocks[j], axis_name, 1)
    return [blocks[j] for j in range(count)]


def add_rounded(left_side, right_side):
    return (left_side.astype(jnp.float32) + right_side.astype(jnp.float32)).astype(jnp.bfloat16)


def reduce_several(sums, axis_name):
    sums = dict(sums)
    pending = []
    for j in sorted((j for j in sums if len(bits_of(j)) > 1), key=lambda j: (-len(bits_of(j)), j)):
        bit = bits_of(j)[-1]
        piece = exchange(sums[j], axis_name, bit)
        if len(bits_of(j ^ bit)) > 1:
            sums[j ^ bit] = add_rounded(sums[j ^ bit], piece)
        else:
            pending.append((j ^ bit, piece))
    return pending


def reduce_singles(sums, pending, axis_name):
    sums = dict(sums)
    for j, piece in pending:
        sums[j] = add_rounded(sums[j], piece)
    return [sums[0]] + [exchange(sums[j], axis_name, j) for j in sums if len(bits_of(j)) == 1]


def add_all(pieces):
    total = pieces[0].astype(jnp.float32)
    for piece in pieces[1:]:
        total = total + piece.astype(jnp.float32)
    return total


def halves_by_core(values, axis_name):
    count = lax.axis_size(axis_name)
    parity = lax.axis_index(axis_name) % 2
    paired = values.reshape(count // 2, 2, values.shape[0] // count, values.shape[1])
    keep = lax.dynamic_index_in_dim(paired, parity, 1, keepdims=False)
    give = lax.dynamic_index_in_dim(paired, 1 - parity, 1, keepdims=False)
    return keep, give


def chip_sums(keep, arrived, axis_name):
    index = lax.axis_index(axis_name)
    total = add_rounded(keep, arrived)
    return {
        2 * k: lax.dynamic_index_in_dim(total, (index // 2) ^ k, 0, keepdims=False)
        for k in range(total.shape[0])
    }


def reduce_rows(values, axis_name):
    keep, give = halves_by_core(values, axis_name)
    sums = chip_sums(keep, exchange(give, axis_name, 1), axis_name)
    return add_all(reduce_singles(sums, reduce_several(sums, axis_name), axis_name))


def in_order(blocks, index):
    stacked = jnp.stack(blocks)
    return jnp.concatenate(
        [lax.dynamic_index_in_dim(stacked, j ^ index, 0, keepdims=True) for j in range(len(blocks))],
        axis=0,
    )


def expert_body(
    experts_all, index_ref, x_even, x_odd, og_even, og_odd, gate_w, up_w, down_w, *rest
):
    (x_all, og_all, pre_all, hid_all, row_even, row_odd, out_even, out_odd) = rest[-12:-4]
    (row_acc, out_acc, back_acc, _) = rest[-4:]
    expert = pl.program_id(0)
    last = pl.num_programs(0) - 1
    rows = x_even.shape[0]
    width = x_all.shape[1]
    hidden_units = gate_w.shape[2]
    nt_dims = (((1,), (1,)), ((), ()))

    @pl.when(expert == 0)
    def _():
        x_all[:rows, :] = x_even[:, :width]
        x_all[rows:, :] = x_odd[:, :width]
        og_all[:rows, :] = og_even[...]
        og_all[rows:, :] = og_odd[...]

    column = index_ref[0] + expert
    lane = lax.broadcasted_iota(jnp.int32, (2 * rows, LANES), 1)
    coded = jnp.concatenate([x_even[:, width:], x_odd[:, width:]], axis=0).astype(jnp.float32)
    gate = jnp.sum(
        jnp.where((lane == column) | (lane == column + experts_all), coded, 0.0),
        axis=1,
        keepdims=True,
    )
    x_rows = x_all[...]
    og_rows = og_all[...]
    gate_pre = jnp.dot(x_rows, gate_w[0], preferred_element_type=jnp.float32)
    up_pre = jnp.dot(x_rows, up_w[0], preferred_element_type=jnp.float32)
    down_grad = lax.dot_general(og_rows, down_w[0], nt_dims, preferred_element_type=jnp.float32)
    sigmoid = 1.0 / (1.0 + jnp.exp(-gate_pre))
    silu = gate_pre * sigmoid
    hidden = silu * up_pre
    gate_back = jnp.sum(hidden * down_grad, axis=1, keepdims=True)
    hidden_low = (gate * hidden).astype(jnp.bfloat16)
    hidden_grad = gate * down_grad
    gate_pre_low = (
        hidden_grad * up_pre * sigmoid * (1.0 + gate_pre * (1.0 - sigmoid))
    ).astype(jnp.bfloat16)
    up_pre_low = (hidden_grad * silu).astype(jnp.bfloat16)
    hid_all[...] = hidden_low
    pre_all[0, :, :hidden_units] = gate_pre_low
    pre_all[0, :, hidden_units:] = up_pre_low
    row = lax.dot_general(
        gate_pre_low, gate_w[0], nt_dims, preferred_element_type=jnp.float32
    ) + lax.dot_general(up_pre_low, up_w[0], nt_dims, preferred_element_type=jnp.float32)
    out = jnp.dot(hidden_low, down_w[0], preferred_element_type=jnp.float32)
    high = gate_back.astype(jnp.bfloat16).astype(jnp.float32)
    back = jnp.where(lane == column, high, 0.0) + jnp.where(
        lane == column + experts_all, gate_back - high, 0.0
    )

    @pl.when(expert == 0)
    def _():
        row_acc[...] = row
        out_acc[...] = out
        back_acc[...] = back

    @pl.when(expert > 0)
    def _():
        row_acc[...] += row
        out_acc[...] += out
        back_acc[...] += back

    @pl.when(expert == last)
    def _():
        for ref, first in ((row_even, 0), (row_odd, rows)):
            ref[:, :width] = row_acc[first : first + rows, :].astype(jnp.bfloat16)
            ref[:, width:] = back_acc[first : first + rows, :].astype(jnp.bfloat16)
        out_even[...] = out_acc[:rows, :].astype(jnp.bfloat16)
        out_odd[...] = out_acc[rows:, :].astype(jnp.bfloat16)


def expert_pair(position, pairs, first_expert, experts_all, x_pair, og_pair, weights, carried):
    w_gate, w_up, w_down = weights
    rows, coded_width = x_pair[0].shape
    width = coded_width - LANES
    local_experts, _, hidden_units = w_gate.shape
    bf16 = jnp.bfloat16
    whole = 2 * rows
    fixed = lambda e, i: (0, 0)
    once = pl.Buffered(1)
    in_specs = (
        [pl.BlockSpec((rows, coded_width), fixed, pipeline_mode=once)] * 2
        + [pl.BlockSpec((rows, width), fixed, pipeline_mode=once)] * 2
        + [pl.BlockSpec((1, width, hidden_units), lambda e, i: (e, 0, 0))] * 2
        + [pl.BlockSpec((1, hidden_units, width), lambda e, i: (e, 0, 0))]
    )
    operands = [*x_pair, *og_pair, w_gate, w_up, w_down]
    aliases = {}
    if carried is not None:
        in_specs = in_specs + [pl.BlockSpec(memory_space=pl.ANY)] * 4
        aliases = {1 + len(operands) + k: k for k in range(4)}
        operands = operands + list(carried)
    out_shape = [
        jax.ShapeDtypeStruct((pairs * whole, width), bf16),
        jax.ShapeDtypeStruct((pairs * whole, width), bf16),
        jax.ShapeDtypeStruct((local_experts, pairs * whole, 2 * hidden_units), bf16),
        jax.ShapeDtypeStruct((pairs * whole, local_experts * hidden_units), bf16),
        jax.ShapeDtypeStruct((rows, coded_width), bf16),
        jax.ShapeDtypeStruct((rows, coded_width), bf16),
        jax.ShapeDtypeStruct((rows, width), bf16),
        jax.ShapeDtypeStruct((rows, width), bf16),
    ]
    out_specs = [
        pl.BlockSpec((whole, width), lambda e, i: (position, 0)),
        pl.BlockSpec((whole, width), lambda e, i: (position, 0)),
        pl.BlockSpec((1, whole, 2 * hidden_units), lambda e, i: (e, position, 0)),
        pl.BlockSpec((whole, hidden_units), lambda e, i: (position, e)),
        pl.BlockSpec((rows, coded_width), fixed),
        pl.BlockSpec((rows, coded_width), fixed),
        pl.BlockSpec((rows, width), fixed),
        pl.BlockSpec((rows, width), fixed),
    ]
    products = 2 * whole * width * hidden_units * local_experts
    results = pl.pallas_call(
        partial(expert_body, experts_all),
        out_shape=out_shape,
        grid_spec=pltpu.PrefetchScalarGridSpec(
            num_scalar_prefetch=1,
            grid=(local_experts,),
            in_specs=in_specs,
            out_specs=out_specs,
            scratch_shapes=[
                pltpu.VMEM((whole, width), jnp.float32),
                pltpu.VMEM((whole, width), jnp.float32),
                pltpu.VMEM((whole, LANES), jnp.float32),
                pltpu.VMEM((8, LANES), jnp.float32),
            ],
        ),
        input_output_aliases=aliases,
        compiler_params=pltpu.CompilerParams(
            dimension_semantics=("arbitrary",), vmem_limit_bytes=60 * 1024 * 1024
        ),
        cost_estimate=pl.CostEstimate(
            flops=6 * products,
            bytes_accessed=3 * 2 * local_experts * width * hidden_units + 20 * whole * width,
            transcendentals=whole * hidden_units * local_experts,
        ),
        name="experts",
    )(first_expert, *operands)
    return results[:4], results[4:]


def on_device(
    tokens,
    routes,
    w_query,
    key_projection,
    value_projection,
    w_out,
    gain_attn,
    gain_ffn,
    w_router,
    w_gate,
    w_up,
    w_down,
    out_grad,
):
    bf16 = jnp.bfloat16
    shard_count = lax.axis_size("shard")
    seq_count = lax.axis_size("seq")
    shard_index = lax.axis_index("shard")
    seq_index = lax.axis_index("seq")
    tok_count, model_width = tokens.shape
    top_count = routes.shape[1]
    experts_all = w_router.shape[1]
    local_experts = w_gate.shape[0]
    block_len = tok_count * seq_count
    prompt_len = PROMPT_BLK * shard_count
    query_width = w_query.shape[1]
    key_width = key_projection.shape[1]

    singles, several = even_blocks(shard_count)
    small = jnp.concatenate([w_router, gain_attn[:, None], gain_ffn[:, None]], axis=1)
    small = lax.all_gather(small, "seq", axis=0, tiled=True)
    small = lax.all_gather(small, "shard", axis=0, tiled=True)
    router_weight = small[:, :experts_all]
    first_gain = small[:, experts_all].astype(jnp.float32)
    second_gain = small[:, experts_all + 1].astype(jnp.float32)
    block_tokens = lax.all_gather(tokens, "seq", axis=0, tiled=True)
    own_weight = jnp.concatenate([w_query, key_projection, value_projection], axis=1)
    grad_blocks = {0: out_grad}
    near = [exchange(out_grad, "shard", bit) for bit in singles]

    def with_near(blocks):
        blocks, near[:] = lax.optimization_barrier((blocks, near))
        return blocks

    weight_blocks = gather_blocks(own_weight, "shard", with_near)
    grad_blocks.update(zip(singles, near))
    for j in [0] + singles:
        grad_blocks[j + 1] = exchange(grad_blocks[j], "shard", 1)
    out_weight = lax.all_gather(w_out, "seq", axis=0, tiled=True)
    qkv_weight = in_order(weight_blocks, shard_index).reshape(model_width, -1)

    block_rows = jnp.arange(block_len, dtype=jnp.int32)
    cos_table, sin_table = rotary_tables(
        place_of(block_rows, shard_index, prompt_len), HEAD_DIMENSION
    )
    back_tables = [
        jnp.tile(cos_table[:, 0, :], (1, LANES // cos_table.shape[2])),
        jnp.tile(
            jnp.concatenate([sin_table, -sin_table], axis=2)[:, 0, :],
            (1, LANES // HEAD_DIMENSION),
        ),
    ]
    block_tokens, cos_table, sin_table, back_tables = lax.optimization_barrier(
        (block_tokens, cos_table, sin_table, back_tables)
    )
    inputs = block_tokens.astype(jnp.float32)
    first_factor = rms_parts(inputs)
    normed_low = (inputs * first_factor * first_gain).astype(bf16)
    lin = matmul(normed_low, qkv_weight)
    kv_heads = key_width // HEAD_DIMENSION
    group = query_width // key_width
    queries = rotate(lin[:, :query_width], cos_table, sin_table, HEAD_DIMENSION)
    queries = to_lanes((queries * HEAD_DIMENSION ** (-0.5)).astype(bf16))
    key_heads = rotate(
        lin[:, query_width : query_width + key_width], cos_table, sin_table, HEAD_DIMENSION
    ).astype(bf16)
    value_heads = lin[:, query_width + key_width :].astype(bf16)
    kv_own = jnp.concatenate([to_lanes(key_heads), to_lanes(value_heads)], axis=1)
    kv_prompt = lax.all_gather(kv_own[:PROMPT_BLK], "shard", axis=0, tiled=True)
    kv_prompt, out_weight, near = lax.optimization_barrier(
        (kv_prompt, out_weight, [grad_blocks[bit] for bit in singles])
    )
    grad_blocks.update(zip(singles, near))
    out_weight = lax.all_gather(out_weight, "shard", axis=1, tiled=True)
    for j in several:
        low_bit = bits_of(j)[0]
        grad_blocks[j] = exchange(grad_blocks[j ^ low_bit], "shard", low_bit)
    block_number = shard_index.astype(jnp.int32).reshape(1)
    mixed_own, levels = attend_forward(block_number, queries, kv_prompt, kv_own, group, kv_heads)
    sooner = [j for j in range(1, shard_count) if j - 1 not in several]
    mixed_own, held_blocks = lax.optimization_barrier((mixed_own, [grad_blocks[j] for j in sooner]))
    for j, block in zip(sooner, held_blocks):
        grad_blocks[j] = block
    for j in several:
        grad_blocks[j + 1] = exchange(grad_blocks[j], "shard", 1)
    mixed_heads = mixed_own[:, :query_width]
    mixed_tokens = lax.all_to_all(mixed_heads, "seq", split_axis=0, concat_axis=1, tiled=True)

    half_features = model_width // 2
    core_bit = shard_index % 2
    half_weight, mixed_tokens = lax.optimization_barrier(
        (
            lax.dynamic_slice_in_dim(qkv_weight, core_bit * half_features, half_features, axis=0),
            mixed_tokens,
        )
    )
    wide_half = lax.all_gather(half_weight, "seq", axis=0, tiled=False)

    own_inputs = tokens.astype(jnp.float32)
    upstream = out_grad.astype(jnp.float32)
    residual = own_inputs + matmul(mixed_tokens, out_weight)
    second_factor = rms_parts(residual)
    second_low = (residual * second_factor * second_gain).astype(bf16)
    logits = matmul(second_low, router_weight)
    chosen = routes[:, :, None] == jnp.arange(experts_all, dtype=jnp.int32)[None, None, :]
    named = jnp.any(chosen, axis=1)
    gate_dense = jax.nn.softmax(jnp.where(named, logits, negative), axis=-1)
    gate_dense = jnp.where(named, gate_dense, 0.0)

    gate_high = lax.reduce_precision(gate_dense, 8, 7)
    coded = jnp.concatenate(
        [
            second_low,
            gate_high.astype(bf16),
            (gate_dense - gate_high).astype(bf16),
            jnp.zeros((tok_count, LANES - 2 * experts_all), bf16),
        ],
        axis=1,
    )
    row_blocks = {0: coded, 1: exchange(coded, "shard", 1)}
    for bit in singles:
        row_blocks[bit] = exchange(coded, "shard", bit)
    order = [0] + singles[:-1] + several + singles[-1:]
    first_expert = (shard_index * local_experts).astype(jnp.int32).reshape(1)
    carried = None
    pending = []
    row_sums = {}
    out_parts = [None] * shard_count
    for position, j in enumerate(order):
        row_pair = [row_blocks[j], row_blocks[j + 1]]
        if j == order[-1]:
            row_pair, row_sums = lax.optimization_barrier((row_pair, row_sums))
            pending = reduce_several(row_sums, "shard")
        carried, pieces = expert_pair(
            position,
            len(order),
            first_expert,
            experts_all,
            row_pair,
            [grad_blocks[j], grad_blocks[j + 1]],
            (w_gate, w_up, w_down),
            carried,
        )
        if position == 0:
            arrived, pieces = lax.optimization_barrier(
                ([row_blocks[bit] for bit in singles], pieces)
            )
            row_blocks.update(zip(singles, arrived))
            for bit in singles:
                row_blocks[bit + 1] = exchange(row_blocks[bit], "shard", 1)
            for k in several:
                low_bit = bits_of(k)[0]
                row_blocks[k] = exchange(row_blocks[k ^ low_bit], "shard", low_bit)
        elif position == 1:
            arrived, pieces = lax.optimization_barrier(([row_blocks[k] for k in several], pieces))
            row_blocks.update(zip(several, arrived))
            for k in several:
                row_blocks[k + 1] = exchange(row_blocks[k], "shard", 1)
        elif j == order[-1]:
            arrived, pieces, carried = lax.optimization_barrier(
                ([piece for _, piece in pending], pieces, carried)
            )
            pending = [(k, piece) for (k, _), piece in zip(pending, arrived)]
        arrived = exchange(pieces[1], "shard", 1)
        if j != order[-1]:
            row_sums[j] = add_rounded(pieces[0], arrived)
        out_parts[j], out_parts[j + 1] = pieces[2], pieces[3]
    carried, wide_half = lax.optimization_barrier((carried, wide_half))
    all_rows, all_grads, all_pre, all_hidden = carried
    down_sum = transposed_times(all_grads, all_hidden).astype(bf16)
    grad_down = lax.psum_scatter(down_sum, "seq", scatter_dimension=0, tiled=True)
    all_rows, arrived, down_sum = lax.optimization_barrier((all_rows, arrived, down_sum))
    row_sums[order[-1]] = add_rounded(pieces[0], arrived)
    pre_sums = [transposed_times(all_rows, all_pre[0]).astype(bf16)]
    pre_grads = [lax.psum_scatter(pre_sums[0], "seq", scatter_dimension=0, tiled=True)]
    row_pieces = reduce_singles(row_sums, pending, "shard")
    row_pieces, pre_sums[0] = lax.optimization_barrier((row_pieces, pre_sums[0]))
    row_total = add_all(row_pieces)
    row_grad = row_total[:, :model_width]
    gate_grad_dense = (
        row_total[:, model_width : model_width + experts_all]
        + row_total[:, model_width + experts_all : model_width + 2 * experts_all]
    )
    weighted = gate_dense * gate_grad_dense
    logit_grad = weighted - gate_dense * jnp.sum(weighted, axis=-1, keepdims=True)
    second_grad = row_grad + times_transposed(
        logit_grad, router_weight.astype(jnp.float32), highest
    )
    residual_part, grad_gain_ffn = rms_backward(residual, second_factor, second_gain, second_grad)
    residual_grad = upstream + residual_part
    residual_low = residual_grad.astype(bf16)
    mixed_grad_tokens = times_transposed(residual_low, out_weight).astype(bf16)
    other_half = exchange(wide_half, "shard", 1)
    mixed_grad_tokens, out_parts, all_rows, other_half, mixed_late, logit_late = (
        lax.optimization_barrier(
            (mixed_grad_tokens, out_parts, all_rows, other_half, mixed_tokens, logit_grad)
        )
    )
    mixed_grad = lax.all_to_all(mixed_grad_tokens, "seq", split_axis=1, concat_axis=0, tiled=True)
    odd = [exchange(out_parts[j + 1], "shard", 1) for j in order]
    pre_sums += [
        transposed_times(all_rows, all_pre[e]).astype(bf16) for e in range(1, local_experts)
    ]
    pre_grads += [
        lax.psum_scatter(part, "seq", scatter_dimension=0, tiled=True) for part in pre_sums[1:]
    ]
    odd, pre_sums = lax.optimization_barrier((odd, pre_sums))
    odd = dict(zip(order, odd))
    out_sums = {j: add_rounded(out_parts[j], odd[j]) for j in several}
    whole_out = transposed_times(residual_low, mixed_late).astype(bf16)
    whole_keep, whole_give = halves_by_core(whole_out, "shard")
    whole_arrived = exchange(whole_give, "shard", 1)
    grad_router = transposed_times(second_low.astype(jnp.float32), logit_late, highest)
    small_grad = jnp.concatenate([grad_router, grad_gain_ffn[:, None]], axis=1)
    small_keep, small_give = halves_by_core(small_grad.astype(bf16), "shard")
    small_arrived = exchange(small_give, "shard", 1)
    mixed_grad, pre_sums, out_sums, whole_arrived, odd, small_arrived = lax.optimization_barrier(
        (mixed_grad, pre_sums, out_sums, whole_arrived, odd, small_arrived)
    )
    small_sums = chip_sums(small_keep, small_arrived, "shard")
    small_pending = reduce_several(small_sums, "shard")
    out_pending = reduce_several(out_sums, "shard")
    whole_sums = chip_sums(whole_keep, whole_arrived, "shard")
    whole_pending = reduce_several(whole_sums, "shard")

    query_grad, prompt_grad, self_grad = attend_backward(
        block_number,
        queries,
        to_lanes(mixed_grad),
        mixed_own,
        levels,
        back_tables,
        kv_prompt,
        kv_own,
        group,
        kv_heads,
    )
    query_grad, prompt_grad, self_grad, small_arrived, arrived, out_arrived = lax.optimization_barrier(
        (
            query_grad,
            prompt_grad,
            self_grad,
            [piece for _, piece in small_pending],
            [piece for _, piece in whole_pending],
            [piece for _, piece in out_pending],
        )
    )
    whole_pending = [(j, piece) for (j, _), piece in zip(whole_pending, arrived)]
    out_pending = [(j, piece) for (j, _), piece in zip(out_pending, out_arrived)]
    small_pending = [(j, piece) for (j, _), piece in zip(small_pending, small_arrived)]
    small_grad = add_all(reduce_singles(small_sums, small_pending, "shard"))
    lin_query = query_grad[:, :query_width]
    own_prompt = reduce_rows(prompt_grad, "shard")
    key_grad = jnp.concatenate(
        [own_prompt[:, :key_width], self_grad[PROMPT_BLK:, :key_width]], axis=0
    )
    value_low = jnp.concatenate(
        [own_prompt[:, LANES : LANES + key_width], self_grad[PROMPT_BLK:, LANES : LANES + key_width]],
        axis=0,
    ).astype(bf16)
    lin_key = rotate(key_grad, cos_table, -sin_table, HEAD_DIMENSION).astype(bf16)
    lin_all = jnp.concatenate([lin_query, lin_key, value_low], axis=1)
    all_columns = lin_all.shape[1]
    lin_all, whole_sums = lax.optimization_barrier((lin_all, whole_sums))
    lin_tokens = lax.all_to_all(lin_all, "seq", split_axis=0, concat_axis=1, tiled=True)

    keep, give = halves_by_core(transposed_times(normed_low, lin_all).astype(bf16), "shard")
    qkv_sums = chip_sums(keep, exchange(give, "shard", 1), "shard")
    qkv_pending = reduce_several(qkv_sums, "shard")
    arrived, odd = lax.optimization_barrier(([piece for _, piece in qkv_pending], odd))
    qkv_pending = [(j, piece) for (j, _), piece in zip(qkv_pending, arrived)]
    grad_qkv = add_all(reduce_singles(qkv_sums, qkv_pending, "shard"))
    for j in [0] + singles:
        out_sums[j] = add_rounded(out_parts[j], odd[j])
    out_sums = {j: out_sums[j] for j in [0] + singles}
    out_pieces = reduce_singles(out_sums, out_pending, "shard")
    grad_out = add_all(reduce_singles(whole_sums, whole_pending, "shard")).astype(bf16).T
    hidden_units = w_gate.shape[2]
    lin_tokens, grad_down, pre_grads[0] = lax.optimization_barrier(
        (lin_tokens, grad_down, pre_grads[0])
    )
    grad_down = grad_down.T.reshape(local_experts, hidden_units, -1).astype(jnp.float32)
    parts = [0.0, 0.0]
    for k, weight in enumerate((wide_half, other_half)):
        for group_index in range(seq_count):
            columns = slice(group_index * all_columns, (group_index + 1) * all_columns)
            parts[k] = parts[k] + times_transposed(lin_tokens[:, columns], weight[group_index])
    normed_grad = jnp.concatenate(
        [
            jnp.where(core_bit == 0, parts[0], parts[1]),
            jnp.where(core_bit == 0, parts[1], parts[0]),
        ],
        axis=1,
    )
    normed_grad, out_pieces = lax.optimization_barrier((normed_grad, out_pieces))
    output = (residual + add_all(out_pieces)).astype(bf16)
    own_features = own_weight.shape[0]
    gain_own = lax.dynamic_slice_in_dim(first_gain, shard_index * own_features, own_features)
    gain_part = (
        jnp.sum(own_weight.astype(jnp.float32) * grad_qkv[:, :all_columns], axis=1) / gain_own
    )
    grad_query = grad_qkv[:, :query_width]
    grad_key = grad_qkv[:, query_width : query_width + key_width]
    grad_value = grad_qkv[:, query_width + key_width : query_width + 2 * key_width]
    small_grad = jnp.concatenate([small_grad, gain_part[:, None]], axis=1)
    own_small = own_features // seq_count
    small_grad = small_grad.astype(bf16).reshape(seq_count, own_small, -1)
    small_grad = jnp.pad(small_grad, ((0, 0), (0, model_width // seq_count - own_small), (0, 0)))
    last_sum = jnp.concatenate([grad_out, small_grad.reshape(model_width, -1)], axis=1)
    last_sum = lax.psum_scatter(last_sum, "seq", scatter_dimension=0, tiled=True)
    last_sum = last_sum.astype(jnp.float32)
    grad_out = last_sum[:, : w_out.shape[1]]
    small_grad = last_sum[:own_small, w_out.shape[1] :]
    own_factor = rms_parts(own_inputs)
    input_part, _ = rms_backward(own_inputs, own_factor, first_gain, normed_grad)
    tokens_grad = residual_grad + input_part
    pre_grads = [part.astype(jnp.float32) for part in pre_grads]
    grad_gate = jnp.stack([part[:, :hidden_units] for part in pre_grads])
    grad_up = jnp.stack([part[:, hidden_units:] for part in pre_grads])
    return (
        output,
        tokens_grad,
        grad_query,
        grad_key,
        grad_value,
        grad_out,
        small_grad[:, experts_all + 1],
        small_grad[:, experts_all],
        small_grad[:, :experts_all],
        grad_gate,
        grad_up,
        grad_down,
    )


def solution(mesh):
    return jax.shard_map(
        on_device,
        mesh=mesh,
        in_specs=(
            P(("shard", "seq"), None),
            P(("shard", "seq"), None),
            P("shard", "seq"),
            P("shard", "seq"),
            P("shard", "seq"),
            P("seq", "shard"),
            P(("shard", "seq")),
            P(("shard", "seq")),
            P(("shard", "seq"), None),
            P("shard", None, None),
            P("shard", None, None),
            P("shard", None, None),
            P(("shard", "seq"), None),
        ),
        out_specs=(
            P(("shard", "seq"), None),
            P(("shard", "seq"), None),
            P("shard", "seq"),
            P("shard", "seq"),
            P("shard", "seq"),
            P("seq", "shard"),
            P(("shard", "seq")),
            P(("shard", "seq")),
            P(("shard", "seq"), None),
            P("shard", "seq", None),
            P("shard", "seq", None),
            P("shard", None, "seq"),
        ),
        check_vma=False,
    )
```

```python
from functools import partial

import jax
import jax.numpy as jnp
from jax import lax
from jax.experimental import pallas as pl
from jax.experimental.pallas import tpu as pltpu
from jax.sharding import PartitionSpec as P

HEAD_DIMENSION = 64
CONT_LEN = 512
PROMPT_BLK = 128


norm_eps = 1e-05
negative = -1e30
rope_base = 10000.0
highest = lax.Precision.HIGHEST


def rms_norm(values, scaling):
    factor = lax.rsqrt(jnp.mean(values * values, axis=-1, keepdims=True) + norm_eps)
    return values * factor * scaling


def swiglu(gate_pre, up_pre):
    return jax.nn.silu(gate_pre) * up_pre


def rotary_tables(places, head_size):
    half_size = head_size // 2
    frequency = jnp.exp(
        jnp.arange(half_size, dtype=jnp.float32) * (-2.0 * jnp.log(rope_base) / head_size)
    )
    angles = places.astype(jnp.float32)[:, None] * frequency[None, :]
    return (jnp.cos(angles)[:, None, :], jnp.sin(angles)[:, None, :])


def rotate(values, cosine, sine, head_size):
    total_row_count = values.shape[0]
    by_head = values.reshape(total_row_count, -1, head_size)
    half_size = head_size // 2
    first_half = by_head[..., :half_size]
    second_half = by_head[..., half_size:]
    turned = jnp.concatenate(
        [first_half * cosine - second_half * sine, second_half * cosine + first_half * sine],
        axis=-1,
    )
    return turned.reshape(total_row_count, -1)


def place_of(within, block_index, prompt_len):
    return jnp.where(
        within < PROMPT_BLK,
        block_index * PROMPT_BLK + within,
        prompt_len + (within - PROMPT_BLK) % CONT_LEN,
    )


def times_transposed(left_side, right_side, precision=None):
    return lax.dot_general(
        left_side,
        right_side,
        (((1,), (1,)), ((), ())),
        precision=precision,
        preferred_element_type=jnp.float32,
    )


def transposed_times(left_side, right_side, precision=None):
    return lax.dot_general(
        left_side,
        right_side,
        (((0,), (0,)), ((), ())),
        precision=precision,
        preferred_element_type=jnp.float32,
    )


def rms_parts(values):
    return lax.rsqrt(jnp.mean(values * values, axis=-1, keepdims=True) + norm_eps)


def rms_backward(values, factor, scaling, normed_grad):
    scaled = scaling * normed_grad
    inner = jnp.mean(scaled * values, axis=-1, keepdims=True)
    values_grad = factor * scaled - values * (factor * factor * factor) * inner
    gain_grad = jnp.sum(normed_grad * values * factor, axis=0)
    return values_grad, gain_grad


def matmul(left_side, right_side):
    return jnp.dot(left_side, right_side, preferred_element_type=jnp.float32)


LANES = 128


def relane(values, source, target):
    lane = lax.broadcasted_iota(jnp.int32, values.shape, 1)
    swapped = jnp.where(source != target, pltpu.roll(values, HEAD_DIMENSION, 1), values)
    return jnp.where(lane // HEAD_DIMENSION == target, swapped, 0.0)


def head_rows(ref, first, count, source, target):
    values = ref[pl.ds(first, count), :].astype(jnp.float32)
    return relane(values, source, target).astype(jnp.bfloat16)


def nt_dot(left_side, right_side):
    return lax.dot_general(
        left_side, right_side, (((1,), (1,)), ((), ())), preferred_element_type=jnp.float32
    )


def nn_dot(left_side, right_side):
    return jnp.dot(left_side, right_side, preferred_element_type=jnp.float32)


def below_diagonal(scores):
    key_row = lax.broadcasted_iota(jnp.int32, scores.shape, 0)
    query_column = lax.broadcasted_iota(jnp.int32, scores.shape, 1)
    return jnp.where(key_row <= query_column, scores, negative)


def seen_prompt(scores, first_key, shard_index):
    key_row = lax.broadcasted_iota(jnp.int32, scores.shape, 0) + first_key
    query_column = lax.broadcasted_iota(jnp.int32, scores.shape, 1) % PROMPT_BLK
    return jnp.where(key_row <= query_column + shard_index * PROMPT_BLK, scores, negative)


def transposed(values):
    return values.astype(jnp.float32).T


QUERY_CHUNK = 512
KEY_CHUNK = 1024
FORWARD_CHUNK = 256


def attend_forward_body(
    group, kv_heads, index_ref, q_ref, kp_ref, vp_ref, ko_ref, vo_ref, mixed_ref, level_ref, vt_all, acc
):
    pair = pl.program_id(0)
    prompt_len = kp_ref.shape[0]
    block_len = ko_ref.shape[0]
    conts = (block_len - PROMPT_BLK) // CONT_LEN
    shard_index = index_ref[0]

    @pl.when(pair == 0)
    def _():
        vt_all[:, :prompt_len] = transposed(vp_ref[...]).astype(jnp.bfloat16)
        vt_all[:, prompt_len:] = transposed(vo_ref[...]).astype(jnp.bfloat16)

    acc[...] = jnp.zeros_like(acc)
    size = min(FORWARD_CHUNK, prompt_len)
    prompt_keys = [slice(first, first + size) for first in range(0, prompt_len, size)]

    def kv_half(side):
        return jnp.minimum((2 * pair + side) // group, kv_heads - 1)

    def finish(scores, value_columns):
        level = jnp.max(scores[0], axis=0, keepdims=True)
        for part in scores[1:]:
            level = jnp.maximum(level, jnp.max(part, axis=0, keepdims=True))
        total = None
        mixed = None
        for part, columns in zip(scores, value_columns):
            weights = jnp.exp(part - level)
            part_total = jnp.sum(weights, axis=0, keepdims=True)
            part_mixed = nn_dot(columns, weights.astype(jnp.bfloat16))
            total = part_total if total is None else total + part_total
            mixed = part_mixed if mixed is None else mixed + part_mixed
        return mixed / total, level + jnp.log(total)

    both = jnp.concatenate(
        [head_rows(q_ref, 0, PROMPT_BLK, side, kv_half(side)) for side in range(2)], axis=0
    )
    mixed, level = finish(
        [
            seen_prompt(nt_dot(kp_ref[keys, :], both), keys.start, shard_index)
            for keys in prompt_keys
        ],
        [vt_all[:, keys] for keys in prompt_keys],
    )
    mixed = mixed.T
    for side in range(2):
        rows = slice(side * PROMPT_BLK, (side + 1) * PROMPT_BLK)
        acc[:PROMPT_BLK, :] += relane(mixed[rows], kv_half(side), side)
        level_ref[side, :, :PROMPT_BLK] = level[:, rows]

    def step(turn, _):
        side = turn // conts
        number = turn % conts
        half = kv_half(side)
        first_own = PROMPT_BLK + number * CONT_LEN
        for chunk in range(CONT_LEN // QUERY_CHUNK):
            before = chunk * QUERY_CHUNK
            first_row = pl.multiple_of(first_own + before, PROMPT_BLK)
            queries = head_rows(q_ref, first_row, QUERY_CHUNK, side, half)
            scores = [nt_dot(kp_ref[keys, :], queries) for keys in prompt_keys]
            columns = [vt_all[:, keys] for keys in prompt_keys]
            if before:
                start = pl.multiple_of(first_own, PROMPT_BLK)
                scores.append(nt_dot(ko_ref[pl.ds(start, before), :], queries))
                columns.append(
                    vt_all[:, pl.ds(pl.multiple_of(prompt_len + start, PROMPT_BLK), before)]
                )
            scores.append(below_diagonal(nt_dot(ko_ref[pl.ds(first_row, QUERY_CHUNK), :], queries)))
            columns.append(
                vt_all[:, pl.ds(pl.multiple_of(prompt_len + first_row, PROMPT_BLK), QUERY_CHUNK)]
            )
            mixed, level = finish(scores, columns)
            acc[pl.ds(first_row, QUERY_CHUNK), :] += relane(mixed.T, half, side)
            level_ref[side, :, pl.ds(first_row, QUERY_CHUNK)] = level
        return 0

    lax.fori_loop(0, 2 * conts, step, 0)
    mixed_ref[...] = acc[...].astype(jnp.bfloat16)


def attend_backward_body(
    group,
    kv_heads,
    index_ref,
    q_ref,
    grad_ref,
    mixed_ref,
    level_ref,
    cos_ref,
    sin_ref,
    kp_ref,
    vp_ref,
    ko_ref,
    vo_ref,
    dq_ref,
    dprompt_ref,
    down_ref,
    kt_all,
    acc,
    prompt_acc,
):
    pair = pl.program_id(0)
    last = pl.num_programs(0) - 1
    prompt_len = kp_ref.shape[0]
    block_len = ko_ref.shape[0]
    conts = (block_len - PROMPT_BLK) // CONT_LEN
    shard_index = index_ref[0]
    bf16 = jnp.bfloat16

    @pl.when(pair == 0)
    def _():
        kt_all[:, :prompt_len] = transposed(kp_ref[...]).astype(bf16)
        kt_all[:, prompt_len:] = transposed(ko_ref[...]).astype(bf16)
        prompt_acc[...] = jnp.zeros_like(prompt_acc)
        down_ref[...] = jnp.zeros_like(down_ref)

    acc[...] = jnp.zeros_like(acc)

    def kv_half(side):
        return jnp.minimum((2 * pair + side) // group, kv_heads - 1)

    def inner_sums(first_row, count, side):
        rows = pl.ds(first_row, count)
        product = mixed_ref[rows, :].astype(jnp.float32) * grad_ref[rows, :].astype(jnp.float32)
        return jnp.sum(relane(product, side, side).T, axis=0, keepdims=True)

    def part(keys, values, key_columns, queries, grads, level, inner, mask, sums, first_key):
        scores = nt_dot(keys, queries)
        if mask is not None:
            scores = mask(scores)
        probs = jnp.exp(scores - level)
        score_grad = (probs * (nt_dot(values, grads) - inner)).astype(bf16)
        rows = pl.ds(first_key, keys.shape[0])
        sums[rows, :LANES] += nn_dot(score_grad, queries)
        sums[rows, LANES:] += nn_dot(probs.astype(bf16), grads)
        return nn_dot(key_columns, score_grad)

    def prompt_parts(queries, grads, level, inner, masked):
        total = None
        size = min(KEY_CHUNK, prompt_len)
        for first_key in range(0, prompt_len, size):
            rows = slice(first_key, first_key + size)
            mask = (lambda s, f=first_key: seen_prompt(s, f, shard_index)) if masked else None
            piece = part(
                kp_ref[rows, :], vp_ref[rows, :], kt_all[:, rows], queries, grads, level, inner,
                mask, prompt_acc, first_key,
            )
            total = piece if total is None else total + piece
        return total

    both_q, both_g, both_level, both_inner = [], [], [], []
    for side in range(2):
        both_q.append(head_rows(q_ref, 0, PROMPT_BLK, side, kv_half(side)))
        both_g.append(head_rows(grad_ref, 0, PROMPT_BLK, side, kv_half(side)))
        both_level.append(level_ref[side, :, :PROMPT_BLK])
        both_inner.append(inner_sums(0, PROMPT_BLK, side))
    grad_q = prompt_parts(
        jnp.concatenate(both_q, axis=0),
        jnp.concatenate(both_g, axis=0),
        jnp.concatenate(both_level, axis=1),
        jnp.concatenate(both_inner, axis=1),
        True,
    ).T
    for side in range(2):
        rows = slice(side * PROMPT_BLK, (side + 1) * PROMPT_BLK)
        acc[:PROMPT_BLK, :] += relane(grad_q[rows], kv_half(side), side)

    def step(turn, _):
        side = turn // conts
        number = turn % conts
        half = kv_half(side)
        first_own = PROMPT_BLK + number * CONT_LEN
        for chunk in range(CONT_LEN // QUERY_CHUNK):
            before = chunk * QUERY_CHUNK
            first_row = pl.multiple_of(first_own + before, PROMPT_BLK)
            queries = head_rows(q_ref, first_row, QUERY_CHUNK, side, half)
            grads = head_rows(grad_ref, first_row, QUERY_CHUNK, side, half)
            level = level_ref[side, :, pl.ds(first_row, QUERY_CHUNK)]
            inner = inner_sums(first_row, QUERY_CHUNK, side)
            grad_q = prompt_parts(queries, grads, level, inner, False)
            own = [(first_row, QUERY_CHUNK, below_diagonal)]
            if before:
                own.append((pl.multiple_of(first_own, PROMPT_BLK), before, None))
            for start, size, mask in own:
                rows = pl.ds(start, size)
                columns = pl.ds(pl.multiple_of(prompt_len + start, PROMPT_BLK), size)
                grad_q += part(
                    ko_ref[rows, :], vo_ref[rows, :], kt_all[:, columns], queries, grads, level,
                    inner, mask, down_ref, start,
                )
            acc[pl.ds(first_row, QUERY_CHUNK), :] += relane(grad_q.T, half, side)
        return 0

    lax.fori_loop(0, 2 * conts, step, 0)
    grads = acc[...] * HEAD_DIMENSION ** (-0.5)
    half = HEAD_DIMENSION // 2
    lane = lax.broadcasted_iota(jnp.int32, grads.shape, 1)
    swapped = jnp.where(
        lane % HEAD_DIMENSION < half,
        pltpu.roll(grads, LANES - half, 1),
        pltpu.roll(grads, half, 1),
    )
    dq_ref[...] = (grads * cos_ref[...] + swapped * sin_ref[...]).astype(bf16)

    @pl.when(pair == last)
    def _():
        dprompt_ref[...] = prompt_acc[...].astype(bf16)


def pair_specs(block_len, prompt_len):
    by_pair = pl.BlockSpec((block_len, LANES), lambda b, i: (0, b))
    levels = pl.BlockSpec((2, 1, block_len), lambda b, i: (b, 0, 0))
    sources = [
        pl.BlockSpec((prompt_len, LANES), lambda b, i: (0, 0)),
        pl.BlockSpec((prompt_len, LANES), lambda b, i: (0, 1)),
        pl.BlockSpec((block_len, LANES), lambda b, i: (0, 0)),
        pl.BlockSpec((block_len, LANES), lambda b, i: (0, 1)),
    ]
    return by_pair, levels, sources


def attention_cost(block_len, prompt_len, width, products):
    pairs = (block_len * prompt_len + block_len * CONT_LEN // 2) * (width // HEAD_DIMENSION)
    return pl.CostEstimate(
        flops=products * 2 * pairs * 2 * LANES,
        bytes_accessed=8 * block_len * width,
        transcendentals=pairs,
    )


def attend_forward(index, queries, kv_prompt, kv_own, group, kv_heads):
    block_len, width = queries.shape
    prompt_len = kv_prompt.shape[0]
    by_pair, levels, sources = pair_specs(block_len, prompt_len)
    return pl.pallas_call(
        partial(attend_forward_body, group, kv_heads),
        out_shape=[
            jax.ShapeDtypeStruct((block_len, width), jnp.bfloat16),
            jax.ShapeDtypeStruct((width // HEAD_DIMENSION, 1, block_len), jnp.float32),
        ],
        grid_spec=pltpu.PrefetchScalarGridSpec(
            num_scalar_prefetch=1,
            grid=(width // LANES,),
            in_specs=[by_pair] + sources,
            out_specs=[by_pair, levels],
            scratch_shapes=[
                pltpu.VMEM((LANES, prompt_len + block_len), jnp.bfloat16),
                pltpu.VMEM((block_len, LANES), jnp.float32),
            ],
        ),
        compiler_params=pltpu.CompilerParams(
            dimension_semantics=("arbitrary",), vmem_limit_bytes=56 * 1024 * 1024
        ),
        cost_estimate=attention_cost(block_len, prompt_len, width, 2),
        name="attend_forward",
    )(index, queries, kv_prompt, kv_prompt, kv_own, kv_own)


def attend_backward(
    index, queries, grads, mixed, level, tables, kv_prompt, kv_own, group, kv_heads
):
    block_len, width = queries.shape
    prompt_len = kv_prompt.shape[0]
    by_pair, levels, sources = pair_specs(block_len, prompt_len)
    return pl.pallas_call(
        partial(attend_backward_body, group, kv_heads),
        out_shape=[
            jax.ShapeDtypeStruct((block_len, width), jnp.bfloat16),
            jax.ShapeDtypeStruct((prompt_len, 2 * LANES), jnp.bfloat16),
            jax.ShapeDtypeStruct((block_len, 2 * LANES), jnp.float32),
        ],
        grid_spec=pltpu.PrefetchScalarGridSpec(
            num_scalar_prefetch=1,
            grid=(width // LANES,),
            in_specs=[by_pair, by_pair, by_pair, levels]
            + [pl.BlockSpec((block_len, LANES), lambda b, i: (0, 0))] * 2
            + sources,
            out_specs=[
                by_pair,
                pl.BlockSpec((prompt_len, 2 * LANES), lambda b, i: (0, 0)),
                pl.BlockSpec((block_len, 2 * LANES), lambda b, i: (0, 0)),
            ],
            scratch_shapes=[
                pltpu.VMEM((LANES, prompt_len + block_len), jnp.bfloat16),
                pltpu.VMEM((block_len, LANES), jnp.float32),
                pltpu.VMEM((prompt_len, 2 * LANES), jnp.float32),
            ],
        ),
        compiler_params=pltpu.CompilerParams(
            dimension_semantics=("arbitrary",), vmem_limit_bytes=56 * 1024 * 1024
        ),
        cost_estimate=attention_cost(block_len, prompt_len, width, 5),
        name="attend_backward",
    )(index, queries, grads, mixed, level, *tables, kv_prompt, kv_prompt, kv_own, kv_own)


def to_lanes(values):
    extra = -values.shape[1] % LANES
    return jnp.pad(values, ((0, 0), (0, extra))) if extra else values


def exchange(values, axis_name, bit):
    count = lax.axis_size(axis_name)
    return lax.ppermute(values, axis_name, [(i, i ^ bit) for i in range(count)])


def bits_of(number):
    return [1 << k for k in range(number.bit_length()) if number >> k & 1]


def even_blocks(count):
    even = sorted(range(2, count, 2), key=lambda j: (len(bits_of(j)), j))
    singles = [j for j in even if len(bits_of(j)) == 1]
    return singles, even[len(singles) :]


def gather_blocks(own, axis_name, after_first=None):
    count = lax.axis_size(axis_name)
    singles, several = even_blocks(count)
    blocks = {0: own, 1: exchange(own, axis_name, 1)}
    for j in singles:
        blocks[j] = exchange(own, axis_name, j)
    if after_first is not None:
        blocks.update(zip(singles, after_first([blocks[j] for j in singles])))
    for j in several:
        low_bit = bits_of(j)[0]
        blocks[j] = exchange(blocks[j ^ low_bit], axis_name, low_bit)
    for j in singles + several:
        blocks[j + 1] = exchange(blocks[j], axis_name, 1)
    return [blocks[j] for j in range(count)]


def add_rounded(left_side, right_side):
    return (left_side.astype(jnp.float32) + right_side.astype(jnp.float32)).astype(jnp.bfloat16)


def reduce_several(sums, axis_name):
    sums = dict(sums)
    pending = []
    for j in sorted((j for j in sums if len(bits_of(j)) > 1), key=lambda j: (-len(bits_of(j)), j)):
        bit = bits_of(j)[-1]
        piece = exchange(sums[j], axis_name, bit)
        if len(bits_of(j ^ bit)) > 1:
            sums[j ^ bit] = add_rounded(sums[j ^ bit], piece)
        else:
            pending.append((j ^ bit, piece))
    return pending


def reduce_singles(sums, pending, axis_name):
    sums = dict(sums)
    for j, piece in pending:
        sums[j] = add_rounded(sums[j], piece)
    return [sums[0]] + [exchange(sums[j], axis_name, j) for j in sums if len(bits_of(j)) == 1]


def add_all(pieces):
    total = pieces[0].astype(jnp.float32)
    for piece in pieces[1:]:
        total = total + piece.astype(jnp.float32)
    return total


def halves_by_core(values, axis_name):
    count = lax.axis_size(axis_name)
    parity = lax.axis_index(axis_name) % 2
    paired = values.reshape(count // 2, 2, values.shape[0] // count, values.shape[1])
    keep = lax.dynamic_index_in_dim(paired, parity, 1, keepdims=False)
    give = lax.dynamic_index_in_dim(paired, 1 - parity, 1, keepdims=False)
    return keep, give


def chip_sums(keep, arrived, axis_name):
    index = lax.axis_index(axis_name)
    total = add_rounded(keep, arrived)
    return {
        2 * k: lax.dynamic_index_in_dim(total, (index // 2) ^ k, 0, keepdims=False)
        for k in range(total.shape[0])
    }


def reduce_rows(values, axis_name):
    keep, give = halves_by_core(values, axis_name)
    sums = chip_sums(keep, exchange(give, axis_name, 1), axis_name)
    return add_all(reduce_singles(sums, reduce_several(sums, axis_name), axis_name))


def in_order(blocks, index):
    stacked = jnp.stack(blocks)
    return jnp.concatenate(
        [lax.dynamic_index_in_dim(stacked, j ^ index, 0, keepdims=True) for j in range(len(blocks))],
        axis=0,
    )


def expert_body(
    experts_all, index_ref, x_even, x_odd, og_even, og_odd, gate_w, up_w, down_w, *rest
):
    (x_all, og_all, pre_all, hid_all, row_even, row_odd, out_even, out_odd) = rest[-12:-4]
    (row_acc, out_acc, back_acc, _) = rest[-4:]
    expert = pl.program_id(0)
    last = pl.num_programs(0) - 1
    rows = x_even.shape[0]
    width = x_all.shape[1]
    hidden_units = gate_w.shape[2]
    nt_dims = (((1,), (1,)), ((), ()))

    @pl.when(expert == 0)
    def _():
        x_all[:rows, :] = x_even[:, :width]
        x_all[rows:, :] = x_odd[:, :width]
        og_all[:rows, :] = og_even[...]
        og_all[rows:, :] = og_odd[...]

    column = index_ref[0] + expert
    lane = lax.broadcasted_iota(jnp.int32, (2 * rows, LANES), 1)
    coded = jnp.concatenate([x_even[:, width:], x_odd[:, width:]], axis=0).astype(jnp.float32)
    gate = jnp.sum(
        jnp.where((lane == column) | (lane == column + experts_all), coded, 0.0),
        axis=1,
        keepdims=True,
    )
    x_rows = x_all[...]
    og_rows = og_all[...]
    gate_pre = jnp.dot(x_rows, gate_w[0], preferred_element_type=jnp.float32)
    up_pre = jnp.dot(x_rows, up_w[0], preferred_element_type=jnp.float32)
    down_grad = lax.dot_general(og_rows, down_w[0], nt_dims, preferred_element_type=jnp.float32)
    sigmoid = 1.0 / (1.0 + jnp.exp(-gate_pre))
    silu = gate_pre * sigmoid
    hidden = silu * up_pre
    gate_back = jnp.sum(hidden * down_grad, axis=1, keepdims=True)
    hidden_low = (gate * hidden).astype(jnp.bfloat16)
    hidden_grad = gate * down_grad
    gate_pre_low = (
        hidden_grad * up_pre * sigmoid * (1.0 + gate_pre * (1.0 - sigmoid))
    ).astype(jnp.bfloat16)
    up_pre_low = (hidden_grad * silu).astype(jnp.bfloat16)
    hid_all[...] = hidden_low
    pre_all[0, :, :hidden_units] = gate_pre_low
    pre_all[0, :, hidden_units:] = up_pre_low
    row = lax.dot_general(
        gate_pre_low, gate_w[0], nt_dims, preferred_element_type=jnp.float32
    ) + lax.dot_general(up_pre_low, up_w[0], nt_dims, preferred_element_type=jnp.float32)
    out = jnp.dot(hidden_low, down_w[0], preferred_element_type=jnp.float32)
    high = gate_back.astype(jnp.bfloat16).astype(jnp.float32)
    back = jnp.where(lane == column, high, 0.0) + jnp.where(
        lane == column + experts_all, gate_back - high, 0.0
    )

    @pl.when(expert == 0)
    def _():
        row_acc[...] = row
        out_acc[...] = out
        back_acc[...] = back

    @pl.when(expert > 0)
    def _():
        row_acc[...] += row
        out_acc[...] += out
        back_acc[...] += back

    @pl.when(expert == last)
    def _():
        for ref, first in ((row_even, 0), (row_odd, rows)):
            ref[:, :width] = row_acc[first : first + rows, :].astype(jnp.bfloat16)
            ref[:, width:] = back_acc[first : first + rows, :].astype(jnp.bfloat16)
        out_even[...] = out_acc[:rows, :].astype(jnp.bfloat16)
        out_odd[...] = out_acc[rows:, :].astype(jnp.bfloat16)


def expert_pair(position, pairs, first_expert, experts_all, x_pair, og_pair, weights, carried):
    w_gate, w_up, w_down = weights
    rows, coded_width = x_pair[0].shape
    width = coded_width - LANES
    local_experts, _, hidden_units = w_gate.shape
    bf16 = jnp.bfloat16
    whole = 2 * rows
    fixed = lambda e, i: (0, 0)
    once = pl.Buffered(1)
    in_specs = (
        [pl.BlockSpec((rows, coded_width), fixed, pipeline_mode=once)] * 2
        + [pl.BlockSpec((rows, width), fixed, pipeline_mode=once)] * 2
        + [pl.BlockSpec((1, width, hidden_units), lambda e, i: (e, 0, 0))] * 2
        + [pl.BlockSpec((1, hidden_units, width), lambda e, i: (e, 0, 0))]
    )
    operands = [*x_pair, *og_pair, w_gate, w_up, w_down]
    aliases = {}
    if carried is not None:
        in_specs = in_specs + [pl.BlockSpec(memory_space=pl.ANY)] * 4
        aliases = {1 + len(operands) + k: k for k in range(4)}
        operands = operands + list(carried)
    out_shape = [
        jax.ShapeDtypeStruct((pairs * whole, width), bf16),
        jax.ShapeDtypeStruct((pairs * whole, width), bf16),
        jax.ShapeDtypeStruct((local_experts, pairs * whole, 2 * hidden_units), bf16),
        jax.ShapeDtypeStruct((pairs * whole, local_experts * hidden_units), bf16),
        jax.ShapeDtypeStruct((rows, coded_width), bf16),
        jax.ShapeDtypeStruct((rows, coded_width), bf16),
        jax.ShapeDtypeStruct((rows, width), bf16),
        jax.ShapeDtypeStruct((rows, width), bf16),
    ]
    out_specs = [
        pl.BlockSpec((whole, width), lambda e, i: (position, 0)),
        pl.BlockSpec((whole, width), lambda e, i: (position, 0)),
        pl.BlockSpec((1, whole, 2 * hidden_units), lambda e, i: (e, position, 0)),
        pl.BlockSpec((whole, hidden_units), lambda e, i: (position, e)),
        pl.BlockSpec((rows, coded_width), fixed),
        pl.BlockSpec((rows, coded_width), fixed),
        pl.BlockSpec((rows, width), fixed),
        pl.BlockSpec((rows, width), fixed),
    ]
    products = 2 * whole * width * hidden_units * local_experts
    results = pl.pallas_call(
        partial(expert_body, experts_all),
        out_shape=out_shape,
        grid_spec=pltpu.PrefetchScalarGridSpec(
            num_scalar_prefetch=1,
            grid=(local_experts,),
            in_specs=in_specs,
            out_specs=out_specs,
            scratch_shapes=[
                pltpu.VMEM((whole, width), jnp.float32),
                pltpu.VMEM((whole, width), jnp.float32),
                pltpu.VMEM((whole, LANES), jnp.float32),
                pltpu.VMEM((8, LANES), jnp.float32),
            ],
        ),
        input_output_aliases=aliases,
        compiler_params=pltpu.CompilerParams(
            dimension_semantics=("arbitrary",), vmem_limit_bytes=60 * 1024 * 1024
        ),
        cost_estimate=pl.CostEstimate(
            flops=6 * products,
            bytes_accessed=3 * 2 * local_experts * width * hidden_units + 20 * whole * width,
            transcendentals=whole * hidden_units * local_experts,
        ),
        name="experts",
    )(first_expert, *operands)
    return results[:4], results[4:]


def on_device(
    tokens,
    routes,
    w_query,
    key_projection,
    value_projection,
    w_out,
    gain_attn,
    gain_ffn,
    w_router,
    w_gate,
    w_up,
    w_down,
    out_grad,
):
    bf16 = jnp.bfloat16
    shard_count = lax.axis_size("shard")
    seq_count = lax.axis_size("seq")
    shard_index = lax.axis_index("shard")
    seq_index = lax.axis_index("seq")
    tok_count, model_width = tokens.shape
    top_count = routes.shape[1]
    experts_all = w_router.shape[1]
    local_experts = w_gate.shape[0]
    block_len = tok_count * seq_count
    prompt_len = PROMPT_BLK * shard_count
    query_width = w_query.shape[1]
    key_width = key_projection.shape[1]

    singles, several = even_blocks(shard_count)
    small = jnp.concatenate([w_router, gain_attn[:, None], gain_ffn[:, None]], axis=1)
    small = lax.all_gather(small, "seq", axis=0, tiled=True)
    small = lax.all_gather(small, "shard", axis=0, tiled=True)
    router_weight = small[:, :experts_all]
    first_gain = small[:, experts_all].astype(jnp.float32)
    second_gain = small[:, experts_all + 1].astype(jnp.float32)
    block_tokens = lax.all_gather(tokens, "seq", axis=0, tiled=True)
    own_weight = jnp.concatenate([w_query, key_projection, value_projection], axis=1)
    grad_blocks = {0: out_grad}
    near = [exchange(out_grad, "shard", bit) for bit in singles]

    def with_near(blocks):
        blocks, near[:] = lax.optimization_barrier((blocks, near))
        return blocks

    weight_blocks = gather_blocks(own_weight, "shard", with_near)
    grad_blocks.update(zip(singles, near))
    for j in [0] + singles:
        grad_blocks[j + 1] = exchange(grad_blocks[j], "shard", 1)
    out_weight = lax.all_gather(w_out, "seq", axis=0, tiled=True)
    qkv_weight = in_order(weight_blocks, shard_index).reshape(model_width, -1)

    block_rows = jnp.arange(block_len, dtype=jnp.int32)
    cos_table, sin_table = rotary_tables(
        place_of(block_rows, shard_index, prompt_len), HEAD_DIMENSION
    )
    back_tables = [
        jnp.tile(cos_table[:, 0, :], (1, LANES // cos_table.shape[2])),
        jnp.tile(
            jnp.concatenate([sin_table, -sin_table], axis=2)[:, 0, :],
            (1, LANES // HEAD_DIMENSION),
        ),
    ]
    block_tokens, cos_table, sin_table, back_tables = lax.optimization_barrier(
        (block_tokens, cos_table, sin_table, back_tables)
    )
    inputs = block_tokens.astype(jnp.float32)
    first_factor = rms_parts(inputs)
    normed_low = (inputs * first_factor * first_gain).astype(bf16)
    lin = matmul(normed_low, qkv_weight)
    kv_heads = key_width // HEAD_DIMENSION
    group = query_width // key_width
    queries = rotate(lin[:, :query_width], cos_table, sin_table, HEAD_DIMENSION)
    queries = to_lanes((queries * HEAD_DIMENSION ** (-0.5)).astype(bf16))
    key_heads = rotate(
        lin[:, query_width : query_width + key_width], cos_table, sin_table, HEAD_DIMENSION
    ).astype(bf16)
    value_heads = lin[:, query_width + key_width :].astype(bf16)
    kv_own = jnp.concatenate([to_lanes(key_heads), to_lanes(value_heads)], axis=1)
    kv_prompt = lax.all_gather(kv_own[:PROMPT_BLK], "shard", axis=0, tiled=True)
    kv_prompt, out_weight, near = lax.optimization_barrier(
        (kv_prompt, out_weight, [grad_blocks[bit] for bit in singles])
    )
    grad_blocks.update(zip(singles, near))
    out_weight = lax.all_gather(out_weight, "shard", axis=1, tiled=True)
    for j in several:
        low_bit = bits_of(j)[0]
        grad_blocks[j] = exchange(grad_blocks[j ^ low_bit], "shard", low_bit)
    block_number = shard_index.astype(jnp.int32).reshape(1)
    mixed_own, levels = attend_forward(block_number, queries, kv_prompt, kv_own, group, kv_heads)
    sooner = [j for j in range(1, shard_count) if j - 1 not in several]
    mixed_own, held_blocks = lax.optimization_barrier((mixed_own, [grad_blocks[j] for j in sooner]))
    for j, block in zip(sooner, held_blocks):
        grad_blocks[j] = block
    for j in several:
        grad_blocks[j + 1] = exchange(grad_blocks[j], "shard", 1)
    mixed_heads = mixed_own[:, :query_width]
    mixed_tokens = lax.all_to_all(mixed_heads, "seq", split_axis=0, concat_axis=1, tiled=True)

    half_features = model_width // 2
    core_bit = shard_index % 2
    half_weight, mixed_tokens = lax.optimization_barrier(
        (
            lax.dynamic_slice_in_dim(qkv_weight, core_bit * half_features, half_features, axis=0),
            mixed_tokens,
        )
    )
    wide_half = lax.all_gather(half_weight, "seq", axis=0, tiled=False)

    own_inputs = tokens.astype(jnp.float32)
    upstream = out_grad.astype(jnp.float32)
    residual = own_inputs + matmul(mixed_tokens, out_weight)
    second_factor = rms_parts(residual)
    second_low = (residual * second_factor * second_gain).astype(bf16)
    logits = matmul(second_low, router_weight)
    chosen = routes[:, :, None] == jnp.arange(experts_all, dtype=jnp.int32)[None, None, :]
    named = jnp.any(chosen, axis=1)
    gate_dense = jax.nn.softmax(jnp.where(named, logits, negative), axis=-1)
    gate_dense = jnp.where(named, gate_dense, 0.0)

    gate_high = lax.reduce_precision(gate_dense, 8, 7)
    coded = jnp.concatenate(
        [
            second_low,
            gate_high.astype(bf16),
            (gate_dense - gate_high).astype(bf16),
            jnp.zeros((tok_count, LANES - 2 * experts_all), bf16),
        ],
        axis=1,
    )
    row_blocks = {0: coded, 1: exchange(coded, "shard", 1)}
    for bit in singles:
        row_blocks[bit] = exchange(coded, "shard", bit)
    order = [0] + singles[:-1] + several + singles[-1:]
    first_expert = (shard_index * local_experts).astype(jnp.int32).reshape(1)
    carried = None
    pending = []
    row_sums = {}
    out_parts = [None] * shard_count
    for position, j in enumerate(order):
        row_pair = [row_blocks[j], row_blocks[j + 1]]
        if j == order[-1]:
            row_pair, row_sums = lax.optimization_barrier((row_pair, row_sums))
            pending = reduce_several(row_sums, "shard")
        carried, pieces = expert_pair(
            position,
            len(order),
            first_expert,
            experts_all,
            row_pair,
            [grad_blocks[j], grad_blocks[j + 1]],
            (w_gate, w_up, w_down),
            carried,
        )
        if position == 0:
            arrived, pieces = lax.optimization_barrier(
                ([row_blocks[bit] for bit in singles], pieces)
            )
            row_blocks.update(zip(singles, arrived))
            for bit in singles:
                row_blocks[bit + 1] = exchange(row_blocks[bit], "shard", 1)
            for k in several:
                low_bit = bits_of(k)[0]
                row_blocks[k] = exchange(row_blocks[k ^ low_bit], "shard", low_bit)
        elif position == 1:
            arrived, pieces = lax.optimization_barrier(([row_blocks[k] for k in several], pieces))
            row_blocks.update(zip(several, arrived))
            for k in several:
                row_blocks[k + 1] = exchange(row_blocks[k], "shard", 1)
        elif j == order[-1]:
            arrived, pieces, carried = lax.optimization_barrier(
                ([piece for _, piece in pending], pieces, carried)
            )
            pending = [(k, piece) for (k, _), piece in zip(pending, arrived)]
        arrived = exchange(pieces[1], "shard", 1)
        if j != order[-1]:
            row_sums[j] = add_rounded(pieces[0], arrived)
        out_parts[j], out_parts[j + 1] = pieces[2], pieces[3]
    carried, wide_half = lax.optimization_barrier((carried, wide_half))
    all_rows, all_grads, all_pre, all_hidden = carried
    down_sum = transposed_times(all_grads, all_hidden).astype(bf16)
    grad_down = lax.psum_scatter(down_sum, "seq", scatter_dimension=0, tiled=True)
    all_rows, arrived, down_sum = lax.optimization_barrier((all_rows, arrived, down_sum))
    row_sums[order[-1]] = add_rounded(pieces[0], arrived)
    pre_sums = [transposed_times(all_rows, all_pre[0]).astype(bf16)]
    pre_grads = [lax.psum_scatter(pre_sums[0], "seq", scatter_dimension=0, tiled=True)]
    row_pieces = reduce_singles(row_sums, pending, "shard")
    row_pieces, pre_sums[0] = lax.optimization_barrier((row_pieces, pre_sums[0]))
    row_total = add_all(row_pieces)
    row_grad = row_total[:, :model_width]
    gate_grad_dense = (
        row_total[:, model_width : model_width + experts_all]
        + row_total[:, model_width + experts_all : model_width + 2 * experts_all]
    )
    weighted = gate_dense * gate_grad_dense
    logit_grad = weighted - gate_dense * jnp.sum(weighted, axis=-1, keepdims=True)
    second_grad = row_grad + times_transposed(
        logit_grad, router_weight.astype(jnp.float32), highest
    )
    residual_part, grad_gain_ffn = rms_backward(residual, second_factor, second_gain, second_grad)
    residual_grad = upstream + residual_part
    residual_low = residual_grad.astype(bf16)
    mixed_grad_tokens = times_transposed(residual_low, out_weight).astype(bf16)
    other_half = exchange(wide_half, "shard", 1)
    mixed_grad_tokens, out_parts, all_rows, other_half, mixed_late, logit_late = (
        lax.optimization_barrier(
            (mixed_grad_tokens, out_parts, all_rows, other_half, mixed_tokens, logit_grad)
        )
    )
    mixed_grad = lax.all_to_all(mixed_grad_tokens, "seq", split_axis=1, concat_axis=0, tiled=True)
    odd = [exchange(out_parts[j + 1], "shard", 1) for j in order]
    pre_sums += [
        transposed_times(all_rows, all_pre[e]).astype(bf16) for e in range(1, local_experts)
    ]
    pre_grads += [
        lax.psum_scatter(part, "seq", scatter_dimension=0, tiled=True) for part in pre_sums[1:]
    ]
    odd, pre_sums = lax.optimization_barrier((odd, pre_sums))
    odd = dict(zip(order, odd))
    out_sums = {j: add_rounded(out_parts[j], odd[j]) for j in several}
    whole_out = transposed_times(residual_low, mixed_late).astype(bf16)
    whole_keep, whole_give = halves_by_core(whole_out, "shard")
    whole_arrived = exchange(whole_give, "shard", 1)
    grad_router = transposed_times(second_low.astype(jnp.float32), logit_late, highest)
    small_grad = jnp.concatenate([grad_router, grad_gain_ffn[:, None]], axis=1)
    small_keep, small_give = halves_by_core(small_grad.astype(bf16), "shard")
    small_arrived = exchange(small_give, "shard", 1)
    mixed_grad, pre_sums, out_sums, whole_arrived, odd, small_arrived = lax.optimization_barrier(
        (mixed_grad, pre_sums, out_sums, whole_arrived, odd, small_arrived)
    )
    small_sums = chip_sums(small_keep, small_arrived, "shard")
    small_pending = reduce_several(small_sums, "shard")
    out_pending = reduce_several(out_sums, "shard")
    whole_sums = chip_sums(whole_keep, whole_arrived, "shard")
    whole_pending = reduce_several(whole_sums, "shard")

    query_grad, prompt_grad, self_grad = attend_backward(
        block_number,
        queries,
        to_lanes(mixed_grad),
        mixed_own,
        levels,
        back_tables,
        kv_prompt,
        kv_own,
        group,
        kv_heads,
    )
    query_grad, prompt_grad, self_grad, small_arrived, arrived, out_arrived = lax.optimization_barrier(
        (
            query_grad,
            prompt_grad,
            self_grad,
            [piece for _, piece in small_pending],
            [piece for _, piece in whole_pending],
            [piece for _, piece in out_pending],
        )
    )
    whole_pending = [(j, piece) for (j, _), piece in zip(whole_pending, arrived)]
    out_pending = [(j, piece) for (j, _), piece in zip(out_pending, out_arrived)]
    small_pending = [(j, piece) for (j, _), piece in zip(small_pending, small_arrived)]
    small_grad = add_all(reduce_singles(small_sums, small_pending, "shard"))
    lin_query = query_grad[:, :query_width]
    own_prompt = reduce_rows(prompt_grad, "shard")
    key_grad = jnp.concatenate(
        [own_prompt[:, :key_width], self_grad[PROMPT_BLK:, :key_width]], axis=0
    )
    value_low = jnp.concatenate(
        [own_prompt[:, LANES : LANES + key_width], self_grad[PROMPT_BLK:, LANES : LANES + key_width]],
        axis=0,
    ).astype(bf16)
    lin_key = rotate(key_grad, cos_table, -sin_table, HEAD_DIMENSION).astype(bf16)
    lin_all = jnp.concatenate([lin_query, lin_key, value_low], axis=1)
    all_columns = lin_all.shape[1]
    lin_all, whole_sums = lax.optimization_barrier((lin_all, whole_sums))
    lin_tokens = lax.all_to_all(lin_all, "seq", split_axis=0, concat_axis=1, tiled=True)

    keep, give = halves_by_core(transposed_times(normed_low, lin_all).astype(bf16), "shard")
    qkv_sums = chip_sums(keep, exchange(give, "shard", 1), "shard")
    qkv_pending = reduce_several(qkv_sums, "shard")
    qkv_pieces = reduce_singles(qkv_sums, qkv_pending, "shard")
    qkv_pieces, odd = lax.optimization_barrier((qkv_pieces, odd))
    grad_qkv = add_all(qkv_pieces)
    for j in [0] + singles:
        out_sums[j] = add_rounded(out_parts[j], odd[j])
    out_sums = {j: out_sums[j] for j in [0] + singles}
    out_pieces = reduce_singles(out_sums, out_pending, "shard")
    grad_out = add_all(reduce_singles(whole_sums, whole_pending, "shard")).astype(bf16).T
    hidden_units = w_gate.shape[2]
    lin_tokens, grad_down, pre_grads[0] = lax.optimization_barrier(
        (lin_tokens, grad_down, pre_grads[0])
    )
    grad_down = grad_down.T.reshape(local_experts, hidden_units, -1).astype(jnp.float32)
    parts = [0.0, 0.0]
    for k, weight in enumerate((wide_half, other_half)):
        for group_index in range(seq_count):
            columns = slice(group_index * all_columns, (group_index + 1) * all_columns)
            parts[k] = parts[k] + times_transposed(lin_tokens[:, columns], weight[group_index])
    normed_grad = jnp.concatenate(
        [
            jnp.where(core_bit == 0, parts[0], parts[1]),
            jnp.where(core_bit == 0, parts[1], parts[0]),
        ],
        axis=1,
    )
    normed_grad, out_pieces = lax.optimization_barrier((normed_grad, out_pieces))
    output = (residual + add_all(out_pieces)).astype(bf16)
    own_features = own_weight.shape[0]
    gain_own = lax.dynamic_slice_in_dim(first_gain, shard_index * own_features, own_features)
    gain_part = (
        jnp.sum(own_weight.astype(jnp.float32) * grad_qkv[:, :all_columns], axis=1) / gain_own
    )
    grad_query = grad_qkv[:, :query_width]
    grad_key = grad_qkv[:, query_width : query_width + key_width]
    grad_value = grad_qkv[:, query_width + key_width : query_width + 2 * key_width]
    small_grad = jnp.concatenate([small_grad, gain_part[:, None]], axis=1)
    own_small = own_features // seq_count
    small_grad = small_grad.astype(bf16).reshape(seq_count, own_small, -1)
    small_grad = jnp.pad(small_grad, ((0, 0), (0, model_width // seq_count - own_small), (0, 0)))
    last_sum = jnp.concatenate([grad_out, small_grad.reshape(model_width, -1)], axis=1)
    last_sum = lax.psum_scatter(last_sum, "seq", scatter_dimension=0, tiled=True)
    last_sum = last_sum.astype(jnp.float32)
    grad_out = last_sum[:, : w_out.shape[1]]
    small_grad = last_sum[:own_small, w_out.shape[1] :]
    own_factor = rms_parts(own_inputs)
    input_part, _ = rms_backward(own_inputs, own_factor, first_gain, normed_grad)
    tokens_grad = residual_grad + input_part
    pre_grads = [part.astype(jnp.float32) for part in pre_grads]
    grad_gate = jnp.stack([part[:, :hidden_units] for part in pre_grads])
    grad_up = jnp.stack([part[:, hidden_units:] for part in pre_grads])
    return (
        output,
        tokens_grad,
        grad_query,
        grad_key,
        grad_value,
        grad_out,
        small_grad[:, experts_all + 1],
        small_grad[:, experts_all],
        small_grad[:, :experts_all],
        grad_gate,
        grad_up,
        grad_down,
    )


def solution(mesh):
    return jax.shard_map(
        on_device,
        mesh=mesh,
        in_specs=(
            P(("shard", "seq"), None),
            P(("shard", "seq"), None),
            P("shard", "seq"),
            P("shard", "seq"),
            P("shard", "seq"),
            P("seq", "shard"),
            P(("shard", "seq")),
            P(("shard", "seq")),
            P(("shard", "seq"), None),
            P("shard", None, None),
            P("shard", None, None),
            P("shard", None, None),
            P(("shard", "seq"), None),
        ),
        out_specs=(
            P(("shard", "seq"), None),
            P(("shard", "seq"), None),
            P("shard", "seq"),
            P("shard", "seq"),
            P("shard", "seq"),
            P("seq", "shard"),
            P(("shard", "seq")),
            P(("shard", "seq")),
            P(("shard", "seq"), None),
            P("shard", "seq", None),
            P("shard", "seq", None),
            P("shard", None, "seq"),
        ),
        check_vma=False,
    )
```

```python
from functools import partial

import jax
import jax.numpy as jnp
from jax import lax
from jax.experimental import pallas as pl
from jax.experimental.pallas import tpu as pltpu
from jax.sharding import PartitionSpec as P

HEAD_DIMENSION = 64
CONT_LEN = 512
PROMPT_BLK = 128


norm_eps = 1e-05
negative = -1e30
rope_base = 10000.0
highest = lax.Precision.HIGHEST


def rms_norm(values, scaling):
    factor = lax.rsqrt(jnp.mean(values * values, axis=-1, keepdims=True) + norm_eps)
    return values * factor * scaling


def swiglu(gate_pre, up_pre):
    return jax.nn.silu(gate_pre) * up_pre


def rotary_tables(places, head_size):
    half_size = head_size // 2
    frequency = jnp.exp(
        jnp.arange(half_size, dtype=jnp.float32) * (-2.0 * jnp.log(rope_base) / head_size)
    )
    angles = places.astype(jnp.float32)[:, None] * frequency[None, :]
    return (jnp.cos(angles)[:, None, :], jnp.sin(angles)[:, None, :])


def rotate(values, cosine, sine, head_size):
    total_row_count = values.shape[0]
    by_head = values.reshape(total_row_count, -1, head_size)
    half_size = head_size // 2
    first_half = by_head[..., :half_size]
    second_half = by_head[..., half_size:]
    turned = jnp.concatenate(
        [first_half * cosine - second_half * sine, second_half * cosine + first_half * sine],
        axis=-1,
    )
    return turned.reshape(total_row_count, -1)


def place_of(within, block_index, prompt_len):
    return jnp.where(
        within < PROMPT_BLK,
        block_index * PROMPT_BLK + within,
        prompt_len + (within - PROMPT_BLK) % CONT_LEN,
    )


def times_transposed(left_side, right_side, precision=None):
    return lax.dot_general(
        left_side,
        right_side,
        (((1,), (1,)), ((), ())),
        precision=precision,
        preferred_element_type=jnp.float32,
    )


def transposed_times(left_side, right_side, precision=None):
    return lax.dot_general(
        left_side,
        right_side,
        (((0,), (0,)), ((), ())),
        precision=precision,
        preferred_element_type=jnp.float32,
    )


def rms_parts(values):
    return lax.rsqrt(jnp.mean(values * values, axis=-1, keepdims=True) + norm_eps)


def rms_backward(values, factor, scaling, normed_grad):
    scaled = scaling * normed_grad
    inner = jnp.mean(scaled * values, axis=-1, keepdims=True)
    values_grad = factor * scaled - values * (factor * factor * factor) * inner
    gain_grad = jnp.sum(normed_grad * values * factor, axis=0)
    return values_grad, gain_grad


def matmul(left_side, right_side):
    return jnp.dot(left_side, right_side, preferred_element_type=jnp.float32)


LANES = 128


def relane(values, source, target):
    lane = lax.broadcasted_iota(jnp.int32, values.shape, 1)
    swapped = jnp.where(source != target, pltpu.roll(values, HEAD_DIMENSION, 1), values)
    return jnp.where(lane // HEAD_DIMENSION == target, swapped, 0.0)


def head_rows(ref, first, count, source, target):
    values = ref[pl.ds(first, count), :].astype(jnp.float32)
    return relane(values, source, target).astype(jnp.bfloat16)


def nt_dot(left_side, right_side):
    return lax.dot_general(
        left_side, right_side, (((1,), (1,)), ((), ())), preferred_element_type=jnp.float32
    )


def nn_dot(left_side, right_side):
    return jnp.dot(left_side, right_side, preferred_element_type=jnp.float32)


def below_diagonal(scores):
    key_row = lax.broadcasted_iota(jnp.int32, scores.shape, 0)
    query_column = lax.broadcasted_iota(jnp.int32, scores.shape, 1)
    return jnp.where(key_row <= query_column, scores, negative)


def seen_prompt(scores, first_key, shard_index):
    key_row = lax.broadcasted_iota(jnp.int32, scores.shape, 0) + first_key
    query_column = lax.broadcasted_iota(jnp.int32, scores.shape, 1) % PROMPT_BLK
    return jnp.where(key_row <= query_column + shard_index * PROMPT_BLK, scores, negative)


def transposed(values):
    return values.astype(jnp.float32).T


QUERY_CHUNK = 512
KEY_CHUNK = 1024
FORWARD_CHUNK = 256


def attend_forward_body(
    group, kv_heads, index_ref, q_ref, kp_ref, vp_ref, ko_ref, vo_ref, mixed_ref, level_ref, vt_all, acc
):
    pair = pl.program_id(0)
    prompt_len = kp_ref.shape[0]
    block_len = ko_ref.shape[0]
    conts = (block_len - PROMPT_BLK) // CONT_LEN
    shard_index = index_ref[0]

    @pl.when(pair == 0)
    def _():
        vt_all[:, :prompt_len] = transposed(vp_ref[...]).astype(jnp.bfloat16)
        vt_all[:, prompt_len:] = transposed(vo_ref[...]).astype(jnp.bfloat16)

    acc[...] = jnp.zeros_like(acc)
    size = min(FORWARD_CHUNK, prompt_len)
    prompt_keys = [slice(first, first + size) for first in range(0, prompt_len, size)]

    def kv_half(side):
        return jnp.minimum((2 * pair + side) // group, kv_heads - 1)

    def finish(scores, value_columns):
        level = jnp.max(scores[0], axis=0, keepdims=True)
        for part in scores[1:]:
            level = jnp.maximum(level, jnp.max(part, axis=0, keepdims=True))
        total = None
        mixed = None
        for part, columns in zip(scores, value_columns):
            weights = jnp.exp(part - level)
            part_total = jnp.sum(weights, axis=0, keepdims=True)
            part_mixed = nn_dot(columns, weights.astype(jnp.bfloat16))
            total = part_total if total is None else total + part_total
            mixed = part_mixed if mixed is None else mixed + part_mixed
        return mixed / total, level + jnp.log(total)

    both = jnp.concatenate(
        [head_rows(q_ref, 0, PROMPT_BLK, side, kv_half(side)) for side in range(2)], axis=0
    )
    mixed, level = finish(
        [
            seen_prompt(nt_dot(kp_ref[keys, :], both), keys.start, shard_index)
            for keys in prompt_keys
        ],
        [vt_all[:, keys] for keys in prompt_keys],
    )
    mixed = mixed.T
    for side in range(2):
        rows = slice(side * PROMPT_BLK, (side + 1) * PROMPT_BLK)
        acc[:PROMPT_BLK, :] += relane(mixed[rows], kv_half(side), side)
        level_ref[side, :, :PROMPT_BLK] = level[:, rows]

    def step(turn, _):
        side = turn // conts
        number = turn % conts
        half = kv_half(side)
        first_own = PROMPT_BLK + number * CONT_LEN
        for chunk in range(CONT_LEN // QUERY_CHUNK):
            before = chunk * QUERY_CHUNK
            first_row = pl.multiple_of(first_own + before, PROMPT_BLK)
            queries = head_rows(q_ref, first_row, QUERY_CHUNK, side, half)
            scores = [nt_dot(kp_ref[keys, :], queries) for keys in prompt_keys]
            columns = [vt_all[:, keys] for keys in prompt_keys]
            if before:
                start = pl.multiple_of(first_own, PROMPT_BLK)
                scores.append(nt_dot(ko_ref[pl.ds(start, before), :], queries))
                columns.append(
                    vt_all[:, pl.ds(pl.multiple_of(prompt_len + start, PROMPT_BLK), before)]
                )
            scores.append(below_diagonal(nt_dot(ko_ref[pl.ds(first_row, QUERY_CHUNK), :], queries)))
            columns.append(
                vt_all[:, pl.ds(pl.multiple_of(prompt_len + first_row, PROMPT_BLK), QUERY_CHUNK)]
            )
            mixed, level = finish(scores, columns)
            acc[pl.ds(first_row, QUERY_CHUNK), :] += relane(mixed.T, half, side)
            level_ref[side, :, pl.ds(first_row, QUERY_CHUNK)] = level
        return 0

    lax.fori_loop(0, 2 * conts, step, 0)
    mixed_ref[...] = acc[...].astype(jnp.bfloat16)


def attend_backward_body(
    group,
    kv_heads,
    index_ref,
    q_ref,
    grad_ref,
    mixed_ref,
    level_ref,
    cos_ref,
    sin_ref,
    kp_ref,
    vp_ref,
    ko_ref,
    vo_ref,
    dq_ref,
    dprompt_ref,
    down_ref,
    kt_all,
    acc,
    prompt_acc,
):
    pair = pl.program_id(0)
    last = pl.num_programs(0) - 1
    prompt_len = kp_ref.shape[0]
    block_len = ko_ref.shape[0]
    conts = (block_len - PROMPT_BLK) // CONT_LEN
    shard_index = index_ref[0]
    bf16 = jnp.bfloat16

    @pl.when(pair == 0)
    def _():
        kt_all[:, :prompt_len] = transposed(kp_ref[...]).astype(bf16)
        kt_all[:, prompt_len:] = transposed(ko_ref[...]).astype(bf16)
        prompt_acc[...] = jnp.zeros_like(prompt_acc)
        down_ref[...] = jnp.zeros_like(down_ref)

    acc[...] = jnp.zeros_like(acc)

    def kv_half(side):
        return jnp.minimum((2 * pair + side) // group, kv_heads - 1)

    def inner_sums(first_row, count, side):
        rows = pl.ds(first_row, count)
        product = mixed_ref[rows, :].astype(jnp.float32) * grad_ref[rows, :].astype(jnp.float32)
        return jnp.sum(relane(product, side, side).T, axis=0, keepdims=True)

    def part(keys, values, key_columns, queries, grads, level, inner, mask, sums, first_key):
        scores = nt_dot(keys, queries)
        if mask is not None:
            scores = mask(scores)
        probs = jnp.exp(scores - level)
        score_grad = (probs * (nt_dot(values, grads) - inner)).astype(bf16)
        rows = pl.ds(first_key, keys.shape[0])
        sums[rows, :LANES] += nn_dot(score_grad, queries)
        sums[rows, LANES:] += nn_dot(probs.astype(bf16), grads)
        return nn_dot(key_columns, score_grad)

    def prompt_parts(queries, grads, level, inner, masked):
        total = None
        size = min(KEY_CHUNK, prompt_len)
        for first_key in range(0, prompt_len, size):
            rows = slice(first_key, first_key + size)
            mask = (lambda s, f=first_key: seen_prompt(s, f, shard_index)) if masked else None
            piece = part(
                kp_ref[rows, :], vp_ref[rows, :], kt_all[:, rows], queries, grads, level, inner,
                mask, prompt_acc, first_key,
            )
            total = piece if total is None else total + piece
        return total

    both_q, both_g, both_level, both_inner = [], [], [], []
    for side in range(2):
        both_q.append(head_rows(q_ref, 0, PROMPT_BLK, side, kv_half(side)))
        both_g.append(head_rows(grad_ref, 0, PROMPT_BLK, side, kv_half(side)))
        both_level.append(level_ref[side, :, :PROMPT_BLK])
        both_inner.append(inner_sums(0, PROMPT_BLK, side))
    grad_q = prompt_parts(
        jnp.concatenate(both_q, axis=0),
        jnp.concatenate(both_g, axis=0),
        jnp.concatenate(both_level, axis=1),
        jnp.concatenate(both_inner, axis=1),
        True,
    ).T
    for side in range(2):
        rows = slice(side * PROMPT_BLK, (side + 1) * PROMPT_BLK)
        acc[:PROMPT_BLK, :] += relane(grad_q[rows], kv_half(side), side)

    def step(turn, _):
        side = turn // conts
        number = turn % conts
        half = kv_half(side)
        first_own = PROMPT_BLK + number * CONT_LEN
        for chunk in range(CONT_LEN // QUERY_CHUNK):
            before = chunk * QUERY_CHUNK
            first_row = pl.multiple_of(first_own + before, PROMPT_BLK)
            queries = head_rows(q_ref, first_row, QUERY_CHUNK, side, half)
            grads = head_rows(grad_ref, first_row, QUERY_CHUNK, side, half)
            level = level_ref[side, :, pl.ds(first_row, QUERY_CHUNK)]
            inner = inner_sums(first_row, QUERY_CHUNK, side)
            grad_q = prompt_parts(queries, grads, level, inner, False)
            own = [(first_row, QUERY_CHUNK, below_diagonal)]
            if before:
                own.append((pl.multiple_of(first_own, PROMPT_BLK), before, None))
            for start, size, mask in own:
                rows = pl.ds(start, size)
                columns = pl.ds(pl.multiple_of(prompt_len + start, PROMPT_BLK), size)
                grad_q += part(
                    ko_ref[rows, :], vo_ref[rows, :], kt_all[:, columns], queries, grads, level,
                    inner, mask, down_ref, start,
                )
            acc[pl.ds(first_row, QUERY_CHUNK), :] += relane(grad_q.T, half, side)
        return 0

    lax.fori_loop(0, 2 * conts, step, 0)
    grads = acc[...] * HEAD_DIMENSION ** (-0.5)
    half = HEAD_DIMENSION // 2
    lane = lax.broadcasted_iota(jnp.int32, grads.shape, 1)
    swapped = jnp.where(
        lane % HEAD_DIMENSION < half,
        pltpu.roll(grads, LANES - half, 1),
        pltpu.roll(grads, half, 1),
    )
    dq_ref[...] = (grads * cos_ref[...] + swapped * sin_ref[...]).astype(bf16)

    @pl.when(pair == last)
    def _():
        dprompt_ref[...] = prompt_acc[...].astype(bf16)


def pair_specs(block_len, prompt_len):
    by_pair = pl.BlockSpec((block_len, LANES), lambda b, i: (0, b))
    levels = pl.BlockSpec((2, 1, block_len), lambda b, i: (b, 0, 0))
    sources = [
        pl.BlockSpec((prompt_len, LANES), lambda b, i: (0, 0)),
        pl.BlockSpec((prompt_len, LANES), lambda b, i: (0, 1)),
        pl.BlockSpec((block_len, LANES), lambda b, i: (0, 0)),
        pl.BlockSpec((block_len, LANES), lambda b, i: (0, 1)),
    ]
    return by_pair, levels, sources


def attention_cost(block_len, prompt_len, width, products):
    pairs = (block_len * prompt_len + block_len * CONT_LEN // 2) * (width // HEAD_DIMENSION)
    return pl.CostEstimate(
        flops=products * 2 * pairs * 2 * LANES,
        bytes_accessed=8 * block_len * width,
        transcendentals=pairs,
    )


def attend_forward(index, queries, kv_prompt, kv_own, group, kv_heads):
    block_len, width = queries.shape
    prompt_len = kv_prompt.shape[0]
    by_pair, levels, sources = pair_specs(block_len, prompt_len)
    return pl.pallas_call(
        partial(attend_forward_body, group, kv_heads),
        out_shape=[
            jax.ShapeDtypeStruct((block_len, width), jnp.bfloat16),
            jax.ShapeDtypeStruct((width // HEAD_DIMENSION, 1, block_len), jnp.float32),
        ],
        grid_spec=pltpu.PrefetchScalarGridSpec(
            num_scalar_prefetch=1,
            grid=(width // LANES,),
            in_specs=[by_pair] + sources,
            out_specs=[by_pair, levels],
            scratch_shapes=[
                pltpu.VMEM((LANES, prompt_len + block_len), jnp.bfloat16),
                pltpu.VMEM((block_len, LANES), jnp.float32),
            ],
        ),
        compiler_params=pltpu.CompilerParams(
            dimension_semantics=("arbitrary",), vmem_limit_bytes=56 * 1024 * 1024
        ),
        cost_estimate=attention_cost(block_len, prompt_len, width, 2),
        name="attend_forward",
    )(index, queries, kv_prompt, kv_prompt, kv_own, kv_own)


def attend_backward(
    index, queries, grads, mixed, level, tables, kv_prompt, kv_own, group, kv_heads
):
    block_len, width = queries.shape
    prompt_len = kv_prompt.shape[0]
    by_pair, levels, sources = pair_specs(block_len, prompt_len)
    return pl.pallas_call(
        partial(attend_backward_body, group, kv_heads),
        out_shape=[
            jax.ShapeDtypeStruct((block_len, width), jnp.bfloat16),
            jax.ShapeDtypeStruct((prompt_len, 2 * LANES), jnp.bfloat16),
            jax.ShapeDtypeStruct((block_len, 2 * LANES), jnp.float32),
        ],
        grid_spec=pltpu.PrefetchScalarGridSpec(
            num_scalar_prefetch=1,
            grid=(width // LANES,),
            in_specs=[by_pair, by_pair, by_pair, levels]
            + [pl.BlockSpec((block_len, LANES), lambda b, i: (0, 0))] * 2
            + sources,
            out_specs=[
                by_pair,
                pl.BlockSpec((prompt_len, 2 * LANES), lambda b, i: (0, 0)),
                pl.BlockSpec((block_len, 2 * LANES), lambda b, i: (0, 0)),
            ],
            scratch_shapes=[
                pltpu.VMEM((LANES, prompt_len + block_len), jnp.bfloat16),
                pltpu.VMEM((block_len, LANES), jnp.float32),
                pltpu.VMEM((prompt_len, 2 * LANES), jnp.float32),
            ],
        ),
        compiler_params=pltpu.CompilerParams(
            dimension_semantics=("arbitrary",), vmem_limit_bytes=56 * 1024 * 1024
        ),
        cost_estimate=attention_cost(block_len, prompt_len, width, 5),
        name="attend_backward",
    )(index, queries, grads, mixed, level, *tables, kv_prompt, kv_prompt, kv_own, kv_own)


def to_lanes(values):
    extra = -values.shape[1] % LANES
    return jnp.pad(values, ((0, 0), (0, extra))) if extra else values


def exchange(values, axis_name, bit):
    count = lax.axis_size(axis_name)
    return lax.ppermute(values, axis_name, [(i, i ^ bit) for i in range(count)])


def bits_of(number):
    return [1 << k for k in range(number.bit_length()) if number >> k & 1]


def even_blocks(count):
    even = sorted(range(2, count, 2), key=lambda j: (len(bits_of(j)), j))
    singles = [j for j in even if len(bits_of(j)) == 1]
    return singles, even[len(singles) :]


def gather_blocks(own, axis_name, after_first=None):
    count = lax.axis_size(axis_name)
    singles, several = even_blocks(count)
    blocks = {0: own, 1: exchange(own, axis_name, 1)}
    for j in singles:
        blocks[j] = exchange(own, axis_name, j)
    if after_first is not None:
        blocks.update(zip(singles, after_first([blocks[j] for j in singles])))
    for j in several:
        low_bit = bits_of(j)[0]
        blocks[j] = exchange(blocks[j ^ low_bit], axis_name, low_bit)
    for j in singles + several:
        blocks[j + 1] = exchange(blocks[j], axis_name, 1)
    return [blocks[j] for j in range(count)]


def add_rounded(left_side, right_side):
    return (left_side.astype(jnp.float32) + right_side.astype(jnp.float32)).astype(jnp.bfloat16)


def reduce_several(sums, axis_name):
    sums = dict(sums)
    pending = []
    for j in sorted((j for j in sums if len(bits_of(j)) > 1), key=lambda j: (-len(bits_of(j)), j)):
        bit = bits_of(j)[-1]
        piece = exchange(sums[j], axis_name, bit)
        if len(bits_of(j ^ bit)) > 1:
            sums[j ^ bit] = add_rounded(sums[j ^ bit], piece)
        else:
            pending.append((j ^ bit, piece))
    return pending


def reduce_singles(sums, pending, axis_name):
    sums = dict(sums)
    for j, piece in pending:
        sums[j] = add_rounded(sums[j], piece)
    return [sums[0]] + [exchange(sums[j], axis_name, j) for j in sums if len(bits_of(j)) == 1]


def add_all(pieces):
    total = pieces[0].astype(jnp.float32)
    for piece in pieces[1:]:
        total = total + piece.astype(jnp.float32)
    return total


def halves_by_core(values, axis_name):
    count = lax.axis_size(axis_name)
    parity = lax.axis_index(axis_name) % 2
    paired = values.reshape(count // 2, 2, values.shape[0] // count, values.shape[1])
    keep = lax.dynamic_index_in_dim(paired, parity, 1, keepdims=False)
    give = lax.dynamic_index_in_dim(paired, 1 - parity, 1, keepdims=False)
    return keep, give


def chip_sums(keep, arrived, axis_name):
    index = lax.axis_index(axis_name)
    total = add_rounded(keep, arrived)
    return {
        2 * k: lax.dynamic_index_in_dim(total, (index // 2) ^ k, 0, keepdims=False)
        for k in range(total.shape[0])
    }


def reduce_rows(values, axis_name):
    keep, give = halves_by_core(values, axis_name)
    sums = chip_sums(keep, exchange(give, axis_name, 1), axis_name)
    return add_all(reduce_singles(sums, reduce_several(sums, axis_name), axis_name))


def in_order(blocks, index):
    stacked = jnp.stack(blocks)
    return jnp.concatenate(
        [lax.dynamic_index_in_dim(stacked, j ^ index, 0, keepdims=True) for j in range(len(blocks))],
        axis=0,
    )


def expert_body(
    experts_all, index_ref, x_even, x_odd, og_even, og_odd, gate_w, up_w, down_w, *rest
):
    (x_all, og_all, pre_all, hid_all, row_even, row_odd, out_even, out_odd) = rest[-12:-4]
    (row_acc, out_acc, back_acc, _) = rest[-4:]
    expert = pl.program_id(0)
    last = pl.num_programs(0) - 1
    rows = x_even.shape[0]
    width = x_all.shape[1]
    hidden_units = gate_w.shape[2]
    nt_dims = (((1,), (1,)), ((), ()))

    @pl.when(expert == 0)
    def _():
        x_all[:rows, :] = x_even[:, :width]
        x_all[rows:, :] = x_odd[:, :width]
        og_all[:rows, :] = og_even[...]
        og_all[rows:, :] = og_odd[...]

    column = index_ref[0] + expert
    lane = lax.broadcasted_iota(jnp.int32, (2 * rows, LANES), 1)
    coded = jnp.concatenate([x_even[:, width:], x_odd[:, width:]], axis=0).astype(jnp.float32)
    gate = jnp.sum(
        jnp.where((lane == column) | (lane == column + experts_all), coded, 0.0),
        axis=1,
        keepdims=True,
    )
    x_rows = x_all[...]
    og_rows = og_all[...]
    gate_pre = jnp.dot(x_rows, gate_w[0], preferred_element_type=jnp.float32)
    up_pre = jnp.dot(x_rows, up_w[0], preferred_element_type=jnp.float32)
    down_grad = lax.dot_general(og_rows, down_w[0], nt_dims, preferred_element_type=jnp.float32)
    sigmoid = 1.0 / (1.0 + jnp.exp(-gate_pre))
    silu = gate_pre * sigmoid
    hidden = silu * up_pre
    gate_back = jnp.sum(hidden * down_grad, axis=1, keepdims=True)
    hidden_low = (gate * hidden).astype(jnp.bfloat16)
    hidden_grad = gate * down_grad
    gate_pre_low = (
        hidden_grad * up_pre * sigmoid * (1.0 + gate_pre * (1.0 - sigmoid))
    ).astype(jnp.bfloat16)
    up_pre_low = (hidden_grad * silu).astype(jnp.bfloat16)
    hid_all[...] = hidden_low
    pre_all[0, :, :hidden_units] = gate_pre_low
    pre_all[0, :, hidden_units:] = up_pre_low
    row = lax.dot_general(
        gate_pre_low, gate_w[0], nt_dims, preferred_element_type=jnp.float32
    ) + lax.dot_general(up_pre_low, up_w[0], nt_dims, preferred_element_type=jnp.float32)
    out = jnp.dot(hidden_low, down_w[0], preferred_element_type=jnp.float32)
    high = gate_back.astype(jnp.bfloat16).astype(jnp.float32)
    back = jnp.where(lane == column, high, 0.0) + jnp.where(
        lane == column + experts_all, gate_back - high, 0.0
    )

    @pl.when(expert == 0)
    def _():
        row_acc[...] = row
        out_acc[...] = out
        back_acc[...] = back

    @pl.when(expert > 0)
    def _():
        row_acc[...] += row
        out_acc[...] += out
        back_acc[...] += back

    @pl.when(expert == last)
    def _():
        for ref, first in ((row_even, 0), (row_odd, rows)):
            ref[:, :width] = row_acc[first : first + rows, :].astype(jnp.bfloat16)
            ref[:, width:] = back_acc[first : first + rows, :].astype(jnp.bfloat16)
        out_even[...] = out_acc[:rows, :].astype(jnp.bfloat16)
        out_odd[...] = out_acc[rows:, :].astype(jnp.bfloat16)


def expert_pair(position, pairs, first_expert, experts_all, x_pair, og_pair, weights, carried):
    w_gate, w_up, w_down = weights
    rows, coded_width = x_pair[0].shape
    width = coded_width - LANES
    local_experts, _, hidden_units = w_gate.shape
    bf16 = jnp.bfloat16
    whole = 2 * rows
    fixed = lambda e, i: (0, 0)
    once = pl.Buffered(1)
    in_specs = (
        [pl.BlockSpec((rows, coded_width), fixed, pipeline_mode=once)] * 2
        + [pl.BlockSpec((rows, width), fixed, pipeline_mode=once)] * 2
        + [pl.BlockSpec((1, width, hidden_units), lambda e, i: (e, 0, 0))] * 2
        + [pl.BlockSpec((1, hidden_units, width), lambda e, i: (e, 0, 0))]
    )
    operands = [*x_pair, *og_pair, w_gate, w_up, w_down]
    aliases = {}
    if carried is not None:
        in_specs = in_specs + [pl.BlockSpec(memory_space=pl.ANY)] * 4
        aliases = {1 + len(operands) + k: k for k in range(4)}
        operands = operands + list(carried)
    out_shape = [
        jax.ShapeDtypeStruct((pairs * whole, width), bf16),
        jax.ShapeDtypeStruct((pairs * whole, width), bf16),
        jax.ShapeDtypeStruct((local_experts, pairs * whole, 2 * hidden_units), bf16),
        jax.ShapeDtypeStruct((pairs * whole, local_experts * hidden_units), bf16),
        jax.ShapeDtypeStruct((rows, coded_width), bf16),
        jax.ShapeDtypeStruct((rows, coded_width), bf16),
        jax.ShapeDtypeStruct((rows, width), bf16),
        jax.ShapeDtypeStruct((rows, width), bf16),
    ]
    out_specs = [
        pl.BlockSpec((whole, width), lambda e, i: (position, 0)),
        pl.BlockSpec((whole, width), lambda e, i: (position, 0)),
        pl.BlockSpec((1, whole, 2 * hidden_units), lambda e, i: (e, position, 0)),
        pl.BlockSpec((whole, hidden_units), lambda e, i: (position, e)),
        pl.BlockSpec((rows, coded_width), fixed),
        pl.BlockSpec((rows, coded_width), fixed),
        pl.BlockSpec((rows, width), fixed),
        pl.BlockSpec((rows, width), fixed),
    ]
    products = 2 * whole * width * hidden_units * local_experts
    results = pl.pallas_call(
        partial(expert_body, experts_all),
        out_shape=out_shape,
        grid_spec=pltpu.PrefetchScalarGridSpec(
            num_scalar_prefetch=1,
            grid=(local_experts,),
            in_specs=in_specs,
            out_specs=out_specs,
            scratch_shapes=[
                pltpu.VMEM((whole, width), jnp.float32),
                pltpu.VMEM((whole, width), jnp.float32),
                pltpu.VMEM((whole, LANES), jnp.float32),
                pltpu.VMEM((8, LANES), jnp.float32),
            ],
        ),
        input_output_aliases=aliases,
        compiler_params=pltpu.CompilerParams(
            dimension_semantics=("arbitrary",), vmem_limit_bytes=60 * 1024 * 1024
        ),
        cost_estimate=pl.CostEstimate(
            flops=6 * products,
            bytes_accessed=3 * 2 * local_experts * width * hidden_units + 20 * whole * width,
            transcendentals=whole * hidden_units * local_experts,
        ),
        name="experts",
    )(first_expert, *operands)
    return results[:4], results[4:]


def on_device(
    tokens,
    routes,
    w_query,
    key_projection,
    value_projection,
    w_out,
    gain_attn,
    gain_ffn,
    w_router,
    w_gate,
    w_up,
    w_down,
    out_grad,
):
    bf16 = jnp.bfloat16
    shard_count = lax.axis_size("shard")
    seq_count = lax.axis_size("seq")
    shard_index = lax.axis_index("shard")
    seq_index = lax.axis_index("seq")
    tok_count, model_width = tokens.shape
    top_count = routes.shape[1]
    experts_all = w_router.shape[1]
    local_experts = w_gate.shape[0]
    block_len = tok_count * seq_count
    prompt_len = PROMPT_BLK * shard_count
    query_width = w_query.shape[1]
    key_width = key_projection.shape[1]

    singles, several = even_blocks(shard_count)
    small = jnp.concatenate([w_router, gain_attn[:, None], gain_ffn[:, None]], axis=1)
    small = lax.all_gather(small, "seq", axis=0, tiled=True)
    small = lax.all_gather(small, "shard", axis=0, tiled=True)
    router_weight = small[:, :experts_all]
    first_gain = small[:, experts_all].astype(jnp.float32)
    second_gain = small[:, experts_all + 1].astype(jnp.float32)
    block_tokens = lax.all_gather(tokens, "seq", axis=0, tiled=True)
    own_weight = jnp.concatenate([w_query, key_projection, value_projection], axis=1)
    grad_blocks = {0: out_grad}
    near = [exchange(out_grad, "shard", bit) for bit in singles]

    def with_near(blocks):
        blocks, near[:] = lax.optimization_barrier((blocks, near))
        return blocks

    weight_blocks = gather_blocks(own_weight, "shard", with_near)
    grad_blocks.update(zip(singles, near))
    for j in [0] + singles:
        grad_blocks[j + 1] = exchange(grad_blocks[j], "shard", 1)
    out_weight = lax.all_gather(w_out, "seq", axis=0, tiled=True)
    qkv_weight = in_order(weight_blocks, shard_index).reshape(model_width, -1)

    block_rows = jnp.arange(block_len, dtype=jnp.int32)
    cos_table, sin_table = rotary_tables(
        place_of(block_rows, shard_index, prompt_len), HEAD_DIMENSION
    )
    back_tables = [
        jnp.tile(cos_table[:, 0, :], (1, LANES // cos_table.shape[2])),
        jnp.tile(
            jnp.concatenate([sin_table, -sin_table], axis=2)[:, 0, :],
            (1, LANES // HEAD_DIMENSION),
        ),
    ]
    block_tokens, cos_table, sin_table, back_tables = lax.optimization_barrier(
        (block_tokens, cos_table, sin_table, back_tables)
    )
    inputs = block_tokens.astype(jnp.float32)
    first_factor = rms_parts(inputs)
    normed_low = (inputs * first_factor * first_gain).astype(bf16)
    lin = matmul(normed_low, qkv_weight)
    kv_heads = key_width // HEAD_DIMENSION
    group = query_width // key_width
    queries = rotate(lin[:, :query_width], cos_table, sin_table, HEAD_DIMENSION)
    queries = to_lanes((queries * HEAD_DIMENSION ** (-0.5)).astype(bf16))
    key_heads = rotate(
        lin[:, query_width : query_width + key_width], cos_table, sin_table, HEAD_DIMENSION
    ).astype(bf16)
    value_heads = lin[:, query_width + key_width :].astype(bf16)
    kv_own = jnp.concatenate([to_lanes(key_heads), to_lanes(value_heads)], axis=1)
    kv_prompt = lax.all_gather(kv_own[:PROMPT_BLK], "shard", axis=0, tiled=True)
    kv_prompt, out_weight, near = lax.optimization_barrier(
        (kv_prompt, out_weight, [grad_blocks[bit] for bit in singles])
    )
    grad_blocks.update(zip(singles, near))
    out_weight = lax.all_gather(out_weight, "shard", axis=1, tiled=True)
    for j in several:
        low_bit = bits_of(j)[0]
        grad_blocks[j] = exchange(grad_blocks[j ^ low_bit], "shard", low_bit)
    block_number = shard_index.astype(jnp.int32).reshape(1)
    mixed_own, levels = attend_forward(block_number, queries, kv_prompt, kv_own, group, kv_heads)
    sooner = [j for j in range(1, shard_count) if j - 1 not in several]
    mixed_own, held_blocks = lax.optimization_barrier((mixed_own, [grad_blocks[j] for j in sooner]))
    for j, block in zip(sooner, held_blocks):
        grad_blocks[j] = block
    for j in several:
        grad_blocks[j + 1] = exchange(grad_blocks[j], "shard", 1)
    mixed_heads = mixed_own[:, :query_width]
    mixed_tokens = lax.all_to_all(mixed_heads, "seq", split_axis=0, concat_axis=1, tiled=True)

    half_features = model_width // 2
    core_bit = shard_index % 2
    half_weight, mixed_tokens = lax.optimization_barrier(
        (
            lax.dynamic_slice_in_dim(qkv_weight, core_bit * half_features, half_features, axis=0),
            mixed_tokens,
        )
    )
    wide_half = lax.all_gather(half_weight, "seq", axis=0, tiled=False)

    own_inputs = tokens.astype(jnp.float32)
    upstream = out_grad.astype(jnp.float32)
    residual = own_inputs + matmul(mixed_tokens, out_weight)
    second_factor = rms_parts(residual)
    second_low = (residual * second_factor * second_gain).astype(bf16)
    logits = matmul(second_low, router_weight)
    chosen = routes[:, :, None] == jnp.arange(experts_all, dtype=jnp.int32)[None, None, :]
    named = jnp.any(chosen, axis=1)
    gate_dense = jax.nn.softmax(jnp.where(named, logits, negative), axis=-1)
    gate_dense = jnp.where(named, gate_dense, 0.0)

    gate_high = lax.reduce_precision(gate_dense, 8, 7)
    coded = jnp.concatenate(
        [
            second_low,
            gate_high.astype(bf16),
            (gate_dense - gate_high).astype(bf16),
            jnp.zeros((tok_count, LANES - 2 * experts_all), bf16),
        ],
        axis=1,
    )
    row_blocks = {0: coded, 1: exchange(coded, "shard", 1)}
    for bit in singles:
        row_blocks[bit] = exchange(coded, "shard", bit)
    order = [0] + singles[:-1] + several + singles[-1:]
    first_expert = (shard_index * local_experts).astype(jnp.int32).reshape(1)
    carried = None
    pending = []
    row_sums = {}
    out_parts = [None] * shard_count
    for position, j in enumerate(order):
        row_pair = [row_blocks[j], row_blocks[j + 1]]
        if j == order[-1]:
            row_pair, row_sums = lax.optimization_barrier((row_pair, row_sums))
            pending = reduce_several(row_sums, "shard")
        carried, pieces = expert_pair(
            position,
            len(order),
            first_expert,
            experts_all,
            row_pair,
            [grad_blocks[j], grad_blocks[j + 1]],
            (w_gate, w_up, w_down),
            carried,
        )
        if position == 0:
            arrived, pieces = lax.optimization_barrier(
                ([row_blocks[bit] for bit in singles], pieces)
            )
            row_blocks.update(zip(singles, arrived))
            for bit in singles:
                row_blocks[bit + 1] = exchange(row_blocks[bit], "shard", 1)
            for k in several:
                low_bit = bits_of(k)[0]
                row_blocks[k] = exchange(row_blocks[k ^ low_bit], "shard", low_bit)
        elif position == 1:
            arrived, pieces = lax.optimization_barrier(([row_blocks[k] for k in several], pieces))
            row_blocks.update(zip(several, arrived))
            for k in several:
                row_blocks[k + 1] = exchange(row_blocks[k], "shard", 1)
        elif j == order[-1]:
            arrived, pieces, carried = lax.optimization_barrier(
                ([piece for _, piece in pending], pieces, carried)
            )
            pending = [(k, piece) for (k, _), piece in zip(pending, arrived)]
        arrived = exchange(pieces[1], "shard", 1)
        if j != order[-1]:
            row_sums[j] = add_rounded(pieces[0], arrived)
        out_parts[j], out_parts[j + 1] = pieces[2], pieces[3]
    carried, wide_half = lax.optimization_barrier((carried, wide_half))
    all_rows, all_grads, all_pre, all_hidden = carried
    down_sum = transposed_times(all_grads, all_hidden).astype(bf16)
    grad_down = lax.psum_scatter(down_sum, "seq", scatter_dimension=0, tiled=True)
    all_rows, arrived, down_sum = lax.optimization_barrier((all_rows, arrived, down_sum))
    row_sums[order[-1]] = add_rounded(pieces[0], arrived)
    pre_sums = [transposed_times(all_rows, all_pre[0]).astype(bf16)]
    pre_grads = [lax.psum_scatter(pre_sums[0], "seq", scatter_dimension=0, tiled=True)]
    row_pieces = reduce_singles(row_sums, pending, "shard")
    row_pieces, pre_sums[0] = lax.optimization_barrier((row_pieces, pre_sums[0]))
    row_total = add_all(row_pieces)
    row_grad = row_total[:, :model_width]
    gate_grad_dense = (
        row_total[:, model_width : model_width + experts_all]
        + row_total[:, model_width + experts_all : model_width + 2 * experts_all]
    )
    weighted = gate_dense * gate_grad_dense
    logit_grad = weighted - gate_dense * jnp.sum(weighted, axis=-1, keepdims=True)
    second_grad = row_grad + times_transposed(
        logit_grad, router_weight.astype(jnp.float32), highest
    )
    residual_part, grad_gain_ffn = rms_backward(residual, second_factor, second_gain, second_grad)
    residual_grad = upstream + residual_part
    residual_low = residual_grad.astype(bf16)
    mixed_grad_tokens = times_transposed(residual_low, out_weight).astype(bf16)
    other_half = exchange(wide_half, "shard", 1)
    mixed_grad_tokens, out_parts, all_rows, other_half, mixed_late, logit_late = (
        lax.optimization_barrier(
            (mixed_grad_tokens, out_parts, all_rows, other_half, mixed_tokens, logit_grad)
        )
    )
    mixed_grad = lax.all_to_all(mixed_grad_tokens, "seq", split_axis=1, concat_axis=0, tiled=True)
    odd = [exchange(out_parts[j + 1], "shard", 1) for j in order]
    pre_sums += [
        transposed_times(all_rows, all_pre[e]).astype(bf16) for e in range(1, local_experts)
    ]
    pre_grads += [
        lax.psum_scatter(part, "seq", scatter_dimension=0, tiled=True) for part in pre_sums[1:]
    ]
    odd, pre_sums = lax.optimization_barrier((odd, pre_sums))
    odd = dict(zip(order, odd))
    out_sums = {j: add_rounded(out_parts[j], odd[j]) for j in several}
    whole_out = transposed_times(residual_low, mixed_late).astype(bf16)
    whole_keep, whole_give = halves_by_core(whole_out, "shard")
    whole_arrived = exchange(whole_give, "shard", 1)
    grad_router = transposed_times(second_low.astype(jnp.float32), logit_late, highest)
    small_grad = jnp.concatenate([grad_router, grad_gain_ffn[:, None]], axis=1)
    small_keep, small_give = halves_by_core(small_grad.astype(bf16), "shard")
    small_arrived = exchange(small_give, "shard", 1)
    mixed_grad, pre_sums, out_sums, whole_arrived, odd, small_arrived = lax.optimization_barrier(
        (mixed_grad, pre_sums, out_sums, whole_arrived, odd, small_arrived)
    )
    small_sums = chip_sums(small_keep, small_arrived, "shard")
    small_pending = reduce_several(small_sums, "shard")
    out_pending = reduce_several(out_sums, "shard")
    whole_sums = chip_sums(whole_keep, whole_arrived, "shard")
    whole_pending = reduce_several(whole_sums, "shard")

    query_grad, prompt_grad, self_grad = attend_backward(
        block_number,
        queries,
        to_lanes(mixed_grad),
        mixed_own,
        levels,
        back_tables,
        kv_prompt,
        kv_own,
        group,
        kv_heads,
    )
    query_grad, prompt_grad, self_grad, small_arrived, arrived, out_arrived = lax.optimization_barrier(
        (
            query_grad,
            prompt_grad,
            self_grad,
            [piece for _, piece in small_pending],
            [piece for _, piece in whole_pending],
            [piece for _, piece in out_pending],
        )
    )
    whole_pending = [(j, piece) for (j, _), piece in zip(whole_pending, arrived)]
    out_pending = [(j, piece) for (j, _), piece in zip(out_pending, out_arrived)]
    small_pending = [(j, piece) for (j, _), piece in zip(small_pending, small_arrived)]
    small_grad = add_all(reduce_singles(small_sums, small_pending, "shard"))
    lin_query = query_grad[:, :query_width]
    own_prompt = reduce_rows(prompt_grad, "shard")
    key_grad = jnp.concatenate(
        [own_prompt[:, :key_width], self_grad[PROMPT_BLK:, :key_width]], axis=0
    )
    value_low = jnp.concatenate(
        [own_prompt[:, LANES : LANES + key_width], self_grad[PROMPT_BLK:, LANES : LANES + key_width]],
        axis=0,
    ).astype(bf16)
    lin_key = rotate(key_grad, cos_table, -sin_table, HEAD_DIMENSION).astype(bf16)
    lin_all = jnp.concatenate([lin_query, lin_key, value_low], axis=1)
    all_columns = lin_all.shape[1]
    lin_all, whole_sums = lax.optimization_barrier((lin_all, whole_sums))
    lin_tokens = lax.all_to_all(lin_all, "seq", split_axis=0, concat_axis=1, tiled=True)

    keep, give = halves_by_core(transposed_times(normed_low, lin_all).astype(bf16), "shard")
    qkv_sums = chip_sums(keep, exchange(give, "shard", 1), "shard")
    qkv_pending = reduce_several(qkv_sums, "shard")
    arrived, odd = lax.optimization_barrier(([piece for _, piece in qkv_pending], odd))
    qkv_pending = [(j, piece) for (j, _), piece in zip(qkv_pending, arrived)]
    grad_qkv = add_all(reduce_singles(qkv_sums, qkv_pending, "shard"))
    for j in [0] + singles:
        out_sums[j] = add_rounded(out_parts[j], odd[j])
    out_sums = {j: out_sums[j] for j in [0] + singles}
    out_pieces = reduce_singles(out_sums, out_pending, "shard")
    grad_out = add_all(reduce_singles(whole_sums, whole_pending, "shard")).astype(bf16).T
    hidden_units = w_gate.shape[2]
    grad_down, first_sums = lax.optimization_barrier((grad_down, pre_grads[0], grad_qkv))[:2]
    grad_down = grad_down.T.reshape(local_experts, hidden_units, -1).astype(jnp.float32)
    pre_grads[0] = first_sums.astype(jnp.float32)
    lin_tokens, grad_down, pre_grads[0] = lax.optimization_barrier(
        (lin_tokens, grad_down, pre_grads[0])
    )
    parts = [0.0, 0.0]
    for k, weight in enumerate((wide_half, other_half)):
        for group_index in range(seq_count):
            columns = slice(group_index * all_columns, (group_index + 1) * all_columns)
            parts[k] = parts[k] + times_transposed(lin_tokens[:, columns], weight[group_index])
    normed_grad = jnp.concatenate(
        [
            jnp.where(core_bit == 0, parts[0], parts[1]),
            jnp.where(core_bit == 0, parts[1], parts[0]),
        ],
        axis=1,
    )
    normed_grad, out_pieces = lax.optimization_barrier((normed_grad, out_pieces))
    output = (residual + add_all(out_pieces)).astype(bf16)
    own_features = own_weight.shape[0]
    gain_own = lax.dynamic_slice_in_dim(first_gain, shard_index * own_features, own_features)
    gain_part = (
        jnp.sum(own_weight.astype(jnp.float32) * grad_qkv[:, :all_columns], axis=1) / gain_own
    )
    grad_query = grad_qkv[:, :query_width]
    grad_key = grad_qkv[:, query_width : query_width + key_width]
    grad_value = grad_qkv[:, query_width + key_width : query_width + 2 * key_width]
    small_grad = jnp.concatenate([small_grad, gain_part[:, None]], axis=1)
    own_small = own_features // seq_count
    small_grad = small_grad.astype(bf16).reshape(seq_count, own_small, -1)
    small_grad = jnp.pad(small_grad, ((0, 0), (0, model_width // seq_count - own_small), (0, 0)))
    last_sum = jnp.concatenate([grad_out, small_grad.reshape(model_width, -1)], axis=1)
    last_sum = lax.psum_scatter(last_sum, "seq", scatter_dimension=0, tiled=True)
    last_sum = last_sum.astype(jnp.float32)
    grad_out = last_sum[:, : w_out.shape[1]]
    small_grad = last_sum[:own_small, w_out.shape[1] :]
    own_factor = rms_parts(own_inputs)
    input_part, _ = rms_backward(own_inputs, own_factor, first_gain, normed_grad)
    tokens_grad = residual_grad + input_part
    pre_grads = [part.astype(jnp.float32) for part in pre_grads]
    grad_gate = jnp.stack([part[:, :hidden_units] for part in pre_grads])
    grad_up = jnp.stack([part[:, hidden_units:] for part in pre_grads])
    return (
        output,
        tokens_grad,
        grad_query,
        grad_key,
        grad_value,
        grad_out,
        small_grad[:, experts_all + 1],
        small_grad[:, experts_all],
        small_grad[:, :experts_all],
        grad_gate,
        grad_up,
        grad_down,
    )


def solution(mesh):
    return jax.shard_map(
        on_device,
        mesh=mesh,
        in_specs=(
            P(("shard", "seq"), None),
            P(("shard", "seq"), None),
            P("shard", "seq"),
            P("shard", "seq"),
            P("shard", "seq"),
            P("seq", "shard"),
            P(("shard", "seq")),
            P(("shard", "seq")),
            P(("shard", "seq"), None),
            P("shard", None, None),
            P("shard", None, None),
            P("shard", None, None),
            P(("shard", "seq"), None),
        ),
        out_specs=(
            P(("shard", "seq"), None),
            P(("shard", "seq"), None),
            P("shard", "seq"),
            P("shard", "seq"),
            P("shard", "seq"),
            P("seq", "shard"),
            P(("shard", "seq")),
            P(("shard", "seq")),
            P(("shard", "seq"), None),
            P("shard", "seq", None),
            P("shard", "seq", None),
            P("shard", None, "seq"),
        ),
        check_vma=False,
    )
```

```python
from functools import partial

import jax
import jax.numpy as jnp
from jax import lax
from jax.experimental import pallas as pl
from jax.experimental.pallas import tpu as pltpu
from jax.sharding import PartitionSpec as P

HEAD_DIMENSION = 64
CONT_LEN = 512
PROMPT_BLK = 128


norm_eps = 1e-05
negative = -1e30
rope_base = 10000.0
highest = lax.Precision.HIGHEST


def rms_norm(values, scaling):
    factor = lax.rsqrt(jnp.mean(values * values, axis=-1, keepdims=True) + norm_eps)
    return values * factor * scaling


def swiglu(gate_pre, up_pre):
    return jax.nn.silu(gate_pre) * up_pre


def rotary_tables(places, head_size):
    half_size = head_size // 2
    frequency = jnp.exp(
        jnp.arange(half_size, dtype=jnp.float32) * (-2.0 * jnp.log(rope_base) / head_size)
    )
    angles = places.astype(jnp.float32)[:, None] * frequency[None, :]
    return (jnp.cos(angles)[:, None, :], jnp.sin(angles)[:, None, :])


def rotate(values, cosine, sine, head_size):
    total_row_count = values.shape[0]
    by_head = values.reshape(total_row_count, -1, head_size)
    half_size = head_size // 2
    first_half = by_head[..., :half_size]
    second_half = by_head[..., half_size:]
    turned = jnp.concatenate(
        [first_half * cosine - second_half * sine, second_half * cosine + first_half * sine],
        axis=-1,
    )
    return turned.reshape(total_row_count, -1)


def place_of(within, block_index, prompt_len):
    return jnp.where(
        within < PROMPT_BLK,
        block_index * PROMPT_BLK + within,
        prompt_len + (within - PROMPT_BLK) % CONT_LEN,
    )


def times_transposed(left_side, right_side, precision=None):
    return lax.dot_general(
        left_side,
        right_side,
        (((1,), (1,)), ((), ())),
        precision=precision,
        preferred_element_type=jnp.float32,
    )


def transposed_times(left_side, right_side, precision=None):
    return lax.dot_general(
        left_side,
        right_side,
        (((0,), (0,)), ((), ())),
        precision=precision,
        preferred_element_type=jnp.float32,
    )


def rms_parts(values):
    return lax.rsqrt(jnp.mean(values * values, axis=-1, keepdims=True) + norm_eps)


def rms_backward(values, factor, scaling, normed_grad):
    scaled = scaling * normed_grad
    inner = jnp.mean(scaled * values, axis=-1, keepdims=True)
    values_grad = factor * scaled - values * (factor * factor * factor) * inner
    gain_grad = jnp.sum(normed_grad * values * factor, axis=0)
    return values_grad, gain_grad


def matmul(left_side, right_side):
    return jnp.dot(left_side, right_side, preferred_element_type=jnp.float32)


LANES = 128


def relane(values, source, target):
    lane = lax.broadcasted_iota(jnp.int32, values.shape, 1)
    swapped = jnp.where(source != target, pltpu.roll(values, HEAD_DIMENSION, 1), values)
    return jnp.where(lane // HEAD_DIMENSION == target, swapped, 0.0)


def head_rows(ref, first, count, source, target):
    values = ref[pl.ds(first, count), :].astype(jnp.float32)
    return relane(values, source, target).astype(jnp.bfloat16)


def nt_dot(left_side, right_side):
    return lax.dot_general(
        left_side, right_side, (((1,), (1,)), ((), ())), preferred_element_type=jnp.float32
    )


def nn_dot(left_side, right_side):
    return jnp.dot(left_side, right_side, preferred_element_type=jnp.float32)


def below_diagonal(scores):
    key_row = lax.broadcasted_iota(jnp.int32, scores.shape, 0)
    query_column = lax.broadcasted_iota(jnp.int32, scores.shape, 1)
    return jnp.where(key_row <= query_column, scores, negative)


def seen_prompt(scores, first_key, shard_index):
    key_row = lax.broadcasted_iota(jnp.int32, scores.shape, 0) + first_key
    query_column = lax.broadcasted_iota(jnp.int32, scores.shape, 1) % PROMPT_BLK
    return jnp.where(key_row <= query_column + shard_index * PROMPT_BLK, scores, negative)


def transposed(values):
    return values.astype(jnp.float32).T


QUERY_CHUNK = 512
KEY_CHUNK = 1024
FORWARD_CHUNK = 256


def attend_forward_body(
    group, kv_heads, index_ref, q_ref, kp_ref, vp_ref, ko_ref, vo_ref, mixed_ref, level_ref, vt_all, acc
):
    pair = pl.program_id(0)
    prompt_len = kp_ref.shape[0]
    block_len = ko_ref.shape[0]
    conts = (block_len - PROMPT_BLK) // CONT_LEN
    shard_index = index_ref[0]

    @pl.when(pair == 0)
    def _():
        vt_all[:, :prompt_len] = transposed(vp_ref[...]).astype(jnp.bfloat16)
        vt_all[:, prompt_len:] = transposed(vo_ref[...]).astype(jnp.bfloat16)

    acc[...] = jnp.zeros_like(acc)
    size = min(FORWARD_CHUNK, prompt_len)
    prompt_keys = [slice(first, first + size) for first in range(0, prompt_len, size)]

    def kv_half(side):
        return jnp.minimum((2 * pair + side) // group, kv_heads - 1)

    def finish(scores, value_columns):
        level = jnp.max(scores[0], axis=0, keepdims=True)
        for part in scores[1:]:
            level = jnp.maximum(level, jnp.max(part, axis=0, keepdims=True))
        total = None
        mixed = None
        for part, columns in zip(scores, value_columns):
            weights = jnp.exp(part - level)
            part_total = jnp.sum(weights, axis=0, keepdims=True)
            part_mixed = nn_dot(columns, weights.astype(jnp.bfloat16))
            total = part_total if total is None else total + part_total
            mixed = part_mixed if mixed is None else mixed + part_mixed
        return mixed / total, level + jnp.log(total)

    both = jnp.concatenate(
        [head_rows(q_ref, 0, PROMPT_BLK, side, kv_half(side)) for side in range(2)], axis=0
    )
    mixed, level = finish(
        [
            seen_prompt(nt_dot(kp_ref[keys, :], both), keys.start, shard_index)
            for keys in prompt_keys
        ],
        [vt_all[:, keys] for keys in prompt_keys],
    )
    mixed = mixed.T
    for side in range(2):
        rows = slice(side * PROMPT_BLK, (side + 1) * PROMPT_BLK)
        acc[:PROMPT_BLK, :] += relane(mixed[rows], kv_half(side), side)
        level_ref[side, :, :PROMPT_BLK] = level[:, rows]

    def step(turn, _):
        side = turn // conts
        number = turn % conts
        half = kv_half(side)
        first_own = PROMPT_BLK + number * CONT_LEN
        for chunk in range(CONT_LEN // QUERY_CHUNK):
            before = chunk * QUERY_CHUNK
            first_row = pl.multiple_of(first_own + before, PROMPT_BLK)
            queries = head_rows(q_ref, first_row, QUERY_CHUNK, side, half)
            scores = [nt_dot(kp_ref[keys, :], queries) for keys in prompt_keys]
            columns = [vt_all[:, keys] for keys in prompt_keys]
            if before:
                start = pl.multiple_of(first_own, PROMPT_BLK)
                scores.append(nt_dot(ko_ref[pl.ds(start, before), :], queries))
                columns.append(
                    vt_all[:, pl.ds(pl.multiple_of(prompt_len + start, PROMPT_BLK), before)]
                )
            scores.append(below_diagonal(nt_dot(ko_ref[pl.ds(first_row, QUERY_CHUNK), :], queries)))
            columns.append(
                vt_all[:, pl.ds(pl.multiple_of(prompt_len + first_row, PROMPT_BLK), QUERY_CHUNK)]
            )
            mixed, level = finish(scores, columns)
            acc[pl.ds(first_row, QUERY_CHUNK), :] += relane(mixed.T, half, side)
            level_ref[side, :, pl.ds(first_row, QUERY_CHUNK)] = level
        return 0

    lax.fori_loop(0, 2 * conts, step, 0)
    mixed_ref[...] = acc[...].astype(jnp.bfloat16)


def attend_backward_body(
    group,
    kv_heads,
    index_ref,
    q_ref,
    grad_ref,
    mixed_ref,
    level_ref,
    cos_ref,
    sin_ref,
    kp_ref,
    vp_ref,
    ko_ref,
    vo_ref,
    dq_ref,
    dprompt_ref,
    down_ref,
    kt_all,
    acc,
    prompt_acc,
):
    pair = pl.program_id(0)
    last = pl.num_programs(0) - 1
    prompt_len = kp_ref.shape[0]
    block_len = ko_ref.shape[0]
    conts = (block_len - PROMPT_BLK) // CONT_LEN
    shard_index = index_ref[0]
    bf16 = jnp.bfloat16

    @pl.when(pair == 0)
    def _():
        kt_all[:, :prompt_len] = transposed(kp_ref[...]).astype(bf16)
        kt_all[:, prompt_len:] = transposed(ko_ref[...]).astype(bf16)
        prompt_acc[...] = jnp.zeros_like(prompt_acc)
        down_ref[...] = jnp.zeros_like(down_ref)

    acc[...] = jnp.zeros_like(acc)

    def kv_half(side):
        return jnp.minimum((2 * pair + side) // group, kv_heads - 1)

    def inner_sums(first_row, count, side):
        rows = pl.ds(first_row, count)
        product = mixed_ref[rows, :].astype(jnp.float32) * grad_ref[rows, :].astype(jnp.float32)
        return jnp.sum(relane(product, side, side).T, axis=0, keepdims=True)

    def part(keys, values, key_columns, queries, grads, level, inner, mask, sums, first_key):
        scores = nt_dot(keys, queries)
        if mask is not None:
            scores = mask(scores)
        probs = jnp.exp(scores - level)
        score_grad = (probs * (nt_dot(values, grads) - inner)).astype(bf16)
        rows = pl.ds(first_key, keys.shape[0])
        sums[rows, :LANES] += nn_dot(score_grad, queries)
        sums[rows, LANES:] += nn_dot(probs.astype(bf16), grads)
        return nn_dot(key_columns, score_grad)

    def prompt_parts(queries, grads, level, inner, masked):
        total = None
        size = min(KEY_CHUNK, prompt_len)
        for first_key in range(0, prompt_len, size):
            rows = slice(first_key, first_key + size)
            mask = (lambda s, f=first_key: seen_prompt(s, f, shard_index)) if masked else None
            piece = part(
                kp_ref[rows, :], vp_ref[rows, :], kt_all[:, rows], queries, grads, level, inner,
                mask, prompt_acc, first_key,
            )
            total = piece if total is None else total + piece
        return total

    both_q, both_g, both_level, both_inner = [], [], [], []
    for side in range(2):
        both_q.append(head_rows(q_ref, 0, PROMPT_BLK, side, kv_half(side)))
        both_g.append(head_rows(grad_ref, 0, PROMPT_BLK, side, kv_half(side)))
        both_level.append(level_ref[side, :, :PROMPT_BLK])
        both_inner.append(inner_sums(0, PROMPT_BLK, side))
    grad_q = prompt_parts(
        jnp.concatenate(both_q, axis=0),
        jnp.concatenate(both_g, axis=0),
        jnp.concatenate(both_level, axis=1),
        jnp.concatenate(both_inner, axis=1),
        True,
    ).T
    for side in range(2):
        rows = slice(side * PROMPT_BLK, (side + 1) * PROMPT_BLK)
        acc[:PROMPT_BLK, :] += relane(grad_q[rows], kv_half(side), side)

    def step(turn, _):
        side = turn // conts
        number = turn % conts
        half = kv_half(side)
        first_own = PROMPT_BLK + number * CONT_LEN
        for chunk in range(CONT_LEN // QUERY_CHUNK):
            before = chunk * QUERY_CHUNK
            first_row = pl.multiple_of(first_own + before, PROMPT_BLK)
            queries = head_rows(q_ref, first_row, QUERY_CHUNK, side, half)
            grads = head_rows(grad_ref, first_row, QUERY_CHUNK, side, half)
            level = level_ref[side, :, pl.ds(first_row, QUERY_CHUNK)]
            inner = inner_sums(first_row, QUERY_CHUNK, side)
            grad_q = prompt_parts(queries, grads, level, inner, False)
            own = [(first_row, QUERY_CHUNK, below_diagonal)]
            if before:
                own.append((pl.multiple_of(first_own, PROMPT_BLK), before, None))
            for start, size, mask in own:
                rows = pl.ds(start, size)
                columns = pl.ds(pl.multiple_of(prompt_len + start, PROMPT_BLK), size)
                grad_q += part(
                    ko_ref[rows, :], vo_ref[rows, :], kt_all[:, columns], queries, grads, level,
                    inner, mask, down_ref, start,
                )
            acc[pl.ds(first_row, QUERY_CHUNK), :] += relane(grad_q.T, half, side)
        return 0

    lax.fori_loop(0, 2 * conts, step, 0)
    grads = acc[...] * HEAD_DIMENSION ** (-0.5)
    half = HEAD_DIMENSION // 2
    lane = lax.broadcasted_iota(jnp.int32, grads.shape, 1)
    swapped = jnp.where(
        lane % HEAD_DIMENSION < half,
        pltpu.roll(grads, LANES - half, 1),
        pltpu.roll(grads, half, 1),
    )
    dq_ref[...] = (grads * cos_ref[...] + swapped * sin_ref[...]).astype(bf16)

    @pl.when(pair == last)
    def _():
        dprompt_ref[...] = prompt_acc[...].astype(bf16)


def pair_specs(block_len, prompt_len):
    by_pair = pl.BlockSpec((block_len, LANES), lambda b, i: (0, b))
    levels = pl.BlockSpec((2, 1, block_len), lambda b, i: (b, 0, 0))
    sources = [
        pl.BlockSpec((prompt_len, LANES), lambda b, i: (0, 0)),
        pl.BlockSpec((prompt_len, LANES), lambda b, i: (0, 1)),
        pl.BlockSpec((block_len, LANES), lambda b, i: (0, 0)),
        pl.BlockSpec((block_len, LANES), lambda b, i: (0, 1)),
    ]
    return by_pair, levels, sources


def attention_cost(block_len, prompt_len, width, products):
    pairs = (block_len * prompt_len + block_len * CONT_LEN // 2) * (width // HEAD_DIMENSION)
    return pl.CostEstimate(
        flops=products * 2 * pairs * 2 * LANES,
        bytes_accessed=8 * block_len * width,
        transcendentals=pairs,
    )


def attend_forward(index, queries, kv_prompt, kv_own, group, kv_heads):
    block_len, width = queries.shape
    prompt_len = kv_prompt.shape[0]
    by_pair, levels, sources = pair_specs(block_len, prompt_len)
    return pl.pallas_call(
        partial(attend_forward_body, group, kv_heads),
        out_shape=[
            jax.ShapeDtypeStruct((block_len, width), jnp.bfloat16),
            jax.ShapeDtypeStruct((width // HEAD_DIMENSION, 1, block_len), jnp.float32),
        ],
        grid_spec=pltpu.PrefetchScalarGridSpec(
            num_scalar_prefetch=1,
            grid=(width // LANES,),
            in_specs=[by_pair] + sources,
            out_specs=[by_pair, levels],
            scratch_shapes=[
                pltpu.VMEM((LANES, prompt_len + block_len), jnp.bfloat16),
                pltpu.VMEM((block_len, LANES), jnp.float32),
            ],
        ),
        compiler_params=pltpu.CompilerParams(
            dimension_semantics=("arbitrary",), vmem_limit_bytes=56 * 1024 * 1024
        ),
        cost_estimate=attention_cost(block_len, prompt_len, width, 2),
        name="attend_forward",
    )(index, queries, kv_prompt, kv_prompt, kv_own, kv_own)


def attend_backward(
    index, queries, grads, mixed, level, tables, kv_prompt, kv_own, group, kv_heads
):
    block_len, width = queries.shape
    prompt_len = kv_prompt.shape[0]
    by_pair, levels, sources = pair_specs(block_len, prompt_len)
    return pl.pallas_call(
        partial(attend_backward_body, group, kv_heads),
        out_shape=[
            jax.ShapeDtypeStruct((block_len, width), jnp.bfloat16),
            jax.ShapeDtypeStruct((prompt_len, 2 * LANES), jnp.bfloat16),
            jax.ShapeDtypeStruct((block_len, 2 * LANES), jnp.float32),
        ],
        grid_spec=pltpu.PrefetchScalarGridSpec(
            num_scalar_prefetch=1,
            grid=(width // LANES,),
            in_specs=[by_pair, by_pair, by_pair, levels]
            + [pl.BlockSpec((block_len, LANES), lambda b, i: (0, 0))] * 2
            + sources,
            out_specs=[
                by_pair,
                pl.BlockSpec((prompt_len, 2 * LANES), lambda b, i: (0, 0)),
                pl.BlockSpec((block_len, 2 * LANES), lambda b, i: (0, 0)),
            ],
            scratch_shapes=[
                pltpu.VMEM((LANES, prompt_len + block_len), jnp.bfloat16),
                pltpu.VMEM((block_len, LANES), jnp.float32),
                pltpu.VMEM((prompt_len, 2 * LANES), jnp.float32),
            ],
        ),
        compiler_params=pltpu.CompilerParams(
            dimension_semantics=("arbitrary",), vmem_limit_bytes=56 * 1024 * 1024
        ),
        cost_estimate=attention_cost(block_len, prompt_len, width, 5),
        name="attend_backward",
    )(index, queries, grads, mixed, level, *tables, kv_prompt, kv_prompt, kv_own, kv_own)


def to_lanes(values):
    extra = -values.shape[1] % LANES
    return jnp.pad(values, ((0, 0), (0, extra))) if extra else values


def exchange(values, axis_name, bit):
    count = lax.axis_size(axis_name)
    return lax.ppermute(values, axis_name, [(i, i ^ bit) for i in range(count)])


def bits_of(number):
    return [1 << k for k in range(number.bit_length()) if number >> k & 1]


def even_blocks(count):
    even = sorted(range(2, count, 2), key=lambda j: (len(bits_of(j)), j))
    singles = [j for j in even if len(bits_of(j)) == 1]
    return singles, even[len(singles) :]


def gather_blocks(own, axis_name, after_first=None):
    count = lax.axis_size(axis_name)
    singles, several = even_blocks(count)
    blocks = {0: own, 1: exchange(own, axis_name, 1)}
    for j in singles:
        blocks[j] = exchange(own, axis_name, j)
    if after_first is not None:
        blocks.update(zip(singles, after_first([blocks[j] for j in singles])))
    for j in several:
        low_bit = bits_of(j)[0]
        blocks[j] = exchange(blocks[j ^ low_bit], axis_name, low_bit)
    for j in singles + several:
        blocks[j + 1] = exchange(blocks[j], axis_name, 1)
    return [blocks[j] for j in range(count)]


def add_rounded(left_side, right_side):
    return (left_side.astype(jnp.float32) + right_side.astype(jnp.float32)).astype(jnp.bfloat16)


def reduce_several(sums, axis_name):
    sums = dict(sums)
    pending = []
    for j in sorted((j for j in sums if len(bits_of(j)) > 1), key=lambda j: (-len(bits_of(j)), j)):
        bit = bits_of(j)[-1]
        piece = exchange(sums[j], axis_name, bit)
        if len(bits_of(j ^ bit)) > 1:
            sums[j ^ bit] = add_rounded(sums[j ^ bit], piece)
        else:
            pending.append((j ^ bit, piece))
    return pending


def reduce_singles(sums, pending, axis_name):
    sums = dict(sums)
    for j, piece in pending:
        sums[j] = add_rounded(sums[j], piece)
    return [sums[0]] + [exchange(sums[j], axis_name, j) for j in sums if len(bits_of(j)) == 1]


def add_all(pieces):
    total = pieces[0].astype(jnp.float32)
    for piece in pieces[1:]:
        total = total + piece.astype(jnp.float32)
    return total


def halves_by_core(values, axis_name):
    count = lax.axis_size(axis_name)
    parity = lax.axis_index(axis_name) % 2
    paired = values.reshape(count // 2, 2, values.shape[0] // count, values.shape[1])
    keep = lax.dynamic_index_in_dim(paired, parity, 1, keepdims=False)
    give = lax.dynamic_index_in_dim(paired, 1 - parity, 1, keepdims=False)
    return keep, give


def chip_sums(keep, arrived, axis_name):
    index = lax.axis_index(axis_name)
    total = add_rounded(keep, arrived)
    return {
        2 * k: lax.dynamic_index_in_dim(total, (index // 2) ^ k, 0, keepdims=False)
        for k in range(total.shape[0])
    }


def reduce_rows(values, axis_name):
    keep, give = halves_by_core(values, axis_name)
    sums = chip_sums(keep, exchange(give, axis_name, 1), axis_name)
    return add_all(reduce_singles(sums, reduce_several(sums, axis_name), axis_name))


def in_order(blocks, index):
    stacked = jnp.stack(blocks)
    return jnp.concatenate(
        [lax.dynamic_index_in_dim(stacked, j ^ index, 0, keepdims=True) for j in range(len(blocks))],
        axis=0,
    )


def expert_body(
    experts_all, index_ref, x_even, x_odd, og_even, og_odd, gate_w, up_w, down_w, *rest
):
    (x_all, og_all, pre_all, hid_all, row_even, row_odd, out_even, out_odd) = rest[-12:-4]
    (row_acc, out_acc, back_acc, _) = rest[-4:]
    expert = pl.program_id(0)
    last = pl.num_programs(0) - 1
    rows = x_even.shape[0]
    width = x_all.shape[1]
    hidden_units = gate_w.shape[2]
    nt_dims = (((1,), (1,)), ((), ()))

    @pl.when(expert == 0)
    def _():
        x_all[:rows, :] = x_even[:, :width]
        x_all[rows:, :] = x_odd[:, :width]
        og_all[:rows, :] = og_even[...]
        og_all[rows:, :] = og_odd[...]

    column = index_ref[0] + expert
    lane = lax.broadcasted_iota(jnp.int32, (2 * rows, LANES), 1)
    coded = jnp.concatenate([x_even[:, width:], x_odd[:, width:]], axis=0).astype(jnp.float32)
    gate = jnp.sum(
        jnp.where((lane == column) | (lane == column + experts_all), coded, 0.0),
        axis=1,
        keepdims=True,
    )
    x_rows = x_all[...]
    og_rows = og_all[...]
    gate_pre = jnp.dot(x_rows, gate_w[0], preferred_element_type=jnp.float32)
    up_pre = jnp.dot(x_rows, up_w[0], preferred_element_type=jnp.float32)
    down_grad = lax.dot_general(og_rows, down_w[0], nt_dims, preferred_element_type=jnp.float32)
    sigmoid = 1.0 / (1.0 + jnp.exp(-gate_pre))
    silu = gate_pre * sigmoid
    hidden = silu * up_pre
    gate_back = jnp.sum(hidden * down_grad, axis=1, keepdims=True)
    hidden_low = (gate * hidden).astype(jnp.bfloat16)
    hidden_grad = gate * down_grad
    gate_pre_low = (
        hidden_grad * up_pre * sigmoid * (1.0 + gate_pre * (1.0 - sigmoid))
    ).astype(jnp.bfloat16)
    up_pre_low = (hidden_grad * silu).astype(jnp.bfloat16)
    hid_all[...] = hidden_low
    pre_all[0, :, :hidden_units] = gate_pre_low
    pre_all[0, :, hidden_units:] = up_pre_low
    row = lax.dot_general(
        gate_pre_low, gate_w[0], nt_dims, preferred_element_type=jnp.float32
    ) + lax.dot_general(up_pre_low, up_w[0], nt_dims, preferred_element_type=jnp.float32)
    out = jnp.dot(hidden_low, down_w[0], preferred_element_type=jnp.float32)
    high = gate_back.astype(jnp.bfloat16).astype(jnp.float32)
    back = jnp.where(lane == column, high, 0.0) + jnp.where(
        lane == column + experts_all, gate_back - high, 0.0
    )

    @pl.when(expert == 0)
    def _():
        row_acc[...] = row
        out_acc[...] = out
        back_acc[...] = back

    @pl.when(expert > 0)
    def _():
        row_acc[...] += row
        out_acc[...] += out
        back_acc[...] += back

    @pl.when(expert == last)
    def _():
        for ref, first in ((row_even, 0), (row_odd, rows)):
            ref[:, :width] = row_acc[first : first + rows, :].astype(jnp.bfloat16)
            ref[:, width:] = back_acc[first : first + rows, :].astype(jnp.bfloat16)
        out_even[...] = out_acc[:rows, :].astype(jnp.bfloat16)
        out_odd[...] = out_acc[rows:, :].astype(jnp.bfloat16)


def expert_pair(position, pairs, first_expert, experts_all, x_pair, og_pair, weights, carried):
    w_gate, w_up, w_down = weights
    rows, coded_width = x_pair[0].shape
    width = coded_width - LANES
    local_experts, _, hidden_units = w_gate.shape
    bf16 = jnp.bfloat16
    whole = 2 * rows
    fixed = lambda e, i: (0, 0)
    once = pl.Buffered(1)
    in_specs = (
        [pl.BlockSpec((rows, coded_width), fixed, pipeline_mode=once)] * 2
        + [pl.BlockSpec((rows, width), fixed, pipeline_mode=once)] * 2
        + [pl.BlockSpec((1, width, hidden_units), lambda e, i: (e, 0, 0))] * 2
        + [pl.BlockSpec((1, hidden_units, width), lambda e, i: (e, 0, 0))]
    )
    operands = [*x_pair, *og_pair, w_gate, w_up, w_down]
    aliases = {}
    if carried is not None:
        in_specs = in_specs + [pl.BlockSpec(memory_space=pl.ANY)] * 4
        aliases = {1 + len(operands) + k: k for k in range(4)}
        operands = operands + list(carried)
    out_shape = [
        jax.ShapeDtypeStruct((pairs * whole, width), bf16),
        jax.ShapeDtypeStruct((pairs * whole, width), bf16),
        jax.ShapeDtypeStruct((local_experts, pairs * whole, 2 * hidden_units), bf16),
        jax.ShapeDtypeStruct((pairs * whole, local_experts * hidden_units), bf16),
        jax.ShapeDtypeStruct((rows, coded_width), bf16),
        jax.ShapeDtypeStruct((rows, coded_width), bf16),
        jax.ShapeDtypeStruct((rows, width), bf16),
        jax.ShapeDtypeStruct((rows, width), bf16),
    ]
    out_specs = [
        pl.BlockSpec((whole, width), lambda e, i: (position, 0)),
        pl.BlockSpec((whole, width), lambda e, i: (position, 0)),
        pl.BlockSpec((1, whole, 2 * hidden_units), lambda e, i: (e, position, 0)),
        pl.BlockSpec((whole, hidden_units), lambda e, i: (position, e)),
        pl.BlockSpec((rows, coded_width), fixed),
        pl.BlockSpec((rows, coded_width), fixed),
        pl.BlockSpec((rows, width), fixed),
        pl.BlockSpec((rows, width), fixed),
    ]
    products = 2 * whole * width * hidden_units * local_experts
    results = pl.pallas_call(
        partial(expert_body, experts_all),
        out_shape=out_shape,
        grid_spec=pltpu.PrefetchScalarGridSpec(
            num_scalar_prefetch=1,
            grid=(local_experts,),
            in_specs=in_specs,
            out_specs=out_specs,
            scratch_shapes=[
                pltpu.VMEM((whole, width), jnp.float32),
                pltpu.VMEM((whole, width), jnp.float32),
                pltpu.VMEM((whole, LANES), jnp.float32),
                pltpu.VMEM((8, LANES), jnp.float32),
            ],
        ),
        input_output_aliases=aliases,
        compiler_params=pltpu.CompilerParams(
            dimension_semantics=("arbitrary",), vmem_limit_bytes=60 * 1024 * 1024
        ),
        cost_estimate=pl.CostEstimate(
            flops=6 * products,
            bytes_accessed=3 * 2 * local_experts * width * hidden_units + 20 * whole * width,
            transcendentals=whole * hidden_units * local_experts,
        ),
        name="experts",
    )(first_expert, *operands)
    return results[:4], results[4:]


def on_device(
    tokens,
    routes,
    w_query,
    key_projection,
    value_projection,
    w_out,
    gain_attn,
    gain_ffn,
    w_router,
    w_gate,
    w_up,
    w_down,
    out_grad,
):
    bf16 = jnp.bfloat16
    shard_count = lax.axis_size("shard")
    seq_count = lax.axis_size("seq")
    shard_index = lax.axis_index("shard")
    seq_index = lax.axis_index("seq")
    tok_count, model_width = tokens.shape
    top_count = routes.shape[1]
    experts_all = w_router.shape[1]
    local_experts = w_gate.shape[0]
    block_len = tok_count * seq_count
    prompt_len = PROMPT_BLK * shard_count
    query_width = w_query.shape[1]
    key_width = key_projection.shape[1]

    singles, several = even_blocks(shard_count)
    small = jnp.concatenate([w_router, gain_attn[:, None], gain_ffn[:, None]], axis=1)
    small = lax.all_gather(small, "seq", axis=0, tiled=True)
    small = lax.all_gather(small, "shard", axis=0, tiled=True)
    router_weight = small[:, :experts_all]
    first_gain = small[:, experts_all].astype(jnp.float32)
    second_gain = small[:, experts_all + 1].astype(jnp.float32)
    block_tokens = lax.all_gather(tokens, "seq", axis=0, tiled=True)
    own_weight = jnp.concatenate([w_query, key_projection, value_projection], axis=1)
    grad_blocks = {0: out_grad}
    near = [exchange(out_grad, "shard", bit) for bit in singles]

    def with_near(blocks):
        blocks, near[:] = lax.optimization_barrier((blocks, near))
        return blocks

    weight_blocks = gather_blocks(own_weight, "shard", with_near)
    grad_blocks.update(zip(singles, near))
    for j in [0] + singles:
        grad_blocks[j + 1] = exchange(grad_blocks[j], "shard", 1)
    out_weight = lax.all_gather(w_out, "seq", axis=0, tiled=True)
    qkv_weight = in_order(weight_blocks, shard_index).reshape(model_width, -1)

    block_rows = jnp.arange(block_len, dtype=jnp.int32)
    cos_table, sin_table = rotary_tables(
        place_of(block_rows, shard_index, prompt_len), HEAD_DIMENSION
    )
    back_tables = [
        jnp.tile(cos_table[:, 0, :], (1, LANES // cos_table.shape[2])),
        jnp.tile(
            jnp.concatenate([sin_table, -sin_table], axis=2)[:, 0, :],
            (1, LANES // HEAD_DIMENSION),
        ),
    ]
    block_tokens, cos_table, sin_table, back_tables = lax.optimization_barrier(
        (block_tokens, cos_table, sin_table, back_tables)
    )
    inputs = block_tokens.astype(jnp.float32)
    first_factor = rms_parts(inputs)
    normed_low = (inputs * first_factor * first_gain).astype(bf16)
    lin = matmul(normed_low, qkv_weight)
    kv_heads = key_width // HEAD_DIMENSION
    group = query_width // key_width
    queries = rotate(lin[:, :query_width], cos_table, sin_table, HEAD_DIMENSION)
    queries = to_lanes((queries * HEAD_DIMENSION ** (-0.5)).astype(bf16))
    key_heads = rotate(
        lin[:, query_width : query_width + key_width], cos_table, sin_table, HEAD_DIMENSION
    ).astype(bf16)
    value_heads = lin[:, query_width + key_width :].astype(bf16)
    kv_own = jnp.concatenate([to_lanes(key_heads), to_lanes(value_heads)], axis=1)
    kv_prompt = lax.all_gather(kv_own[:PROMPT_BLK], "shard", axis=0, tiled=True)
    kv_prompt, out_weight, near = lax.optimization_barrier(
        (kv_prompt, out_weight, [grad_blocks[bit] for bit in singles])
    )
    grad_blocks.update(zip(singles, near))
    out_weight = lax.all_gather(out_weight, "shard", axis=1, tiled=True)
    for j in several:
        low_bit = bits_of(j)[0]
        grad_blocks[j] = exchange(grad_blocks[j ^ low_bit], "shard", low_bit)
    block_number = shard_index.astype(jnp.int32).reshape(1)
    mixed_own, levels = attend_forward(block_number, queries, kv_prompt, kv_own, group, kv_heads)
    sooner = [j for j in range(1, shard_count) if j - 1 not in several]
    mixed_own, held_blocks = lax.optimization_barrier((mixed_own, [grad_blocks[j] for j in sooner]))
    for j, block in zip(sooner, held_blocks):
        grad_blocks[j] = block
    for j in several:
        grad_blocks[j + 1] = exchange(grad_blocks[j], "shard", 1)
    mixed_heads = mixed_own[:, :query_width]
    mixed_tokens = lax.all_to_all(mixed_heads, "seq", split_axis=0, concat_axis=1, tiled=True)

    half_features = model_width // 2
    core_bit = shard_index % 2
    half_weight, mixed_tokens = lax.optimization_barrier(
        (
            lax.dynamic_slice_in_dim(qkv_weight, core_bit * half_features, half_features, axis=0),
            mixed_tokens,
        )
    )
    wide_half = lax.all_gather(half_weight, "seq", axis=0, tiled=False)

    own_inputs = tokens.astype(jnp.float32)
    upstream = out_grad.astype(jnp.float32)
    residual = own_inputs + matmul(mixed_tokens, out_weight)
    second_factor = rms_parts(residual)
    second_low = (residual * second_factor * second_gain).astype(bf16)
    logits = matmul(second_low, router_weight)
    chosen = routes[:, :, None] == jnp.arange(experts_all, dtype=jnp.int32)[None, None, :]
    named = jnp.any(chosen, axis=1)
    gate_dense = jax.nn.softmax(jnp.where(named, logits, negative), axis=-1)
    gate_dense = jnp.where(named, gate_dense, 0.0)

    gate_high = lax.reduce_precision(gate_dense, 8, 7)
    coded = jnp.concatenate(
        [
            second_low,
            gate_high.astype(bf16),
            (gate_dense - gate_high).astype(bf16),
            jnp.zeros((tok_count, LANES - 2 * experts_all), bf16),
        ],
        axis=1,
    )
    row_blocks = {0: coded, 1: exchange(coded, "shard", 1)}
    for bit in singles:
        row_blocks[bit] = exchange(coded, "shard", bit)
    order = [0] + singles[:-1] + several + singles[-1:]
    first_expert = (shard_index * local_experts).astype(jnp.int32).reshape(1)
    carried = None
    pending = []
    row_sums = {}
    out_parts = [None] * shard_count
    for position, j in enumerate(order):
        row_pair = [row_blocks[j], row_blocks[j + 1]]
        if j == order[-1]:
            row_pair, row_sums = lax.optimization_barrier((row_pair, row_sums))
            pending = reduce_several(row_sums, "shard")
        carried, pieces = expert_pair(
            position,
            len(order),
            first_expert,
            experts_all,
            row_pair,
            [grad_blocks[j], grad_blocks[j + 1]],
            (w_gate, w_up, w_down),
            carried,
        )
        if position == 0:
            arrived, pieces = lax.optimization_barrier(
                ([row_blocks[bit] for bit in singles], pieces)
            )
            row_blocks.update(zip(singles, arrived))
            for bit in singles:
                row_blocks[bit + 1] = exchange(row_blocks[bit], "shard", 1)
            for k in several:
                low_bit = bits_of(k)[0]
                row_blocks[k] = exchange(row_blocks[k ^ low_bit], "shard", low_bit)
        elif position == 1:
            arrived, pieces = lax.optimization_barrier(([row_blocks[k] for k in several], pieces))
            row_blocks.update(zip(several, arrived))
            for k in several:
                row_blocks[k + 1] = exchange(row_blocks[k], "shard", 1)
        elif j == order[-1]:
            arrived, pieces, carried = lax.optimization_barrier(
                ([piece for _, piece in pending], pieces, carried)
            )
            pending = [(k, piece) for (k, _), piece in zip(pending, arrived)]
        arrived = exchange(pieces[1], "shard", 1)
        if j != order[-1]:
            row_sums[j] = add_rounded(pieces[0], arrived)
        out_parts[j], out_parts[j + 1] = pieces[2], pieces[3]
    carried, wide_half = lax.optimization_barrier((carried, wide_half))
    all_rows, all_grads, all_pre, all_hidden = carried
    down_sum = transposed_times(all_grads, all_hidden).astype(bf16)
    grad_down = lax.psum_scatter(down_sum, "seq", scatter_dimension=0, tiled=True)
    all_rows, arrived, down_sum = lax.optimization_barrier((all_rows, arrived, down_sum))
    row_sums[order[-1]] = add_rounded(pieces[0], arrived)
    pre_sums = [transposed_times(all_rows, all_pre[0]).astype(bf16)]
    pre_grads = [lax.psum_scatter(pre_sums[0], "seq", scatter_dimension=0, tiled=True)]
    row_pieces = reduce_singles(row_sums, pending, "shard")
    row_pieces, pre_sums[0] = lax.optimization_barrier((row_pieces, pre_sums[0]))
    row_total = add_all(row_pieces)
    row_grad = row_total[:, :model_width]
    gate_grad_dense = (
        row_total[:, model_width : model_width + experts_all]
        + row_total[:, model_width + experts_all : model_width + 2 * experts_all]
    )
    weighted = gate_dense * gate_grad_dense
    logit_grad = weighted - gate_dense * jnp.sum(weighted, axis=-1, keepdims=True)
    second_grad = row_grad + times_transposed(
        logit_grad, router_weight.astype(jnp.float32), highest
    )
    residual_part, grad_gain_ffn = rms_backward(residual, second_factor, second_gain, second_grad)
    residual_grad = upstream + residual_part
    residual_low = residual_grad.astype(bf16)
    mixed_grad_tokens = times_transposed(residual_low, out_weight).astype(bf16)
    other_half = exchange(wide_half, "shard", 1)
    mixed_grad_tokens, out_parts, all_rows, other_half, mixed_late, logit_late = (
        lax.optimization_barrier(
            (mixed_grad_tokens, out_parts, all_rows, other_half, mixed_tokens, logit_grad)
        )
    )
    mixed_grad = lax.all_to_all(mixed_grad_tokens, "seq", split_axis=1, concat_axis=0, tiled=True)
    odd = [exchange(out_parts[j + 1], "shard", 1) for j in order]
    pre_sums += [
        transposed_times(all_rows, all_pre[e]).astype(bf16) for e in range(1, local_experts)
    ]
    pre_grads += [
        lax.psum_scatter(part, "seq", scatter_dimension=0, tiled=True) for part in pre_sums[1:]
    ]
    odd, pre_sums = lax.optimization_barrier((odd, pre_sums))
    odd = dict(zip(order, odd))
    out_sums = {j: add_rounded(out_parts[j], odd[j]) for j in several}
    whole_out = transposed_times(residual_low, mixed_late).astype(bf16)
    whole_keep, whole_give = halves_by_core(whole_out, "shard")
    whole_arrived = exchange(whole_give, "shard", 1)
    grad_router = transposed_times(second_low.astype(jnp.float32), logit_late, highest)
    small_grad = jnp.concatenate([grad_router, grad_gain_ffn[:, None]], axis=1)
    small_keep, small_give = halves_by_core(small_grad.astype(bf16), "shard")
    small_arrived = exchange(small_give, "shard", 1)
    mixed_grad, pre_sums, out_sums, whole_arrived, odd, small_arrived = lax.optimization_barrier(
        (mixed_grad, pre_sums, out_sums, whole_arrived, odd, small_arrived)
    )
    small_sums = chip_sums(small_keep, small_arrived, "shard")
    small_pending = reduce_several(small_sums, "shard")
    out_pending = reduce_several(out_sums, "shard")
    whole_sums = chip_sums(whole_keep, whole_arrived, "shard")
    whole_pending = reduce_several(whole_sums, "shard")

    query_grad, prompt_grad, self_grad = attend_backward(
        block_number,
        queries,
        to_lanes(mixed_grad),
        mixed_own,
        levels,
        back_tables,
        kv_prompt,
        kv_own,
        group,
        kv_heads,
    )
    query_grad, prompt_grad, self_grad, small_arrived, arrived, out_arrived = lax.optimization_barrier(
        (
            query_grad,
            prompt_grad,
            self_grad,
            [piece for _, piece in small_pending],
            [piece for _, piece in whole_pending],
            [piece for _, piece in out_pending],
        )
    )
    whole_pending = [(j, piece) for (j, _), piece in zip(whole_pending, arrived)]
    out_pending = [(j, piece) for (j, _), piece in zip(out_pending, out_arrived)]
    small_pending = [(j, piece) for (j, _), piece in zip(small_pending, small_arrived)]
    small_grad = add_all(reduce_singles(small_sums, small_pending, "shard"))
    lin_query = query_grad[:, :query_width]
    own_prompt = reduce_rows(prompt_grad, "shard")
    key_grad = jnp.concatenate(
        [own_prompt[:, :key_width], self_grad[PROMPT_BLK:, :key_width]], axis=0
    )
    value_low = jnp.concatenate(
        [own_prompt[:, LANES : LANES + key_width], self_grad[PROMPT_BLK:, LANES : LANES + key_width]],
        axis=0,
    ).astype(bf16)
    lin_key = rotate(key_grad, cos_table, -sin_table, HEAD_DIMENSION).astype(bf16)
    lin_all = jnp.concatenate([lin_query, lin_key, value_low], axis=1)
    all_columns = lin_all.shape[1]
    lin_all, whole_sums = lax.optimization_barrier((lin_all, whole_sums))
    lin_tokens = lax.all_to_all(lin_all, "seq", split_axis=0, concat_axis=1, tiled=True)

    keep, give = halves_by_core(transposed_times(normed_low, lin_all).astype(bf16), "shard")
    qkv_sums = chip_sums(keep, exchange(give, "shard", 1), "shard")
    qkv_pending = reduce_several(qkv_sums, "shard")
    arrived, odd = lax.optimization_barrier(([piece for _, piece in qkv_pending], odd))
    qkv_pending = [(j, piece) for (j, _), piece in zip(qkv_pending, arrived)]
    grad_qkv = add_all(reduce_singles(qkv_sums, qkv_pending, "shard"))
    for j in [0] + singles:
        out_sums[j] = add_rounded(out_parts[j], odd[j])
    out_sums = {j: out_sums[j] for j in [0] + singles}
    out_pieces = reduce_singles(out_sums, out_pending, "shard")
    grad_out = add_all(reduce_singles(whole_sums, whole_pending, "shard")).astype(bf16).T
    hidden_units = w_gate.shape[2]
    grad_down, first_sums, grad_qkv = lax.optimization_barrier(
        (grad_down, pre_grads[0], grad_qkv)
    )
    grad_down = grad_down.T.reshape(local_experts, hidden_units, -1).astype(jnp.float32)
    pre_grads[0] = first_sums.astype(jnp.float32)
    lin_tokens, grad_down, pre_grads[0] = lax.optimization_barrier(
        (lin_tokens, grad_down, pre_grads[0])
    )
    parts = [0.0, 0.0]
    for k, weight in enumerate((wide_half, other_half)):
        for group_index in range(seq_count):
            columns = slice(group_index * all_columns, (group_index + 1) * all_columns)
            parts[k] = parts[k] + times_transposed(lin_tokens[:, columns], weight[group_index])
    normed_grad = jnp.concatenate(
        [
            jnp.where(core_bit == 0, parts[0], parts[1]),
            jnp.where(core_bit == 0, parts[1], parts[0]),
        ],
        axis=1,
    )
    normed_grad, out_pieces = lax.optimization_barrier((normed_grad, out_pieces))
    output = (residual + add_all(out_pieces)).astype(bf16)
    own_features = own_weight.shape[0]
    gain_own = lax.dynamic_slice_in_dim(first_gain, shard_index * own_features, own_features)
    gain_part = (
        jnp.sum(own_weight.astype(jnp.float32) * grad_qkv[:, :all_columns], axis=1) / gain_own
    )
    grad_query = grad_qkv[:, :query_width]
    grad_key = grad_qkv[:, query_width : query_width + key_width]
    grad_value = grad_qkv[:, query_width + key_width : query_width + 2 * key_width]
    small_grad = jnp.concatenate([small_grad, gain_part[:, None]], axis=1)
    own_small = own_features // seq_count
    small_grad = small_grad.astype(bf16).reshape(seq_count, own_small, -1)
    small_grad = jnp.pad(small_grad, ((0, 0), (0, model_width // seq_count - own_small), (0, 0)))
    last_sum = jnp.concatenate([grad_out, small_grad.reshape(model_width, -1)], axis=1)
    last_sum = lax.psum_scatter(last_sum, "seq", scatter_dimension=0, tiled=True)
    last_sum = last_sum.astype(jnp.float32)
    grad_out = last_sum[:, : w_out.shape[1]]
    small_grad = last_sum[:own_small, w_out.shape[1] :]
    own_factor = rms_parts(own_inputs)
    input_part, _ = rms_backward(own_inputs, own_factor, first_gain, normed_grad)
    tokens_grad = residual_grad + input_part
    pre_grads = [part.astype(jnp.float32) for part in pre_grads]
    grad_gate = jnp.stack([part[:, :hidden_units] for part in pre_grads])
    grad_up = jnp.stack([part[:, hidden_units:] for part in pre_grads])
    return (
        output,
        tokens_grad,
        grad_query,
        grad_key,
        grad_value,
        grad_out,
        small_grad[:, experts_all + 1],
        small_grad[:, experts_all],
        small_grad[:, :experts_all],
        grad_gate,
        grad_up,
        grad_down,
    )


def solution(mesh):
    return jax.shard_map(
        on_device,
        mesh=mesh,
        in_specs=(
            P(("shard", "seq"), None),
            P(("shard", "seq"), None),
            P("shard", "seq"),
            P("shard", "seq"),
            P("shard", "seq"),
            P("seq", "shard"),
            P(("shard", "seq")),
            P(("shard", "seq")),
            P(("shard", "seq"), None),
            P("shard", None, None),
            P("shard", None, None),
            P("shard", None, None),
            P(("shard", "seq"), None),
        ),
        out_specs=(
            P(("shard", "seq"), None),
            P(("shard", "seq"), None),
            P("shard", "seq"),
            P("shard", "seq"),
            P("shard", "seq"),
            P("seq", "shard"),
            P(("shard", "seq")),
            P(("shard", "seq")),
            P(("shard", "seq"), None),
            P("shard", "seq", None),
            P("shard", "seq", None),
            P("shard", None, "seq"),
        ),
        check_vma=False,
    )
```
